32 devices in a mesh: ctx: 2 (over core), fsdp: 16 (over z, y, x).
Axes of the slice: x: 2, y: 2, z: 4, core: 2. Of those that a mesh axis runs over, the one named last changes fastest.
Arguments:
- states: bfloat16 [16, 1024, 768], P('fsdp', 'ctx'), may hold values from -6 to 6
- encoded: bfloat16 [16, 1024, 768], P('fsdp', 'ctx'), may hold values from -6 to 6
- lengths: int32 [16], P('fsdp'), may hold values from 256 to 1024, as said below
- block_order: int32 [8], replicated, may hold values from 0 to 7, as said below
- cotangent: bfloat16 [16, 1024, 768], P('fsdp', 'ctx'), may hold values from -6 to 6
- self_project: bfloat16 [768, 2304], P('fsdp'), may hold values from -0.3125 to 0.3125
- self_bias: bfloat16 [2, 768], P(None, 'fsdp'), may hold values from -4 to 4
- self_output: bfloat16 [768, 768], P('fsdp'), may hold values from -1.25 to 1.25
- self_shift: bfloat16 [768], P('fsdp'), may hold values from -4 to 4
- cross_query: bfloat16 [768, 768], P('fsdp'), may hold values from -0.3125 to 0.3125
- cross_keyval: bfloat16 [768, 1536], P('fsdp'), may hold values from -0.3125 to 0.3125
- cross_bias: bfloat16 [2, 768], P(None, 'fsdp'), may hold values from -4 to 4
- cross_output: bfloat16 [768, 768], P('fsdp'), may hold values from -0.875 to 0.875
- cross_shift: bfloat16 [768], P('fsdp'), may hold values from -4 to 4
- feed_inner: bfloat16 [768, 3072], P('fsdp'), may hold values from -0.21875 to 0.21875
- inner_bias: bfloat16 [3072], P('fsdp'), may hold values from -4 to 4
- feed_outer: bfloat16 [3072, 768], P('fsdp'), may hold values from -0.109375 to 0.109375
- outer_bias: bfloat16 [768], P('fsdp'), may hold values from -4 to 4
- norm_gain: bfloat16 [3, 768], P(None, 'fsdp'), may hold values from 0.5 to 1.5
- norm_shift: bfloat16 [3, 768], P(None, 'fsdp'), may hold values from -4 to 4
Outputs:
- output: float32 [16, 1024, 768], P('fsdp', 'ctx')
- grad_states: float32 [16, 1024, 768], P('fsdp', 'ctx')
- grad_encoded: float32 [16, 1024, 768], P('fsdp', 'ctx')
- grad_self_project: float32 [768, 2304], P('fsdp')
- grad_self_bias: float32 [2, 768], P(None, 'fsdp')
- grad_self_output: float32 [768, 768], P('fsdp')
- grad_self_shift: float32 [768], P('fsdp')
- grad_cross_query: float32 [768, 768], P('fsdp')
- grad_cross_keyval: float32 [768, 1536], P('fsdp')
- grad_cross_bias: float32 [2, 768], P(None, 'fsdp')
- grad_cross_output: float32 [768, 768], P('fsdp')
- grad_cross_shift: float32 [768], P('fsdp')
- grad_feed_inner: float32 [768, 3072], P('fsdp')
- grad_inner_bias: float32 [3072], P('fsdp')
- grad_feed_outer: float32 [3072, 768], P('fsdp')
- grad_outer_bias: float32 [768], P('fsdp')
- grad_norm_gain: float32 [3, 768], P(None, 'fsdp')
- grad_norm_shift: float32 [3, 768], P(None, 'fsdp')
The draws below stay inside these ranges and needn't reach their ends.
Inputs may be any that keep to these rules, and one draw needn't show every extreme that they name: `lengths`: every sequence has 256 or more valid positions; in every draw some sequence is full. `block_order`: A permutation of the position blocks; entries 2 i and 2 i + 1 add up to 7 for every i.
All inputs are finite; a program needn't handle non-finite values.
Results may differ from the reference program's by a relative error of at most 0.03.
Values may be sent and summed in bfloat16 or wider, within the bound.
A program may use at most 192 MiB of HBM per device.

```python
import math
import jax
import jax.numpy as jnp
from jax import lax

D = 768
H = 12
HD = 64
FF = 3072
QBLK = 128
ENC = 1024
NSEQ = 16
L = 1024
NBLK = 8


def draw_lengths(key, part):
    pick_key, fill_key = jax.random.split(key)
    drawn_values = jax.random.randint(fill_key, (NSEQ,), L // 4, L + 1)
    chosen = jax.random.randint(pick_key, (), 0, NSEQ)
    return jnp.where(jnp.arange(NSEQ) == chosen, L, drawn_values).astype(jnp.int32)


def draw_block_order(key, part):
    pair_key, flip_key = jax.random.split(key)
    half_count = NBLK // 2
    pair_ids = jax.random.permutation(pair_key, half_count)
    flip_bits = jax.random.randint(flip_key, (half_count,), 0, 2)
    leading = jnp.where(flip_bits == 1, pair_ids, NBLK - 1 - pair_ids)
    return jnp.stack([leading, NBLK - 1 - leading], axis=1).reshape(NBLK).astype(jnp.int32)


def steps_of(key, extent, pieces, low, largest):
    level = 1.0
    for axis_at, parts in pieces:
        draws = jax.random.uniform(jax.random.fold_in(jax.random.fold_in(key, 6), axis_at), (parts,), jnp.float32, low / len(pieces), largest / len(pieces))
        level = level * jnp.repeat(jnp.exp(draws), extent[axis_at] // parts).reshape((-1,) + (1,) * (len(extent) - 1 - axis_at))
    return level


def noise(key, extent, spread, limit, shards=(), kind=jnp.bfloat16):
    drawn = spread * jax.random.normal(key, extent, jnp.float32)
    if shards:
        drawn = drawn * steps_of(key, extent, shards, -0.22, 0.18)
    return jnp.clip(drawn, -limit, limit).astype(kind)


def setup_inputs(seed: int = 0) -> dict:
    key_of = jax.random.split(jax.random.key(seed), 21)
    return {
        "states": noise(key_of[0], (NSEQ, L, D), 1.0, 6.0, ((0, 16), (1, 2))),
        "encoded": noise(key_of[1], (NSEQ, ENC, D), 1.0, 6.0, ((0, 16), (1, 2))),
        "lengths": draw_lengths(jax.random.fold_in(key_of[20], 71), 0),
        "block_order": draw_block_order(jax.random.fold_in(key_of[20], 71), 0),
        "cotangent": noise(key_of[4], (NSEQ, L, D), 1.0, 6.0, ((0, 16), (1, 2))),
        "self_project": noise(key_of[5], (D, 3 * D), (D // 2) ** -0.5, 0.3125, ((0, 16),)),
        "self_bias": noise(key_of[6], (2, D), 0.3, 4.0, ((1, 16),)),
        "self_output": noise(key_of[7], (D, D), (D // 32) ** -0.5, 1.25, ((0, 16),)),
        "self_shift": noise(key_of[8], (D,), 0.3, 4.0, ((0, 16),)),
        "cross_query": noise(key_of[9], (D, D), (D // 2) ** -0.5, 0.3125, ((0, 16),)),
        "cross_keyval": noise(key_of[10], (D, 2 * D), (D // 2) ** -0.5, 0.3125, ((0, 16),)),
        "cross_bias": noise(key_of[11], (2, D), 0.3, 4.0, ((1, 16),)),
        "cross_output": noise(key_of[12], (D, D), (D // 16) ** -0.5, 0.875, ((0, 16),)),
        "cross_shift": noise(key_of[13], (D,), 0.3, 4.0, ((0, 16),)),
        "feed_inner": noise(key_of[14], (D, FF), D ** -0.5, 0.21875, ((0, 16),)),
        "inner_bias": noise(key_of[15], (FF,), 0.3, 4.0, ((0, 16),)),
        "feed_outer": noise(key_of[16], (FF, D), FF ** -0.5, 0.109375, ((0, 16),)),
        "outer_bias": noise(key_of[17], (D,), 0.3, 4.0, ((0, 16),)),
        "norm_gain": jnp.clip(1.0 + 0.1 * jax.random.normal(key_of[18], (3, D), jnp.float32), 0.5, 1.5).astype(jnp.bfloat16),
        "norm_shift": noise(key_of[19], (3, D), 0.3, 4.0, ((1, 16),)),
    }


EPSILON = 1e-05
ATTN_SCALE = 0.125
MASKED_SCORE = -1e+30
PRECISE = lax.Precision.HIGHEST

@jax.custom_vjp
def low(v):
    return lax.optimization_barrier(v.astype(jnp.bfloat16)).astype(jnp.float32)

@jax.custom_vjp
def low_back(v):
    return v

def low_keep(v):
    return (low(v), None)

def low_pass(kept, grad):
    return (grad,)

def back_keep(v):
    return (v, None)

def back_low(kept, grad):
    return (low(grad),)
low.defvjp(low_keep, low_pass)
low_back.defvjp(back_keep, back_low)

def matmul(left, right):
    return jnp.dot(left, right, precision=PRECISE, preferred_element_type=jnp.float32)

def layer_norm(inputs, scale_vec, shift_vec):
    average = lax.optimization_barrier(jnp.mean(inputs, axis=-1, keepdims=True))
    centred = inputs - average
    variance = lax.optimization_barrier(jnp.mean(centred * centred, axis=-1, keepdims=True))
    return centred * lax.rsqrt(variance + EPSILON) * scale_vec + shift_vec

def gelu_exact(inputs):
    return jax.nn.gelu(inputs, approximate=False)

def attend(queries, all_keys, all_values, query_places, key_places, seq_length, causal):
    row_count = queries.shape[0]
    block_size = math.gcd(row_count, 512)
    key_heads = all_keys.reshape(all_keys.shape[0], H, HD)
    value_heads = all_values.reshape(all_values.shape[0], H, HD)
    query_blocks = queries.reshape(row_count // block_size, block_size, H, HD)
    place_blocks = query_places.reshape(row_count // block_size, block_size)

    def one_block(element):
        query_block, query_place = element
        scores = low_back(jnp.einsum('qhd,khd->hqk', query_block, key_heads, precision=PRECISE))
        if causal:
            allowed = (key_places[None, :] <= query_place[:, None]) & (key_places[None, :] < seq_length)
            scores = jnp.where(allowed[None], scores, MASKED_SCORE)
        highest = lax.optimization_barrier(jnp.max(scores, axis=-1, keepdims=True))
        exponent = jnp.exp(scores - highest)
        attn_prob = low(exponent / lax.optimization_barrier(jnp.sum(exponent, axis=-1, keepdims=True)))
        attended = jnp.einsum('hqk,khd->qhd', attn_prob, value_heads, precision=PRECISE)
        return attended.reshape(block_size, H * HD)
    return lax.map(jax.checkpoint(one_block), (query_blocks, place_blocks)).reshape(row_count, H * HD)

def one_sequence(parameters, inputs, encoder, seq_length, places):
    self_project, self_bias, self_output, self_shift, cross_query, cross_keyval, cross_bias, cross_output, cross_shift, feed_inner, inner_bias, feed_outer, outer_bias, norm_gain, norm_shift = parameters
    projected = low_back(matmul(inputs, self_project))
    queries = low((projected[:, :D] + self_bias[0]) * ATTN_SCALE)
    self_keys = low(projected[:, D:2 * D])
    self_values = low(projected[:, 2 * D:] + self_bias[1])
    self_mixed = low(low_back(attend(queries, self_keys, self_values, places, places, seq_length, True)))
    after_self = layer_norm(inputs + low_back(matmul(self_mixed, self_output)) + self_shift, norm_gain[0], norm_shift[0])
    after_self_low = low(after_self)
    cross_queries = low((low_back(matmul(after_self_low, cross_query)) + cross_bias[0]) * ATTN_SCALE)
    encoder_proj = low_back(matmul(encoder, cross_keyval))
    cross_keys = low(encoder_proj[:, :D])
    cross_values = low(encoder_proj[:, D:] + cross_bias[1])
    encoder_places = jnp.zeros((encoder.shape[0],), jnp.int32)
    cross_mixed = low(low_back(attend(cross_queries, cross_keys, cross_values, places, encoder_places, seq_length, False)))
    after_cross = layer_norm(after_self + low_back(matmul(cross_mixed, cross_output)) + cross_shift, norm_gain[1], norm_shift[1])
    hidden = low(gelu_exact(low_back(matmul(low(after_cross), feed_inner)) + inner_bias))
    finished = layer_norm(after_cross + low_back(matmul(hidden, feed_outer)) + outer_bias, norm_gain[2], norm_shift[2])
    return jnp.where((places < seq_length)[:, None], finished, 0.0)

def reference(states, encoded, lengths, block_order, cotangent, self_project, self_bias, self_output, self_shift, cross_query, cross_keyval, cross_bias, cross_output, cross_shift, feed_inner, inner_bias, feed_outer, outer_bias, norm_gain, norm_shift):
    places = (block_order[:, None] * QBLK + jnp.arange(QBLK, dtype=jnp.int32)[None, :]).reshape(-1).astype(jnp.int32)
    parameters = tuple((weight.astype(jnp.float32) for weight in (self_project, self_bias, self_output, self_shift, cross_query, cross_keyval, cross_bias, cross_output, cross_shift, feed_inner, inner_bias, feed_outer, outer_bias, norm_gain, norm_shift)))
    sequence_fn = jax.checkpoint(one_sequence)

    def forward(parameters, inputs_all, encoder_all):

        def scan_step(carried, element):
            inputs, encoder, seq_length = element
            return (carried, sequence_fn(parameters, inputs, encoder, seq_length, places))
        _, outputs = lax.scan(scan_step, jnp.zeros((), jnp.float32), (inputs_all, encoder_all, lengths))
        return outputs
    outputs, pullback = jax.vjp(forward, parameters, states.astype(jnp.float32), encoded.astype(jnp.float32))
    grad_params, grad_states, grad_encoded = pullback(cotangent.astype(jnp.float32))
    return (outputs, grad_states, grad_encoded, grad_params[0], grad_params[1], grad_params[2], grad_params[3], grad_params[4], grad_params[5], grad_params[6], grad_params[7], grad_params[8], grad_params[9], grad_params[10], grad_params[11], grad_params[12], grad_params[13], grad_params[14])
```

```python
import functools

import jax
import jax.numpy as jnp
from jax import lax
from jax.experimental import pallas as pl
from jax.experimental.pallas import tpu as pltpu
from jax.sharding import PartitionSpec as P

H = 12
HD = 64
QBLK = 128
PAIR = 2 * HD
ATTN_SCALE = 0.125
MASKED_SCORE = -1e30
EPSILON = 1e-05
MESH = pl.DeviceIdType.MESH
VMEM_LIMIT = 60 * 1024 * 1024
BF16 = jnp.bfloat16
F32 = jnp.float32


def dot_nn(left, right):
    return lax.dot_general(left, right, (((1,), (0,)), ((), ())), preferred_element_type=F32)


def dot_nt(left, right):
    return lax.dot_general(left, right, (((1,), (1,)), ((), ())), preferred_element_type=F32)


def dot_tn(left, right):
    return lax.dot_general(left, right, (((0,), (0,)), ((), ())), preferred_element_type=F32)


def layer_norm(inputs, scale_vec, shift_vec):
    average = jnp.mean(inputs, axis=-1, keepdims=True)
    centred = inputs - average
    variance = jnp.mean(centred * centred, axis=-1, keepdims=True)
    return centred * lax.rsqrt(variance + EPSILON) * scale_vec + shift_vec


def gelu_exact(inputs):
    return jax.nn.gelu(inputs, approximate=False)


def stack_heads(rows):
    first = lax.broadcasted_iota(jnp.int32, rows.shape, 1) < HD
    zero = jnp.zeros_like(rows)
    return jnp.concatenate([jnp.where(first, rows, zero), jnp.where(first, zero, rows)], axis=0)


def unstack_heads(both, count):
    return jnp.concatenate([both[:HD, :count], both[HD:, count:]], axis=0).T


def variants_of(key_count, causal):
    if not causal:
        return [key_count]
    step = max(2 * QBLK, key_count // 4)
    return [step * (i + 1) for i in range(key_count // step)]


def load_keys(causal, places, sources, target):
    block = 0
    for source in sources:
        for local in range(source.shape[0] // QBLK):
            rows = source[local * QBLK : (local + 1) * QBLK, :]
            if causal:
                at = pl.multiple_of(places[block] * QBLK, QBLK)
                target[pl.ds(at, QBLK), :] = rows
            else:
                target[block * QBLK : (block + 1) * QBLK, :] = rows
            block += 1


def masked_scores(causal, keys, both, place, length, count):
    scores = dot_nt(keys, both)
    if causal:
        column = lax.broadcasted_iota(jnp.int32, (1, 2 * count), 1)
        row_place = place * QBLK + jnp.where(column >= count, column - count, column)
        limit = jnp.minimum(row_place, length - 1)
        key_place = lax.broadcasted_iota(jnp.int32, scores.shape, 0)
        scores = jnp.where(key_place <= limit, scores, MASKED_SCORE)
    return scores


def for_each_block(causal, sizes, block_count, own_places, length, body):
    def step(i, carry):
        if not causal:
            body(i, 0, sizes[0])
            return carry
        place = own_places[i]
        needed = jnp.minimum((place + 1) * QBLK, length)
        for at, size in enumerate(sizes):
            low = sizes[at - 1] if at else 0

            @pl.when((needed > low) & (needed <= size))
            def _(size=size):
                body(i, place, size)

        return carry

    lax.fori_loop(0, block_count, step, 0)


def forward_body(causal, n_src, places, own_places, length_ref, q_ref, *refs):
    key_refs, value_refs = refs[:n_src], refs[n_src : 2 * n_src]
    out_ref, total_ref, keys, values_t = refs[2 * n_src :]
    load_keys(causal, places, key_refs, keys)
    length = length_ref[0]
    block = 0
    for source in value_refs:
        for local in range(source.shape[0] // QBLK):
            rows = source[local * QBLK : (local + 1) * QBLK, :].astype(F32).T.astype(BF16)
            at = pl.multiple_of(places[block] * QBLK, QBLK) if causal else block * QBLK
            values_t[:, pl.ds(at, QBLK)] = rows
            block += 1

    def body(i, place, size):
        rows = pl.ds(pl.multiple_of(i * QBLK, QBLK), QBLK)
        both = stack_heads(q_ref[rows, :])
        scores = masked_scores(causal, keys[:size, :], both, place, length, QBLK)
        highest = jnp.max(scores, axis=0, keepdims=True)
        exponent = jnp.exp(scores - highest)
        total = jnp.sum(exponent, axis=0, keepdims=True)
        mixed = dot_nn(values_t[:, :size], exponent.astype(BF16)) * (1.0 / total)
        out_ref[rows, :] = unstack_heads(mixed, QBLK)
        total_ref[0, pl.ds(i, 1), :] = highest + jnp.log(total)

    for_each_block(
        causal,
        variants_of(keys.shape[0], causal),
        q_ref.shape[0] // QBLK,
        own_places,
        length,
        body,
    )


def attention_forward(causal, queries, keys, values, places, own_places, length):
    rows, width = queries.shape
    n_src = len(keys)
    key_count = sum(k.shape[0] for k in keys)
    pairs = width // PAIR
    column = lambda i, *_: (0, i)
    spec = lambda n: pl.BlockSpec((n, PAIR), column)
    return pl.pallas_call(
        functools.partial(forward_body, causal, n_src),
        grid_spec=pltpu.PrefetchScalarGridSpec(
            num_scalar_prefetch=3,
            grid=(pairs,),
            in_specs=[spec(rows)] + [spec(k.shape[0]) for k in (*keys, *values)],
            out_specs=[
                spec(rows),
                pl.BlockSpec((1, rows // QBLK, 2 * QBLK), lambda i, *_: (i, 0, 0)),
            ],
            scratch_shapes=[
                pltpu.VMEM((key_count, PAIR), BF16),
                pltpu.VMEM((PAIR, key_count), BF16),
            ],
        ),
        out_shape=[
            jax.ShapeDtypeStruct((rows, width), F32),
            jax.ShapeDtypeStruct((pairs, rows // QBLK, 2 * QBLK), F32),
        ],
        compiler_params=pltpu.CompilerParams(vmem_limit_bytes=VMEM_LIMIT),
        name="self_forward" if causal else "cross_forward",
    )(places, own_places, length, queries, *keys, *values)


def backward_body(causal, n_src, places, own_places, length_ref, q_ref, g_ref, o_ref, t_ref, *refs):
    key_refs, value_refs = refs[:n_src], refs[n_src : 2 * n_src]
    dq_ref = refs[2 * n_src]
    dk_refs = refs[2 * n_src + 1 : 3 * n_src + 1]
    dv_refs = refs[3 * n_src + 1 : 4 * n_src + 1]
    keys, values, keys_t, dk, dv = refs[4 * n_src + 1 :]
    load_keys(causal, places, key_refs, keys)
    load_keys(causal, places, value_refs, values)
    length = length_ref[0]
    key_count = keys.shape[0]
    for block in range(key_count // QBLK):
        rows = slice(block * QBLK, (block + 1) * QBLK)
        keys_t[:, rows] = keys[rows, :].astype(F32).T.astype(BF16)
    dk[...] = jnp.zeros_like(dk)
    dv[...] = jnp.zeros_like(dv)

    def body(i, place, size):
        rows = pl.ds(pl.multiple_of(i * QBLK, QBLK), QBLK)
        both = stack_heads(q_ref[rows, :])
        grads = g_ref[rows, :]
        both_grads = stack_heads(grads)
        products = (grads.astype(F32) * o_ref[rows, :]).T
        delta = jnp.concatenate(
            [
                jnp.sum(products[:HD], axis=0, keepdims=True),
                jnp.sum(products[HD:], axis=0, keepdims=True),
            ],
            axis=1,
        )
        scores = masked_scores(causal, keys[:size, :], both, place, length, QBLK)
        prob = jnp.exp(scores - t_ref[0, pl.ds(i, 1), :])
        prob_grad = dot_nt(values[:size, :], both_grads)
        score_grad = (prob * (prob_grad - delta)).astype(BF16)
        dv[:size, :] += dot_nn(prob.astype(BF16), both_grads)
        dk[:size, :] += dot_nn(score_grad, both)
        dq = dot_nn(keys_t[:, :size], score_grad)
        dq_ref[rows, :] = unstack_heads(dq, QBLK) * ATTN_SCALE

    for_each_block(
        causal, variants_of(key_count, causal), q_ref.shape[0] // QBLK, own_places, length, body
    )
    block = 0
    for dk_out, dv_out in zip(dk_refs, dv_refs):
        for local in range(dk_out.shape[0] // QBLK):
            at = pl.multiple_of(places[block] * QBLK, QBLK) if causal else block * QBLK
            rows = slice(local * QBLK, (local + 1) * QBLK)
            dk_out[rows, :] = dk[pl.ds(at, QBLK), :].astype(BF16)
            dv_out[rows, :] = dv[pl.ds(at, QBLK), :].astype(BF16)
            block += 1


def attention_backward(
    causal, queries, grads, mixed, totals, keys, values, places, own_places, length
):
    rows, width = queries.shape
    n_src = len(keys)
    key_count = sum(k.shape[0] for k in keys)
    pairs = width // PAIR
    column = lambda i, *_: (0, i)
    spec = lambda n: pl.BlockSpec((n, PAIR), column)
    key_specs = [spec(k.shape[0]) for k in (*keys, *values)]
    outs = pl.pallas_call(
        functools.partial(backward_body, causal, n_src),
        grid_spec=pltpu.PrefetchScalarGridSpec(
            num_scalar_prefetch=3,
            grid=(pairs,),
            in_specs=[
                spec(rows),
                spec(rows),
                spec(rows),
                pl.BlockSpec((1, rows // QBLK, 2 * QBLK), lambda i, *_: (i, 0, 0)),
            ]
            + key_specs,
            out_specs=[spec(rows)] + key_specs,
            scratch_shapes=[
                pltpu.VMEM((key_count, PAIR), BF16),
                pltpu.VMEM((key_count, PAIR), BF16),
                pltpu.VMEM((PAIR, key_count), BF16),
                pltpu.VMEM((key_count, PAIR), F32),
                pltpu.VMEM((key_count, PAIR), F32),
            ],
        ),
        out_shape=[jax.ShapeDtypeStruct((rows, width), F32)]
        + [jax.ShapeDtypeStruct(k.shape, BF16) for k in (*keys, *values)],
        compiler_params=pltpu.CompilerParams(vmem_limit_bytes=VMEM_LIMIT),
        name="self_backward" if causal else "cross_backward",
    )(places, own_places, length, queries, grads, mixed, totals, *keys, *values)
    return outs[0], outs[1 : n_src + 1], outs[n_src + 1 :]


UNITS = 16
FIRST = 12
HALF = UNITS // 2


def coordinates(n_ctx):
    core, f = lax.axis_index("ctx"), lax.axis_index("fsdp")
    odd = core % 2
    return core, odd, f // 4, (f // 2) % 2, f % 2


def flip(odd, y, x, a, b):
    dx = a * (1 - odd) + b * odd
    dy = b * (1 - odd) + a * odd
    return y + dy * (1 - 2 * y), x + dx * (1 - 2 * x)


def peers_of(core, odd, z, y, x, depth):
    fsdp = lambda zz, yy, xx: (zz * 2 + yy) * 2 + xx
    ups = [(core, fsdp((z + k) % depth, y, x)) for k in range(1, depth)]
    first = (core, fsdp(z, *flip(odd, y, x, 1, 0)))
    second = (core, fsdp(z, *flip(odd, y, x, 0, 1)))
    partner = (core + 1 - 2 * odd, fsdp(z, y, x))
    return ups, first, second, partner


def enter(ups, first, second, partner):
    barrier = pltpu.get_barrier_semaphore()
    for peer in (*ups, first, second, partner):
        pl.semaphore_signal(barrier, inc=1, device_id=peer, device_id_type=MESH)
    pl.semaphore_wait(barrier, len(ups) + 3)


def unit_set(g1, g2, i, odd, y, x):
    if 2 * i < FIRST:
        return g1.at[2 * i + odd, :, y, x]
    return g2.at[:, y, x, 2 * i - FIRST + odd]


def unit_block(g1, g2, i, odd, z, y, x):
    if 2 * i < FIRST:
        return g1.at[2 * i + odd, z, y, x]
    return g2.at[z, y, x, 2 * i - FIRST + odd]


def gather_body(
    depth, sp, so, cq, ckv, co, fi, fo, g1, g2, own, load_sem, own_sem,
    zs, zr, fs, fr, ss, sr, ps, pr,
):
    core, odd, z, y, x = coordinates(None)
    ups, first, second, partner = peers_of(core, odd, z, y, x, depth)
    width = so.shape[1]
    rows = so.shape[0]
    sources = (
        [sp.at[:, pl.ds(j * width, width)] for j in range(3)]
        + [so, cq]
        + [ckv.at[:, pl.ds(j * width, width)] for j in range(2)]
        + [co]
        + [fi.at[:, pl.ds(j * width, width)] for j in range(4)]
        + [fo.at[pl.ds(j * rows, rows), :] for j in range(4)]
    )
    loads = [pltpu.make_async_copy(s, own.at[u], load_sem.at[u]) for u, s in enumerate(sources)]
    for load in loads:
        load.start()
    enter(ups, first, second, partner)

    def remote(source, target, send, recv, peer):
        return pltpu.make_async_remote_copy(
            source, target, send, recv, device_id=peer, device_id_type=MESH
        )

    def set_of(i, a, b):
        return unit_set(g1, g2, i, odd, *flip(odd, y, x, a, b))

    def up_copy(i, k):
        block = own.at[2 * i + odd]
        return remote(
            block, unit_block(g1, g2, i, odd, z, y, x), zs.at[i, k], zr.at[i, k], ups[k]
        )

    def up_arrival(i, k):
        block = unit_block(g1, g2, i, odd, (z + depth - 1 - k) % depth, y, x)
        return remote(block, block, zs.at[i, k], zr.at[i, k], ups[k])

    def first_copy(i):
        return remote(set_of(i, 0, 0), set_of(i, 0, 0), fs.at[i], fr.at[i], first)

    def second_copy(i, a):
        return remote(set_of(i, a, 0), set_of(i, a, 0), ss.at[i, a], sr.at[i, a], second)

    def partner_copy(i, a, b):
        at = a + 2 * b
        return remote(set_of(i, a, b), set_of(i, a, b), ps.at[i, at], pr.at[i, at], partner)

    def arrival(target, send, recv, peer):
        return remote(target, target, send, recv, peer)

    keeps = []
    for i in range(HALF):
        loads[2 * i].wait()
        loads[2 * i + 1].wait()
        keep = pltpu.make_async_copy(
            own.at[2 * i + odd], unit_block(g1, g2, i, odd, z, y, x), own_sem.at[i]
        )
        keep.start()
        keeps.append(keep)
        for k in range(depth - 1):
            up_copy(i, k).start()
    for step in range(HALF + 2):
        i = step
        if i < HALF:
            keeps[i].wait()
            for k in range(depth - 1):
                up_arrival(i, k).wait_recv()
            first_copy(i).start()
            second_copy(i, 0).start()
            partner_copy(i, 0, 0).start()
        i = step - 1
        if 0 <= i < HALF:
            arrival(set_of(i, 1, 0), fs.at[i], fr.at[i], first).wait_recv()
            second_copy(i, 1).start()
            partner_copy(i, 1, 0).start()
        i = step - 2
        if 0 <= i < HALF:
            for a in range(2):
                arrival(set_of(i, a, 1), ss.at[i, a], sr.at[i, a], second).wait_recv()
                partner_copy(i, a, 1).start()
    for i in range(HALF):
        for a in range(2):
            for b in range(2):
                at = a + 2 * b
                there = unit_set(g1, g2, i, 1 - odd, *flip(1 - odd, y, x, a, b))
                arrival(there, ps.at[i, at], pr.at[i, at], partner).wait_recv()
                partner_copy(i, a, b).wait_send()
            second_copy(i, a).wait_send()
        first_copy(i).wait_send()
        for k in range(depth - 1):
            up_copy(i, k).wait_send()


def gather_weights(n_fsdp, sp, so, cq, ckv, co, fi, fo):
    rows, width = so.shape
    depth = n_fsdp // 4
    dma = pltpu.SemaphoreType.DMA
    g1, g2 = pl.pallas_call(
        functools.partial(gather_body, depth),
        in_specs=[pl.BlockSpec(memory_space=pl.ANY)] * 7,
        out_specs=[pl.BlockSpec(memory_space=pl.ANY)] * 2,
        out_shape=[
            jax.ShapeDtypeStruct((FIRST, depth, 2, 2, rows, width), BF16),
            jax.ShapeDtypeStruct((depth, 2, 2, UNITS - FIRST, rows, width), BF16),
        ],
        scratch_shapes=[
            pltpu.VMEM((UNITS, rows, width), BF16),
            dma((UNITS,)),
            dma((HALF,)),
            dma((HALF, depth - 1)),
            dma((HALF, depth - 1)),
            dma((HALF,)),
            dma((HALF,)),
            dma((HALF, 2)),
            dma((HALF, 2)),
            dma((HALF, 4)),
            dma((HALF, 4)),
        ],
        compiler_params=pltpu.CompilerParams(
            collective_id=0, has_side_effects=True, vmem_limit_bytes=VMEM_LIMIT
        ),
        name="gather_weights",
    )(sp, so, cq, ckv, co, fi, fo)
    return g1.reshape(FIRST, n_fsdp * rows, width), g2.reshape(-1, width)


def scatter_body(
    depth, g1, g2, out, own, from_partner, from_second, from_first, from_up, final, final_in,
    own_sem, zs, zr, fs, fr, ss, sr, ps, pr, xs, xr,
):
    core, odd, z, y, x = coordinates(None)
    ups, first, second, partner = peers_of(core, odd, z, y, x, depth)

    def remote(source, target, send, recv, peer):
        return pltpu.make_async_remote_copy(
            source, target, send, recv, device_id=peer, device_id_type=MESH
        )

    order = ((0, 1), (1, 1), (1, 0), (0, 0))

    def own_copy(i, a, b):
        at = a + 2 * b
        source = unit_set(g1, g2, i, odd, *flip(odd, y, x, a, b))
        return pltpu.make_async_copy(source, own.at[i, at], own_sem.at[i, at])

    def partner_copy(i, a, b):
        at = a + 2 * b
        source = unit_set(g1, g2, i, 1 - odd, *flip(1 - odd, y, x, a, b))
        return remote(source, from_partner.at[i, at], ps.at[i, at], pr.at[i, at], partner)

    def second_copy(i, a):
        return remote(
            own.at[i, a + 2], from_second.at[i, a], ss.at[i, a], sr.at[i, a], second
        )

    def first_copy(i):
        return remote(own.at[i, 1], from_first.at[i], fs.at[i], fr.at[i], first)

    def up_copy(i, k):
        return remote(
            own.at[i, 0, (z + 1 + k) % depth],
            from_up.at[i, k],
            zs.at[i, k],
            zr.at[i, k],
            ups[k],
        )

    def final_copy(i):
        return remote(final.at[i], final_in.at[i], xs.at[i], xr.at[i], partner)

    def add(target, source):
        def step(j, carry):
            target[j] = target[j] + source[j]
            return carry

        lax.fori_loop(0, depth, step, 0)

    for i in range(HALF):
        for a, b in order:
            own_copy(i, a, b).start()
    enter(ups, first, second, partner)
    for i in range(HALF):
        for a, b in order:
            partner_copy(i, a, b).start()

    for step in range(HALF + 3):
        i = step
        if i < HALF:
            for a, b in order:
                at = a + 2 * b
                own_copy(i, a, b).wait()
                partner_copy(i, a, b).wait_recv()
                add(own.at[i, at], from_partner.at[i, at])
                if b:
                    second_copy(i, a).start()
        i = step - 1
        if 0 <= i < HALF:
            for a in (1, 0):
                second_copy(i, a).wait_recv()
                add(own.at[i, a], from_second.at[i, a])
                if a:
                    first_copy(i).start()
        i = step - 2
        if 0 <= i < HALF:
            first_copy(i).wait_recv()
            add(own.at[i, 0], from_first.at[i])
            for k in range(depth - 1):
                up_copy(i, k).start()
        i = step - 3
        if 0 <= i < HALF:
            total = own[i, 0, z].astype(F32)
            for k in range(depth - 1):
                up_copy(i, k).wait_recv()
                total = total + from_up[i, k].astype(F32)
            final[i] = total
            final_copy(i).start()
            out[2 * i + odd] = total
    for i in range(HALF):
        final_copy(i).wait()
        out[2 * i + 1 - odd] = final_in[i]
        for a, b in order:
            partner_copy(i, a, b).wait_send()
        for a in range(2):
            second_copy(i, a).wait_send()
        first_copy(i).wait_send()
        for k in range(depth - 1):
            up_copy(i, k).wait_send()


def scatter_gradients(n_fsdp, g1, g2):
    width = g1.shape[-1]
    depth = n_fsdp // 4
    rows = width // n_fsdp
    dma = pltpu.SemaphoreType.DMA
    vmem = pltpu.VMEM
    return pl.pallas_call(
        functools.partial(scatter_body, depth),
        in_specs=[pl.BlockSpec(memory_space=pl.ANY)] * 2,
        out_specs=pl.BlockSpec(memory_space=pltpu.VMEM),
        out_shape=jax.ShapeDtypeStruct((UNITS, rows, width), F32),
        scratch_shapes=[
            vmem((HALF, 4, depth, rows, width), BF16),
            vmem((HALF, 4, depth, rows, width), BF16),
            vmem((HALF, 2, depth, rows, width), BF16),
            vmem((HALF, depth, rows, width), BF16),
            vmem((HALF, depth - 1, rows, width), BF16),
            vmem((HALF, rows, width), F32),
            vmem((HALF, rows, width), F32),
            dma((HALF, 4)),
            dma((HALF, depth - 1)),
            dma((HALF, depth - 1)),
            dma((HALF,)),
            dma((HALF,)),
            dma((HALF, 2)),
            dma((HALF, 2)),
            dma((HALF, 4)),
            dma((HALF, 4)),
            dma((HALF,)),
            dma((HALF,)),
        ],
        compiler_params=pltpu.CompilerParams(
            collective_id=1, has_side_effects=True, vmem_limit_bytes=VMEM_LIMIT
        ),
        name="scatter_gradients",
    )(
        g1.reshape(FIRST, depth, 2, 2, rows, width),
        g2.reshape(depth, 2, 2, UNITS - FIRST, rows, width),
    )


def per_device(
    n_ctx,
    n_fsdp,
    states,
    encoded,
    lengths,
    block_order,
    cotangent,
    self_project,
    self_bias,
    self_output,
    self_shift,
    cross_query,
    cross_keyval,
    cross_bias,
    cross_output,
    cross_shift,
    feed_inner,
    inner_bias,
    feed_outer,
    outer_bias,
    norm_gain,
    norm_shift,
):
    local_rows = states.shape[1]
    width = states.shape[2]
    rows = self_output.shape[0]
    local_blocks = local_rows // QBLK
    core = lax.axis_index("ctx")
    own_order = lax.dynamic_slice_in_dim(block_order, core * local_blocks, local_blocks)
    own_places = (own_order[:, None] * QBLK + jnp.arange(QBLK, dtype=jnp.int32)).reshape(-1)
    valid_rows = (own_places < lengths[0])[:, None]

    def exchange(array):
        perm = [
            (c * n_fsdp + f, (c ^ 1) * n_fsdp + f) for c in range(n_ctx) for f in range(n_fsdp)
        ]
        return lax.ppermute(array, ("ctx", "fsdp"), perm)

    if n_ctx == 2:
        other_order = lax.dynamic_slice_in_dim(
            block_order, (1 - core) * local_blocks, local_blocks
        )
        places = jnp.concatenate([own_order, other_order])
        spread = lambda array: (array, exchange(array))
        collect = lambda parts: parts[0].astype(F32) + exchange(parts[1]).astype(F32)
    else:
        places = block_order
        spread = lambda array: (lax.all_gather(array, "ctx", axis=0, tiled=True),)
        collect = lambda parts: lax.psum_scatter(
            parts[0], "ctx", scatter_dimension=0, tiled=True
        ).astype(F32)

    vectors = jnp.concatenate(
        [
            self_bias,
            self_shift[None],
            cross_bias,
            cross_shift[None],
            inner_bias.reshape(-1, rows),
            outer_bias[None],
            norm_gain,
            norm_shift,
        ],
        axis=0,
    )
    inner_rows = inner_bias.shape[0] // rows
    all_vectors = lax.all_gather(vectors, "fsdp", axis=0)
    inner_full = all_vectors[:, 6 : 6 + inner_rows].reshape(-1).astype(F32)
    flat = jnp.transpose(all_vectors, (1, 0, 2)).reshape(vectors.shape[0], -1).astype(F32)
    b_q, b_v, b_so, b_cq, b_cv, b_co = (flat[i] for i in range(6))
    at = 6 + inner_rows
    b_fo = flat[at]
    gain = flat[at + 1 : at + 4]
    shift = flat[at + 4 : at + 7]

    units, w_fo = gather_weights(
        n_fsdp, self_project, self_output, cross_query, cross_keyval, cross_output, feed_inner, feed_outer
    )
    w_q, w_k, w_v, w_so, w_cq, w_ck, w_cv, w_co = (units[i] for i in range(8))
    w_fi = [units[8 + i] for i in range(4)]

    inputs = states[0]
    encoder_rows = encoded[0]
    queries = ((dot_nn(inputs, w_q) + b_q) * ATTN_SCALE).astype(BF16)
    own_keys = dot_nn(inputs, w_k).astype(BF16)
    own_values = (dot_nn(inputs, w_v) + b_v).astype(BF16)
    own_cross_keys = dot_nn(encoder_rows, w_ck).astype(BF16)
    own_cross_values = (dot_nn(encoder_rows, w_cv) + b_cv).astype(BF16)
    keys, values = spread(own_keys), spread(own_values)
    cross_keys, cross_values = spread(own_cross_keys), spread(own_cross_values)

    attend = functools.partial(attention_forward, places=places, own_places=own_order, length=lengths)
    self_attended, self_total = attend(True, queries, keys, values)
    self_mixed = self_attended.astype(BF16)
    after_self, norm_back_one = jax.vjp(
        layer_norm, inputs.astype(F32) + dot_nn(self_mixed, w_so) + b_so, gain[0], shift[0]
    )
    after_self_low = after_self.astype(BF16)
    cross_queries = ((dot_nn(after_self_low, w_cq) + b_cq) * ATTN_SCALE).astype(BF16)
    cross_attended, cross_total = attend(False, cross_queries, cross_keys, cross_values)
    cross_mixed = cross_attended.astype(BF16)
    after_cross, norm_back_two = jax.vjp(
        layer_norm, after_self + dot_nn(cross_mixed, w_co) + b_co, gain[1], shift[1]
    )
    after_cross_low = after_cross.astype(BF16)
    inner_pre = jnp.concatenate([dot_nn(after_cross_low, w) for w in w_fi], axis=1) + inner_full
    inner_act, gelu_back = jax.vjp(gelu_exact, inner_pre)
    inner_low = inner_act.astype(BF16)
    finished, norm_back_three = jax.vjp(
        layer_norm, after_cross + dot_nn(inner_low, w_fo) + b_fo, gain[2], shift[2]
    )
    output = jnp.where(valid_rows, finished, 0.0)

    grad_final = jnp.where(valid_rows, cotangent[0].astype(F32), 0.0)
    grad_three, gain_three, shift_three = norm_back_three(grad_final)
    grad_three_low = grad_three.astype(BF16)
    d_fo = dot_tn(inner_low, grad_three_low).astype(BF16)
    (grad_inner_pre,) = gelu_back(dot_nt(grad_three_low, w_fo))
    grad_inner_low = grad_inner_pre.astype(BF16)
    parts = [grad_inner_low[:, i * width : (i + 1) * width] for i in range(4)]
    d_fi = [dot_tn(after_cross_low, p).astype(BF16) for p in parts]
    back = sum(dot_nt(p, w) for p, w in zip(parts, w_fi))
    grad_two, gain_two, shift_two = norm_back_two(grad_three + back)
    grad_two_low = grad_two.astype(BF16)
    d_co = dot_tn(cross_mixed, grad_two_low).astype(BF16)
    grad_cross_mixed = dot_nt(grad_two_low, w_co).astype(BF16)
    attend_back = functools.partial(
        attention_backward, places=places, own_places=own_order, length=lengths
    )
    cross_query_grad, ck_parts, cv_parts = attend_back(
        False, cross_queries, grad_cross_mixed, cross_attended, cross_total, cross_keys, cross_values
    )
    cross_query_low = cross_query_grad.astype(BF16)
    d_cq = dot_tn(after_self_low, cross_query_low).astype(BF16)
    ck_grad, cv_grad = collect(ck_parts), collect(cv_parts)
    ck_low, cv_low = ck_grad.astype(BF16), cv_grad.astype(BF16)
    d_ck = dot_tn(encoder_rows, ck_low).astype(BF16)
    d_cv = dot_tn(encoder_rows, cv_low).astype(BF16)
    grad_encoded = dot_nt(ck_low, w_ck) + dot_nt(cv_low, w_cv)
    grad_one, gain_one, shift_one = norm_back_one(grad_two + dot_nt(cross_query_low, w_cq))
    grad_one_low = grad_one.astype(BF16)
    d_so = dot_tn(self_mixed, grad_one_low).astype(BF16)
    grad_self_mixed = dot_nt(grad_one_low, w_so).astype(BF16)
    query_grad, k_parts, v_parts = attend_back(
        True, queries, grad_self_mixed, self_attended, self_total, keys, values
    )
    query_low = query_grad.astype(BF16)
    key_grad, value_grad = collect(k_parts), collect(v_parts)
    key_low, value_low = key_grad.astype(BF16), value_grad.astype(BF16)
    d_q = dot_tn(inputs, query_low).astype(BF16)
    d_k = dot_tn(inputs, key_low).astype(BF16)
    d_v = dot_tn(inputs, value_low).astype(BF16)
    grad_states = grad_one + dot_nt(query_low, w_q) + dot_nt(key_low, w_k) + dot_nt(value_low, w_v)

    column_sum = lambda array: jnp.sum(array, axis=0)
    grad_vectors = jnp.stack(
        [
            column_sum(query_grad),
            column_sum(value_grad),
            column_sum(grad_one),
            column_sum(cross_query_grad),
            column_sum(cv_grad),
            column_sum(grad_two),
            column_sum(grad_three),
            gain_one,
            gain_two,
            gain_three,
            shift_one,
            shift_two,
            shift_three,
        ]
    ).reshape(13, n_fsdp, rows)
    inner_vector = column_sum(grad_inner_pre).reshape(n_fsdp, inner_rows, rows)
    packed = jnp.concatenate([jnp.transpose(grad_vectors, (1, 0, 2)), inner_vector], axis=1)
    summed = lax.psum(packed.astype(BF16), ("ctx", "fsdp")).astype(F32)
    mine = lax.dynamic_index_in_dim(summed, lax.axis_index("fsdp"), 0, keepdims=False)

    shards = scatter_gradients(
        n_fsdp,
        jnp.stack([d_q, d_k, d_v, d_so, d_cq, d_ck, d_cv, d_co, *d_fi]),
        d_fo,
    )
    if n_ctx > 2:
        groups = [[c for c in range(n_ctx) if c % 2 == odd] for odd in range(2)]
        shards = lax.psum(shards.astype(BF16), "ctx", axis_index_groups=groups).astype(F32)
    return (
        output[None],
        grad_states[None],
        grad_encoded[None],
        jnp.concatenate([shards[0], shards[1], shards[2]], axis=1),
        mine[0:2],
        shards[3],
        mine[2],
        shards[4],
        jnp.concatenate([shards[5], shards[6]], axis=1),
        mine[3:5],
        shards[7],
        mine[5],
        jnp.concatenate([shards[8 + i] for i in range(4)], axis=1),
        mine[13:].reshape(-1),
        shards[12:].reshape(-1, width),
        mine[6],
        mine[7:10],
        mine[10:13],
    )


def solution(mesh):
    return jax.shard_map(
        functools.partial(per_device, mesh.shape["ctx"], mesh.shape["fsdp"]),
        mesh=mesh,
        in_specs=(
            P("fsdp", "ctx", None),
            P("fsdp", "ctx", None),
            P("fsdp"),
            P(),
            P("fsdp", "ctx", None),
            P("fsdp", None),
            P(None, "fsdp"),
            P("fsdp", None),
            P("fsdp"),
            P("fsdp", None),
            P("fsdp", None),
            P(None, "fsdp"),
            P("fsdp", None),
            P("fsdp"),
            P("fsdp", None),
            P("fsdp"),
            P("fsdp", None),
            P("fsdp"),
            P(None, "fsdp"),
            P(None, "fsdp"),
        ),
        out_specs=(
            P("fsdp", "ctx", None),
            P("fsdp", "ctx", None),
            P("fsdp", "ctx", None),
            P("fsdp", None),
            P(None, "fsdp"),
            P("fsdp", None),
            P("fsdp"),
            P("fsdp", None),
            P("fsdp", None),
            P(None, "fsdp"),
            P("fsdp", None),
            P("fsdp"),
            P("fsdp", None),
            P("fsdp"),
            P("fsdp", None),
            P("fsdp"),
            P(None, "fsdp"),
            P(None, "fsdp"),
        ),
        check_vma=False,
    )
```

```python
import functools

import jax
import jax.numpy as jnp
from jax import lax
from jax.experimental import pallas as pl
from jax.experimental.pallas import tpu as pltpu
from jax.sharding import PartitionSpec as P

H = 12
HD = 64
QBLK = 128
PAIR = 2 * HD
ATTN_SCALE = 0.125
MASKED_SCORE = -1e30
EPSILON = 1e-05
MESH = pl.DeviceIdType.MESH
VMEM_LIMIT = 60 * 1024 * 1024
BF16 = jnp.bfloat16
F32 = jnp.float32


def dot_nn(left, right):
    return lax.dot_general(left, right, (((1,), (0,)), ((), ())), preferred_element_type=F32)


def dot_nt(left, right):
    return lax.dot_general(left, right, (((1,), (1,)), ((), ())), preferred_element_type=F32)


def dot_tn(left, right):
    return lax.dot_general(left, right, (((0,), (0,)), ((), ())), preferred_element_type=F32)


def layer_norm(inputs, scale_vec, shift_vec):
    average = jnp.mean(inputs, axis=-1, keepdims=True)
    centred = inputs - average
    variance = jnp.mean(centred * centred, axis=-1, keepdims=True)
    return centred * lax.rsqrt(variance + EPSILON) * scale_vec + shift_vec


def gelu_exact(inputs):
    return jax.nn.gelu(inputs, approximate=False)


def stack_heads(rows):
    first = lax.broadcasted_iota(jnp.int32, rows.shape, 1) < HD
    zero = jnp.zeros_like(rows)
    return jnp.concatenate([jnp.where(first, rows, zero), jnp.where(first, zero, rows)], axis=0)


def unstack_heads(both, count):
    return jnp.concatenate([both[:HD, :count], both[HD:, count:]], axis=0).T


def variants_of(key_count, causal):
    if not causal:
        return [key_count]
    step = max(2 * QBLK, key_count // 4)
    return [step * (i + 1) for i in range(key_count // step)]


def load_keys(causal, places, sources, target):
    block = 0
    for source in sources:
        for local in range(source.shape[0] // QBLK):
            rows = source[local * QBLK : (local + 1) * QBLK, :]
            if causal:
                at = pl.multiple_of(places[block] * QBLK, QBLK)
                target[pl.ds(at, QBLK), :] = rows
            else:
                target[block * QBLK : (block + 1) * QBLK, :] = rows
            block += 1


def masked_scores(causal, keys, both, place, length, count):
    scores = dot_nt(keys, both)
    if causal:
        column = lax.broadcasted_iota(jnp.int32, (1, 2 * count), 1)
        row_place = place * QBLK + jnp.where(column >= count, column - count, column)
        limit = jnp.minimum(row_place, length - 1)
        key_place = lax.broadcasted_iota(jnp.int32, scores.shape, 0)
        scores = jnp.where(key_place <= limit, scores, MASKED_SCORE)
    return scores


def for_each_block(causal, sizes, block_count, own_places, length, body):
    def step(i, carry):
        if not causal:
            body(i, 0, sizes[0])
            return carry
        place = own_places[i]
        needed = jnp.minimum((place + 1) * QBLK, length)
        for at, size in enumerate(sizes):
            low = sizes[at - 1] if at else 0

            @pl.when((needed > low) & (needed <= size))
            def _(size=size):
                body(i, place, size)

        return carry

    lax.fori_loop(0, block_count, step, 0)


def forward_body(causal, n_src, places, own_places, length_ref, q_ref, *refs):
    key_refs, value_refs = refs[:n_src], refs[n_src : 2 * n_src]
    out_ref, total_ref, keys, values_t = refs[2 * n_src :]
    load_keys(causal, places, key_refs, keys)
    length = length_ref[0]
    block = 0
    for source in value_refs:
        for local in range(source.shape[0] // QBLK):
            rows = source[local * QBLK : (local + 1) * QBLK, :].astype(F32).T.astype(BF16)
            at = pl.multiple_of(places[block] * QBLK, QBLK) if causal else block * QBLK
            values_t[:, pl.ds(at, QBLK)] = rows
            block += 1

    def body(i, place, size):
        rows = pl.ds(pl.multiple_of(i * QBLK, QBLK), QBLK)
        both = stack_heads(q_ref[rows, :])
        scores = masked_scores(causal, keys[:size, :], both, place, length, QBLK)
        highest = jnp.max(scores, axis=0, keepdims=True)
        exponent = jnp.exp(scores - highest)
        total = jnp.sum(exponent, axis=0, keepdims=True)
        mixed = dot_nn(values_t[:, :size], exponent.astype(BF16)) * (1.0 / total)
        out_ref[rows, :] = unstack_heads(mixed, QBLK)
        total_ref[0, pl.ds(i, 1), :] = highest + jnp.log(total)

    for_each_block(
        causal,
        variants_of(keys.shape[0], causal),
        q_ref.shape[0] // QBLK,
        own_places,
        length,
        body,
    )


def attention_forward(causal, queries, keys, values, places, own_places, length):
    rows, width = queries.shape
    n_src = len(keys)
    key_count = sum(k.shape[0] for k in keys)
    pairs = width // PAIR
    column = lambda i, *_: (0, i)
    spec = lambda n: pl.BlockSpec((n, PAIR), column)
    return pl.pallas_call(
        functools.partial(forward_body, causal, n_src),
        grid_spec=pltpu.PrefetchScalarGridSpec(
            num_scalar_prefetch=3,
            grid=(pairs,),
            in_specs=[spec(rows)] + [spec(k.shape[0]) for k in (*keys, *values)],
            out_specs=[
                spec(rows),
                pl.BlockSpec((1, rows // QBLK, 2 * QBLK), lambda i, *_: (i, 0, 0)),
            ],
            scratch_shapes=[
                pltpu.VMEM((key_count, PAIR), BF16),
                pltpu.VMEM((PAIR, key_count), BF16),
            ],
        ),
        out_shape=[
            jax.ShapeDtypeStruct((rows, width), F32),
            jax.ShapeDtypeStruct((pairs, rows // QBLK, 2 * QBLK), F32),
        ],
        compiler_params=pltpu.CompilerParams(vmem_limit_bytes=VMEM_LIMIT),
        name="self_forward" if causal else "cross_forward",
    )(places, own_places, length, queries, *keys, *values)


def backward_body(causal, n_src, places, own_places, length_ref, q_ref, g_ref, o_ref, t_ref, *refs):
    key_refs, value_refs = refs[:n_src], refs[n_src : 2 * n_src]
    dq_ref = refs[2 * n_src]
    dk_refs = refs[2 * n_src + 1 : 3 * n_src + 1]
    dv_refs = refs[3 * n_src + 1 : 4 * n_src + 1]
    keys, values, keys_t, dk, dv = refs[4 * n_src + 1 :]
    load_keys(causal, places, key_refs, keys)
    load_keys(causal, places, value_refs, values)
    length = length_ref[0]
    key_count = keys.shape[0]
    for block in range(key_count // QBLK):
        rows = slice(block * QBLK, (block + 1) * QBLK)
        keys_t[:, rows] = keys[rows, :].astype(F32).T.astype(BF16)
    dk[...] = jnp.zeros_like(dk)
    dv[...] = jnp.zeros_like(dv)

    def body(i, place, size):
        rows = pl.ds(pl.multiple_of(i * QBLK, QBLK), QBLK)
        both = stack_heads(q_ref[rows, :])
        grads = g_ref[rows, :]
        both_grads = stack_heads(grads)
        products = (grads.astype(F32) * o_ref[rows, :]).T
        delta = jnp.concatenate(
            [
                jnp.sum(products[:HD], axis=0, keepdims=True),
                jnp.sum(products[HD:], axis=0, keepdims=True),
            ],
            axis=1,
        )
        scores = masked_scores(causal, keys[:size, :], both, place, length, QBLK)
        prob = jnp.exp(scores - t_ref[0, pl.ds(i, 1), :])
        prob_grad = dot_nt(values[:size, :], both_grads)
        score_grad = (prob * (prob_grad - delta)).astype(BF16)
        dv[:size, :] += dot_nn(prob.astype(BF16), both_grads)
        dk[:size, :] += dot_nn(score_grad, both)
        dq = dot_nn(keys_t[:, :size], score_grad)
        dq_ref[rows, :] = unstack_heads(dq, QBLK) * ATTN_SCALE

    for_each_block(
        causal, variants_of(key_count, causal), q_ref.shape[0] // QBLK, own_places, length, body
    )
    block = 0
    for dk_out, dv_out in zip(dk_refs, dv_refs):
        for local in range(dk_out.shape[0] // QBLK):
            at = pl.multiple_of(places[block] * QBLK, QBLK) if causal else block * QBLK
            rows = slice(local * QBLK, (local + 1) * QBLK)
            dk_out[rows, :] = dk[pl.ds(at, QBLK), :].astype(BF16)
            dv_out[rows, :] = dv[pl.ds(at, QBLK), :].astype(BF16)
            block += 1


def attention_backward(
    causal, queries, grads, mixed, totals, keys, values, places, own_places, length
):
    rows, width = queries.shape
    n_src = len(keys)
    key_count = sum(k.shape[0] for k in keys)
    pairs = width // PAIR
    column = lambda i, *_: (0, i)
    spec = lambda n: pl.BlockSpec((n, PAIR), column)
    key_specs = [spec(k.shape[0]) for k in (*keys, *values)]
    outs = pl.pallas_call(
        functools.partial(backward_body, causal, n_src),
        grid_spec=pltpu.PrefetchScalarGridSpec(
            num_scalar_prefetch=3,
            grid=(pairs,),
            in_specs=[
                spec(rows),
                spec(rows),
                spec(rows),
                pl.BlockSpec((1, rows // QBLK, 2 * QBLK), lambda i, *_: (i, 0, 0)),
            ]
            + key_specs,
            out_specs=[spec(rows)] + key_specs,
            scratch_shapes=[
                pltpu.VMEM((key_count, PAIR), BF16),
                pltpu.VMEM((key_count, PAIR), BF16),
                pltpu.VMEM((PAIR, key_count), BF16),
                pltpu.VMEM((key_count, PAIR), F32),
                pltpu.VMEM((key_count, PAIR), F32),
            ],
        ),
        out_shape=[jax.ShapeDtypeStruct((rows, width), F32)]
        + [jax.ShapeDtypeStruct(k.shape, BF16) for k in (*keys, *values)],
        compiler_params=pltpu.CompilerParams(vmem_limit_bytes=VMEM_LIMIT),
        name="self_backward" if causal else "cross_backward",
    )(places, own_places, length, queries, grads, mixed, totals, *keys, *values)
    return outs[0], outs[1 : n_src + 1], outs[n_src + 1 :]


UNITS = 16
FIRST = 12
HALF = UNITS // 2
VECTORS = HALF
VROWS = 16
LANES = 128


def coordinates():
    core, f = lax.axis_index("ctx"), lax.axis_index("fsdp")
    return core, core % 2, f // 4, (f // 2) % 2, f % 2


def flip(odd, y, x, a, b):
    dx = a * (1 - odd) + b * odd
    dy = b * (1 - odd) + a * odd
    return y + dy * (1 - 2 * y), x + dx * (1 - 2 * x)


def peers_of(core, odd, z, y, x, depth):
    fsdp = lambda zz, yy, xx: (zz * 2 + yy) * 2 + xx
    ups = [(core, fsdp((z + k) % depth, y, x)) for k in range(1, depth)]
    first = (core, fsdp(z, *flip(odd, y, x, 1, 0)))
    second = (core, fsdp(z, *flip(odd, y, x, 0, 1)))
    partner = (core + 1 - 2 * odd, fsdp(z, y, x))
    return ups, first, second, partner


def enter(ups, first, second, partner):
    barrier = pltpu.get_barrier_semaphore()
    for peer in (*ups, first, second, partner):
        pl.semaphore_signal(barrier, inc=1, device_id=peer, device_id_type=MESH)
    pl.semaphore_wait(barrier, len(ups) + 3)


def remote(source, target, send, recv, peer):
    return pltpu.make_async_remote_copy(
        source, target, send, recv, device_id=peer, device_id_type=MESH
    )


def unit_set(g1, g2, gv, i, odd, y, x):
    if i == VECTORS:
        return gv.at[odd, :, y, x]
    if 2 * i < FIRST:
        return g1.at[2 * i + odd, :, y, x]
    return g2.at[:, y, x, 2 * i - FIRST + odd]


def unit_block(g1, g2, gv, i, odd, z, y, x):
    if i == VECTORS:
        return gv.at[odd, z, y, x]
    if 2 * i < FIRST:
        return g1.at[2 * i + odd, z, y, x]
    return g2.at[z, y, x, 2 * i - FIRST + odd]


def gather_body(
    depth, vectors, sp, so, cq, ckv, co, fi, fo, g1, g2, gv, own, load_sem, own_sem,
    zs, zr, fs, fr, ss, sr, ps, pr,
):
    core, odd, z, y, x = coordinates()
    ups, first, second, partner = peers_of(core, odd, z, y, x, depth)
    width = so.shape[1]
    rows = so.shape[0]
    sources = (
        [sp.at[:, pl.ds(j * width, width)] for j in range(3)]
        + [so, cq]
        + [ckv.at[:, pl.ds(j * width, width)] for j in range(2)]
        + [co]
        + [fi.at[:, pl.ds(j * width, width)] for j in range(4)]
        + [fo.at[pl.ds(j * rows, rows), :] for j in range(4)]
    )
    loads = [pltpu.make_async_copy(s, own.at[u], load_sem.at[u]) for u, s in enumerate(sources)]
    for load in loads:
        load.start()
    enter(ups, first, second, partner)

    def mine(i):
        return vectors.at[odd] if i == VECTORS else own.at[2 * i + odd]

    def set_of(i, a, b):
        return unit_set(g1, g2, gv, i, odd, *flip(odd, y, x, a, b))

    def up_copy(i, k):
        block = unit_block(g1, g2, gv, i, odd, z, y, x)
        return remote(mine(i), block, zs.at[i, k], zr.at[i, k], ups[k])

    def up_arrival(i, k):
        block = unit_block(g1, g2, gv, i, odd, (z + depth - 1 - k) % depth, y, x)
        return remote(block, block, zs.at[i, k], zr.at[i, k], ups[k])

    def first_copy(i):
        return remote(set_of(i, 0, 0), set_of(i, 0, 0), fs.at[i], fr.at[i], first)

    def second_copy(i, a):
        return remote(set_of(i, a, 0), set_of(i, a, 0), ss.at[i, a], sr.at[i, a], second)

    def partner_copy(i, a, b):
        at = a + 2 * b
        return remote(set_of(i, a, b), set_of(i, a, b), ps.at[i, at], pr.at[i, at], partner)

    def arrival(target, send, recv, peer):
        return remote(target, target, send, recv, peer)

    steps = [VECTORS, *range(HALF)]
    keeps = []
    for i in steps:
        if i != VECTORS:
            loads[2 * i].wait()
            loads[2 * i + 1].wait()
        keep = pltpu.make_async_copy(
            mine(i), unit_block(g1, g2, gv, i, odd, z, y, x), own_sem.at[i]
        )
        keep.start()
        keeps.append(keep)
        for k in range(depth - 1):
            up_copy(i, k).start()
    for step in range(len(steps) + 2):
        if step < len(steps):
            i = steps[step]
            keeps[step].wait()
            for k in range(depth - 1):
                up_arrival(i, k).wait_recv()
            first_copy(i).start()
            second_copy(i, 0).start()
            partner_copy(i, 0, 0).start()
        if 0 <= step - 1 < len(steps):
            i = steps[step - 1]
            arrival(set_of(i, 1, 0), fs.at[i], fr.at[i], first).wait_recv()
            second_copy(i, 1).start()
            partner_copy(i, 1, 0).start()
        if 0 <= step - 2 < len(steps):
            i = steps[step - 2]
            for a in range(2):
                arrival(set_of(i, a, 1), ss.at[i, a], sr.at[i, a], second).wait_recv()
                partner_copy(i, a, 1).start()
    for i in steps:
        for a in range(2):
            for b in range(2):
                at = a + 2 * b
                there = unit_set(g1, g2, gv, i, 1 - odd, *flip(1 - odd, y, x, a, b))
                arrival(there, ps.at[i, at], pr.at[i, at], partner).wait_recv()
                partner_copy(i, a, b).wait_send()
            second_copy(i, a).wait_send()
        first_copy(i).wait_send()
        for k in range(depth - 1):
            up_copy(i, k).wait_send()


def gather_weights(n_fsdp, vectors, sp, so, cq, ckv, co, fi, fo):
    rows, width = so.shape
    depth = n_fsdp // 4
    dma = pltpu.SemaphoreType.DMA
    steps = HALF + 1
    g1, g2, gv = pl.pallas_call(
        functools.partial(gather_body, depth),
        in_specs=[pl.BlockSpec(memory_space=pl.ANY)] * 8,
        out_specs=[pl.BlockSpec(memory_space=pl.ANY)] * 3,
        out_shape=[
            jax.ShapeDtypeStruct((FIRST, depth, 2, 2, rows, width), BF16),
            jax.ShapeDtypeStruct((depth, 2, 2, UNITS - FIRST, rows, width), BF16),
            jax.ShapeDtypeStruct((2, depth, 2, 2, VROWS, LANES), BF16),
        ],
        scratch_shapes=[
            pltpu.VMEM((UNITS, rows, width), BF16),
            dma((UNITS,)),
            dma((steps,)),
            dma((steps, depth - 1)),
            dma((steps, depth - 1)),
            dma((steps,)),
            dma((steps,)),
            dma((steps, 2)),
            dma((steps, 2)),
            dma((steps, 4)),
            dma((steps, 4)),
        ],
        compiler_params=pltpu.CompilerParams(
            collective_id=0, has_side_effects=True, vmem_limit_bytes=VMEM_LIMIT
        ),
        name="gather_weights",
    )(vectors, sp, so, cq, ckv, co, fi, fo)
    return (
        g1.reshape(FIRST, n_fsdp * rows, width),
        g2.reshape(-1, width),
        gv.reshape(2, n_fsdp, VROWS, LANES),
    )


def scatter_body(depth, *refs):
    units = refs[:7]
    (
        g1, g2, gv, out, out_v, own, from_partner, from_second, from_first, from_up, final, final_in,
        own_v, from_partner_v, from_second_v, from_first_v, from_up_v, final_v, final_in_v,
        own_sem, zs, zr, fs, fr, ss, sr, ps, pr, xs, xr,
    ) = refs[7:]
    core, odd, z, y, x = coordinates()
    ups, first, second, partner = peers_of(core, odd, z, y, x, depth)
    order = ((0, 1), (1, 1), (1, 0), (0, 0))

    def pick(i, main, small):
        return small if i == VECTORS else main.at[i]

    def source(i, parity, yy, xx):
        u = 2 * i + parity
        if i == VECTORS:
            return gv.at[parity, :, yy, xx]
        if 2 * i >= FIRST:
            return g2.at[:, yy, xx, u - FIRST]
        if 2 * i >= 8:
            return g1.at[u - 7, :, yy, xx]
        return units[u].at[:, yy, xx] if u < 7 else g1.at[0, :, yy, xx]

    def own_copy(i, a, b, parity):
        at = a + 2 * b
        return pltpu.make_async_copy(
            source(i, parity, *flip(odd, y, x, a, b)),
            pick(i, own, own_v).at[at],
            own_sem.at[i, at],
        )

    def partner_copy(i, a, b, parity):
        at = a + 2 * b
        return remote(
            source(i, parity, *flip(1 - odd, y, x, a, b)),
            pick(i, from_partner, from_partner_v).at[at],
            ps.at[i, at],
            pr.at[i, at],
            partner,
        )

    def second_copy(i, a):
        return remote(
            pick(i, own, own_v).at[a + 2],
            pick(i, from_second, from_second_v).at[a],
            ss.at[i, a],
            sr.at[i, a],
            second,
        )

    def first_copy(i):
        return remote(
            pick(i, own, own_v).at[1],
            pick(i, from_first, from_first_v),
            fs.at[i],
            fr.at[i],
            first,
        )

    def up_copy(i, k):
        return remote(
            pick(i, own, own_v).at[0, (z + 1 + k) % depth],
            pick(i, from_up, from_up_v).at[k],
            zs.at[i, k],
            zr.at[i, k],
            ups[k],
        )

    def final_copy(i):
        return remote(
            pick(i, final, final_v), pick(i, final_in, final_in_v), xs.at[i], xr.at[i], partner
        )

    def add(target, addend):
        def step(j, carry):
            target[j] = target[j] + addend[j]
            return carry

        lax.fori_loop(0, depth, step, 0)

    def start_all(copy, parity_of):
        for i in steps:
            if i != VECTORS and 2 * i < 8:
                for q in range(2):

                    @pl.when(odd == q)
                    def _(i=i, q=q):
                        for a, b in order:
                            copy(i, a, b, parity_of(q)).start()

            else:
                for a, b in order:
                    copy(i, a, b, parity_of(odd)).start()

    steps = [*range(HALF - 1, -1, -1), VECTORS]
    start_all(own_copy, lambda q: q)
    enter(ups, first, second, partner)
    start_all(partner_copy, lambda q: 1 - q)

    for step in range(len(steps) + 3):
        if step < len(steps):
            i = steps[step]
            for a, b in order:
                at = a + 2 * b
                own_copy(i, a, b, 0).wait()
                partner_copy(i, a, b, 0).wait_recv()
                add(pick(i, own, own_v).at[at], pick(i, from_partner, from_partner_v).at[at])
                if b:
                    second_copy(i, a).start()
        if 0 <= step - 1 < len(steps):
            i = steps[step - 1]
            for a in (1, 0):
                second_copy(i, a).wait_recv()
                add(pick(i, own, own_v).at[a], pick(i, from_second, from_second_v).at[a])
                if a:
                    first_copy(i).start()
        if 0 <= step - 2 < len(steps):
            i = steps[step - 2]
            first_copy(i).wait_recv()
            add(pick(i, own, own_v).at[0], pick(i, from_first, from_first_v))
            for k in range(depth - 1):
                up_copy(i, k).start()
        if 0 <= step - 3 < len(steps):
            i = steps[step - 3]
            total = pick(i, own, own_v)[0, z].astype(F32)
            for k in range(depth - 1):
                up_copy(i, k).wait_recv()
                total = total + pick(i, from_up, from_up_v)[k].astype(F32)
            pick(i, final, final_v)[...] = total
            final_copy(i).start()
            if i == VECTORS:
                out_v[odd] = total
            else:
                out[2 * i + odd] = total
    for i in steps:
        final_copy(i).wait()
        if i == VECTORS:
            out_v[1 - odd] = final_in_v[...]
        else:
            out[2 * i + 1 - odd] = final_in[i]
        for a, b in order:
            partner_copy(i, a, b, 0).wait_send()
        for a in range(2):
            second_copy(i, a).wait_send()
        first_copy(i).wait_send()
        for k in range(depth - 1):
            up_copy(i, k).wait_send()


def scatter_gradients(n_fsdp, units, g1, g2, gv):
    width = g1.shape[-1]
    depth = n_fsdp // 4
    rows = width // n_fsdp
    dma = pltpu.SemaphoreType.DMA
    vmem = pltpu.VMEM
    steps = HALF + 1
    block, small = (rows, width), (VROWS, LANES)
    return pl.pallas_call(
        functools.partial(scatter_body, depth),
        in_specs=[pl.BlockSpec(memory_space=pl.ANY)] * 10,
        out_specs=[pl.BlockSpec(memory_space=pltpu.VMEM)] * 2,
        out_shape=[
            jax.ShapeDtypeStruct((UNITS, *block), F32),
            jax.ShapeDtypeStruct((2, *small), F32),
        ],
        scratch_shapes=[
            vmem((HALF, 4, depth, *block), BF16),
            vmem((HALF, 4, depth, *block), BF16),
            vmem((HALF, 2, depth, *block), BF16),
            vmem((HALF, depth, *block), BF16),
            vmem((HALF, depth - 1, *block), BF16),
            vmem((HALF, *block), F32),
            vmem((HALF, *block), F32),
            vmem((4, depth, *small), BF16),
            vmem((4, depth, *small), BF16),
            vmem((2, depth, *small), BF16),
            vmem((depth, *small), BF16),
            vmem((depth - 1, *small), BF16),
            vmem(small, F32),
            vmem(small, F32),
            dma((steps, 4)),
            dma((steps, depth - 1)),
            dma((steps, depth - 1)),
            dma((steps,)),
            dma((steps,)),
            dma((steps, 2)),
            dma((steps, 2)),
            dma((steps, 4)),
            dma((steps, 4)),
            dma((steps,)),
            dma((steps,)),
        ],
        compiler_params=pltpu.CompilerParams(
            collective_id=1, has_side_effects=True, vmem_limit_bytes=VMEM_LIMIT
        ),
        name="scatter_gradients",
    )(
        *[u.reshape(depth, 2, 2, *block) for u in units],
        g1.reshape(-1, depth, 2, 2, *block),
        g2.reshape(depth, 2, 2, UNITS - FIRST, *block),
        gv.reshape(2, depth, 2, 2, *small),
    )


CHUNK = 256
VECTOR_ROWS = (5, 6, 8, 11, 9, 12)


def valid_of(own_places, length, chunk):
    row = lax.broadcasted_iota(jnp.int32, (CHUNK, 1), 0)
    place = row
    for block in range(CHUNK // QBLK):
        base = (own_places[chunk * (CHUNK // QBLK) + block] - block) * QBLK
        place = jnp.where((row >= block * QBLK) & (row < (block + 1) * QBLK), row + base, place)
    return place < length


def norm_stats(value):
    average = jnp.mean(value, axis=-1, keepdims=True)
    centred = value - average
    scale = lax.rsqrt(jnp.mean(centred * centred, axis=-1, keepdims=True) + EPSILON)
    return centred * scale, scale


def norm_back(grad, normed, scale):
    inner = jnp.mean(grad * normed, axis=-1, keepdims=True)
    return (grad - jnp.mean(grad, axis=-1, keepdims=True) - normed * inner) * scale


def feed_body(
    own_places, length_ref, mixed_ref, after_ref, cot_ref, vec_ref, b_fi_ref, g1, g2,
    out_ref, gmix_ref, grad_ref, sums_ref, isum_ref, d1, d2,
    w_co, w_fi, w_fo, mixed_low, normed, scale_ref, cross, cross_low, hidden, slope, grad_inner,
    total, grad_low, buffer, load_sem, store_sem,
):
    rows, width = after_ref.shape
    chunks = [pl.ds(c * CHUNK, CHUNK) for c in range(rows // CHUNK)]
    loads = [pltpu.make_async_copy(g1.at[7], w_co, load_sem.at[0])]
    for j in range(4):
        loads.append(pltpu.make_async_copy(g1.at[8 + j], w_fi.at[j], load_sem.at[1 + j]))
    for j in range(4):
        loads.append(
            pltpu.make_async_copy(
                g2.at[pl.ds(j * width, width), :], w_fo.at[j], load_sem.at[5 + j]
            )
        )
    for load in loads:
        load.start()
    vec = lambda i: vec_ref[VECTOR_ROWS[i] : VECTOR_ROWS[i] + 1, :]
    column_sum = lambda array: jnp.sum(array, axis=0, keepdims=True)

    loads[0].wait()
    for c in chunks:
        mixed_low[c, :] = mixed_ref[c, :].astype(BF16)
        value = after_ref[c, :] + dot_nn(mixed_low[c, :], w_co[...]) + vec(0)
        hat, scale = norm_stats(value)
        normed[c, :] = hat
        scale_ref[c, :] = scale
        value = hat * vec(2) + vec(3)
        cross[c, :] = value
        cross_low[c, :] = value.astype(BF16)
        total[c, :] = value + vec(1)
    for j in range(4):
        loads[1 + j].wait()
        loads[5 + j].wait()
        bias = b_fi_ref[:, j * width : (j + 1) * width]

        def inner_step(at, carry, j=j, bias=bias):
            c = pl.ds(pl.multiple_of(at * CHUNK, CHUNK), CHUNK)
            pre = dot_nn(cross_low[c, :], w_fi[j]) + bias
            share = 0.5 + 0.5 * lax.erf(pre * (0.5**0.5))
            act = (pre * share).astype(BF16)
            hidden[j, c, :] = act
            density = jnp.exp(-0.5 * pre * pre) * ((0.5 / jnp.pi) ** 0.5)
            slope[j, c, :] = (share + pre * density).astype(BF16)
            total[c, :] += dot_nn(act, w_fo[j])
            return carry

        lax.fori_loop(0, rows // CHUNK, inner_step, 0)
    gain_sum = jnp.zeros((1, width), F32)
    shift_sum = jnp.zeros((1, width), F32)
    grad_sum = jnp.zeros((1, width), F32)
    for at, c in enumerate(chunks):
        hat, scale = norm_stats(total[c, :])
        valid = valid_of(own_places, length_ref[0], at)
        out_ref[c, :] = jnp.where(valid, hat * vec(4) + vec(5), 0.0)
        incoming = jnp.where(valid, cot_ref[c, :].astype(F32), 0.0)
        gain_sum += column_sum(incoming * hat)
        shift_sum += column_sum(incoming)
        grad = norm_back(incoming * vec(4), hat, scale)
        grad_sum += column_sum(grad)
        total[c, :] = grad
        grad_low[c, :] = grad.astype(BF16)
    sums_ref[1:2, :] = grad_sum
    sums_ref[3:4, :] = gain_sum
    sums_ref[5:6, :] = shift_sum

    stores = []

    def store(value, target):
        at = len(stores)
        if at >= 2:
            stores[at - 2].wait()
        buffer[at % 2] = value.astype(BF16)
        copy = pltpu.make_async_copy(buffer.at[at % 2], target, store_sem.at[at % 2])
        copy.start()
        stores.append(copy)

    for j in range(4):

        def back_step(at, carry, j=j):
            c = pl.ds(pl.multiple_of(at * CHUNK, CHUNK), CHUNK)
            grad = dot_nt(grad_low[c, :], w_fo[j]) * slope[j, c, :].astype(F32)
            low = grad.astype(BF16)
            grad_inner[j, c, :] = low
            total[c, :] += dot_nt(low, w_fi[j])
            return carry + column_sum(grad)

        columns = slice(j * width, (j + 1) * width)
        isum_ref[:, columns] = lax.fori_loop(
            0, rows // CHUNK, back_step, jnp.zeros((1, width), F32)
        )
        store(dot_tn(hidden[j], grad_low[...]), d2.at[pl.ds(j * width, width), :])
        store(dot_tn(cross_low[...], grad_inner[j]), d1.at[1 + j])
    gain_sum = jnp.zeros((1, width), F32)
    shift_sum = jnp.zeros((1, width), F32)
    grad_sum = jnp.zeros((1, width), F32)
    for c in chunks:
        incoming = total[c, :]
        hat = normed[c, :]
        gain_sum += column_sum(incoming * hat)
        shift_sum += column_sum(incoming)
        grad = norm_back(incoming * vec(2), hat, scale_ref[c, :])
        grad_sum += column_sum(grad)
        grad_ref[c, :] = grad
        low = grad.astype(BF16)
        grad_low[c, :] = low
        gmix_ref[c, :] = dot_nt(low, w_co[...]).astype(BF16)
    sums_ref[0:1, :] = grad_sum
    sums_ref[2:3, :] = gain_sum
    sums_ref[4:5, :] = shift_sum
    store(dot_tn(mixed_low[...], grad_low[...]), d1.at[0])
    stores[-2].wait()
    stores[-1].wait()


def feed_forward(own_places, length, mixed, after, cotangent, vectors, inner_bias, units, outer):
    rows, width = after.shape
    hidden = outer.shape[0]
    any_spec = pl.BlockSpec(memory_space=pl.ANY)
    vmem_spec = pl.BlockSpec(memory_space=pltpu.VMEM)
    vmem = pltpu.VMEM
    return pl.pallas_call(
        feed_body,
        in_specs=[pl.BlockSpec(memory_space=pltpu.SMEM)] * 2 + [vmem_spec] * 5 + [any_spec] * 2,
        out_specs=[vmem_spec] * 5 + [any_spec] * 2,
        out_shape=[
            jax.ShapeDtypeStruct((rows, width), F32),
            jax.ShapeDtypeStruct((rows, width), BF16),
            jax.ShapeDtypeStruct((rows, width), F32),
            jax.ShapeDtypeStruct((8, width), F32),
            jax.ShapeDtypeStruct((1, hidden), F32),
            jax.ShapeDtypeStruct((5, width, width), BF16),
            jax.ShapeDtypeStruct((hidden, width), BF16),
        ],
        scratch_shapes=[
            vmem((width, width), BF16),
            vmem((4, width, width), BF16),
            vmem((4, width, width), BF16),
            vmem((rows, width), BF16),
            vmem((rows, width), F32),
            vmem((rows, 1), F32),
            vmem((rows, width), F32),
            vmem((rows, width), BF16),
            vmem((4, rows, width), BF16),
            vmem((4, rows, width), BF16),
            vmem((4, rows, width), BF16),
            vmem((rows, width), F32),
            vmem((rows, width), BF16),
            vmem((2, width, width), BF16),
            pltpu.SemaphoreType.DMA((9,)),
            pltpu.SemaphoreType.DMA((2,)),
        ],
        compiler_params=pltpu.CompilerParams(vmem_limit_bytes=VMEM_LIMIT),
        name="feed_forward",
    )(own_places, length, mixed, after, cotangent, vectors, inner_bias, units, outer)


VLANES = 256
WINDOW = 384


def spread_lanes(pieces, width):
    count = WINDOW // width
    lanes = pieces[0].shape[1]
    row = lax.broadcasted_iota(jnp.int32, (lanes, WINDOW), 0)
    column = lax.broadcasted_iota(jnp.int32, (lanes, WINDOW), 1)
    windows = [None] * (len(pieces) // count)
    for k in range(count):
        select = ((column == row + k * width) & (row < width)).astype(F32).astype(BF16)
        for w in range(len(windows)):
            part = dot_nn(pieces[w * count + k], select)
            windows[w] = part if k == 0 else windows[w] + part
    return jnp.concatenate(windows, axis=1)


def pair_forward(causal, p, q, k_all, v_all, values_t, out, totals, own_places, places, length):
    lanes = pl.ds(pl.multiple_of(p * PAIR, PAIR), PAIR)
    parts, part_rows = k_all.shape[0], k_all.shape[1]
    for h in range(parts):
        for block in range(part_rows // QBLK):
            rows = slice(block * QBLK, (block + 1) * QBLK)
            at = h * part_rows + block * QBLK
            values_t[:, at : at + QBLK] = v_all[h, rows, lanes].astype(F32).T.astype(BF16)

    def step(i, carry):
        rows = pl.ds(pl.multiple_of(i * QBLK, QBLK), QBLK)
        both = stack_heads(q[rows, lanes])
        scores = [dot_nt(k_all[h, :, lanes], both) for h in range(parts)]
        if causal:
            limit = row_limit(own_places[i], length)
            scores = [
                mask_part(s, limit, places, h * (part_rows // QBLK)) for h, s in enumerate(scores)
            ]
        highest = jnp.max(scores[0], axis=0, keepdims=True)
        for s in scores[1:]:
            highest = jnp.maximum(highest, jnp.max(s, axis=0, keepdims=True))
        total, mixed = 0.0, 0.0
        for h, s in enumerate(scores):
            exponent = jnp.exp(s - highest)
            total += jnp.sum(exponent, axis=0, keepdims=True)
            mixed += dot_nn(
                values_t[:, h * part_rows : (h + 1) * part_rows], exponent.astype(BF16)
            )
        out[rows, lanes] = unstack_heads(mixed * (1.0 / total), QBLK)
        totals[p, pl.ds(i, 1), :] = highest + jnp.log(total)
        return carry

    lax.fori_loop(0, q.shape[0] // QBLK, step, 0)


def row_limit(place, length):
    column = lax.broadcasted_iota(jnp.int32, (1, 2 * QBLK), 1)
    own = place * QBLK + jnp.where(column >= QBLK, column - QBLK, column)
    return jnp.minimum(own, length - 1)


def mask_part(scores, limit, places, first_block):
    row = lax.broadcasted_iota(jnp.int32, (QBLK, 2 * QBLK), 0)
    blocks = []
    for block in range(scores.shape[0] // QBLK):
        part = scores[block * QBLK : (block + 1) * QBLK]
        kept = row <= limit - places[first_block + block] * QBLK
        blocks.append(jnp.where(kept, part, MASKED_SCORE))
    return jnp.concatenate(blocks, axis=0)


def encode_body(
    depth, own_places, places, length_ref, states, encoder, vectors, sp, so, cq, ckv, co, fi, fo,
    g1, g2, q_out, k_out, v_out, cq_out, ck_out, cv_out, o_out, total_out, after_out, low_out, hat_out,
    scale_out, co_out, ctotal_out, flat_out, inner_out,
    gv, own, w, q, k_all, v_all, c_q, ck_all, cv_all, mixed, after, low, hat, values_t, cvalues_t,
    load_sem, own_sem, weight_sem, store_sem, zs, zr, fs, fr, ss, sr, ps, pr, ks, kr,
):
    core, odd, z, y, x = coordinates()
    ups, first, second, partner = peers_of(core, odd, z, y, x, depth)
    rows, width = so.shape
    length = length_ref[0]
    sources = (
        [sp.at[:, pl.ds(j * width, width)] for j in range(3)]
        + [so, cq]
        + [ckv.at[:, pl.ds(j * width, width)] for j in range(2)]
        + [co]
        + [fi.at[:, pl.ds(j * width, width)] for j in range(4)]
        + [fo.at[pl.ds(j * rows, rows), :] for j in range(4)]
    )
    loads = [pltpu.make_async_copy(s, own.at[u], load_sem.at[u]) for u, s in enumerate(sources)]
    for load in loads:
        load.start()
    enter(ups, first, second, partner)

    def mine(i):
        return vectors if i == VECTORS else own.at[2 * i + odd]

    def set_at(i, parity, yy, xx):
        return gv.at[:, yy, xx] if i == VECTORS else unit_set(g1, g2, None, i, parity, yy, xx)

    def block_at(i, zz):
        return gv.at[zz, y, x] if i == VECTORS else unit_block(g1, g2, None, i, odd, zz, y, x)

    def set_of(i, a, b):
        return set_at(i, odd, *flip(odd, y, x, a, b))

    def up_copy(i, k):
        return remote(mine(i), block_at(i, z), zs.at[i, k], zr.at[i, k], ups[k])

    def up_arrival(i, k):
        block = block_at(i, (z + depth - 1 - k) % depth)
        return remote(block, block, zs.at[i, k], zr.at[i, k], ups[k])

    def first_copy(i):
        return remote(set_of(i, 0, 0), set_of(i, 0, 0), fs.at[i], fr.at[i], first)

    def first_arrival(i):
        return remote(set_of(i, 1, 0), set_of(i, 1, 0), fs.at[i], fr.at[i], first)

    def second_copy(i, a):
        return remote(set_of(i, a, 0), set_of(i, a, 0), ss.at[i, a], sr.at[i, a], second)

    def second_arrival(i, a):
        return remote(set_of(i, a, 1), set_of(i, a, 1), ss.at[i, a], sr.at[i, a], second)

    def partner_copy(i, a, b):
        at = a + 2 * b
        return remote(set_of(i, a, b), set_of(i, a, b), ps.at[i, at], pr.at[i, at], partner)

    def partner_arrival(i, a, b):
        at = a + 2 * b
        there = set_at(i, 1 - odd, *flip(1 - odd, y, x, a, b))
        return remote(there, there, ps.at[i, at], pr.at[i, at], partner)

    keeps = {}

    def begin(i):
        keeps[i] = pltpu.make_async_copy(mine(i), block_at(i, z), own_sem.at[i])
        keeps[i].start()
        for k in range(depth - 1):
            up_copy(i, k).start()

    def stage_2(i):
        keeps[i].wait()
        for k in range(depth - 1):
            up_arrival(i, k).wait_recv()
        first_copy(i).start()
        second_copy(i, 0).start()
        if i != VECTORS:
            partner_copy(i, 0, 0).start()

    def stage_3(i):
        first_arrival(i).wait_recv()
        second_copy(i, 1).start()
        if i != VECTORS:
            partner_copy(i, 1, 0).start()

    def stage_4(i):
        for a in range(2):
            second_arrival(i, a).wait_recv()
            if i != VECTORS:
                partner_copy(i, a, 1).start()

    def finish(i):
        for a in range(2):
            for b in range(2):
                partner_arrival(i, a, b).wait_recv()

    def weight(u):
        return pltpu.make_async_copy(
            g1.at[u].reshape(width, width), w.at[u], weight_sem.at[u]
        )

    stores = []

    def store(source, target):
        copy = pltpu.make_async_copy(source, target, store_sem.at[len(stores)])
        copy.start()
        stores.append(copy)

    begin(VECTORS)
    for i in range(HALF):
        loads[2 * i].wait()
        loads[2 * i + 1].wait()
        begin(i)
    stage_2(VECTORS)
    stage_2(0)
    stage_3(VECTORS)
    stage_2(1)
    stage_3(0)
    stage_4(VECTORS)
    flat = spread_lanes([gv[f // 4, (f // 2) % 2, f % 2] for f in range(4 * depth)], rows)
    flat_out[...] = flat
    inner_rows = fo.shape[0]
    inner_out[...] = spread_lanes(
        [gv[f // 4, (f // 2) % 2, f % 2] for f in range(4 * depth)], inner_rows
    )[13:14, :]
    vec = lambda i: flat[i : i + 1, :]
    stage_2(2)
    stage_3(1)
    stage_4(0)
    stage_2(3)
    stage_3(2)
    stage_4(1)
    finish(0)
    finish(1)
    for u in range(4):
        weight(u).start()
    stage_2(4)

    row_count = states.shape[0]
    chunks = [pl.ds(c * CHUNK, CHUNK) for c in range(row_count // CHUNK)]
    encoder_count = encoder.shape[0]
    step = min(CHUNK, encoder_count)
    encoder_chunks = [pl.ds(c * step, step) for c in range(encoder_count // step)]

    def share(number, array):
        copy = remote(array.at[0], array.at[1], ks.at[number], kr.at[number], partner)
        copy.start()
        return copy

    weight(1).wait()
    for c in chunks:
        k_all[0, c, :] = dot_nn(states[c, :], w[1]).astype(BF16)
    shares = [share(0, k_all)]
    weight(2).wait()
    for c in chunks:
        v_all[0, c, :] = (dot_nn(states[c, :], w[2]) + vec(1)).astype(BF16)
    shares.append(share(1, v_all))
    weight(0).wait()
    for c in chunks:
        q[c, :] = ((dot_nn(states[c, :], w[0]) + vec(0)) * ATTN_SCALE).astype(BF16)
    store(q, q_out)
    stage_3(3)
    stage_4(2)
    shares[0].wait_recv()
    shares[1].wait_recv()
    store(k_all, k_out)
    store(v_all, v_out)

    def self_pairs(begin_at, end_at):
        def body(p, carry):
            pair_forward(
                True, p, q, k_all, v_all, values_t, mixed, total_out, own_places, places, length
            )
            return carry

        lax.fori_loop(begin_at, end_at, body, 0)

    pairs = width // PAIR
    self_pairs(0, pairs // 3)
    stage_2(5)
    stage_3(4)
    stage_4(3)
    self_pairs(pairs // 3, 2 * pairs // 3)
    stage_2(6)
    stage_3(5)
    stage_4(4)
    finish(2)
    finish(3)
    for u in range(4, 8):
        weight(u).start()
    self_pairs(2 * pairs // 3, pairs)
    store(mixed, o_out)
    stage_2(7)
    stage_3(6)
    stage_4(5)
    weight(5).wait()
    for c in encoder_chunks:
        ck_all[0, c, :] = dot_nn(encoder[c, :], w[5]).astype(BF16)
    shares.append(share(2, ck_all))
    weight(6).wait()
    for c in encoder_chunks:
        cv_all[0, c, :] = (dot_nn(encoder[c, :], w[6]) + vec(4)).astype(BF16)
    shares.append(share(3, cv_all))
    weight(3).wait()
    weight(4).wait()
    for c in chunks:
        value = states[c, :].astype(F32) + dot_nn(mixed[c, :].astype(BF16), w[3]) + vec(2)
        normed, scale = norm_stats(value)
        hat[c, :] = normed
        scale_out[c, :] = scale
        value = normed * vec(7) + vec(10)
        after[c, :] = value
        low[c, :] = value.astype(BF16)
        c_q[c, :] = ((dot_nn(low[c, :], w[4]) + vec(3)) * ATTN_SCALE).astype(BF16)
    store(hat, hat_out)
    store(after, after_out)
    store(low, low_out)
    store(c_q, cq_out)
    stage_3(7)
    stage_4(6)
    shares[2].wait_recv()
    shares[3].wait_recv()
    store(ck_all, ck_out)
    store(cv_all, cv_out)
    stores[3].wait()

    def cross_pairs(begin_at, end_at):
        def body(p, carry):
            pair_forward(
                False, p, c_q, ck_all, cv_all, cvalues_t, mixed, ctotal_out, None, None, None
            )
            return carry

        lax.fori_loop(begin_at, end_at, body, 0)

    cross_pairs(0, pairs // 2)
    stage_4(7)
    cross_pairs(pairs // 2, pairs)
    store(mixed, co_out)
    weight(7).wait()
    for at, copy in enumerate(stores):
        if at != 3:
            copy.wait()
    for copy in shares:
        copy.wait_send()
    for i in [VECTORS, *range(HALF)]:
        if i >= 4 and i != VECTORS:
            finish(i)
        for a in range(2):
            for b in range(2):
                if i != VECTORS:
                    partner_copy(i, a, b).wait_send()
            second_copy(i, a).wait_send()
        first_copy(i).wait_send()
        for k in range(depth - 1):
            up_copy(i, k).wait_send()


def encode(
    n_fsdp, own_places, places, length, states, encoder, vectors, sp, so, cq, ckv, co, fi, fo
):
    rows, width = so.shape
    depth = n_fsdp // 4
    row_count, encoder_count = states.shape[0], encoder.shape[0]
    pairs = width // PAIR
    steps = HALF + 1
    dma = pltpu.SemaphoreType.DMA
    vmem = pltpu.VMEM
    any_spec = pl.BlockSpec(memory_space=pl.ANY)
    vmem_spec = pl.BlockSpec(memory_space=pltpu.VMEM)
    smem_spec = pl.BlockSpec(memory_space=pltpu.SMEM)
    shape = jax.ShapeDtypeStruct
    totals = (pairs, row_count // QBLK, 2 * QBLK)
    outs = [
        (any_spec, (FIRST, depth, 2, 2, rows, width), BF16),
        (any_spec, (depth, 2, 2, UNITS - FIRST, rows, width), BF16),
        (any_spec, (row_count, width), BF16),
        (any_spec, (2, row_count, width), BF16),
        (any_spec, (2, row_count, width), BF16),
        (any_spec, (row_count, width), BF16),
        (any_spec, (2, encoder_count, width), BF16),
        (any_spec, (2, encoder_count, width), BF16),
        (any_spec, (row_count, width), F32),
        (vmem_spec, totals, F32),
        (any_spec, (row_count, width), F32),
        (any_spec, (row_count, width), BF16),
        (any_spec, (row_count, width), F32),
        (vmem_spec, (row_count, 1), F32),
        (any_spec, (row_count, width), F32),
        (vmem_spec, totals, F32),
        (vmem_spec, (VROWS, width), F32),
        (vmem_spec, (1, fo.shape[0] * n_fsdp), F32),
    ]
    return pl.pallas_call(
        functools.partial(encode_body, depth),
        in_specs=[smem_spec] * 3 + [vmem_spec] * 3 + [any_spec] * 7,
        out_specs=[spec for spec, _, _ in outs],
        out_shape=[shape(extent, kind) for _, extent, kind in outs],
        scratch_shapes=[
            vmem((depth, 2, 2, VROWS, VLANES), BF16),
            vmem((UNITS, rows, width), BF16),
            vmem((8, width, width), BF16),
            vmem((row_count, width), BF16),
            vmem((2, row_count, width), BF16),
            vmem((2, row_count, width), BF16),
            vmem((row_count, width), BF16),
            vmem((2, encoder_count, width), BF16),
            vmem((2, encoder_count, width), BF16),
            vmem((row_count, width), F32),
            vmem((row_count, width), F32),
            vmem((row_count, width), BF16),
            vmem((row_count, width), F32),
            vmem((PAIR, 2 * row_count), BF16),
            vmem((PAIR, 2 * encoder_count), BF16),
            dma((UNITS,)),
            dma((steps,)),
            dma((8,)),
            dma((12,)),
            dma((steps, depth - 1)),
            dma((steps, depth - 1)),
            dma((steps,)),
            dma((steps,)),
            dma((steps, 2)),
            dma((steps, 2)),
            dma((steps, 4)),
            dma((steps, 4)),
            dma((4,)),
            dma((4,)),
        ],
        compiler_params=pltpu.CompilerParams(
            collective_id=2, has_side_effects=True, vmem_limit_bytes=VMEM_LIMIT
        ),
        name="encode",
    )(own_places, places, length, states, encoder, vectors, sp, so, cq, ckv, co, fi, fo)


def per_device_wide(
    n_ctx,
    n_fsdp,
    states,
    encoded,
    lengths,
    block_order,
    cotangent,
    self_project,
    self_bias,
    self_output,
    self_shift,
    cross_query,
    cross_keyval,
    cross_bias,
    cross_output,
    cross_shift,
    feed_inner,
    inner_bias,
    feed_outer,
    outer_bias,
    norm_gain,
    norm_shift,
):
    local_rows = states.shape[1]
    width = states.shape[2]
    rows = self_output.shape[0]
    local_blocks = local_rows // QBLK
    core = lax.axis_index("ctx")
    own_order = lax.dynamic_slice_in_dim(block_order, core * local_blocks, local_blocks)
    places = block_order
    spread = lambda array: (lax.all_gather(array, "ctx", axis=0, tiled=True),)
    collect = lambda parts: lax.psum_scatter(
        parts[0], "ctx", scatter_dimension=0, tiled=True
    ).astype(F32)

    vectors = jnp.concatenate(
        [
            self_bias,
            self_shift[None],
            cross_bias,
            cross_shift[None],
            outer_bias[None],
            norm_gain,
            norm_shift,
            inner_bias.reshape(-1, rows),
        ],
        axis=0,
    )
    inner_rows = inner_bias.shape[0] // rows
    count = vectors.shape[0]
    pad = ((0, 2 * VROWS - count), (0, LANES - rows))
    units, w_fo, all_vectors = gather_weights(
        n_fsdp, jnp.pad(vectors, pad).reshape(2, VROWS, LANES), self_project, self_output, cross_query,
        cross_keyval, cross_output, feed_inner, feed_outer,
    )
    all_vectors = jnp.transpose(all_vectors, (1, 0, 2, 3)).reshape(n_fsdp, 2 * VROWS, LANES)
    all_vectors = all_vectors[:, :count, :rows].astype(F32)
    inner_full = all_vectors[:, 13:].reshape(1, -1)
    flat = jnp.transpose(all_vectors, (1, 0, 2)).reshape(count, -1)
    b_q, b_v, b_so, b_cq, b_cv = (flat[i] for i in range(5))

    w_q, w_k, w_v, w_so, w_cq, w_ck, w_cv, w_co = (units[i] for i in range(8))

    inputs = states[0]
    encoder_rows = encoded[0]
    queries = ((dot_nn(inputs, w_q) + b_q) * ATTN_SCALE).astype(BF16)
    own_keys = dot_nn(inputs, w_k).astype(BF16)
    own_values = (dot_nn(inputs, w_v) + b_v).astype(BF16)
    own_cross_keys = dot_nn(encoder_rows, w_ck).astype(BF16)
    own_cross_values = (dot_nn(encoder_rows, w_cv) + b_cv).astype(BF16)
    keys, values = spread(own_keys), spread(own_values)
    cross_keys, cross_values = spread(own_cross_keys), spread(own_cross_values)

    attend = functools.partial(attention_forward, places=places, own_places=own_order, length=lengths)
    self_attended, self_total = attend(True, queries, keys, values)
    self_mixed = self_attended.astype(BF16)
    after_self, norm_back_one = jax.vjp(
        layer_norm, inputs.astype(F32) + dot_nn(self_mixed, w_so) + b_so, flat[7], flat[10]
    )
    after_self_low = after_self.astype(BF16)
    cross_queries = ((dot_nn(after_self_low, w_cq) + b_cq) * ATTN_SCALE).astype(BF16)
    cross_attended, cross_total = attend(False, cross_queries, cross_keys, cross_values)
    output, grad_cross_mixed, grad_two, feed_sums, inner_sum, d_low, d_outer = feed_forward(
        own_order, lengths, cross_attended, after_self, cotangent[0], flat[:16], inner_full, units, w_fo
    )
    attend_back = functools.partial(
        attention_backward, places=places, own_places=own_order, length=lengths
    )
    cross_query_grad, ck_parts, cv_parts = attend_back(
        False, cross_queries, grad_cross_mixed, cross_attended, cross_total, cross_keys, cross_values
    )
    cross_query_low = cross_query_grad.astype(BF16)
    d_cq = dot_tn(after_self_low, cross_query_low).astype(BF16)
    ck_grad, cv_grad = collect(ck_parts), collect(cv_parts)
    ck_low, cv_low = ck_grad.astype(BF16), cv_grad.astype(BF16)
    d_ck = dot_tn(encoder_rows, ck_low).astype(BF16)
    d_cv = dot_tn(encoder_rows, cv_low).astype(BF16)
    grad_encoded = dot_nt(ck_low, w_ck) + dot_nt(cv_low, w_cv)
    grad_one, gain_one, shift_one = norm_back_one(grad_two + dot_nt(cross_query_low, w_cq))
    grad_one_low = grad_one.astype(BF16)
    d_so = dot_tn(self_mixed, grad_one_low).astype(BF16)
    grad_self_mixed = dot_nt(grad_one_low, w_so).astype(BF16)
    query_grad, k_parts, v_parts = attend_back(
        True, queries, grad_self_mixed, self_attended, self_total, keys, values
    )
    query_low = query_grad.astype(BF16)
    key_grad, value_grad = collect(k_parts), collect(v_parts)
    key_low, value_low = key_grad.astype(BF16), value_grad.astype(BF16)
    d_q = dot_tn(inputs, query_low).astype(BF16)
    d_k = dot_tn(inputs, key_low).astype(BF16)
    d_v = dot_tn(inputs, value_low).astype(BF16)
    grad_states = grad_one + dot_nt(query_low, w_q) + dot_nt(key_low, w_k) + dot_nt(value_low, w_v)

    column_sum = lambda array: jnp.sum(array, axis=0)
    grad_vectors = jnp.stack(
        [
            column_sum(query_grad),
            column_sum(value_grad),
            column_sum(grad_one),
            column_sum(cross_query_grad),
            column_sum(cv_grad),
            feed_sums[0],
            feed_sums[1],
            gain_one,
            feed_sums[2],
            feed_sums[3],
            shift_one,
            feed_sums[4],
            feed_sums[5],
        ]
    ).reshape(13, n_fsdp, rows)
    inner_vector = inner_sum.reshape(n_fsdp, inner_rows, rows)
    packed = jnp.concatenate([jnp.transpose(grad_vectors, (1, 0, 2)), inner_vector], axis=1)
    packed = jnp.pad(packed, ((0, 0), *pad)).astype(BF16)
    packed = jnp.transpose(packed.reshape(n_fsdp, 2, VROWS, LANES), (1, 0, 2, 3))

    shards, mine = scatter_gradients(
        n_fsdp, [d_q, d_k, d_v, d_so, d_cq, d_ck, d_cv], d_low, d_outer, packed
    )
    if n_ctx > 2:
        groups = [[c for c in range(n_ctx) if c % 2 == odd] for odd in range(2)]
        total = lambda part: lax.psum(part.astype(BF16), "ctx", axis_index_groups=groups).astype(F32)
        shards, mine = total(shards), total(mine)
    mine = mine.reshape(2 * VROWS, LANES)[:, :rows]
    return (
        output[None],
        grad_states[None],
        grad_encoded[None],
        jnp.concatenate([shards[0], shards[1], shards[2]], axis=1),
        mine[0:2],
        shards[3],
        mine[2],
        shards[4],
        jnp.concatenate([shards[5], shards[6]], axis=1),
        mine[3:5],
        shards[7],
        mine[5],
        jnp.concatenate([shards[8 + i] for i in range(4)], axis=1),
        mine[13 : 13 + inner_rows].reshape(-1),
        shards[12:].reshape(-1, width),
        mine[6],
        mine[7:10],
        mine[10:13],
    )


def per_device(
    n_ctx,
    n_fsdp,
    states,
    encoded,
    lengths,
    block_order,
    cotangent,
    self_project,
    self_bias,
    self_output,
    self_shift,
    cross_query,
    cross_keyval,
    cross_bias,
    cross_output,
    cross_shift,
    feed_inner,
    inner_bias,
    feed_outer,
    outer_bias,
    norm_gain,
    norm_shift,
):
    local_rows = states.shape[1]
    width = states.shape[2]
    rows = self_output.shape[0]
    inner_rows = inner_bias.shape[0] // rows
    local_blocks = local_rows // QBLK
    core = lax.axis_index("ctx")
    own_order = lax.dynamic_slice_in_dim(block_order, core * local_blocks, local_blocks)
    other_order = lax.dynamic_slice_in_dim(block_order, (1 - core) * local_blocks, local_blocks)
    places = jnp.concatenate([own_order, other_order])
    narrow = jnp.concatenate(
        [
            self_bias,
            self_shift[None],
            cross_bias,
            cross_shift[None],
            outer_bias[None],
            norm_gain,
            norm_shift,
        ],
        axis=0,
    )
    vectors = jnp.concatenate(
        [
            jnp.pad(narrow, ((0, 0), (0, VLANES - rows))),
            jnp.pad(inner_bias[None], ((0, VROWS - 14), (0, VLANES - inner_bias.shape[0]))),
        ],
        axis=0,
    )
    (
        units, w_fo, queries, keys, values, cross_queries, cross_keys, cross_values, self_attended,
        self_total, after_self, after_self_low, hat, scale, cross_attended, cross_total, flat, inner_full,
    ) = encode(
        n_fsdp, own_order, places, lengths, states[0], encoded[0], vectors, self_project, self_output,
        cross_query, cross_keyval, cross_output, feed_inner, feed_outer,
    )
    units = units.reshape(FIRST, width, width)
    w_fo = w_fo.reshape(-1, width)
    w_q, w_k, w_v, w_so, w_cq, w_ck, w_cv = (units[i] for i in range(7))
    output, grad_cross_mixed, grad_two, feed_sums, inner_sum, d_low, d_outer = feed_forward(
        own_order, lengths, cross_attended, after_self, cotangent[0], flat, inner_full, units, w_fo
    )

    def exchange(array):
        perm = [
            (c * n_fsdp + f, (1 - c) * n_fsdp + f) for c in range(n_ctx) for f in range(n_fsdp)
        ]
        return lax.ppermute(array, ("ctx", "fsdp"), perm)

    collect = lambda parts: parts[0].astype(F32) + exchange(parts[1]).astype(F32)
    inputs = states[0]
    encoder_rows = encoded[0]
    self_mixed = self_attended.astype(BF16)
    attend_back = functools.partial(
        attention_backward, places=places, own_places=own_order, length=lengths
    )
    cross_query_grad, ck_parts, cv_parts = attend_back(
        False, cross_queries, grad_cross_mixed, cross_attended, cross_total,
        [cross_keys[0], cross_keys[1]], [cross_values[0], cross_values[1]],
    )
    cross_query_low = cross_query_grad.astype(BF16)
    d_cq = dot_tn(after_self_low, cross_query_low).astype(BF16)
    ck_grad, cv_grad = collect(ck_parts), collect(cv_parts)
    ck_low, cv_low = ck_grad.astype(BF16), cv_grad.astype(BF16)
    d_ck = dot_tn(encoder_rows, ck_low).astype(BF16)
    d_cv = dot_tn(encoder_rows, cv_low).astype(BF16)
    grad_encoded = dot_nt(ck_low, w_ck) + dot_nt(cv_low, w_cv)
    incoming = grad_two + dot_nt(cross_query_low, w_cq)
    column_sum = lambda array: jnp.sum(array, axis=0)
    gain_one, shift_one = column_sum(incoming * hat), column_sum(incoming)
    grad_one = norm_back(incoming * flat[7], hat, scale)
    grad_one_low = grad_one.astype(BF16)
    d_so = dot_tn(self_mixed, grad_one_low).astype(BF16)
    grad_self_mixed = dot_nt(grad_one_low, w_so).astype(BF16)
    query_grad, k_parts, v_parts = attend_back(
        True, queries, grad_self_mixed, self_attended, self_total,
        [keys[0], keys[1]], [values[0], values[1]],
    )
    query_low = query_grad.astype(BF16)
    key_grad, value_grad = collect(k_parts), collect(v_parts)
    key_low, value_low = key_grad.astype(BF16), value_grad.astype(BF16)
    d_q = dot_tn(inputs, query_low).astype(BF16)
    d_k = dot_tn(inputs, key_low).astype(BF16)
    d_v = dot_tn(inputs, value_low).astype(BF16)
    grad_states = grad_one + dot_nt(query_low, w_q) + dot_nt(key_low, w_k) + dot_nt(value_low, w_v)

    grad_vectors = jnp.stack(
        [
            column_sum(query_grad),
            column_sum(value_grad),
            column_sum(grad_one),
            column_sum(cross_query_grad),
            column_sum(cv_grad),
            feed_sums[0],
            feed_sums[1],
            gain_one,
            feed_sums[2],
            feed_sums[3],
            shift_one,
            feed_sums[4],
            feed_sums[5],
        ]
    ).reshape(13, n_fsdp, rows)
    inner_vector = inner_sum.reshape(n_fsdp, inner_rows, rows)
    packed = jnp.concatenate([jnp.transpose(grad_vectors, (1, 0, 2)), inner_vector], axis=1)
    pad = ((0, 2 * VROWS - 13 - inner_rows), (0, LANES - rows))
    packed = jnp.pad(packed, ((0, 0), *pad)).astype(BF16)
    packed = jnp.transpose(packed.reshape(n_fsdp, 2, VROWS, LANES), (1, 0, 2, 3))

    shards, mine = scatter_gradients(
        n_fsdp, [d_q, d_k, d_v, d_so, d_cq, d_ck, d_cv], d_low, d_outer, packed
    )
    mine = mine.reshape(2 * VROWS, LANES)[:, :rows]
    return (
        output[None],
        grad_states[None],
        grad_encoded[None],
        jnp.concatenate([shards[0], shards[1], shards[2]], axis=1),
        mine[0:2],
        shards[3],
        mine[2],
        shards[4],
        jnp.concatenate([shards[5], shards[6]], axis=1),
        mine[3:5],
        shards[7],
        mine[5],
        jnp.concatenate([shards[8 + i] for i in range(4)], axis=1),
        mine[13 : 13 + inner_rows].reshape(-1),
        shards[12:].reshape(-1, width),
        mine[6],
        mine[7:10],
        mine[10:13],
    )


def solution(mesh):
    return jax.shard_map(
        functools.partial(
            per_device if mesh.shape["ctx"] == 2 else per_device_wide,
            mesh.shape["ctx"],
            mesh.shape["fsdp"],
        ),
        mesh=mesh,
        in_specs=(
            P("fsdp", "ctx", None),
            P("fsdp", "ctx", None),
            P("fsdp"),
            P(),
            P("fsdp", "ctx", None),
            P("fsdp", None),
            P(None, "fsdp"),
            P("fsdp", None),
            P("fsdp"),
            P("fsdp", None),
            P("fsdp", None),
            P(None, "fsdp"),
            P("fsdp", None),
            P("fsdp"),
            P("fsdp", None),
            P("fsdp"),
            P("fsdp", None),
            P("fsdp"),
            P(None, "fsdp"),
            P(None, "fsdp"),
        ),
        out_specs=(
            P("fsdp", "ctx", None),
            P("fsdp", "ctx", None),
            P("fsdp", "ctx", None),
            P("fsdp", None),
            P(None, "fsdp"),
            P("fsdp", None),
            P("fsdp"),
            P("fsdp", None),
            P("fsdp", None),
            P(None, "fsdp"),
            P("fsdp", None),
            P("fsdp"),
            P("fsdp", None),
            P("fsdp"),
            P("fsdp", None),
            P("fsdp"),
            P(None, "fsdp"),
            P(None, "fsdp"),
        ),
        check_vma=False,
    )
```

```python
import functools

import jax
import jax.numpy as jnp
from jax import lax
from jax.experimental import pallas as pl
from jax.experimental.pallas import tpu as pltpu
from jax.sharding import PartitionSpec as P

H = 12
HD = 64
QBLK = 128
PAIR = 2 * HD
ATTN_SCALE = 0.125
MASKED_SCORE = -1e30
EPSILON = 1e-05
MESH = pl.DeviceIdType.MESH
VMEM_LIMIT = 60 * 1024 * 1024
DECODE_LIMIT = 67043328
BF16 = jnp.bfloat16
F32 = jnp.float32


def dot_nn(left, right):
    return lax.dot_general(left, right, (((1,), (0,)), ((), ())), preferred_element_type=F32)


def dot_nt(left, right):
    return lax.dot_general(left, right, (((1,), (1,)), ((), ())), preferred_element_type=F32)


def dot_tn(left, right):
    return lax.dot_general(left, right, (((0,), (0,)), ((), ())), preferred_element_type=F32)


def layer_norm(inputs, scale_vec, shift_vec):
    average = jnp.mean(inputs, axis=-1, keepdims=True)
    centred = inputs - average
    variance = jnp.mean(centred * centred, axis=-1, keepdims=True)
    return centred * lax.rsqrt(variance + EPSILON) * scale_vec + shift_vec


def gelu_exact(inputs):
    return jax.nn.gelu(inputs, approximate=False)


def stack_heads(rows):
    first = lax.broadcasted_iota(jnp.int32, rows.shape, 1) < HD
    zero = jnp.zeros_like(rows)
    return jnp.concatenate([jnp.where(first, rows, zero), jnp.where(first, zero, rows)], axis=0)


def unstack_heads(both, count):
    return jnp.concatenate([both[:HD, :count], both[HD:, count:]], axis=0).T


def variants_of(key_count, causal):
    if not causal:
        return [key_count]
    step = max(2 * QBLK, key_count // 4)
    return [step * (i + 1) for i in range(key_count // step)]


def load_keys(causal, places, sources, target):
    block = 0
    for source in sources:
        for local in range(source.shape[0] // QBLK):
            rows = source[local * QBLK : (local + 1) * QBLK, :]
            if causal:
                at = pl.multiple_of(places[block] * QBLK, QBLK)
                target[pl.ds(at, QBLK), :] = rows
            else:
                target[block * QBLK : (block + 1) * QBLK, :] = rows
            block += 1


def masked_scores(causal, keys, both, place, length, count):
    scores = dot_nt(keys, both)
    if causal:
        column = lax.broadcasted_iota(jnp.int32, (1, 2 * count), 1)
        row_place = place * QBLK + jnp.where(column >= count, column - count, column)
        limit = jnp.minimum(row_place, length - 1)
        key_place = lax.broadcasted_iota(jnp.int32, scores.shape, 0)
        scores = jnp.where(key_place <= limit, scores, MASKED_SCORE)
    return scores


def for_each_block(causal, sizes, block_count, own_places, length, body):
    def step(i, carry):
        if not causal:
            body(i, 0, sizes[0])
            return carry
        place = own_places[i]
        needed = jnp.minimum((place + 1) * QBLK, length)
        for at, size in enumerate(sizes):
            low = sizes[at - 1] if at else 0

            @pl.when((needed > low) & (needed <= size))
            def _(size=size):
                body(i, place, size)

        return carry

    lax.fori_loop(0, block_count, step, 0)


def forward_body(causal, n_src, places, own_places, length_ref, q_ref, *refs):
    key_refs, value_refs = refs[:n_src], refs[n_src : 2 * n_src]
    out_ref, total_ref, keys, values_t = refs[2 * n_src :]
    load_keys(causal, places, key_refs, keys)
    length = length_ref[0]
    block = 0
    for source in value_refs:
        for local in range(source.shape[0] // QBLK):
            rows = source[local * QBLK : (local + 1) * QBLK, :].astype(F32).T.astype(BF16)
            at = pl.multiple_of(places[block] * QBLK, QBLK) if causal else block * QBLK
            values_t[:, pl.ds(at, QBLK)] = rows
            block += 1

    def body(i, place, size):
        rows = pl.ds(pl.multiple_of(i * QBLK, QBLK), QBLK)
        both = stack_heads(q_ref[rows, :])
        scores = masked_scores(causal, keys[:size, :], both, place, length, QBLK)
        highest = jnp.max(scores, axis=0, keepdims=True)
        exponent = jnp.exp(scores - highest)
        total = jnp.sum(exponent, axis=0, keepdims=True)
        mixed = dot_nn(values_t[:, :size], exponent.astype(BF16)) * (1.0 / total)
        out_ref[rows, :] = unstack_heads(mixed, QBLK)
        total_ref[0, pl.ds(i, 1), :] = highest + jnp.log(total)

    for_each_block(
        causal,
        variants_of(keys.shape[0], causal),
        q_ref.shape[0] // QBLK,
        own_places,
        length,
        body,
    )


def attention_forward(causal, queries, keys, values, places, own_places, length):
    rows, width = queries.shape
    n_src = len(keys)
    key_count = sum(k.shape[0] for k in keys)
    pairs = width // PAIR
    column = lambda i, *_: (0, i)
    spec = lambda n: pl.BlockSpec((n, PAIR), column)
    return pl.pallas_call(
        functools.partial(forward_body, causal, n_src),
        grid_spec=pltpu.PrefetchScalarGridSpec(
            num_scalar_prefetch=3,
            grid=(pairs,),
            in_specs=[spec(rows)] + [spec(k.shape[0]) for k in (*keys, *values)],
            out_specs=[
                spec(rows),
                pl.BlockSpec((1, rows // QBLK, 2 * QBLK), lambda i, *_: (i, 0, 0)),
            ],
            scratch_shapes=[
                pltpu.VMEM((key_count, PAIR), BF16),
                pltpu.VMEM((PAIR, key_count), BF16),
            ],
        ),
        out_shape=[
            jax.ShapeDtypeStruct((rows, width), F32),
            jax.ShapeDtypeStruct((pairs, rows // QBLK, 2 * QBLK), F32),
        ],
        compiler_params=pltpu.CompilerParams(vmem_limit_bytes=VMEM_LIMIT),
        name="self_forward" if causal else "cross_forward",
    )(places, own_places, length, queries, *keys, *values)


def backward_body(causal, n_src, places, own_places, length_ref, q_ref, g_ref, o_ref, t_ref, *refs):
    key_refs, value_refs = refs[:n_src], refs[n_src : 2 * n_src]
    dq_ref = refs[2 * n_src]
    dk_refs = refs[2 * n_src + 1 : 3 * n_src + 1]
    dv_refs = refs[3 * n_src + 1 : 4 * n_src + 1]
    keys, values, keys_t, dk, dv = refs[4 * n_src + 1 :]
    load_keys(causal, places, key_refs, keys)
    load_keys(causal, places, value_refs, values)
    length = length_ref[0]
    key_count = keys.shape[0]
    for block in range(key_count // QBLK):
        rows = slice(block * QBLK, (block + 1) * QBLK)
        keys_t[:, rows] = keys[rows, :].astype(F32).T.astype(BF16)
    dk[...] = jnp.zeros_like(dk)
    dv[...] = jnp.zeros_like(dv)

    def body(i, place, size):
        rows = pl.ds(pl.multiple_of(i * QBLK, QBLK), QBLK)
        both = stack_heads(q_ref[rows, :])
        grads = g_ref[rows, :]
        both_grads = stack_heads(grads)
        products = (grads.astype(F32) * o_ref[rows, :]).T
        delta = jnp.concatenate(
            [
                jnp.sum(products[:HD], axis=0, keepdims=True),
                jnp.sum(products[HD:], axis=0, keepdims=True),
            ],
            axis=1,
        )
        scores = masked_scores(causal, keys[:size, :], both, place, length, QBLK)
        prob = jnp.exp(scores - t_ref[0, pl.ds(i, 1), :])
        prob_grad = dot_nt(values[:size, :], both_grads)
        score_grad = (prob * (prob_grad - delta)).astype(BF16)
        dv[:size, :] += dot_nn(prob.astype(BF16), both_grads)
        dk[:size, :] += dot_nn(score_grad, both)
        dq = dot_nn(keys_t[:, :size], score_grad)
        dq_ref[rows, :] = unstack_heads(dq, QBLK) * ATTN_SCALE

    for_each_block(
        causal, variants_of(key_count, causal), q_ref.shape[0] // QBLK, own_places, length, body
    )
    block = 0
    for dk_out, dv_out in zip(dk_refs, dv_refs):
        for local in range(dk_out.shape[0] // QBLK):
            at = pl.multiple_of(places[block] * QBLK, QBLK) if causal else block * QBLK
            rows = slice(local * QBLK, (local + 1) * QBLK)
            dk_out[rows, :] = dk[pl.ds(at, QBLK), :].astype(BF16)
            dv_out[rows, :] = dv[pl.ds(at, QBLK), :].astype(BF16)
            block += 1


def attention_backward(
    causal, queries, grads, mixed, totals, keys, values, places, own_places, length
):
    rows, width = queries.shape
    n_src = len(keys)
    key_count = sum(k.shape[0] for k in keys)
    pairs = width // PAIR
    column = lambda i, *_: (0, i)
    spec = lambda n: pl.BlockSpec((n, PAIR), column)
    key_specs = [spec(k.shape[0]) for k in (*keys, *values)]
    outs = pl.pallas_call(
        functools.partial(backward_body, causal, n_src),
        grid_spec=pltpu.PrefetchScalarGridSpec(
            num_scalar_prefetch=3,
            grid=(pairs,),
            in_specs=[
                spec(rows),
                spec(rows),
                spec(rows),
                pl.BlockSpec((1, rows // QBLK, 2 * QBLK), lambda i, *_: (i, 0, 0)),
            ]
            + key_specs,
            out_specs=[spec(rows)] + key_specs,
            scratch_shapes=[
                pltpu.VMEM((key_count, PAIR), BF16),
                pltpu.VMEM((key_count, PAIR), BF16),
                pltpu.VMEM((PAIR, key_count), BF16),
                pltpu.VMEM((key_count, PAIR), F32),
                pltpu.VMEM((key_count, PAIR), F32),
            ],
        ),
        out_shape=[jax.ShapeDtypeStruct((rows, width), F32)]
        + [jax.ShapeDtypeStruct(k.shape, BF16) for k in (*keys, *values)],
        compiler_params=pltpu.CompilerParams(vmem_limit_bytes=VMEM_LIMIT),
        name="self_backward" if causal else "cross_backward",
    )(places, own_places, length, queries, grads, mixed, totals, *keys, *values)
    return outs[0], outs[1 : n_src + 1], outs[n_src + 1 :]


UNITS = 16
FIRST = 12
HALF = UNITS // 2
VECTORS = HALF
VROWS = 16
LANES = 128


def coordinates():
    core, f = lax.axis_index("ctx"), lax.axis_index("fsdp")
    return core, core % 2, f // 4, (f // 2) % 2, f % 2


def flip(odd, y, x, a, b):
    dx = a * (1 - odd) + b * odd
    dy = b * (1 - odd) + a * odd
    return y + dy * (1 - 2 * y), x + dx * (1 - 2 * x)


def peers_of(core, odd, z, y, x, depth):
    fsdp = lambda zz, yy, xx: (zz * 2 + yy) * 2 + xx
    ups = [(core, fsdp((z + k) % depth, y, x)) for k in range(1, depth)]
    first = (core, fsdp(z, *flip(odd, y, x, 1, 0)))
    second = (core, fsdp(z, *flip(odd, y, x, 0, 1)))
    partner = (core + 1 - 2 * odd, fsdp(z, y, x))
    return ups, first, second, partner


def enter(ups, first, second, partner):
    barrier = pltpu.get_barrier_semaphore()
    for peer in (*ups, first, second, partner):
        pl.semaphore_signal(barrier, inc=1, device_id=peer, device_id_type=MESH)
    pl.semaphore_wait(barrier, len(ups) + 3)


def remote(source, target, send, recv, peer):
    return pltpu.make_async_remote_copy(
        source, target, send, recv, device_id=peer, device_id_type=MESH
    )


def unit_set(g1, g2, gv, i, odd, y, x):
    if i == VECTORS:
        return gv.at[odd, :, y, x]
    if 2 * i < FIRST:
        return g1.at[2 * i + odd, :, y, x]
    return g2.at[:, y, x, 2 * i - FIRST + odd]


def unit_block(g1, g2, gv, i, odd, z, y, x):
    if i == VECTORS:
        return gv.at[odd, z, y, x]
    if 2 * i < FIRST:
        return g1.at[2 * i + odd, z, y, x]
    return g2.at[z, y, x, 2 * i - FIRST + odd]


def gather_body(
    depth, vectors, sp, so, cq, ckv, co, fi, fo, g1, g2, gv, own, load_sem, own_sem,
    zs, zr, fs, fr, ss, sr, ps, pr,
):
    core, odd, z, y, x = coordinates()
    ups, first, second, partner = peers_of(core, odd, z, y, x, depth)
    width = so.shape[1]
    rows = so.shape[0]
    sources = (
        [sp.at[:, pl.ds(j * width, width)] for j in range(3)]
        + [so, cq]
        + [ckv.at[:, pl.ds(j * width, width)] for j in range(2)]
        + [co]
        + [fi.at[:, pl.ds(j * width, width)] for j in range(4)]
        + [fo.at[pl.ds(j * rows, rows), :] for j in range(4)]
    )
    loads = [pltpu.make_async_copy(s, own.at[u], load_sem.at[u]) for u, s in enumerate(sources)]
    for load in loads:
        load.start()
    enter(ups, first, second, partner)

    def mine(i):
        return vectors.at[odd] if i == VECTORS else own.at[2 * i + odd]

    def set_of(i, a, b):
        return unit_set(g1, g2, gv, i, odd, *flip(odd, y, x, a, b))

    def up_copy(i, k):
        block = unit_block(g1, g2, gv, i, odd, z, y, x)
        return remote(mine(i), block, zs.at[i, k], zr.at[i, k], ups[k])

    def up_arrival(i, k):
        block = unit_block(g1, g2, gv, i, odd, (z + depth - 1 - k) % depth, y, x)
        return remote(block, block, zs.at[i, k], zr.at[i, k], ups[k])

    def first_copy(i):
        return remote(set_of(i, 0, 0), set_of(i, 0, 0), fs.at[i], fr.at[i], first)

    def second_copy(i, a):
        return remote(set_of(i, a, 0), set_of(i, a, 0), ss.at[i, a], sr.at[i, a], second)

    def partner_copy(i, a, b):
        at = a + 2 * b
        return remote(set_of(i, a, b), set_of(i, a, b), ps.at[i, at], pr.at[i, at], partner)

    def arrival(target, send, recv, peer):
        return remote(target, target, send, recv, peer)

    steps = [VECTORS, *range(HALF)]
    keeps = []
    for i in steps:
        if i != VECTORS:
            loads[2 * i].wait()
            loads[2 * i + 1].wait()
        keep = pltpu.make_async_copy(
            mine(i), unit_block(g1, g2, gv, i, odd, z, y, x), own_sem.at[i]
        )
        keep.start()
        keeps.append(keep)
        for k in range(depth - 1):
            up_copy(i, k).start()
    for step in range(len(steps) + 2):
        if step < len(steps):
            i = steps[step]
            keeps[step].wait()
            for k in range(depth - 1):
                up_arrival(i, k).wait_recv()
            first_copy(i).start()
            second_copy(i, 0).start()
            partner_copy(i, 0, 0).start()
        if 0 <= step - 1 < len(steps):
            i = steps[step - 1]
            arrival(set_of(i, 1, 0), fs.at[i], fr.at[i], first).wait_recv()
            second_copy(i, 1).start()
            partner_copy(i, 1, 0).start()
        if 0 <= step - 2 < len(steps):
            i = steps[step - 2]
            for a in range(2):
                arrival(set_of(i, a, 1), ss.at[i, a], sr.at[i, a], second).wait_recv()
                partner_copy(i, a, 1).start()
    for i in steps:
        for a in range(2):
            for b in range(2):
                at = a + 2 * b
                there = unit_set(g1, g2, gv, i, 1 - odd, *flip(1 - odd, y, x, a, b))
                arrival(there, ps.at[i, at], pr.at[i, at], partner).wait_recv()
                partner_copy(i, a, b).wait_send()
            second_copy(i, a).wait_send()
        first_copy(i).wait_send()
        for k in range(depth - 1):
            up_copy(i, k).wait_send()


def gather_weights(n_fsdp, vectors, sp, so, cq, ckv, co, fi, fo):
    rows, width = so.shape
    depth = n_fsdp // 4
    dma = pltpu.SemaphoreType.DMA
    steps = HALF + 1
    g1, g2, gv = pl.pallas_call(
        functools.partial(gather_body, depth),
        in_specs=[pl.BlockSpec(memory_space=pl.ANY)] * 8,
        out_specs=[pl.BlockSpec(memory_space=pl.ANY)] * 3,
        out_shape=[
            jax.ShapeDtypeStruct((FIRST, depth, 2, 2, rows, width), BF16),
            jax.ShapeDtypeStruct((depth, 2, 2, UNITS - FIRST, rows, width), BF16),
            jax.ShapeDtypeStruct((2, depth, 2, 2, VROWS, LANES), BF16),
        ],
        scratch_shapes=[
            pltpu.VMEM((UNITS, rows, width), BF16),
            dma((UNITS,)),
            dma((steps,)),
            dma((steps, depth - 1)),
            dma((steps, depth - 1)),
            dma((steps,)),
            dma((steps,)),
            dma((steps, 2)),
            dma((steps, 2)),
            dma((steps, 4)),
            dma((steps, 4)),
        ],
        compiler_params=pltpu.CompilerParams(
            collective_id=0, has_side_effects=True, vmem_limit_bytes=VMEM_LIMIT
        ),
        name="gather_weights",
    )(vectors, sp, so, cq, ckv, co, fi, fo)
    return (
        g1.reshape(FIRST, n_fsdp * rows, width),
        g2.reshape(-1, width),
        gv.reshape(2, n_fsdp, VROWS, LANES),
    )


def scatter_body(depth, *refs):
    units = refs[:7]
    (
        g1, g2, gv, out, out_v, own, from_partner, from_second, from_first, from_up, final, final_in,
        own_v, from_partner_v, from_second_v, from_first_v, from_up_v, final_v, final_in_v,
        own_sem, zs, zr, fs, fr, ss, sr, ps, pr, xs, xr,
    ) = refs[7:]
    core, odd, z, y, x = coordinates()
    ups, first, second, partner = peers_of(core, odd, z, y, x, depth)
    order = ((0, 1), (1, 1), (1, 0), (0, 0))

    def pick(i, main, small):
        return small if i == VECTORS else main.at[i]

    def source(i, parity, yy, xx):
        u = 2 * i + parity
        if i == VECTORS:
            return gv.at[parity, :, yy, xx]
        if 2 * i >= FIRST:
            return g2.at[:, yy, xx, u - FIRST]
        if 2 * i >= 8:
            return g1.at[u - 7, :, yy, xx]
        return units[u].at[:, yy, xx] if u < 7 else g1.at[0, :, yy, xx]

    def own_copy(i, a, b, parity):
        at = a + 2 * b
        return pltpu.make_async_copy(
            source(i, parity, *flip(odd, y, x, a, b)),
            pick(i, own, own_v).at[at],
            own_sem.at[i, at],
        )

    def partner_copy(i, a, b, parity):
        at = a + 2 * b
        return remote(
            source(i, parity, *flip(1 - odd, y, x, a, b)),
            pick(i, from_partner, from_partner_v).at[at],
            ps.at[i, at],
            pr.at[i, at],
            partner,
        )

    def second_copy(i, a):
        return remote(
            pick(i, own, own_v).at[a + 2],
            pick(i, from_second, from_second_v).at[a],
            ss.at[i, a],
            sr.at[i, a],
            second,
        )

    def first_copy(i):
        return remote(
            pick(i, own, own_v).at[1],
            pick(i, from_first, from_first_v),
            fs.at[i],
            fr.at[i],
            first,
        )

    def up_copy(i, k):
        return remote(
            pick(i, own, own_v).at[0, (z + 1 + k) % depth],
            pick(i, from_up, from_up_v).at[k],
            zs.at[i, k],
            zr.at[i, k],
            ups[k],
        )

    def final_copy(i):
        return remote(
            pick(i, final, final_v), pick(i, final_in, final_in_v), xs.at[i], xr.at[i], partner
        )

    def add(target, addend):
        def step(j, carry):
            target[j] = target[j] + addend[j]
            return carry

        lax.fori_loop(0, depth, step, 0)

    def start_all(copy, parity_of):
        for i in steps:
            if i != VECTORS and 2 * i < 8:
                for q in range(2):

                    @pl.when(odd == q)
                    def _(i=i, q=q):
                        for a, b in order:
                            copy(i, a, b, parity_of(q)).start()

            else:
                for a, b in order:
                    copy(i, a, b, parity_of(odd)).start()

    steps = [*range(HALF - 1, -1, -1), VECTORS]
    start_all(own_copy, lambda q: q)
    enter(ups, first, second, partner)
    start_all(partner_copy, lambda q: 1 - q)

    for step in range(len(steps) + 3):
        if step < len(steps):
            i = steps[step]
            for a, b in order:
                at = a + 2 * b
                own_copy(i, a, b, 0).wait()
                partner_copy(i, a, b, 0).wait_recv()
                add(pick(i, own, own_v).at[at], pick(i, from_partner, from_partner_v).at[at])
                if b:
                    second_copy(i, a).start()
        if 0 <= step - 1 < len(steps):
            i = steps[step - 1]
            for a in (1, 0):
                second_copy(i, a).wait_recv()
                add(pick(i, own, own_v).at[a], pick(i, from_second, from_second_v).at[a])
                if a:
                    first_copy(i).start()
        if 0 <= step - 2 < len(steps):
            i = steps[step - 2]
            first_copy(i).wait_recv()
            add(pick(i, own, own_v).at[0], pick(i, from_first, from_first_v))
            for k in range(depth - 1):
                up_copy(i, k).start()
        if 0 <= step - 3 < len(steps):
            i = steps[step - 3]
            total = pick(i, own, own_v)[0, z].astype(F32)
            for k in range(depth - 1):
                up_copy(i, k).wait_recv()
                total = total + pick(i, from_up, from_up_v)[k].astype(F32)
            pick(i, final, final_v)[...] = total
            final_copy(i).start()
            if i == VECTORS:
                out_v[odd] = total
            else:
                out[2 * i + odd] = total
    for i in steps:
        final_copy(i).wait()
        if i == VECTORS:
            out_v[1 - odd] = final_in_v[...]
        else:
            out[2 * i + 1 - odd] = final_in[i]
        for a, b in order:
            partner_copy(i, a, b, 0).wait_send()
        for a in range(2):
            second_copy(i, a).wait_send()
        first_copy(i).wait_send()
        for k in range(depth - 1):
            up_copy(i, k).wait_send()


def scatter_gradients(n_fsdp, units, g1, g2, gv):
    width = g1.shape[-1]
    depth = n_fsdp // 4
    rows = width // n_fsdp
    dma = pltpu.SemaphoreType.DMA
    vmem = pltpu.VMEM
    steps = HALF + 1
    block, small = (rows, width), (VROWS, LANES)
    return pl.pallas_call(
        functools.partial(scatter_body, depth),
        in_specs=[pl.BlockSpec(memory_space=pl.ANY)] * 10,
        out_specs=[pl.BlockSpec(memory_space=pltpu.VMEM)] * 2,
        out_shape=[
            jax.ShapeDtypeStruct((UNITS, *block), F32),
            jax.ShapeDtypeStruct((2, *small), F32),
        ],
        scratch_shapes=[
            vmem((HALF, 4, depth, *block), BF16),
            vmem((HALF, 4, depth, *block), BF16),
            vmem((HALF, 2, depth, *block), BF16),
            vmem((HALF, depth, *block), BF16),
            vmem((HALF, depth - 1, *block), BF16),
            vmem((HALF, *block), F32),
            vmem((HALF, *block), F32),
            vmem((4, depth, *small), BF16),
            vmem((4, depth, *small), BF16),
            vmem((2, depth, *small), BF16),
            vmem((depth, *small), BF16),
            vmem((depth - 1, *small), BF16),
            vmem(small, F32),
            vmem(small, F32),
            dma((steps, 4)),
            dma((steps, depth - 1)),
            dma((steps, depth - 1)),
            dma((steps,)),
            dma((steps,)),
            dma((steps, 2)),
            dma((steps, 2)),
            dma((steps, 4)),
            dma((steps, 4)),
            dma((steps,)),
            dma((steps,)),
        ],
        compiler_params=pltpu.CompilerParams(
            collective_id=1, has_side_effects=True, vmem_limit_bytes=VMEM_LIMIT
        ),
        name="scatter_gradients",
    )(
        *[u.reshape(depth, 2, 2, *block) for u in units],
        g1.reshape(-1, depth, 2, 2, *block),
        g2.reshape(depth, 2, 2, UNITS - FIRST, *block),
        gv.reshape(2, depth, 2, 2, *small),
    )


CHUNK = 256
VECTOR_ROWS = (5, 6, 8, 11, 9, 12)


def valid_of(own_places, length, chunk):
    row = lax.broadcasted_iota(jnp.int32, (CHUNK, 1), 0)
    place = row
    for block in range(CHUNK // QBLK):
        base = (own_places[chunk * (CHUNK // QBLK) + block] - block) * QBLK
        place = jnp.where((row >= block * QBLK) & (row < (block + 1) * QBLK), row + base, place)
    return place < length


def norm_stats(value):
    average = jnp.mean(value, axis=-1, keepdims=True)
    centred = value - average
    scale = lax.rsqrt(jnp.mean(centred * centred, axis=-1, keepdims=True) + EPSILON)
    return centred * scale, scale


def norm_back(grad, normed, scale):
    inner = jnp.mean(grad * normed, axis=-1, keepdims=True)
    return (grad - jnp.mean(grad, axis=-1, keepdims=True) - normed * inner) * scale


def feed_body(
    own_places, length_ref, mixed_ref, after_ref, cot_ref, vec_ref, b_fi_ref, g1, g2,
    out_ref, gmix_ref, grad_ref, sums_ref, isum_ref, d1, d2,
    w_co, w_fi, w_fo, mixed_low, normed, scale_ref, cross, cross_low, hidden, slope, grad_inner,
    total, grad_low, buffer, load_sem, store_sem,
):
    rows, width = after_ref.shape
    chunks = [pl.ds(c * CHUNK, CHUNK) for c in range(rows // CHUNK)]
    loads = [pltpu.make_async_copy(g1.at[7], w_co, load_sem.at[0])]
    for j in range(4):
        loads.append(pltpu.make_async_copy(g1.at[8 + j], w_fi.at[j], load_sem.at[1 + j]))
    for j in range(4):
        loads.append(
            pltpu.make_async_copy(
                g2.at[pl.ds(j * width, width), :], w_fo.at[j], load_sem.at[5 + j]
            )
        )
    for load in loads:
        load.start()
    vec = lambda i: vec_ref[VECTOR_ROWS[i] : VECTOR_ROWS[i] + 1, :]
    column_sum = lambda array: jnp.sum(array, axis=0, keepdims=True)

    loads[0].wait()
    for c in chunks:
        mixed_low[c, :] = mixed_ref[c, :].astype(BF16)
        value = after_ref[c, :] + dot_nn(mixed_low[c, :], w_co[...]) + vec(0)
        hat, scale = norm_stats(value)
        normed[c, :] = hat
        scale_ref[c, :] = scale
        value = hat * vec(2) + vec(3)
        cross[c, :] = value
        cross_low[c, :] = value.astype(BF16)
        total[c, :] = value + vec(1)
    for j in range(4):
        loads[1 + j].wait()
        loads[5 + j].wait()
        bias = b_fi_ref[:, j * width : (j + 1) * width]

        def inner_step(at, carry, j=j, bias=bias):
            c = pl.ds(pl.multiple_of(at * CHUNK, CHUNK), CHUNK)
            pre = dot_nn(cross_low[c, :], w_fi[j]) + bias
            share = 0.5 + 0.5 * lax.erf(pre * (0.5**0.5))
            act = (pre * share).astype(BF16)
            hidden[j, c, :] = act
            density = jnp.exp(-0.5 * pre * pre) * ((0.5 / jnp.pi) ** 0.5)
            slope[j, c, :] = (share + pre * density).astype(BF16)
            total[c, :] += dot_nn(act, w_fo[j])
            return carry

        lax.fori_loop(0, rows // CHUNK, inner_step, 0)
    gain_sum = jnp.zeros((1, width), F32)
    shift_sum = jnp.zeros((1, width), F32)
    grad_sum = jnp.zeros((1, width), F32)
    for at, c in enumerate(chunks):
        hat, scale = norm_stats(total[c, :])
        valid = valid_of(own_places, length_ref[0], at)
        out_ref[c, :] = jnp.where(valid, hat * vec(4) + vec(5), 0.0)
        incoming = jnp.where(valid, cot_ref[c, :].astype(F32), 0.0)
        gain_sum += column_sum(incoming * hat)
        shift_sum += column_sum(incoming)
        grad = norm_back(incoming * vec(4), hat, scale)
        grad_sum += column_sum(grad)
        total[c, :] = grad
        grad_low[c, :] = grad.astype(BF16)
    sums_ref[1:2, :] = grad_sum
    sums_ref[3:4, :] = gain_sum
    sums_ref[5:6, :] = shift_sum

    stores = []

    def store(value, target):
        at = len(stores)
        if at >= 2:
            stores[at - 2].wait()
        buffer[at % 2] = value.astype(BF16)
        copy = pltpu.make_async_copy(buffer.at[at % 2], target, store_sem.at[at % 2])
        copy.start()
        stores.append(copy)

    for j in range(4):

        def back_step(at, carry, j=j):
            c = pl.ds(pl.multiple_of(at * CHUNK, CHUNK), CHUNK)
            grad = dot_nt(grad_low[c, :], w_fo[j]) * slope[j, c, :].astype(F32)
            low = grad.astype(BF16)
            grad_inner[j, c, :] = low
            total[c, :] += dot_nt(low, w_fi[j])
            return carry + column_sum(grad)

        columns = slice(j * width, (j + 1) * width)
        isum_ref[:, columns] = lax.fori_loop(
            0, rows // CHUNK, back_step, jnp.zeros((1, width), F32)
        )
        store(dot_tn(hidden[j], grad_low[...]), d2.at[pl.ds(j * width, width), :])
        store(dot_tn(cross_low[...], grad_inner[j]), d1.at[1 + j])
    gain_sum = jnp.zeros((1, width), F32)
    shift_sum = jnp.zeros((1, width), F32)
    grad_sum = jnp.zeros((1, width), F32)
    for c in chunks:
        incoming = total[c, :]
        hat = normed[c, :]
        gain_sum += column_sum(incoming * hat)
        shift_sum += column_sum(incoming)
        grad = norm_back(incoming * vec(2), hat, scale_ref[c, :])
        grad_sum += column_sum(grad)
        grad_ref[c, :] = grad
        low = grad.astype(BF16)
        grad_low[c, :] = low
        gmix_ref[c, :] = dot_nt(low, w_co[...]).astype(BF16)
    sums_ref[0:1, :] = grad_sum
    sums_ref[2:3, :] = gain_sum
    sums_ref[4:5, :] = shift_sum
    store(dot_tn(mixed_low[...], grad_low[...]), d1.at[0])
    stores[-2].wait()
    stores[-1].wait()


def feed_forward(own_places, length, mixed, after, cotangent, vectors, inner_bias, units, outer):
    rows, width = after.shape
    hidden = outer.shape[0]
    any_spec = pl.BlockSpec(memory_space=pl.ANY)
    vmem_spec = pl.BlockSpec(memory_space=pltpu.VMEM)
    vmem = pltpu.VMEM
    return pl.pallas_call(
        feed_body,
        in_specs=[pl.BlockSpec(memory_space=pltpu.SMEM)] * 2 + [vmem_spec] * 5 + [any_spec] * 2,
        out_specs=[vmem_spec] * 5 + [any_spec] * 2,
        out_shape=[
            jax.ShapeDtypeStruct((rows, width), F32),
            jax.ShapeDtypeStruct((rows, width), BF16),
            jax.ShapeDtypeStruct((rows, width), F32),
            jax.ShapeDtypeStruct((8, width), F32),
            jax.ShapeDtypeStruct((1, hidden), F32),
            jax.ShapeDtypeStruct((5, width, width), BF16),
            jax.ShapeDtypeStruct((hidden, width), BF16),
        ],
        scratch_shapes=[
            vmem((width, width), BF16),
            vmem((4, width, width), BF16),
            vmem((4, width, width), BF16),
            vmem((rows, width), BF16),
            vmem((rows, width), F32),
            vmem((rows, 1), F32),
            vmem((rows, width), F32),
            vmem((rows, width), BF16),
            vmem((4, rows, width), BF16),
            vmem((4, rows, width), BF16),
            vmem((4, rows, width), BF16),
            vmem((rows, width), F32),
            vmem((rows, width), BF16),
            vmem((2, width, width), BF16),
            pltpu.SemaphoreType.DMA((9,)),
            pltpu.SemaphoreType.DMA((2,)),
        ],
        compiler_params=pltpu.CompilerParams(vmem_limit_bytes=VMEM_LIMIT),
        name="feed_forward",
    )(own_places, length, mixed, after, cotangent, vectors, inner_bias, units, outer)


VLANES = 256
WINDOW = 384


def spread_lanes(pieces, width):
    count = WINDOW // width
    lanes = pieces[0].shape[1]
    row = lax.broadcasted_iota(jnp.int32, (lanes, WINDOW), 0)
    column = lax.broadcasted_iota(jnp.int32, (lanes, WINDOW), 1)
    windows = [None] * (len(pieces) // count)
    for k in range(count):
        select = ((column == row + k * width) & (row < width)).astype(F32).astype(BF16)
        for w in range(len(windows)):
            part = dot_nn(pieces[w * count + k], select)
            windows[w] = part if k == 0 else windows[w] + part
    return jnp.concatenate(windows, axis=1)


def pair_forward(causal, p, q, k_all, v_all, values_t, out, totals, own_places, places, length):
    lanes = pl.ds(pl.multiple_of(p * PAIR, PAIR), PAIR)
    parts, part_rows = k_all.shape[0], k_all.shape[1]
    for h in range(parts):
        for block in range(part_rows // QBLK):
            rows = slice(block * QBLK, (block + 1) * QBLK)
            at = h * part_rows + block * QBLK
            values_t[:, at : at + QBLK] = v_all[h, rows, lanes].astype(F32).T.astype(BF16)

    def step(i, carry):
        rows = pl.ds(pl.multiple_of(i * QBLK, QBLK), QBLK)
        both = stack_heads(q[rows, lanes])
        scores = [dot_nt(k_all[h, :, lanes], both) for h in range(parts)]
        if causal:
            limit = row_limit(own_places[i], length)
            scores = [
                mask_part(s, limit, places, h * (part_rows // QBLK)) for h, s in enumerate(scores)
            ]
        highest = jnp.max(scores[0], axis=0, keepdims=True)
        for s in scores[1:]:
            highest = jnp.maximum(highest, jnp.max(s, axis=0, keepdims=True))
        total, mixed = 0.0, 0.0
        for h, s in enumerate(scores):
            exponent = jnp.exp(s - highest)
            total += jnp.sum(exponent, axis=0, keepdims=True)
            mixed += dot_nn(
                values_t[:, h * part_rows : (h + 1) * part_rows], exponent.astype(BF16)
            )
        out[rows, lanes] = unstack_heads(mixed * (1.0 / total), QBLK)
        totals[p, pl.ds(i, 1), :] = highest + jnp.log(total)
        return carry

    lax.fori_loop(0, q.shape[0] // QBLK, step, 0)


def row_limit(place, length):
    column = lax.broadcasted_iota(jnp.int32, (1, 2 * QBLK), 1)
    own = place * QBLK + jnp.where(column >= QBLK, column - QBLK, column)
    return jnp.minimum(own, length - 1)


def mask_part(scores, limit, places, first_block):
    row = lax.broadcasted_iota(jnp.int32, (QBLK, 2 * QBLK), 0)
    blocks = []
    for block in range(scores.shape[0] // QBLK):
        part = scores[block * QBLK : (block + 1) * QBLK]
        kept = row <= limit - places[first_block + block] * QBLK
        blocks.append(jnp.where(kept, part, MASKED_SCORE))
    return jnp.concatenate(blocks, axis=0)


def encode_body(
    depth, own_places, places, length_ref, states, encoder, vectors, sp, so, cq, ckv, co, fi, fo,
    g1, g2, q_out, k_out, v_out, cq_out, ck_out, cv_out, o_out, total_out, after_out, low_out, hat_out,
    scale_out, co_out, ctotal_out, flat_out, inner_out,
    gv, own, w, q, k_all, v_all, c_q, ck_all, cv_all, mixed, after, low, hat, values_t, cvalues_t,
    load_sem, own_sem, weight_sem, store_sem, zs, zr, fs, fr, ss, sr, ps, pr, ks, kr,
):
    core, odd, z, y, x = coordinates()
    ups, first, second, partner = peers_of(core, odd, z, y, x, depth)
    rows, width = so.shape
    length = length_ref[0]
    sources = (
        [sp.at[:, pl.ds(j * width, width)] for j in range(3)]
        + [so, cq]
        + [ckv.at[:, pl.ds(j * width, width)] for j in range(2)]
        + [co]
        + [fi.at[:, pl.ds(j * width, width)] for j in range(4)]
        + [fo.at[pl.ds(j * rows, rows), :] for j in range(4)]
    )
    loads = [pltpu.make_async_copy(s, own.at[u], load_sem.at[u]) for u, s in enumerate(sources)]
    for load in loads:
        load.start()
    enter(ups, first, second, partner)

    def mine(i):
        return vectors if i == VECTORS else own.at[2 * i + odd]

    def set_at(i, parity, yy, xx):
        return gv.at[:, yy, xx] if i == VECTORS else unit_set(g1, g2, None, i, parity, yy, xx)

    def block_at(i, zz):
        return gv.at[zz, y, x] if i == VECTORS else unit_block(g1, g2, None, i, odd, zz, y, x)

    def set_of(i, a, b):
        return set_at(i, odd, *flip(odd, y, x, a, b))

    def up_copy(i, k):
        return remote(mine(i), block_at(i, z), zs.at[i, k], zr.at[i, k], ups[k])

    def up_arrival(i, k):
        block = block_at(i, (z + depth - 1 - k) % depth)
        return remote(block, block, zs.at[i, k], zr.at[i, k], ups[k])

    def first_copy(i):
        return remote(set_of(i, 0, 0), set_of(i, 0, 0), fs.at[i], fr.at[i], first)

    def first_arrival(i):
        return remote(set_of(i, 1, 0), set_of(i, 1, 0), fs.at[i], fr.at[i], first)

    def second_copy(i, a):
        return remote(set_of(i, a, 0), set_of(i, a, 0), ss.at[i, a], sr.at[i, a], second)

    def second_arrival(i, a):
        return remote(set_of(i, a, 1), set_of(i, a, 1), ss.at[i, a], sr.at[i, a], second)

    def partner_copy(i, a, b):
        at = a + 2 * b
        return remote(set_of(i, a, b), set_of(i, a, b), ps.at[i, at], pr.at[i, at], partner)

    def partner_arrival(i, a, b):
        at = a + 2 * b
        there = set_at(i, 1 - odd, *flip(1 - odd, y, x, a, b))
        return remote(there, there, ps.at[i, at], pr.at[i, at], partner)

    keeps = {}

    def begin(i):
        keeps[i] = pltpu.make_async_copy(mine(i), block_at(i, z), own_sem.at[i])
        keeps[i].start()
        for k in range(depth - 1):
            up_copy(i, k).start()

    def stage_2(i):
        keeps[i].wait()
        for k in range(depth - 1):
            up_arrival(i, k).wait_recv()
        first_copy(i).start()
        second_copy(i, 0).start()
        if i != VECTORS:
            partner_copy(i, 0, 0).start()

    def stage_3(i):
        first_arrival(i).wait_recv()
        second_copy(i, 1).start()
        if i != VECTORS:
            partner_copy(i, 1, 0).start()

    def stage_4(i):
        for a in range(2):
            second_arrival(i, a).wait_recv()
            if i != VECTORS:
                partner_copy(i, a, 1).start()

    def finish(i):
        for a in range(2):
            for b in range(2):
                partner_arrival(i, a, b).wait_recv()

    def weight(u):
        return pltpu.make_async_copy(
            g1.at[u].reshape(width, width), w.at[u], weight_sem.at[u]
        )

    stores = []

    def store(source, target):
        copy = pltpu.make_async_copy(source, target, store_sem.at[len(stores)])
        copy.start()
        stores.append(copy)

    begin(VECTORS)
    for i in range(HALF):
        loads[2 * i].wait()
        loads[2 * i + 1].wait()
        begin(i)
    stage_2(VECTORS)
    stage_2(0)
    stage_3(VECTORS)
    stage_2(1)
    stage_3(0)
    stage_4(VECTORS)
    flat = spread_lanes([gv[f // 4, (f // 2) % 2, f % 2] for f in range(4 * depth)], rows)
    flat_out[...] = flat
    inner_rows = fo.shape[0]
    inner_out[...] = spread_lanes(
        [gv[f // 4, (f // 2) % 2, f % 2] for f in range(4 * depth)], inner_rows
    )[13:14, :]
    vec = lambda i: flat[i : i + 1, :]
    stage_2(2)
    stage_3(1)
    stage_4(0)
    stage_2(3)
    stage_3(2)
    stage_4(1)
    finish(0)
    finish(1)
    for u in range(4):
        weight(u).start()
    stage_2(4)

    row_count = states.shape[0]
    chunks = [pl.ds(c * CHUNK, CHUNK) for c in range(row_count // CHUNK)]
    encoder_count = encoder.shape[0]
    step = min(CHUNK, encoder_count)
    encoder_chunks = [pl.ds(c * step, step) for c in range(encoder_count // step)]

    def share(number, array):
        copy = remote(array.at[0], array.at[1], ks.at[number], kr.at[number], partner)
        copy.start()
        return copy

    weight(1).wait()
    for c in chunks:
        k_all[0, c, :] = dot_nn(states[c, :], w[1]).astype(BF16)
    shares = [share(0, k_all)]
    weight(2).wait()
    for c in chunks:
        v_all[0, c, :] = (dot_nn(states[c, :], w[2]) + vec(1)).astype(BF16)
    shares.append(share(1, v_all))
    weight(0).wait()
    for c in chunks:
        q[c, :] = ((dot_nn(states[c, :], w[0]) + vec(0)) * ATTN_SCALE).astype(BF16)
    store(q, q_out)
    stage_3(3)
    stage_4(2)
    shares[0].wait_recv()
    shares[1].wait_recv()
    store(k_all, k_out)
    store(v_all, v_out)

    def self_pairs(begin_at, end_at):
        def body(p, carry):
            pair_forward(
                True, p, q, k_all, v_all, values_t, mixed, total_out, own_places, places, length
            )
            return carry

        lax.fori_loop(begin_at, end_at, body, 0)

    pairs = width // PAIR
    self_pairs(0, pairs // 3)
    stage_2(5)
    stage_3(4)
    stage_4(3)
    self_pairs(pairs // 3, 2 * pairs // 3)
    stage_2(6)
    stage_3(5)
    stage_4(4)
    finish(2)
    finish(3)
    for u in range(4, 8):
        weight(u).start()
    self_pairs(2 * pairs // 3, pairs)
    store(mixed, o_out)
    stage_2(7)
    stage_3(6)
    stage_4(5)
    weight(5).wait()
    for c in encoder_chunks:
        ck_all[0, c, :] = dot_nn(encoder[c, :], w[5]).astype(BF16)
    shares.append(share(2, ck_all))
    weight(6).wait()
    for c in encoder_chunks:
        cv_all[0, c, :] = (dot_nn(encoder[c, :], w[6]) + vec(4)).astype(BF16)
    shares.append(share(3, cv_all))
    weight(3).wait()
    weight(4).wait()
    for c in chunks:
        value = states[c, :].astype(F32) + dot_nn(mixed[c, :].astype(BF16), w[3]) + vec(2)
        normed, scale = norm_stats(value)
        hat[c, :] = normed
        scale_out[c, :] = scale
        value = normed * vec(7) + vec(10)
        after[c, :] = value
        low[c, :] = value.astype(BF16)
        c_q[c, :] = ((dot_nn(low[c, :], w[4]) + vec(3)) * ATTN_SCALE).astype(BF16)
    store(hat, hat_out)
    store(after, after_out)
    store(low, low_out)
    store(c_q, cq_out)
    stage_3(7)
    stage_4(6)
    shares[2].wait_recv()
    shares[3].wait_recv()
    store(ck_all, ck_out)
    store(cv_all, cv_out)
    stores[3].wait()

    def cross_pairs(begin_at, end_at):
        def body(p, carry):
            pair_forward(
                False, p, c_q, ck_all, cv_all, cvalues_t, mixed, ctotal_out, None, None, None
            )
            return carry

        lax.fori_loop(begin_at, end_at, body, 0)

    cross_pairs(0, pairs // 2)
    stage_4(7)
    cross_pairs(pairs // 2, pairs)
    store(mixed, co_out)
    weight(7).wait()
    for at, copy in enumerate(stores):
        if at != 3:
            copy.wait()
    for copy in shares:
        copy.wait_send()
    for i in [VECTORS, *range(HALF)]:
        if i >= 4 and i != VECTORS:
            finish(i)
        for a in range(2):
            for b in range(2):
                if i != VECTORS:
                    partner_copy(i, a, b).wait_send()
            second_copy(i, a).wait_send()
        first_copy(i).wait_send()
        for k in range(depth - 1):
            up_copy(i, k).wait_send()


def encode(
    n_fsdp, own_places, places, length, states, encoder, vectors, sp, so, cq, ckv, co, fi, fo
):
    rows, width = so.shape
    depth = n_fsdp // 4
    row_count, encoder_count = states.shape[0], encoder.shape[0]
    pairs = width // PAIR
    steps = HALF + 1
    dma = pltpu.SemaphoreType.DMA
    vmem = pltpu.VMEM
    any_spec = pl.BlockSpec(memory_space=pl.ANY)
    vmem_spec = pl.BlockSpec(memory_space=pltpu.VMEM)
    smem_spec = pl.BlockSpec(memory_space=pltpu.SMEM)
    shape = jax.ShapeDtypeStruct
    totals = (pairs, row_count // QBLK, 2 * QBLK)
    outs = [
        (any_spec, (FIRST, depth, 2, 2, rows, width), BF16),
        (any_spec, (depth, 2, 2, UNITS - FIRST, rows, width), BF16),
        (any_spec, (row_count, width), BF16),
        (any_spec, (2, row_count, width), BF16),
        (any_spec, (2, row_count, width), BF16),
        (any_spec, (row_count, width), BF16),
        (any_spec, (2, encoder_count, width), BF16),
        (any_spec, (2, encoder_count, width), BF16),
        (any_spec, (row_count, width), F32),
        (vmem_spec, totals, F32),
        (any_spec, (row_count, width), F32),
        (any_spec, (row_count, width), BF16),
        (any_spec, (row_count, width), F32),
        (vmem_spec, (row_count, 1), F32),
        (any_spec, (row_count, width), F32),
        (vmem_spec, totals, F32),
        (vmem_spec, (VROWS, width), F32),
        (vmem_spec, (1, fo.shape[0] * n_fsdp), F32),
    ]
    return pl.pallas_call(
        functools.partial(encode_body, depth),
        in_specs=[smem_spec] * 3 + [vmem_spec] * 3 + [any_spec] * 7,
        out_specs=[spec for spec, _, _ in outs],
        out_shape=[shape(extent, kind) for _, extent, kind in outs],
        scratch_shapes=[
            vmem((depth, 2, 2, VROWS, VLANES), BF16),
            vmem((UNITS, rows, width), BF16),
            vmem((8, width, width), BF16),
            vmem((row_count, width), BF16),
            vmem((2, row_count, width), BF16),
            vmem((2, row_count, width), BF16),
            vmem((row_count, width), BF16),
            vmem((2, encoder_count, width), BF16),
            vmem((2, encoder_count, width), BF16),
            vmem((row_count, width), F32),
            vmem((row_count, width), F32),
            vmem((row_count, width), BF16),
            vmem((row_count, width), F32),
            vmem((PAIR, 2 * row_count), BF16),
            vmem((PAIR, 2 * encoder_count), BF16),
            dma((UNITS,)),
            dma((steps,)),
            dma((8,)),
            dma((12,)),
            dma((steps, depth - 1)),
            dma((steps, depth - 1)),
            dma((steps,)),
            dma((steps,)),
            dma((steps, 2)),
            dma((steps, 2)),
            dma((steps, 4)),
            dma((steps, 4)),
            dma((4,)),
            dma((4,)),
        ],
        compiler_params=pltpu.CompilerParams(
            collective_id=2, has_side_effects=True, vmem_limit_bytes=VMEM_LIMIT
        ),
        name="encode",
    )(own_places, places, length, states, encoder, vectors, sp, so, cq, ckv, co, fi, fo)


def pair_backward(
    causal, p, q, g, o, totals, k_all, v_all, keys_t, dk, dv, dq, kept, sent, sums, sum_row,
    own_places, places, length,
):
    lanes = pl.ds(pl.multiple_of(p * PAIR, PAIR), PAIR)
    parts, part_rows = k_all.shape[0], k_all.shape[1]
    for h in range(parts):
        for block in range(part_rows // QBLK):
            rows = slice(block * QBLK, (block + 1) * QBLK)
            at = h * part_rows + block * QBLK
            keys_t[:, at : at + QBLK] = k_all[h, rows, lanes].astype(F32).T.astype(BF16)
    dk[...] = jnp.zeros_like(dk)
    dv[...] = jnp.zeros_like(dv)

    def step(i, carry):
        rows = pl.ds(pl.multiple_of(i * QBLK, QBLK), QBLK)
        both = stack_heads(q[rows, lanes])
        grads = g[rows, lanes]
        both_grads = stack_heads(grads)
        products = (grads.astype(F32) * o[rows, lanes]).T
        delta = jnp.concatenate(
            [
                jnp.sum(products[:HD], axis=0, keepdims=True),
                jnp.sum(products[HD:], axis=0, keepdims=True),
            ],
            axis=1,
        )
        if causal:
            limit = row_limit(own_places[i], length)
        level = totals[p, pl.ds(i, 1), :]
        query_grad = 0.0
        for h in range(parts):
            span = slice(h * part_rows, (h + 1) * part_rows)
            scores = dot_nt(k_all[h, :, lanes], both)
            if causal:
                scores = mask_part(scores, limit, places, h * (part_rows // QBLK))
            prob = jnp.exp(scores - level)
            prob_grad = dot_nt(v_all[h, :, lanes], both_grads)
            score_grad = (prob * (prob_grad - delta)).astype(BF16)
            dv[span, :] += dot_nn(prob.astype(BF16), both_grads)
            dk[span, :] += dot_nn(score_grad, both)
            query_grad += dot_nn(keys_t[:, span], score_grad)
        query_grad = unstack_heads(query_grad, QBLK) * ATTN_SCALE
        dq[rows, lanes] = query_grad.astype(BF16)
        return carry + jnp.sum(query_grad, axis=0, keepdims=True)

    sums[sum_row : sum_row + 1, lanes] = lax.fori_loop(
        0, q.shape[0] // QBLK, step, jnp.zeros((1, PAIR), F32)
    )
    for at, grad in enumerate((dk, dv)):
        kept[at, :, lanes] = grad[:part_rows, :].astype(BF16)
        sent[at, :, lanes] = grad[part_rows:, :].astype(BF16)


def select_lanes(offset, first, limit, lanes):
    lane = lax.broadcasted_iota(jnp.int32, (WINDOW, lanes), 1) + first
    column = lax.broadcasted_iota(jnp.int32, (WINDOW, lanes), 0)
    return ((column == lane + offset) & (lane < limit)).astype(F32).astype(BF16)


def decode_body(
    depth, own_places, places, length_ref, flat, scale_ref, ctotal, total, feed_sums, inner_sum,
    units, cq_in, ck_in, cv_in, co_in, gmix_in, low_in, encoder_in, hat_in, grad_in, q_in, k_in, v_in,
    o_in, states_in, d1, d2,
    gs_out, ge_out, out, out_v,
    own, from_partner, from_second, from_first, from_up, w, q, g, o, k, v, dq, kept, sent, arrived,
    inputs, enc, hat, grad, dk, dv, keys_t, sums,
    gv, from_partner_v, from_second_v, from_first_v, from_up_v,
    load_sem, own_sem, store_sem, zs, zr, fs, fr, ss, sr, ps, pr, xs, xr, ks, kr,
):
    core, odd, z, y, x = coordinates()
    ups, first, second, partner = peers_of(core, odd, z, y, x, depth)
    rows, width = units.shape[-2:]
    row_count = q.shape[0]
    length = length_ref[0]
    order = ((0, 1), (1, 1), (1, 0), (0, 0))
    pairs = width // PAIR
    chunks = [pl.ds(c * CHUNK, CHUNK) for c in range(row_count // CHUNK)]
    column_sum = lambda array: jnp.sum(array, axis=0, keepdims=True)


    def pick(i, main, small):
        return small if i == VECTORS else main.at[i]

    def kept_set(i, a, b):
        yy, xx = flip(odd, y, x, a, b)
        return gv.at[odd, :, yy, xx] if i == VECTORS else own.at[i, :, yy, xx]

    def sent_set(i, a, b):
        yy, xx = flip(1 - odd, y, x, a, b)
        u = 2 * i + 1 - odd
        if i == VECTORS:
            return gv.at[1 - odd, :, yy, xx]
        if 2 * i >= FIRST:
            return d2.at[:, yy, xx, u - FIRST]
        if 2 * i >= 8:
            return d1.at[u - 7, :, yy, xx]
        return own.at[HALF + i, :, yy, xx]

    def own_copy(i):
        u = 2 * i + odd
        source = d2.at[:, :, :, u - FIRST] if 2 * i >= FIRST else d1.at[u - 7]
        return pltpu.make_async_copy(source, own.at[i], own_sem.at[i])

    def partner_copy(i, a, b):
        at = a + 2 * b
        return remote(
            sent_set(i, a, b),
            pick(i, from_partner, from_partner_v).at[at],
            ps.at[i, at],
            pr.at[i, at],
            partner,
        )

    def second_copy(i, a):
        target = pick(i, from_second, from_second_v).at[a]
        return remote(kept_set(i, a, 1), target, ss.at[i, a], sr.at[i, a], second)

    def first_copy(i):
        target = pick(i, from_first, from_first_v)
        return remote(kept_set(i, 1, 0), target, fs.at[i], fr.at[i], first)

    def up_copy(i, n):
        source = kept_set(i, 0, 0).at[(z + 1 + n) % depth]
        target = pick(i, from_up, from_up_v).at[n]
        return remote(source, target, zs.at[i, n], zr.at[i, n], ups[n])

    def final_copy(i, parity):
        target = out_v.at[parity] if i == VECTORS else out.at[2 * i + parity]
        return remote(target, target, xs.at[i], xr.at[i], partner)

    def add(target, addend):
        def step(j, carry):
            target[j] = target[j] + addend[j]
            return carry

        lax.fori_loop(0, depth, step, 0)

    def send(i):
        for a, b in order:
            partner_copy(i, a, b).start()

    def stage_1(i):
        if HALF > i >= 4:
            own_copy(i).wait()
        for a, b in order:
            partner_copy(i, a, b).wait_recv()
            add(kept_set(i, a, b), pick(i, from_partner, from_partner_v).at[a + 2 * b])
            if b:
                second_copy(i, a).start()

    def stage_2(i):
        for a in (1, 0):
            second_copy(i, a).wait_recv()
            add(kept_set(i, a, 0), pick(i, from_second, from_second_v).at[a])
            if a:
                first_copy(i).start()

    def stage_3(i):
        first_copy(i).wait_recv()
        add(kept_set(i, 0, 0), pick(i, from_first, from_first_v))
        for n in range(depth - 1):
            up_copy(i, n).start()

    def stage_4(i):
        value = kept_set(i, 0, 0)[z].astype(F32)
        for n in range(depth - 1):
            up_copy(i, n).wait_recv()
            value = value + pick(i, from_up, from_up_v)[n].astype(F32)
        if i == VECTORS:
            out_v[odd] = value
        else:
            out[2 * i + odd] = value
        final_copy(i, odd).start()

    def put_unit(u, value):
        at = u // 2 + HALF * ((u + odd) % 2)
        own[at] = value.astype(BF16).reshape(depth, 2, 2, rows, width)


    loads = []

    def load(source, target):
        copy = pltpu.make_async_copy(source, target, load_sem.at[len(loads)])
        copy.start()
        loads.append(copy)
        return copy

    def weight(u, at):
        return load(units.at[u].reshape(width, width), w.at[at])

    attention_loads = [load(*pair) for pair in ((cq_in, q), (ck_in, k), (cv_in, v), (gmix_in, g), (co_in, o))]
    for i in range(HALF - 1, 3, -1):
        own_copy(i).start()
    cross_loads = [load(low_in, inputs), weight(4, 0), load(grad_in, grad), load(hat_in, hat), weight(3, 1)]
    encoder_loads = [load(encoder_in, enc), weight(5, 2), weight(6, 3)]
    output_load = load(d1.at[0], own.at[3 + HALF * ((7 + odd) % 2)])
    enter(ups, first, second, partner)
    for i in range(HALF - 1, 3, -1):
        send(i)

    sums[...] = jnp.zeros_like(sums)
    for at, row in enumerate((5, 6, 8, 9, 11, 12)):
        sums[row : row + 1, :] = feed_sums[at : at + 1, :]
    for copy in attention_loads:
        copy.wait()

    def cross_step(p, carry):
        pair_backward(
            False, p, q, g, o, ctotal, k, v, keys_t, dk, dv, dq, kept, sent, sums, 3, None, None, None
        )

        @pl.when(p == 0)
        def _():
            stage_1(7)

        @pl.when(p == 2)
        def _():
            stage_1(6)
            stage_2(7)

        @pl.when(p == 4)
        def _():
            stage_1(5)
            stage_2(6)
            stage_3(7)

        return carry

    lax.fori_loop(0, pairs, cross_step, 0)
    cross_share = remote(sent, arrived.at[0], ks.at[0], kr.at[0], partner)
    cross_share.start()
    self_loads = [load(*pair) for pair in ((o_in, o), (q_in, q), (k_in, k), (v_in, v))]
    for copy in cross_loads:
        copy.wait()
    put_unit(4, dot_tn(inputs[...], dq[...]))
    states_load = load(states_in, inputs)
    gain_sum = jnp.zeros((1, width), F32)
    shift_sum = jnp.zeros((1, width), F32)
    grad_sum = jnp.zeros((1, width), F32)
    for c in chunks:
        incoming = grad[c, :] + dot_nt(dq[c, :], w[0])
        normed = hat[c, :]
        gain_sum += column_sum(incoming * normed)
        shift_sum += column_sum(incoming)
        value = norm_back(incoming * flat[7:8, :], normed, scale_ref[c, :])
        grad_sum += column_sum(value)
        grad[c, :] = value
        low = value.astype(BF16)
        dq[c, :] = low
        g[c, :] = dot_nt(low, w[1]).astype(BF16)
    sums[2:3, :] = grad_sum
    sums[7:8, :] = gain_sum
    sums[10:11, :] = shift_sum
    stage_1(4)
    stage_2(5)
    stage_3(6)
    stage_4(7)
    last_loads = [weight(0, 0)]
    self_loads[0].wait()
    put_unit(3, dot_tn(o[...].astype(BF16), dq[...]))
    last_loads.append(weight(1, 1))

    def total_kept(number, c):
        low = []
        for at in range(2):
            value = kept[at, c, :].astype(F32) + arrived[number, at, c, :].astype(F32)
            kept[at, c, :] = value.astype(BF16)
            low.append(value)
        return column_sum(low[1])

    for copy in encoder_loads:
        copy.wait()
    cross_share.wait_recv()
    sums[4:5, :] = sum(total_kept(0, c) for c in chunks)
    put_unit(5, dot_tn(enc[...], kept[0]))
    send(2)
    put_unit(6, dot_tn(enc[...], kept[1]))
    output_load.wait()
    send(3)
    for c in chunks:
        hat[c, :] = dot_nt(kept[0, c, :], w[2]) + dot_nt(kept[1, c, :], w[3])
    encoder_store = pltpu.make_async_copy(hat, ge_out, store_sem.at[0])
    encoder_store.start()
    last_loads.append(weight(2, 2))
    stage_2(4)
    stage_3(5)
    stage_4(6)
    cross_share.wait_send()
    for copy in self_loads[1:]:
        copy.wait()
    half = (pairs // 2) * PAIR

    def self_share(n):
        span = pl.ds(n * half, half if n == 0 else width - half)
        return remote(
            sent.at[:, :, span], arrived.at[1, :, :, span], ks.at[1 + n], kr.at[1 + n], partner
        )

    def self_step(p, carry):
        pair_backward(
            True, p, q, g, o, total, k, v, keys_t, dk, dv, dq, kept, sent, sums, 0, own_places, places,
            length,
        )

        @pl.when(p == 0)
        def _():
            stage_1(3)
            stage_3(4)
            stage_4(5)

        @pl.when(p == pairs // 2 - 1)
        def _():
            self_share(0).start()
            stage_1(2)
            stage_2(3)
            stage_4(4)

        @pl.when(p == 3)
        def _():
            stage_3(3)

        @pl.when(p == 4)
        def _():
            stage_2(2)

        @pl.when(p == 5)
        def _():
            stage_3(2)

        return carry

    lax.fori_loop(0, pairs, self_step, 0)
    self_share(1).start()
    states_load.wait()
    put_unit(0, dot_tn(inputs[...], dq[...]))
    stage_4(3)
    self_share(0).wait_recv()
    self_share(1).wait_recv()
    sums[1:2, :] = sum(total_kept(1, c) for c in chunks)
    put_unit(1, dot_tn(inputs[...], kept[0]))
    send(0)
    put_unit(2, dot_tn(inputs[...], kept[1]))
    send(1)
    pack_sums(depth, rows, sums, inner_sum, gv)
    send(VECTORS)
    for copy in last_loads:
        copy.wait()
    stage_1(0)
    stage_4(2)
    grad[chunks[0], :] += dot_nt(dq[chunks[0], :], w[0])
    stage_1(1)
    stage_1(VECTORS)
    stage_2(0)
    for c in chunks:
        value = grad[c, :] + dot_nt(kept[0, c, :], w[1]) + dot_nt(kept[1, c, :], w[2])
        grad[c, :] = value if c is chunks[0] else value + dot_nt(dq[c, :], w[0])
    states_store = pltpu.make_async_copy(grad, gs_out, store_sem.at[1])
    states_store.start()
    stage_2(1)
    stage_2(VECTORS)
    stage_3(0)
    stage_3(1)
    stage_3(VECTORS)
    stage_4(0)
    stage_4(1)
    stage_4(VECTORS)
    encoder_store.wait()
    states_store.wait()
    for n in range(2):
        self_share(n).wait_send()
    for i in range(HALF + 1):
        final_copy(i, 1 - odd).wait_recv()
        final_copy(i, odd).wait_send()
        for a, b in order:
            partner_copy(i, a, b).wait_send()
        for a in range(2):
            second_copy(i, a).wait_send()
        first_copy(i).wait_send()
        for n in range(depth - 1):
            up_copy(i, n).wait_send()


def pack_sums(depth, rows, sums, inner_sum, gv):
    lanes = gv.shape[-1]
    width = sums.shape[1]
    low = sums[...].astype(BF16)
    row = lax.broadcasted_iota(jnp.int32, (VROWS, lanes), 0)
    window_row = lax.broadcasted_iota(jnp.int32, (VROWS, WINDOW), 0)
    inner_low = jnp.zeros((VROWS, WINDOW), F32)
    for at in range(inner_sum.shape[1] // WINDOW):
        piece = inner_sum[:, at * WINDOW : (at + 1) * WINDOW]
        inner_low = jnp.where(window_row == at, piece, inner_low)
    inner_low = inner_low.astype(BF16)
    windows = jnp.concatenate([low[:, i : i + WINDOW] for i in range(0, width, WINDOW)], axis=0)
    count, inner_rows = WINDOW // rows, inner_sum.shape[1] // (4 * depth)
    inner_count = WINDOW // inner_rows
    inner = [
        [
            dot_nn(inner_low, select_lanes(n * inner_rows, part * lanes, inner_rows, lanes))
            for part in range(2)
        ]
        for n in range(inner_count)
    ]
    for n in range(count):
        picked = dot_nn(windows, select_lanes(n * rows, 0, rows, lanes))
        for at in range(width // WINDOW):
            f = at * count + n
            for part in range(2):
                own = picked[at * VROWS : (at + 1) * VROWS] if part == 0 else jnp.zeros_like(row, F32)
                at_inner = f // inner_count
                other = inner[f % inner_count][part][at_inner : at_inner + 1, :]
                gv[part, f // 4, (f // 2) % 2, f % 2] = jnp.where(row == 13, other, own).astype(BF16)


def decode(
    n_fsdp, own_places, places, length, flat, scale, ctotal, total, feed_sums, inner_sum, units, cq, ck,
    cv, co, gmix, low, encoder, hat, grad, q, k, v, o, states, d1, d2,
):
    rows, width = units.shape[-2:]
    depth = n_fsdp // 4
    row_count = states.shape[0]
    steps = HALF + 1
    dma = pltpu.SemaphoreType.DMA
    vmem = pltpu.VMEM
    any_spec = pl.BlockSpec(memory_space=pl.ANY)
    vmem_spec = pl.BlockSpec(memory_space=pltpu.VMEM)
    smem_spec = pl.BlockSpec(memory_space=pltpu.SMEM)
    block, small = (rows, width), (VROWS, LANES)
    narrow = vmem((row_count, width), BF16)
    wide = vmem((row_count, width), F32)
    both = vmem((2, row_count, width), BF16)
    return pl.pallas_call(
        functools.partial(decode_body, depth),
        in_specs=[smem_spec] * 3 + [vmem_spec] * 6 + [any_spec] * 17,
        out_specs=[any_spec] * 2 + [vmem_spec] * 2,
        out_shape=[
            jax.ShapeDtypeStruct((row_count, width), F32),
            jax.ShapeDtypeStruct((row_count, width), F32),
            jax.ShapeDtypeStruct((UNITS, *block), F32),
            jax.ShapeDtypeStruct((2, *small), F32),
        ],
        scratch_shapes=[
            vmem((HALF + 4, depth, 2, 2, *block), BF16),
            vmem((HALF, 4, depth, *block), BF16),
            vmem((HALF, 2, depth, *block), BF16),
            vmem((HALF, depth, *block), BF16),
            vmem((HALF, depth - 1, *block), BF16),
            vmem((4, width, width), BF16),
            narrow, narrow, wide, both, both, narrow, both, both,
            vmem((2, 2, row_count, width), BF16),
            narrow, narrow, wide, wide,
            vmem((2 * row_count, PAIR), F32),
            vmem((2 * row_count, PAIR), F32),
            vmem((PAIR, 2 * row_count), BF16),
            vmem((VROWS, width), F32),
            vmem((2, depth, 2, 2, *small), BF16),
            vmem((4, depth, *small), BF16),
            vmem((2, depth, *small), BF16),
            vmem((depth, *small), BF16),
            vmem((depth - 1, *small), BF16),
            dma((24,)),
            dma((HALF,)),
            dma((2,)),
            dma((steps, depth - 1)),
            dma((steps, depth - 1)),
            dma((steps,)),
            dma((steps,)),
            dma((steps, 2)),
            dma((steps, 2)),
            dma((steps, 4)),
            dma((steps, 4)),
            dma((steps,)),
            dma((steps,)),
            dma((3,)),
            dma((3,)),
        ],
        compiler_params=pltpu.CompilerParams(
            collective_id=3, has_side_effects=True, vmem_limit_bytes=DECODE_LIMIT
        ),
        name="decode",
    )(
        own_places, places, length, flat, scale, ctotal, total, feed_sums, inner_sum, units, cq, ck, cv,
        co, gmix, low, encoder, hat, grad, q, k, v, o, states,
        d1.reshape(-1, depth, 2, 2, *block),
        d2.reshape(depth, 2, 2, UNITS - FIRST, *block),
    )


GROUPS = ((0, 1, 2), (3,), (4,), (5, 6), (7,), (8, 9, 10, 11))


def lay_out_body(shards, *outs):
    rows, width = shards.shape[1:]
    for group, target in zip(GROUPS, outs):
        for at, u in enumerate(group):
            target[:, at * width : (at + 1) * width] = shards[u]
    for at in range(UNITS - FIRST):
        outs[-1][at * rows : (at + 1) * rows, :] = shards[FIRST + at]


def lay_out(shards):
    rows, width = shards.shape[1:]
    shapes = [(rows, width * len(group)) for group in GROUPS] + [((UNITS - FIRST) * rows, width)]
    return pl.pallas_call(
        lay_out_body,
        in_specs=[pl.BlockSpec(memory_space=pltpu.VMEM)],
        out_specs=[pl.BlockSpec(memory_space=pltpu.VMEM)] * len(shapes),
        out_shape=[jax.ShapeDtypeStruct(shape, F32) for shape in shapes],
        name="lay_out",
    )(shards)


def per_device_wide(
    n_ctx,
    n_fsdp,
    states,
    encoded,
    lengths,
    block_order,
    cotangent,
    self_project,
    self_bias,
    self_output,
    self_shift,
    cross_query,
    cross_keyval,
    cross_bias,
    cross_output,
    cross_shift,
    feed_inner,
    inner_bias,
    feed_outer,
    outer_bias,
    norm_gain,
    norm_shift,
):
    local_rows = states.shape[1]
    width = states.shape[2]
    rows = self_output.shape[0]
    local_blocks = local_rows // QBLK
    core = lax.axis_index("ctx")
    own_order = lax.dynamic_slice_in_dim(block_order, core * local_blocks, local_blocks)
    places = block_order
    spread = lambda array: (lax.all_gather(array, "ctx", axis=0, tiled=True),)
    collect = lambda parts: lax.psum_scatter(
        parts[0], "ctx", scatter_dimension=0, tiled=True
    ).astype(F32)

    vectors = jnp.concatenate(
        [
            self_bias,
            self_shift[None],
            cross_bias,
            cross_shift[None],
            outer_bias[None],
            norm_gain,
            norm_shift,
            inner_bias.reshape(-1, rows),
        ],
        axis=0,
    )
    inner_rows = inner_bias.shape[0] // rows
    count = vectors.shape[0]
    pad = ((0, 2 * VROWS - count), (0, LANES - rows))
    units, w_fo, all_vectors = gather_weights(
        n_fsdp, jnp.pad(vectors, pad).reshape(2, VROWS, LANES), self_project, self_output, cross_query,
        cross_keyval, cross_output, feed_inner, feed_outer,
    )
    all_vectors = jnp.transpose(all_vectors, (1, 0, 2, 3)).reshape(n_fsdp, 2 * VROWS, LANES)
    all_vectors = all_vectors[:, :count, :rows].astype(F32)
    inner_full = all_vectors[:, 13:].reshape(1, -1)
    flat = jnp.transpose(all_vectors, (1, 0, 2)).reshape(count, -1)
    b_q, b_v, b_so, b_cq, b_cv = (flat[i] for i in range(5))

    w_q, w_k, w_v, w_so, w_cq, w_ck, w_cv, w_co = (units[i] for i in range(8))

    inputs = states[0]
    encoder_rows = encoded[0]
    queries = ((dot_nn(inputs, w_q) + b_q) * ATTN_SCALE).astype(BF16)
    own_keys = dot_nn(inputs, w_k).astype(BF16)
    own_values = (dot_nn(inputs, w_v) + b_v).astype(BF16)
    own_cross_keys = dot_nn(encoder_rows, w_ck).astype(BF16)
    own_cross_values = (dot_nn(encoder_rows, w_cv) + b_cv).astype(BF16)
    keys, values = spread(own_keys), spread(own_values)
    cross_keys, cross_values = spread(own_cross_keys), spread(own_cross_values)

    attend = functools.partial(attention_forward, places=places, own_places=own_order, length=lengths)
    self_attended, self_total = attend(True, queries, keys, values)
    self_mixed = self_attended.astype(BF16)
    after_self, norm_back_one = jax.vjp(
        layer_norm, inputs.astype(F32) + dot_nn(self_mixed, w_so) + b_so, flat[7], flat[10]
    )
    after_self_low = after_self.astype(BF16)
    cross_queries = ((dot_nn(after_self_low, w_cq) + b_cq) * ATTN_SCALE).astype(BF16)
    cross_attended, cross_total = attend(False, cross_queries, cross_keys, cross_values)
    output, grad_cross_mixed, grad_two, feed_sums, inner_sum, d_low, d_outer = feed_forward(
        own_order, lengths, cross_attended, after_self, cotangent[0], flat[:16], inner_full, units, w_fo
    )
    attend_back = functools.partial(
        attention_backward, places=places, own_places=own_order, length=lengths
    )
    cross_query_grad, ck_parts, cv_parts = attend_back(
        False, cross_queries, grad_cross_mixed, cross_attended, cross_total, cross_keys, cross_values
    )
    cross_query_low = cross_query_grad.astype(BF16)
    d_cq = dot_tn(after_self_low, cross_query_low).astype(BF16)
    ck_grad, cv_grad = collect(ck_parts), collect(cv_parts)
    ck_low, cv_low = ck_grad.astype(BF16), cv_grad.astype(BF16)
    d_ck = dot_tn(encoder_rows, ck_low).astype(BF16)
    d_cv = dot_tn(encoder_rows, cv_low).astype(BF16)
    grad_encoded = dot_nt(ck_low, w_ck) + dot_nt(cv_low, w_cv)
    grad_one, gain_one, shift_one = norm_back_one(grad_two + dot_nt(cross_query_low, w_cq))
    grad_one_low = grad_one.astype(BF16)
    d_so = dot_tn(self_mixed, grad_one_low).astype(BF16)
    grad_self_mixed = dot_nt(grad_one_low, w_so).astype(BF16)
    query_grad, k_parts, v_parts = attend_back(
        True, queries, grad_self_mixed, self_attended, self_total, keys, values
    )
    query_low = query_grad.astype(BF16)
    key_grad, value_grad = collect(k_parts), collect(v_parts)
    key_low, value_low = key_grad.astype(BF16), value_grad.astype(BF16)
    d_q = dot_tn(inputs, query_low).astype(BF16)
    d_k = dot_tn(inputs, key_low).astype(BF16)
    d_v = dot_tn(inputs, value_low).astype(BF16)
    grad_states = grad_one + dot_nt(query_low, w_q) + dot_nt(key_low, w_k) + dot_nt(value_low, w_v)

    column_sum = lambda array: jnp.sum(array, axis=0)
    grad_vectors = jnp.stack(
        [
            column_sum(query_grad),
            column_sum(value_grad),
            column_sum(grad_one),
            column_sum(cross_query_grad),
            column_sum(cv_grad),
            feed_sums[0],
            feed_sums[1],
            gain_one,
            feed_sums[2],
            feed_sums[3],
            shift_one,
            feed_sums[4],
            feed_sums[5],
        ]
    ).reshape(13, n_fsdp, rows)
    inner_vector = inner_sum.reshape(n_fsdp, inner_rows, rows)
    packed = jnp.concatenate([jnp.transpose(grad_vectors, (1, 0, 2)), inner_vector], axis=1)
    packed = jnp.pad(packed, ((0, 0), *pad)).astype(BF16)
    packed = jnp.transpose(packed.reshape(n_fsdp, 2, VROWS, LANES), (1, 0, 2, 3))

    shards, mine = scatter_gradients(
        n_fsdp, [d_q, d_k, d_v, d_so, d_cq, d_ck, d_cv], d_low, d_outer, packed
    )
    if n_ctx > 2:
        groups = [[c for c in range(n_ctx) if c % 2 == odd] for odd in range(2)]
        total = lambda part: lax.psum(part.astype(BF16), "ctx", axis_index_groups=groups).astype(F32)
        shards, mine = total(shards), total(mine)
    mine = mine.reshape(2 * VROWS, LANES)[:, :rows]
    return (
        output[None],
        grad_states[None],
        grad_encoded[None],
        jnp.concatenate([shards[0], shards[1], shards[2]], axis=1),
        mine[0:2],
        shards[3],
        mine[2],
        shards[4],
        jnp.concatenate([shards[5], shards[6]], axis=1),
        mine[3:5],
        shards[7],
        mine[5],
        jnp.concatenate([shards[8 + i] for i in range(4)], axis=1),
        mine[13 : 13 + inner_rows].reshape(-1),
        shards[12:].reshape(-1, width),
        mine[6],
        mine[7:10],
        mine[10:13],
    )


def per_device(
    n_ctx,
    n_fsdp,
    states,
    encoded,
    lengths,
    block_order,
    cotangent,
    self_project,
    self_bias,
    self_output,
    self_shift,
    cross_query,
    cross_keyval,
    cross_bias,
    cross_output,
    cross_shift,
    feed_inner,
    inner_bias,
    feed_outer,
    outer_bias,
    norm_gain,
    norm_shift,
):
    local_rows = states.shape[1]
    width = states.shape[2]
    rows = self_output.shape[0]
    local_blocks = local_rows // QBLK
    core = lax.axis_index("ctx")
    own_order = lax.dynamic_slice_in_dim(block_order, core * local_blocks, local_blocks)
    other_order = lax.dynamic_slice_in_dim(block_order, (1 - core) * local_blocks, local_blocks)
    places = jnp.concatenate([own_order, other_order])
    narrow = jnp.concatenate(
        [
            self_bias,
            self_shift[None],
            cross_bias,
            cross_shift[None],
            outer_bias[None],
            norm_gain,
            norm_shift,
        ],
        axis=0,
    )
    vectors = jnp.concatenate(
        [
            jnp.pad(narrow, ((0, 0), (0, VLANES - rows))),
            jnp.pad(inner_bias[None], ((0, VROWS - 14), (0, VLANES - inner_bias.shape[0]))),
        ],
        axis=0,
    )
    (
        units, w_fo, queries, keys, values, cross_queries, cross_keys, cross_values, self_attended,
        self_total, after_self, after_self_low, hat, scale, cross_attended, cross_total, flat, inner_full,
    ) = encode(
        n_fsdp, own_order, places, lengths, states[0], encoded[0], vectors, self_project, self_output,
        cross_query, cross_keyval, cross_output, feed_inner, feed_outer,
    )
    output, grad_cross_mixed, grad_two, feed_sums, inner_sum, d_low, d_outer = feed_forward(
        own_order, lengths, cross_attended, after_self, cotangent[0], flat, inner_full,
        units.reshape(FIRST, width, width), w_fo.reshape(-1, width),
    )
    grad_states, grad_encoded, shards, mine = decode(
        n_fsdp, own_order, places, lengths, flat, scale, cross_total, self_total, feed_sums, inner_sum,
        units, cross_queries, cross_keys, cross_values, cross_attended, grad_cross_mixed, after_self_low,
        encoded[0], hat, grad_two, queries, keys, values, self_attended, states[0], d_low, d_outer,
    )
    d_sp, d_so, d_cq, d_ckv, d_co, d_fi, d_fo = lay_out(shards)
    narrow = mine[0, :, :rows]
    inner = mine[:, 13].reshape(-1)[: inner_bias.shape[0]]
    return (
        output[None],
        grad_states[None],
        grad_encoded[None],
        d_sp,
        narrow[0:2],
        d_so,
        narrow[2],
        d_cq,
        d_ckv,
        narrow[3:5],
        d_co,
        narrow[5],
        d_fi,
        inner,
        d_fo,
        narrow[6],
        narrow[7:10],
        narrow[10:13],
    )


def solution(mesh):
    return jax.shard_map(
        functools.partial(
            per_device if mesh.shape["ctx"] == 2 else per_device_wide,
            mesh.shape["ctx"],
            mesh.shape["fsdp"],
        ),
        mesh=mesh,
        in_specs=(
            P("fsdp", "ctx", None),
            P("fsdp", "ctx", None),
            P("fsdp"),
            P(),
            P("fsdp", "ctx", None),
            P("fsdp", None),
            P(None, "fsdp"),
            P("fsdp", None),
            P("fsdp"),
            P("fsdp", None),
            P("fsdp", None),
            P(None, "fsdp"),
            P("fsdp", None),
            P("fsdp"),
            P("fsdp", None),
            P("fsdp"),
            P("fsdp", None),
            P("fsdp"),
            P(None, "fsdp"),
            P(None, "fsdp"),
        ),
        out_specs=(
            P("fsdp", "ctx", None),
            P("fsdp", "ctx", None),
            P("fsdp", "ctx", None),
            P("fsdp", None),
            P(None, "fsdp"),
            P("fsdp", None),
            P("fsdp"),
            P("fsdp", None),
            P("fsdp", None),
            P(None, "fsdp"),
            P("fsdp", None),
            P("fsdp"),
            P("fsdp", None),
            P("fsdp"),
            P("fsdp", None),
            P("fsdp"),
            P(None, "fsdp"),
            P(None, "fsdp"),
        ),
        check_vma=False,
    )
```

```python
import functools

import jax
import jax.numpy as jnp
from jax import lax
from jax.experimental import pallas as pl
from jax.experimental.pallas import tpu as pltpu
from jax.sharding import PartitionSpec as P

H = 12
HD = 64
QBLK = 128
PAIR = 2 * HD
ATTN_SCALE = 0.125
MASKED_SCORE = -1e30
EPSILON = 1e-05
MESH = pl.DeviceIdType.MESH
VMEM_LIMIT = 60 * 1024 * 1024
DECODE_LIMIT = 67043328
BF16 = jnp.bfloat16
F32 = jnp.float32


def dot_nn(left, right):
    return lax.dot_general(left, right, (((1,), (0,)), ((), ())), preferred_element_type=F32)


def dot_nt(left, right):
    return lax.dot_general(left, right, (((1,), (1,)), ((), ())), preferred_element_type=F32)


def dot_tn(left, right):
    return lax.dot_general(left, right, (((0,), (0,)), ((), ())), preferred_element_type=F32)


def layer_norm(inputs, scale_vec, shift_vec):
    average = jnp.mean(inputs, axis=-1, keepdims=True)
    centred = inputs - average
    variance = jnp.mean(centred * centred, axis=-1, keepdims=True)
    return centred * lax.rsqrt(variance + EPSILON) * scale_vec + shift_vec


def gelu_exact(inputs):
    return jax.nn.gelu(inputs, approximate=False)


def stack_heads(rows):
    first = lax.broadcasted_iota(jnp.int32, rows.shape, 1) < HD
    zero = jnp.zeros_like(rows)
    return jnp.concatenate([jnp.where(first, rows, zero), jnp.where(first, zero, rows)], axis=0)


def unstack_heads(both, count):
    return jnp.concatenate([both[:HD, :count], both[HD:, count:]], axis=0).T


def variants_of(key_count, causal):
    if not causal:
        return [key_count]
    step = max(2 * QBLK, key_count // 4)
    return [step * (i + 1) for i in range(key_count // step)]


def load_keys(causal, places, sources, target):
    block = 0
    for source in sources:
        for local in range(source.shape[0] // QBLK):
            rows = source[local * QBLK : (local + 1) * QBLK, :]
            if causal:
                at = pl.multiple_of(places[block] * QBLK, QBLK)
                target[pl.ds(at, QBLK), :] = rows
            else:
                target[block * QBLK : (block + 1) * QBLK, :] = rows
            block += 1


def masked_scores(causal, keys, both, place, length, count):
    scores = dot_nt(keys, both)
    if causal:
        column = lax.broadcasted_iota(jnp.int32, (1, 2 * count), 1)
        row_place = place * QBLK + jnp.where(column >= count, column - count, column)
        limit = jnp.minimum(row_place, length - 1)
        key_place = lax.broadcasted_iota(jnp.int32, scores.shape, 0)
        scores = jnp.where(key_place <= limit, scores, MASKED_SCORE)
    return scores


def for_each_block(causal, sizes, block_count, own_places, length, body):
    def step(i, carry):
        if not causal:
            body(i, 0, sizes[0])
            return carry
        place = own_places[i]
        needed = jnp.minimum((place + 1) * QBLK, length)
        for at, size in enumerate(sizes):
            low = sizes[at - 1] if at else 0

            @pl.when((needed > low) & (needed <= size))
            def _(size=size):
                body(i, place, size)

        return carry

    lax.fori_loop(0, block_count, step, 0)


def forward_body(causal, n_src, places, own_places, length_ref, q_ref, *refs):
    key_refs, value_refs = refs[:n_src], refs[n_src : 2 * n_src]
    out_ref, total_ref, keys, values_t = refs[2 * n_src :]
    load_keys(causal, places, key_refs, keys)
    length = length_ref[0]
    block = 0
    for source in value_refs:
        for local in range(source.shape[0] // QBLK):
            rows = source[local * QBLK : (local + 1) * QBLK, :].astype(F32).T.astype(BF16)
            at = pl.multiple_of(places[block] * QBLK, QBLK) if causal else block * QBLK
            values_t[:, pl.ds(at, QBLK)] = rows
            block += 1

    def body(i, place, size):
        rows = pl.ds(pl.multiple_of(i * QBLK, QBLK), QBLK)
        both = stack_heads(q_ref[rows, :])
        scores = masked_scores(causal, keys[:size, :], both, place, length, QBLK)
        highest = jnp.max(scores, axis=0, keepdims=True)
        exponent = jnp.exp(scores - highest)
        total = jnp.sum(exponent, axis=0, keepdims=True)
        mixed = dot_nn(values_t[:, :size], exponent.astype(BF16)) * (1.0 / total)
        out_ref[rows, :] = unstack_heads(mixed, QBLK)
        total_ref[0, pl.ds(i, 1), :] = highest + jnp.log(total)

    for_each_block(
        causal,
        variants_of(keys.shape[0], causal),
        q_ref.shape[0] // QBLK,
        own_places,
        length,
        body,
    )


def attention_forward(causal, queries, keys, values, places, own_places, length):
    rows, width = queries.shape
    n_src = len(keys)
    key_count = sum(k.shape[0] for k in keys)
    pairs = width // PAIR
    column = lambda i, *_: (0, i)
    spec = lambda n: pl.BlockSpec((n, PAIR), column)
    return pl.pallas_call(
        functools.partial(forward_body, causal, n_src),
        grid_spec=pltpu.PrefetchScalarGridSpec(
            num_scalar_prefetch=3,
            grid=(pairs,),
            in_specs=[spec(rows)] + [spec(k.shape[0]) for k in (*keys, *values)],
            out_specs=[
                spec(rows),
                pl.BlockSpec((1, rows // QBLK, 2 * QBLK), lambda i, *_: (i, 0, 0)),
            ],
            scratch_shapes=[
                pltpu.VMEM((key_count, PAIR), BF16),
                pltpu.VMEM((PAIR, key_count), BF16),
            ],
        ),
        out_shape=[
            jax.ShapeDtypeStruct((rows, width), F32),
            jax.ShapeDtypeStruct((pairs, rows // QBLK, 2 * QBLK), F32),
        ],
        compiler_params=pltpu.CompilerParams(vmem_limit_bytes=VMEM_LIMIT),
        name="self_forward" if causal else "cross_forward",
    )(places, own_places, length, queries, *keys, *values)


def backward_body(causal, n_src, places, own_places, length_ref, q_ref, g_ref, o_ref, t_ref, *refs):
    key_refs, value_refs = refs[:n_src], refs[n_src : 2 * n_src]
    dq_ref = refs[2 * n_src]
    dk_refs = refs[2 * n_src + 1 : 3 * n_src + 1]
    dv_refs = refs[3 * n_src + 1 : 4 * n_src + 1]
    keys, values, keys_t, dk, dv = refs[4 * n_src + 1 :]
    load_keys(causal, places, key_refs, keys)
    load_keys(causal, places, value_refs, values)
    length = length_ref[0]
    key_count = keys.shape[0]
    for block in range(key_count // QBLK):
        rows = slice(block * QBLK, (block + 1) * QBLK)
        keys_t[:, rows] = keys[rows, :].astype(F32).T.astype(BF16)
    dk[...] = jnp.zeros_like(dk)
    dv[...] = jnp.zeros_like(dv)

    def body(i, place, size):
        rows = pl.ds(pl.multiple_of(i * QBLK, QBLK), QBLK)
        both = stack_heads(q_ref[rows, :])
        grads = g_ref[rows, :]
        both_grads = stack_heads(grads)
        products = (grads.astype(F32) * o_ref[rows, :]).T
        delta = jnp.concatenate(
            [
                jnp.sum(products[:HD], axis=0, keepdims=True),
                jnp.sum(products[HD:], axis=0, keepdims=True),
            ],
            axis=1,
        )
        scores = masked_scores(causal, keys[:size, :], both, place, length, QBLK)
        prob = jnp.exp(scores - t_ref[0, pl.ds(i, 1), :])
        prob_grad = dot_nt(values[:size, :], both_grads)
        score_grad = (prob * (prob_grad - delta)).astype(BF16)
        dv[:size, :] += dot_nn(prob.astype(BF16), both_grads)
        dk[:size, :] += dot_nn(score_grad, both)
        dq = dot_nn(keys_t[:, :size], score_grad)
        dq_ref[rows, :] = unstack_heads(dq, QBLK) * ATTN_SCALE

    for_each_block(
        causal, variants_of(key_count, causal), q_ref.shape[0] // QBLK, own_places, length, body
    )
    block = 0
    for dk_out, dv_out in zip(dk_refs, dv_refs):
        for local in range(dk_out.shape[0] // QBLK):
            at = pl.multiple_of(places[block] * QBLK, QBLK) if causal else block * QBLK
            rows = slice(local * QBLK, (local + 1) * QBLK)
            dk_out[rows, :] = dk[pl.ds(at, QBLK), :].astype(BF16)
            dv_out[rows, :] = dv[pl.ds(at, QBLK), :].astype(BF16)
            block += 1


def attention_backward(
    causal, queries, grads, mixed, totals, keys, values, places, own_places, length
):
    rows, width = queries.shape
    n_src = len(keys)
    key_count = sum(k.shape[0] for k in keys)
    pairs = width // PAIR
    column = lambda i, *_: (0, i)
    spec = lambda n: pl.BlockSpec((n, PAIR), column)
    key_specs = [spec(k.shape[0]) for k in (*keys, *values)]
    outs = pl.pallas_call(
        functools.partial(backward_body, causal, n_src),
        grid_spec=pltpu.PrefetchScalarGridSpec(
            num_scalar_prefetch=3,
            grid=(pairs,),
            in_specs=[
                spec(rows),
                spec(rows),
                spec(rows),
                pl.BlockSpec((1, rows // QBLK, 2 * QBLK), lambda i, *_: (i, 0, 0)),
            ]
            + key_specs,
            out_specs=[spec(rows)] + key_specs,
            scratch_shapes=[
                pltpu.VMEM((key_count, PAIR), BF16),
                pltpu.VMEM((key_count, PAIR), BF16),
                pltpu.VMEM((PAIR, key_count), BF16),
                pltpu.VMEM((key_count, PAIR), F32),
                pltpu.VMEM((key_count, PAIR), F32),
            ],
        ),
        out_shape=[jax.ShapeDtypeStruct((rows, width), F32)]
        + [jax.ShapeDtypeStruct(k.shape, BF16) for k in (*keys, *values)],
        compiler_params=pltpu.CompilerParams(vmem_limit_bytes=VMEM_LIMIT),
        name="self_backward" if causal else "cross_backward",
    )(places, own_places, length, queries, grads, mixed, totals, *keys, *values)
    return outs[0], outs[1 : n_src + 1], outs[n_src + 1 :]


UNITS = 16
FIRST = 12
HALF = UNITS // 2
VECTORS = HALF
VROWS = 16
LANES = 128


def coordinates():
    core, f = lax.axis_index("ctx"), lax.axis_index("fsdp")
    return core, core % 2, f // 4, (f // 2) % 2, f % 2


def flip(odd, y, x, a, b):
    dx = a * (1 - odd) + b * odd
    dy = b * (1 - odd) + a * odd
    return y + dy * (1 - 2 * y), x + dx * (1 - 2 * x)


def peers_of(core, odd, z, y, x, depth):
    fsdp = lambda zz, yy, xx: (zz * 2 + yy) * 2 + xx
    ups = [(core, fsdp((z + k) % depth, y, x)) for k in range(1, depth)]
    first = (core, fsdp(z, *flip(odd, y, x, 1, 0)))
    second = (core, fsdp(z, *flip(odd, y, x, 0, 1)))
    partner = (core + 1 - 2 * odd, fsdp(z, y, x))
    return ups, first, second, partner


def enter(ups, first, second, partner):
    barrier = pltpu.get_barrier_semaphore()
    for peer in (*ups, first, second, partner):
        pl.semaphore_signal(barrier, inc=1, device_id=peer, device_id_type=MESH)
    pl.semaphore_wait(barrier, len(ups) + 3)


def remote(source, target, send, recv, peer):
    return pltpu.make_async_remote_copy(
        source, target, send, recv, device_id=peer, device_id_type=MESH
    )


def unit_set(g1, g2, gv, i, odd, y, x):
    if i == VECTORS:
        return gv.at[odd, :, y, x]
    if 2 * i < FIRST:
        return g1.at[2 * i + odd, :, y, x]
    return g2.at[:, y, x, 2 * i - FIRST + odd]


def unit_block(g1, g2, gv, i, odd, z, y, x):
    if i == VECTORS:
        return gv.at[odd, z, y, x]
    if 2 * i < FIRST:
        return g1.at[2 * i + odd, z, y, x]
    return g2.at[z, y, x, 2 * i - FIRST + odd]


def gather_body(
    depth, vectors, sp, so, cq, ckv, co, fi, fo, g1, g2, gv, own, load_sem, own_sem,
    zs, zr, fs, fr, ss, sr, ps, pr,
):
    core, odd, z, y, x = coordinates()
    ups, first, second, partner = peers_of(core, odd, z, y, x, depth)
    width = so.shape[1]
    rows = so.shape[0]
    sources = (
        [sp.at[:, pl.ds(j * width, width)] for j in range(3)]
        + [so, cq]
        + [ckv.at[:, pl.ds(j * width, width)] for j in range(2)]
        + [co]
        + [fi.at[:, pl.ds(j * width, width)] for j in range(4)]
        + [fo.at[pl.ds(j * rows, rows), :] for j in range(4)]
    )
    loads = [pltpu.make_async_copy(s, own.at[u], load_sem.at[u]) for u, s in enumerate(sources)]
    for load in loads:
        load.start()
    enter(ups, first, second, partner)

    def mine(i):
        return vectors.at[odd] if i == VECTORS else own.at[2 * i + odd]

    def set_of(i, a, b):
        return unit_set(g1, g2, gv, i, odd, *flip(odd, y, x, a, b))

    def up_copy(i, k):
        block = unit_block(g1, g2, gv, i, odd, z, y, x)
        return remote(mine(i), block, zs.at[i, k], zr.at[i, k], ups[k])

    def up_arrival(i, k):
        block = unit_block(g1, g2, gv, i, odd, (z + depth - 1 - k) % depth, y, x)
        return remote(block, block, zs.at[i, k], zr.at[i, k], ups[k])

    def first_copy(i):
        return remote(set_of(i, 0, 0), set_of(i, 0, 0), fs.at[i], fr.at[i], first)

    def second_copy(i, a):
        return remote(set_of(i, a, 0), set_of(i, a, 0), ss.at[i, a], sr.at[i, a], second)

    def partner_copy(i, a, b):
        at = a + 2 * b
        return remote(set_of(i, a, b), set_of(i, a, b), ps.at[i, at], pr.at[i, at], partner)

    def arrival(target, send, recv, peer):
        return remote(target, target, send, recv, peer)

    steps = [VECTORS, *range(HALF)]
    keeps = []
    for i in steps:
        if i != VECTORS:
            loads[2 * i].wait()
            loads[2 * i + 1].wait()
        keep = pltpu.make_async_copy(
            mine(i), unit_block(g1, g2, gv, i, odd, z, y, x), own_sem.at[i]
        )
        keep.start()
        keeps.append(keep)
        for k in range(depth - 1):
            up_copy(i, k).start()
    for step in range(len(steps) + 2):
        if step < len(steps):
            i = steps[step]
            keeps[step].wait()
            for k in range(depth - 1):
                up_arrival(i, k).wait_recv()
            first_copy(i).start()
            second_copy(i, 0).start()
            partner_copy(i, 0, 0).start()
        if 0 <= step - 1 < len(steps):
            i = steps[step - 1]
            arrival(set_of(i, 1, 0), fs.at[i], fr.at[i], first).wait_recv()
            second_copy(i, 1).start()
            partner_copy(i, 1, 0).start()
        if 0 <= step - 2 < len(steps):
            i = steps[step - 2]
            for a in range(2):
                arrival(set_of(i, a, 1), ss.at[i, a], sr.at[i, a], second).wait_recv()
                partner_copy(i, a, 1).start()
    for i in steps:
        for a in range(2):
            for b in range(2):
                at = a + 2 * b
                there = unit_set(g1, g2, gv, i, 1 - odd, *flip(1 - odd, y, x, a, b))
                arrival(there, ps.at[i, at], pr.at[i, at], partner).wait_recv()
                partner_copy(i, a, b).wait_send()
            second_copy(i, a).wait_send()
        first_copy(i).wait_send()
        for k in range(depth - 1):
            up_copy(i, k).wait_send()


def gather_weights(n_fsdp, vectors, sp, so, cq, ckv, co, fi, fo):
    rows, width = so.shape
    depth = n_fsdp // 4
    dma = pltpu.SemaphoreType.DMA
    steps = HALF + 1
    g1, g2, gv = pl.pallas_call(
        functools.partial(gather_body, depth),
        in_specs=[pl.BlockSpec(memory_space=pl.ANY)] * 8,
        out_specs=[pl.BlockSpec(memory_space=pl.ANY)] * 3,
        out_shape=[
            jax.ShapeDtypeStruct((FIRST, depth, 2, 2, rows, width), BF16),
            jax.ShapeDtypeStruct((depth, 2, 2, UNITS - FIRST, rows, width), BF16),
            jax.ShapeDtypeStruct((2, depth, 2, 2, VROWS, LANES), BF16),
        ],
        scratch_shapes=[
            pltpu.VMEM((UNITS, rows, width), BF16),
            dma((UNITS,)),
            dma((steps,)),
            dma((steps, depth - 1)),
            dma((steps, depth - 1)),
            dma((steps,)),
            dma((steps,)),
            dma((steps, 2)),
            dma((steps, 2)),
            dma((steps, 4)),
            dma((steps, 4)),
        ],
        compiler_params=pltpu.CompilerParams(
            collective_id=0, has_side_effects=True, vmem_limit_bytes=VMEM_LIMIT
        ),
        name="gather_weights",
    )(vectors, sp, so, cq, ckv, co, fi, fo)
    return (
        g1.reshape(FIRST, n_fsdp * rows, width),
        g2.reshape(-1, width),
        gv.reshape(2, n_fsdp, VROWS, LANES),
    )


def scatter_body(depth, *refs):
    units = refs[:7]
    (
        g1, g2, gv, out, out_v, own, from_partner, from_second, from_first, from_up, final, final_in,
        own_v, from_partner_v, from_second_v, from_first_v, from_up_v, final_v, final_in_v,
        own_sem, zs, zr, fs, fr, ss, sr, ps, pr, xs, xr,
    ) = refs[7:]
    core, odd, z, y, x = coordinates()
    ups, first, second, partner = peers_of(core, odd, z, y, x, depth)
    order = ((0, 1), (1, 1), (1, 0), (0, 0))

    def pick(i, main, small):
        return small if i == VECTORS else main.at[i]

    def source(i, parity, yy, xx):
        u = 2 * i + parity
        if i == VECTORS:
            return gv.at[parity, :, yy, xx]
        if 2 * i >= FIRST:
            return g2.at[:, yy, xx, u - FIRST]
        if 2 * i >= 8:
            return g1.at[u - 7, :, yy, xx]
        return units[u].at[:, yy, xx] if u < 7 else g1.at[0, :, yy, xx]

    def own_copy(i, a, b, parity):
        at = a + 2 * b
        return pltpu.make_async_copy(
            source(i, parity, *flip(odd, y, x, a, b)),
            pick(i, own, own_v).at[at],
            own_sem.at[i, at],
        )

    def partner_copy(i, a, b, parity):
        at = a + 2 * b
        return remote(
            source(i, parity, *flip(1 - odd, y, x, a, b)),
            pick(i, from_partner, from_partner_v).at[at],
            ps.at[i, at],
            pr.at[i, at],
            partner,
        )

    def second_copy(i, a):
        return remote(
            pick(i, own, own_v).at[a + 2],
            pick(i, from_second, from_second_v).at[a],
            ss.at[i, a],
            sr.at[i, a],
            second,
        )

    def first_copy(i):
        return remote(
            pick(i, own, own_v).at[1],
            pick(i, from_first, from_first_v),
            fs.at[i],
            fr.at[i],
            first,
        )

    def up_copy(i, k):
        return remote(
            pick(i, own, own_v).at[0, (z + 1 + k) % depth],
            pick(i, from_up, from_up_v).at[k],
            zs.at[i, k],
            zr.at[i, k],
            ups[k],
        )

    def final_copy(i):
        return remote(
            pick(i, final, final_v), pick(i, final_in, final_in_v), xs.at[i], xr.at[i], partner
        )

    def add(target, addend):
        def step(j, carry):
            target[j] = target[j] + addend[j]
            return carry

        lax.fori_loop(0, depth, step, 0)

    def start_all(copy, parity_of):
        for i in steps:
            if i != VECTORS and 2 * i < 8:
                for q in range(2):

                    @pl.when(odd == q)
                    def _(i=i, q=q):
                        for a, b in order:
                            copy(i, a, b, parity_of(q)).start()

            else:
                for a, b in order:
                    copy(i, a, b, parity_of(odd)).start()

    steps = [*range(HALF - 1, -1, -1), VECTORS]
    start_all(own_copy, lambda q: q)
    enter(ups, first, second, partner)
    start_all(partner_copy, lambda q: 1 - q)

    for step in range(len(steps) + 3):
        if step < len(steps):
            i = steps[step]
            for a, b in order:
                at = a + 2 * b
                own_copy(i, a, b, 0).wait()
                partner_copy(i, a, b, 0).wait_recv()
                add(pick(i, own, own_v).at[at], pick(i, from_partner, from_partner_v).at[at])
                if b:
                    second_copy(i, a).start()
        if 0 <= step - 1 < len(steps):
            i = steps[step - 1]
            for a in (1, 0):
                second_copy(i, a).wait_recv()
                add(pick(i, own, own_v).at[a], pick(i, from_second, from_second_v).at[a])
                if a:
                    first_copy(i).start()
        if 0 <= step - 2 < len(steps):
            i = steps[step - 2]
            first_copy(i).wait_recv()
            add(pick(i, own, own_v).at[0], pick(i, from_first, from_first_v))
            for k in range(depth - 1):
                up_copy(i, k).start()
        if 0 <= step - 3 < len(steps):
            i = steps[step - 3]
            total = pick(i, own, own_v)[0, z].astype(F32)
            for k in range(depth - 1):
                up_copy(i, k).wait_recv()
                total = total + pick(i, from_up, from_up_v)[k].astype(F32)
            pick(i, final, final_v)[...] = total
            final_copy(i).start()
            if i == VECTORS:
                out_v[odd] = total
            else:
                out[2 * i + odd] = total
    for i in steps:
        final_copy(i).wait()
        if i == VECTORS:
            out_v[1 - odd] = final_in_v[...]
        else:
            out[2 * i + 1 - odd] = final_in[i]
        for a, b in order:
            partner_copy(i, a, b, 0).wait_send()
        for a in range(2):
            second_copy(i, a).wait_send()
        first_copy(i).wait_send()
        for k in range(depth - 1):
            up_copy(i, k).wait_send()


def scatter_gradients(n_fsdp, units, g1, g2, gv):
    width = g1.shape[-1]
    depth = n_fsdp // 4
    rows = width // n_fsdp
    dma = pltpu.SemaphoreType.DMA
    vmem = pltpu.VMEM
    steps = HALF + 1
    block, small = (rows, width), (VROWS, LANES)
    return pl.pallas_call(
        functools.partial(scatter_body, depth),
        in_specs=[pl.BlockSpec(memory_space=pl.ANY)] * 10,
        out_specs=[pl.BlockSpec(memory_space=pltpu.VMEM)] * 2,
        out_shape=[
            jax.ShapeDtypeStruct((UNITS, *block), F32),
            jax.ShapeDtypeStruct((2, *small), F32),
        ],
        scratch_shapes=[
            vmem((HALF, 4, depth, *block), BF16),
            vmem((HALF, 4, depth, *block), BF16),
            vmem((HALF, 2, depth, *block), BF16),
            vmem((HALF, depth, *block), BF16),
            vmem((HALF, depth - 1, *block), BF16),
            vmem((HALF, *block), F32),
            vmem((HALF, *block), F32),
            vmem((4, depth, *small), BF16),
            vmem((4, depth, *small), BF16),
            vmem((2, depth, *small), BF16),
            vmem((depth, *small), BF16),
            vmem((depth - 1, *small), BF16),
            vmem(small, F32),
            vmem(small, F32),
            dma((steps, 4)),
            dma((steps, depth - 1)),
            dma((steps, depth - 1)),
            dma((steps,)),
            dma((steps,)),
            dma((steps, 2)),
            dma((steps, 2)),
            dma((steps, 4)),
            dma((steps, 4)),
            dma((steps,)),
            dma((steps,)),
        ],
        compiler_params=pltpu.CompilerParams(
            collective_id=1, has_side_effects=True, vmem_limit_bytes=VMEM_LIMIT
        ),
        name="scatter_gradients",
    )(
        *[u.reshape(depth, 2, 2, *block) for u in units],
        g1.reshape(-1, depth, 2, 2, *block),
        g2.reshape(depth, 2, 2, UNITS - FIRST, *block),
        gv.reshape(2, depth, 2, 2, *small),
    )


CHUNK = 256
VECTOR_ROWS = (5, 6, 8, 11, 9, 12)


def valid_of(own_places, length, chunk):
    row = lax.broadcasted_iota(jnp.int32, (CHUNK, 1), 0)
    place = row
    for block in range(CHUNK // QBLK):
        base = (own_places[chunk * (CHUNK // QBLK) + block] - block) * QBLK
        place = jnp.where((row >= block * QBLK) & (row < (block + 1) * QBLK), row + base, place)
    return place < length


def norm_stats(value):
    average = jnp.mean(value, axis=-1, keepdims=True)
    centred = value - average
    scale = lax.rsqrt(jnp.mean(centred * centred, axis=-1, keepdims=True) + EPSILON)
    return centred * scale, scale


def norm_back(grad, normed, scale):
    inner = jnp.mean(grad * normed, axis=-1, keepdims=True)
    return (grad - jnp.mean(grad, axis=-1, keepdims=True) - normed * inner) * scale


def feed_body(
    own_places, length_ref, mixed_ref, after_ref, cot_ref, vec_ref, b_fi_ref, g1, g2,
    out_ref, gmix_ref, grad_ref, sums_ref, isum_ref, d1, d2,
    w_co, w_fi, w_fo, mixed_low, normed, scale_ref, cross, cross_low, hidden, slope, grad_inner,
    total, grad_low, buffer, load_sem, store_sem,
):
    rows, width = after_ref.shape
    chunks = [pl.ds(c * CHUNK, CHUNK) for c in range(rows // CHUNK)]
    output_load = pltpu.make_async_copy(g1.at[7], w_co, load_sem.at[0])

    def inner_load(j):
        return pltpu.make_async_copy(g1.at[8 + j], w_fi.at[j], load_sem.at[1 + j])

    def outer_load(j):
        source = g2.at[pl.ds(pl.multiple_of(j * width, width), width), :]
        return pltpu.make_async_copy(source, w_fo.at[j], load_sem.at[5 + j])

    output_load.start()
    for j in range(4):
        inner_load(j).start()
    for j in range(4):
        outer_load(j).start()
    vec = lambda i: vec_ref[VECTOR_ROWS[i] : VECTOR_ROWS[i] + 1, :]
    column_sum = lambda array: jnp.sum(array, axis=0, keepdims=True)

    output_load.wait()
    for c in chunks:
        mixed_low[c, :] = mixed_ref[c, :].astype(BF16)
        value = after_ref[c, :] + dot_nn(mixed_low[c, :], w_co[...]) + vec(0)
        hat, scale = norm_stats(value)
        normed[c, :] = hat
        scale_ref[c, :] = scale
        value = hat * vec(2) + vec(3)
        cross[c, :] = value
        cross_low[c, :] = value.astype(BF16)
        total[c, :] = value + vec(1)

    def forward(j, carry):
        inner_load(j).wait()
        outer_load(j).wait()
        bias = b_fi_ref[:, pl.ds(pl.multiple_of(j * width, width), width)]

        def inner_step(at, carry):
            c = pl.ds(pl.multiple_of(at * CHUNK, CHUNK), CHUNK)
            pre = dot_nn(cross_low[c, :], w_fi[j]) + bias
            share = 0.5 + 0.5 * lax.erf(pre * (0.5**0.5))
            act = (pre * share).astype(BF16)
            hidden[j, c, :] = act
            density = jnp.exp(-0.5 * pre * pre) * ((0.5 / jnp.pi) ** 0.5)
            slope[j, c, :] = (share + pre * density).astype(BF16)
            total[c, :] += dot_nn(act, w_fo[j])
            return carry

        return lax.fori_loop(0, rows // CHUNK, inner_step, carry)

    lax.fori_loop(0, 4, forward, 0)
    gain_sum = jnp.zeros((1, width), F32)
    shift_sum = jnp.zeros((1, width), F32)
    grad_sum = jnp.zeros((1, width), F32)
    for at, c in enumerate(chunks):
        hat, scale = norm_stats(total[c, :])
        valid = valid_of(own_places, length_ref[0], at)
        out_ref[c, :] = jnp.where(valid, hat * vec(4) + vec(5), 0.0)
        incoming = jnp.where(valid, cot_ref[c, :].astype(F32), 0.0)
        gain_sum += column_sum(incoming * hat)
        shift_sum += column_sum(incoming)
        grad = norm_back(incoming * vec(4), hat, scale)
        grad_sum += column_sum(grad)
        total[c, :] = grad
        grad_low[c, :] = grad.astype(BF16)
    sums_ref[1:2, :] = grad_sum
    sums_ref[3:4, :] = gain_sum
    sums_ref[5:6, :] = shift_sum

    def store(at, target):
        return pltpu.make_async_copy(buffer.at[at], target, store_sem.at[at])

    def outer_store(j):
        return store(0, d2.at[pl.ds(pl.multiple_of(j * width, width), width), :])

    def inner_store(j):
        return store(1, d1.at[1 + j])

    def back(j, carry):
        def back_step(at, carry):
            c = pl.ds(pl.multiple_of(at * CHUNK, CHUNK), CHUNK)
            grad = dot_nt(grad_low[c, :], w_fo[j]) * slope[j, c, :].astype(F32)
            low = grad.astype(BF16)
            grad_inner[c, :] = low
            total[c, :] += dot_nt(low, w_fi[j])
            return carry + column_sum(grad)

        isum_ref[:, pl.ds(pl.multiple_of(j * width, width), width)] = lax.fori_loop(
            0, rows // CHUNK, back_step, jnp.zeros((1, width), F32)
        )

        @pl.when(j > 0)
        def _():
            outer_store(j - 1).wait()
            inner_store(j - 1).wait()

        buffer[0] = dot_tn(hidden[j], grad_low[...]).astype(BF16)
        outer_store(j).start()
        buffer[1] = dot_tn(cross_low[...], grad_inner[...]).astype(BF16)
        inner_store(j).start()
        return carry

    lax.fori_loop(0, 4, back, 0)
    gain_sum = jnp.zeros((1, width), F32)
    shift_sum = jnp.zeros((1, width), F32)
    grad_sum = jnp.zeros((1, width), F32)
    for c in chunks:
        incoming = total[c, :]
        hat = normed[c, :]
        gain_sum += column_sum(incoming * hat)
        shift_sum += column_sum(incoming)
        grad = norm_back(incoming * vec(2), hat, scale_ref[c, :])
        grad_sum += column_sum(grad)
        grad_ref[c, :] = grad
        low = grad.astype(BF16)
        grad_low[c, :] = low
        gmix_ref[c, :] = dot_nt(low, w_co[...]).astype(BF16)
    sums_ref[0:1, :] = grad_sum
    sums_ref[2:3, :] = gain_sum
    sums_ref[4:5, :] = shift_sum
    outer_store(3).wait()
    buffer[0] = dot_tn(mixed_low[...], grad_low[...]).astype(BF16)
    store(0, d1.at[0]).start()
    store(0, d1.at[0]).wait()
    inner_store(3).wait()


def feed_forward(own_places, length, mixed, after, cotangent, vectors, inner_bias, units, outer):
    rows, width = after.shape
    hidden = outer.shape[0]
    any_spec = pl.BlockSpec(memory_space=pl.ANY)
    vmem_spec = pl.BlockSpec(memory_space=pltpu.VMEM)
    vmem = pltpu.VMEM
    return pl.pallas_call(
        feed_body,
        in_specs=[pl.BlockSpec(memory_space=pltpu.SMEM)] * 2 + [vmem_spec] * 5 + [any_spec] * 2,
        out_specs=[vmem_spec] * 5 + [any_spec] * 2,
        out_shape=[
            jax.ShapeDtypeStruct((rows, width), F32),
            jax.ShapeDtypeStruct((rows, width), BF16),
            jax.ShapeDtypeStruct((rows, width), F32),
            jax.ShapeDtypeStruct((8, width), F32),
            jax.ShapeDtypeStruct((1, hidden), F32),
            jax.ShapeDtypeStruct((5, width, width), BF16),
            jax.ShapeDtypeStruct((hidden, width), BF16),
        ],
        scratch_shapes=[
            vmem((width, width), BF16),
            vmem((4, width, width), BF16),
            vmem((4, width, width), BF16),
            vmem((rows, width), BF16),
            vmem((rows, width), F32),
            vmem((rows, 1), F32),
            vmem((rows, width), F32),
            vmem((rows, width), BF16),
            vmem((4, rows, width), BF16),
            vmem((4, rows, width), BF16),
            vmem((rows, width), BF16),
            vmem((rows, width), F32),
            vmem((rows, width), BF16),
            vmem((2, width, width), BF16),
            pltpu.SemaphoreType.DMA((9,)),
            pltpu.SemaphoreType.DMA((2,)),
        ],
        compiler_params=pltpu.CompilerParams(vmem_limit_bytes=VMEM_LIMIT),
        name="feed_forward",
    )(own_places, length, mixed, after, cotangent, vectors, inner_bias, units, outer)


VLANES = 256
WINDOW = 384


def spread_lanes(pieces, width):
    count = WINDOW // width
    lanes = pieces[0].shape[1]
    row = lax.broadcasted_iota(jnp.int32, (lanes, WINDOW), 0)
    column = lax.broadcasted_iota(jnp.int32, (lanes, WINDOW), 1)
    windows = [None] * (len(pieces) // count)
    for k in range(count):
        select = ((column == row + k * width) & (row < width)).astype(F32).astype(BF16)
        for w in range(len(windows)):
            part = dot_nn(pieces[w * count + k], select)
            windows[w] = part if k == 0 else windows[w] + part
    return jnp.concatenate(windows, axis=1)


def pair_forward(causal, p, q, k_all, v_all, values_t, out, totals, own_places, places, length):
    lanes = pl.ds(pl.multiple_of(p * PAIR, PAIR), PAIR)
    parts, part_rows = k_all.shape[0], k_all.shape[1]
    for h in range(parts):
        for block in range(part_rows // QBLK):
            rows = slice(block * QBLK, (block + 1) * QBLK)
            at = h * part_rows + block * QBLK
            values_t[:, at : at + QBLK] = v_all[h, rows, lanes].astype(F32).T.astype(BF16)

    def step(i, carry):
        rows = pl.ds(pl.multiple_of(i * QBLK, QBLK), QBLK)
        both = stack_heads(q[rows, lanes])
        scores = [dot_nt(k_all[h, :, lanes], both) for h in range(parts)]
        if causal:
            limit = row_limit(own_places[i], length)
            scores = [
                mask_part(s, limit, places, h * (part_rows // QBLK)) for h, s in enumerate(scores)
            ]
        highest = jnp.max(scores[0], axis=0, keepdims=True)
        for s in scores[1:]:
            highest = jnp.maximum(highest, jnp.max(s, axis=0, keepdims=True))
        total, mixed = 0.0, 0.0
        for h, s in enumerate(scores):
            exponent = jnp.exp(s - highest)
            total += jnp.sum(exponent, axis=0, keepdims=True)
            mixed += dot_nn(
                values_t[:, h * part_rows : (h + 1) * part_rows], exponent.astype(BF16)
            )
        out[rows, lanes] = unstack_heads(mixed * (1.0 / total), QBLK)
        totals[p, pl.ds(i, 1), :] = highest + jnp.log(total)
        return carry

    lax.fori_loop(0, q.shape[0] // QBLK, step, 0)


def row_limit(place, length):
    column = lax.broadcasted_iota(jnp.int32, (1, 2 * QBLK), 1)
    own = place * QBLK + jnp.where(column >= QBLK, column - QBLK, column)
    return jnp.minimum(own, length - 1)


def mask_part(scores, limit, places, first_block):
    row = lax.broadcasted_iota(jnp.int32, (QBLK, 2 * QBLK), 0)
    blocks = []
    for block in range(scores.shape[0] // QBLK):
        part = scores[block * QBLK : (block + 1) * QBLK]
        kept = row <= limit - places[first_block + block] * QBLK
        blocks.append(jnp.where(kept, part, MASKED_SCORE))
    return jnp.concatenate(blocks, axis=0)


def encode_body(
    depth, own_places, places, length_ref, states, encoder, vectors, sp, so, cq, ckv, co, fi, fo,
    g1, g2, q_out, k_out, v_out, cq_out, ck_out, cv_out, o_out, total_out, after_out, low_out, hat_out,
    scale_out, co_out, ctotal_out, flat_out, inner_out,
    gv, own, w, q, k_all, v_all, c_q, ck_all, cv_all, mixed, after, low, hat, values_t, cvalues_t,
    load_sem, own_sem, weight_sem, store_sem, zs, zr, fs, fr, ss, sr, ps, pr, ks, kr,
):
    core, odd, z, y, x = coordinates()
    ups, first, second, partner = peers_of(core, odd, z, y, x, depth)
    rows, width = so.shape
    length = length_ref[0]
    sources = (
        [sp.at[:, pl.ds(j * width, width)] for j in (1, 2, 0)]
        + [so, cq]
        + [ckv.at[:, pl.ds(j * width, width)] for j in range(2)]
        + [co]
        + [fi.at[:, pl.ds(j * width, width)] for j in range(4)]
        + [fo.at[pl.ds(j * rows, rows), :] for j in range(4)]
    )
    loads = [pltpu.make_async_copy(s, own.at[u], load_sem.at[u]) for u, s in enumerate(sources)]
    for load in loads:
        load.start()
    enter(ups, first, second, partner)

    def mine(i):
        return vectors if i == VECTORS else own.at[2 * i + odd]

    def set_at(i, parity, yy, xx):
        return gv.at[:, yy, xx] if i == VECTORS else unit_set(g1, g2, None, i, parity, yy, xx)

    def block_at(i, zz):
        return gv.at[zz, y, x] if i == VECTORS else unit_block(g1, g2, None, i, odd, zz, y, x)

    def set_of(i, a, b):
        return set_at(i, odd, *flip(odd, y, x, a, b))

    def up_copy(i, k):
        return remote(mine(i), block_at(i, z), zs.at[i, k], zr.at[i, k], ups[k])

    def up_arrival(i, k):
        block = block_at(i, (z + depth - 1 - k) % depth)
        return remote(block, block, zs.at[i, k], zr.at[i, k], ups[k])

    def first_copy(i):
        return remote(set_of(i, 0, 0), set_of(i, 0, 0), fs.at[i], fr.at[i], first)

    def first_arrival(i):
        return remote(set_of(i, 1, 0), set_of(i, 1, 0), fs.at[i], fr.at[i], first)

    def second_copy(i, a):
        return remote(set_of(i, a, 0), set_of(i, a, 0), ss.at[i, a], sr.at[i, a], second)

    def second_arrival(i, a):
        return remote(set_of(i, a, 1), set_of(i, a, 1), ss.at[i, a], sr.at[i, a], second)

    def partner_copy(i, a, b):
        at = a + 2 * b
        return remote(set_of(i, a, b), set_of(i, a, b), ps.at[i, at], pr.at[i, at], partner)

    def partner_arrival(i, a, b):
        at = a + 2 * b
        there = set_at(i, 1 - odd, *flip(1 - odd, y, x, a, b))
        return remote(there, there, ps.at[i, at], pr.at[i, at], partner)

    keeps = {}

    def begin(i):
        keeps[i] = pltpu.make_async_copy(mine(i), block_at(i, z), own_sem.at[i])
        keeps[i].start()
        for k in range(depth - 1):
            up_copy(i, k).start()

    def stage_2(i):
        keeps[i].wait()
        for k in range(depth - 1):
            up_arrival(i, k).wait_recv()
        first_copy(i).start()
        second_copy(i, 0).start()
        if i != VECTORS:
            partner_copy(i, 0, 0).start()

    def stage_3(i):
        first_arrival(i).wait_recv()
        second_copy(i, 1).start()
        if i != VECTORS:
            partner_copy(i, 1, 0).start()

    def stage_4(i):
        for a in range(2):
            second_arrival(i, a).wait_recv()
            if i != VECTORS:
                partner_copy(i, a, 1).start()

    def finish(i):
        for a in range(2):
            for b in range(2):
                partner_arrival(i, a, b).wait_recv()

    def weight(u):
        return pltpu.make_async_copy(
            g1.at[u].reshape(width, width), w.at[u], weight_sem.at[u]
        )

    stores = []

    def store(source, target):
        copy = pltpu.make_async_copy(source, target, store_sem.at[len(stores)])
        copy.start()
        stores.append(copy)

    begin(VECTORS)
    for i in range(HALF):
        loads[2 * i].wait()
        loads[2 * i + 1].wait()
        begin(i)
    stage_2(VECTORS)
    stage_3(VECTORS)
    stage_2(0)
    stage_4(VECTORS)
    flat = spread_lanes([gv[f // 4, (f // 2) % 2, f % 2] for f in range(4 * depth)], rows)
    flat_out[...] = flat
    inner_rows = fo.shape[0]
    inner_out[...] = spread_lanes(
        [gv[f // 4, (f // 2) % 2, f % 2] for f in range(4 * depth)], inner_rows
    )[13:14, :]
    vec = lambda i: flat[i : i + 1, :]
    stage_3(0)
    stage_2(1)
    stage_4(0)
    finish(0)
    for u in range(2):
        weight(u).start()

    row_count = states.shape[0]
    chunks = [pl.ds(c * CHUNK, CHUNK) for c in range(row_count // CHUNK)]
    encoder_count = encoder.shape[0]
    step = min(CHUNK, encoder_count)
    encoder_chunks = [pl.ds(c * step, step) for c in range(encoder_count // step)]

    def share(number, array):
        copy = remote(array.at[0], array.at[1], ks.at[number], kr.at[number], partner)
        copy.start()
        return copy

    weight(0).wait()
    for c in chunks:
        k_all[0, c, :] = dot_nn(states[c, :], w[0]).astype(BF16)
    shares = [share(0, k_all)]
    stage_3(1)
    stage_2(2)
    weight(1).wait()
    for c in chunks:
        v_all[0, c, :] = (dot_nn(states[c, :], w[1]) + vec(1)).astype(BF16)
    shares.append(share(1, v_all))
    stage_2(3)
    stage_4(1)
    finish(1)
    for u in range(2, 4):
        weight(u).start()
    weight(2).wait()
    for c in chunks:
        q[c, :] = ((dot_nn(states[c, :], w[2]) + vec(0)) * ATTN_SCALE).astype(BF16)
    store(q, q_out)
    shares[0].wait_recv()
    shares[1].wait_recv()
    store(k_all, k_out)
    store(v_all, v_out)
    pairs = width // PAIR

    def self_step(p, carry):
        pair_forward(
            True, p, q, k_all, v_all, values_t, mixed, total_out, own_places, places, length
        )

        @pl.when(p == 0)
        def _():
            stage_3(2)
            stage_2(4)

        @pl.when(p == 2)
        def _():
            stage_3(3)
            stage_4(2)
            stage_2(5)

        @pl.when(p == 4)
        def _():
            stage_3(4)
            stage_2(6)

        return carry

    lax.fori_loop(0, pairs, self_step, 0)
    store(mixed, o_out)
    stage_4(3)
    stage_2(7)
    finish(2)
    finish(3)
    for u in (5, 6, 4, 7):
        weight(u).start()
    weight(5).wait()
    for c in encoder_chunks:
        ck_all[0, c, :] = dot_nn(encoder[c, :], w[5]).astype(BF16)
    shares.append(share(2, ck_all))
    weight(6).wait()
    for c in encoder_chunks:
        cv_all[0, c, :] = (dot_nn(encoder[c, :], w[6]) + vec(4)).astype(BF16)
    shares.append(share(3, cv_all))
    weight(3).wait()
    weight(4).wait()
    for c in chunks:
        value = states[c, :].astype(F32) + dot_nn(mixed[c, :].astype(BF16), w[3]) + vec(2)
        normed, scale = norm_stats(value)
        hat[c, :] = normed
        scale_out[c, :] = scale
        value = normed * vec(7) + vec(10)
        after[c, :] = value
        low[c, :] = value.astype(BF16)
        c_q[c, :] = ((dot_nn(low[c, :], w[4]) + vec(3)) * ATTN_SCALE).astype(BF16)
    store(hat, hat_out)
    store(after, after_out)
    store(low, low_out)
    store(c_q, cq_out)
    stage_3(5)
    stage_4(4)
    shares[2].wait_recv()
    shares[3].wait_recv()
    store(ck_all, ck_out)
    store(cv_all, cv_out)
    stores[3].wait()

    def cross_step(p, carry):
        pair_forward(
            False, p, c_q, ck_all, cv_all, cvalues_t, mixed, ctotal_out, None, None, None
        )

        @pl.when(p == 0)
        def _():
            stage_3(6)

        @pl.when(p == 2)
        def _():
            stage_3(7)
            stage_4(5)

        @pl.when(p == 4)
        def _():
            stage_4(6)

        @pl.when(p == 5)
        def _():
            stage_4(7)

        return carry

    lax.fori_loop(0, pairs, cross_step, 0)
    store(mixed, co_out)
    weight(7).wait()
    for at, copy in enumerate(stores):
        if at != 3:
            copy.wait()
    for copy in shares:
        copy.wait_send()
    for i in [VECTORS, *range(HALF)]:
        if i >= 4 and i != VECTORS:
            finish(i)
        for a in range(2):
            for b in range(2):
                if i != VECTORS:
                    partner_copy(i, a, b).wait_send()
            second_copy(i, a).wait_send()
        first_copy(i).wait_send()
        for k in range(depth - 1):
            up_copy(i, k).wait_send()


def encode(
    n_fsdp, own_places, places, length, states, encoder, vectors, sp, so, cq, ckv, co, fi, fo
):
    rows, width = so.shape
    depth = n_fsdp // 4
    row_count, encoder_count = states.shape[0], encoder.shape[0]
    pairs = width // PAIR
    steps = HALF + 1
    dma = pltpu.SemaphoreType.DMA
    vmem = pltpu.VMEM
    any_spec = pl.BlockSpec(memory_space=pl.ANY)
    vmem_spec = pl.BlockSpec(memory_space=pltpu.VMEM)
    smem_spec = pl.BlockSpec(memory_space=pltpu.SMEM)
    shape = jax.ShapeDtypeStruct
    totals = (pairs, row_count // QBLK, 2 * QBLK)
    outs = [
        (any_spec, (FIRST, depth, 2, 2, rows, width), BF16),
        (any_spec, (depth, 2, 2, UNITS - FIRST, rows, width), BF16),
        (any_spec, (row_count, width), BF16),
        (any_spec, (2, row_count, width), BF16),
        (any_spec, (2, row_count, width), BF16),
        (any_spec, (row_count, width), BF16),
        (any_spec, (2, encoder_count, width), BF16),
        (any_spec, (2, encoder_count, width), BF16),
        (any_spec, (row_count, width), F32),
        (vmem_spec, totals, F32),
        (any_spec, (row_count, width), F32),
        (any_spec, (row_count, width), BF16),
        (any_spec, (row_count, width), F32),
        (vmem_spec, (row_count, 1), F32),
        (any_spec, (row_count, width), F32),
        (vmem_spec, totals, F32),
        (vmem_spec, (VROWS, width), F32),
        (vmem_spec, (1, fo.shape[0] * n_fsdp), F32),
    ]
    return pl.pallas_call(
        functools.partial(encode_body, depth),
        in_specs=[smem_spec] * 3 + [vmem_spec] * 3 + [any_spec] * 7,
        out_specs=[spec for spec, _, _ in outs],
        out_shape=[shape(extent, kind) for _, extent, kind in outs],
        scratch_shapes=[
            vmem((depth, 2, 2, VROWS, VLANES), BF16),
            vmem((UNITS, rows, width), BF16),
            vmem((8, width, width), BF16),
            vmem((row_count, width), BF16),
            vmem((2, row_count, width), BF16),
            vmem((2, row_count, width), BF16),
            vmem((row_count, width), BF16),
            vmem((2, encoder_count, width), BF16),
            vmem((2, encoder_count, width), BF16),
            vmem((row_count, width), F32),
            vmem((row_count, width), F32),
            vmem((row_count, width), BF16),
            vmem((row_count, width), F32),
            vmem((PAIR, 2 * row_count), BF16),
            vmem((PAIR, 2 * encoder_count), BF16),
            dma((UNITS,)),
            dma((steps,)),
            dma((8,)),
            dma((12,)),
            dma((steps, depth - 1)),
            dma((steps, depth - 1)),
            dma((steps,)),
            dma((steps,)),
            dma((steps, 2)),
            dma((steps, 2)),
            dma((steps, 4)),
            dma((steps, 4)),
            dma((4,)),
            dma((4,)),
        ],
        compiler_params=pltpu.CompilerParams(
            collective_id=2, has_side_effects=True, vmem_limit_bytes=VMEM_LIMIT
        ),
        name="encode",
    )(own_places, places, length, states, encoder, vectors, sp, so, cq, ckv, co, fi, fo)


def pair_backward(
    causal, p, q, g, o, totals, k_all, v_all, keys_t, dk, dv, dq, kept, sent, sums, sum_row,
    own_places, places, length,
):
    lanes = pl.ds(pl.multiple_of(p * PAIR, PAIR), PAIR)
    parts, part_rows = k_all.shape[0], k_all.shape[1]
    for h in range(parts):
        for block in range(part_rows // QBLK):
            rows = slice(block * QBLK, (block + 1) * QBLK)
            at = h * part_rows + block * QBLK
            keys_t[:, at : at + QBLK] = k_all[h, rows, lanes].astype(F32).T.astype(BF16)
    dk[...] = jnp.zeros_like(dk)
    dv[...] = jnp.zeros_like(dv)

    def step(i, carry):
        rows = pl.ds(pl.multiple_of(i * QBLK, QBLK), QBLK)
        both = stack_heads(q[rows, lanes])
        grads = g[rows, lanes]
        both_grads = stack_heads(grads)
        products = (grads.astype(F32) * o[rows, lanes]).T
        delta = jnp.concatenate(
            [
                jnp.sum(products[:HD], axis=0, keepdims=True),
                jnp.sum(products[HD:], axis=0, keepdims=True),
            ],
            axis=1,
        )
        if causal:
            limit = row_limit(own_places[i], length)
        level = totals[p, pl.ds(i, 1), :]
        query_grad = 0.0
        for h in range(parts):
            span = slice(h * part_rows, (h + 1) * part_rows)
            scores = dot_nt(k_all[h, :, lanes], both)
            if causal:
                scores = mask_part(scores, limit, places, h * (part_rows // QBLK))
            prob = jnp.exp(scores - level)
            prob_grad = dot_nt(v_all[h, :, lanes], both_grads)
            score_grad = (prob * (prob_grad - delta)).astype(BF16)
            dv[span, :] += dot_nn(prob.astype(BF16), both_grads)
            dk[span, :] += dot_nn(score_grad, both)
            query_grad += dot_nn(keys_t[:, span], score_grad)
        query_grad = unstack_heads(query_grad, QBLK) * ATTN_SCALE
        dq[rows, lanes] = query_grad.astype(BF16)
        return carry + jnp.sum(query_grad, axis=0, keepdims=True)

    sums[sum_row : sum_row + 1, lanes] = lax.fori_loop(
        0, q.shape[0] // QBLK, step, jnp.zeros((1, PAIR), F32)
    )
    for at, grad in enumerate((dk, dv)):
        kept[at, :, lanes] = grad[:part_rows, :].astype(BF16)
        sent[at, :, lanes] = grad[part_rows:, :].astype(BF16)


def select_lanes(offset, first, limit, lanes):
    lane = lax.broadcasted_iota(jnp.int32, (WINDOW, lanes), 1) + first
    column = lax.broadcasted_iota(jnp.int32, (WINDOW, lanes), 0)
    return ((column == lane + offset) & (lane < limit)).astype(F32).astype(BF16)


def decode_body(
    depth, own_places, places, length_ref, flat, scale_ref, ctotal, total, feed_sums, inner_sum,
    units, cq_in, ck_in, cv_in, co_in, gmix_in, low_in, encoder_in, hat_in, grad_in, q_in, k_in, v_in,
    o_in, states_in, d1, d2,
    gs_out, ge_out, out, out_v,
    own, from_partner, from_second, from_first, from_up, w, q, g, o, k, v, dq, kept, sent, arrived,
    inputs, enc, hat, grad, dk, dv, keys_t, sums,
    gv, from_partner_v, from_second_v, from_first_v, from_up_v,
    load_sem, own_sem, store_sem, zs, zr, fs, fr, ss, sr, ps, pr, xs, xr, ks, kr,
):
    core, odd, z, y, x = coordinates()
    ups, first, second, partner = peers_of(core, odd, z, y, x, depth)
    rows, width = units.shape[-2:]
    row_count = q.shape[0]
    length = length_ref[0]
    order = ((0, 1), (1, 1), (1, 0), (0, 0))
    pairs = width // PAIR
    chunks = [pl.ds(c * CHUNK, CHUNK) for c in range(row_count // CHUNK)]
    column_sum = lambda array: jnp.sum(array, axis=0, keepdims=True)


    def pick(i, main, small):
        return small if i == VECTORS else main.at[i]

    def kept_set(i, a, b):
        yy, xx = flip(odd, y, x, a, b)
        return gv.at[odd, :, yy, xx] if i == VECTORS else own.at[i, :, yy, xx]

    def sent_set(i, a, b):
        yy, xx = flip(1 - odd, y, x, a, b)
        u = 2 * i + 1 - odd
        if i == VECTORS:
            return gv.at[1 - odd, :, yy, xx]
        if 2 * i >= FIRST:
            return d2.at[:, yy, xx, u - FIRST]
        if 2 * i >= 8:
            return d1.at[u - 7, :, yy, xx]
        return own.at[HALF + i, :, yy, xx]

    def own_copy(i):
        u = 2 * i + odd
        source = d2.at[:, :, :, u - FIRST] if 2 * i >= FIRST else d1.at[u - 7]
        return pltpu.make_async_copy(source, own.at[i], own_sem.at[i])

    def partner_copy(i, a, b):
        at = a + 2 * b
        return remote(
            sent_set(i, a, b),
            pick(i, from_partner, from_partner_v).at[at],
            ps.at[i, at],
            pr.at[i, at],
            partner,
        )

    def second_copy(i, a):
        target = pick(i, from_second, from_second_v).at[a]
        return remote(kept_set(i, a, 1), target, ss.at[i, a], sr.at[i, a], second)

    def first_copy(i):
        target = pick(i, from_first, from_first_v)
        return remote(kept_set(i, 1, 0), target, fs.at[i], fr.at[i], first)

    def up_copy(i, n):
        source = kept_set(i, 0, 0).at[(z + 1 + n) % depth]
        target = pick(i, from_up, from_up_v).at[n]
        return remote(source, target, zs.at[i, n], zr.at[i, n], ups[n])

    def final_copy(i, parity):
        target = out_v.at[parity] if i == VECTORS else out.at[2 * i + parity]
        return remote(target, target, xs.at[i], xr.at[i], partner)

    def add(target, addend):
        def step(j, carry):
            target[j] = target[j] + addend[j]
            return carry

        lax.fori_loop(0, depth, step, 0)

    def send(i):
        for a, b in order:
            partner_copy(i, a, b).start()

    def stage_1(i):
        if HALF > i >= 4:
            own_copy(i).wait()
        for a, b in order:
            partner_copy(i, a, b).wait_recv()
            add(kept_set(i, a, b), pick(i, from_partner, from_partner_v).at[a + 2 * b])
            if b:
                second_copy(i, a).start()

    def stage_2(i):
        for a in (1, 0):
            second_copy(i, a).wait_recv()
            add(kept_set(i, a, 0), pick(i, from_second, from_second_v).at[a])
            if a:
                first_copy(i).start()

    def stage_3(i):
        first_copy(i).wait_recv()
        add(kept_set(i, 0, 0), pick(i, from_first, from_first_v))
        for n in range(depth - 1):
            up_copy(i, n).start()

    def stage_4(i):
        value = kept_set(i, 0, 0)[z].astype(F32)
        for n in range(depth - 1):
            up_copy(i, n).wait_recv()
            value = value + pick(i, from_up, from_up_v)[n].astype(F32)
        if i == VECTORS:
            out_v[odd] = value
        else:
            out[2 * i + odd] = value
        final_copy(i, odd).start()

    def put_unit(u, value):
        at = u // 2 + HALF * ((u + odd) % 2)
        own[at] = value.astype(BF16).reshape(depth, 2, 2, rows, width)


    loads = []

    def load(source, target):
        copy = pltpu.make_async_copy(source, target, load_sem.at[len(loads)])
        copy.start()
        loads.append(copy)
        return copy

    def weight(u, at):
        return load(units.at[u].reshape(width, width), w.at[at])

    attention_loads = [load(*pair) for pair in ((cq_in, q), (ck_in, k), (cv_in, v), (gmix_in, g), (co_in, o))]
    for i in range(HALF - 1, 3, -1):
        own_copy(i).start()
    cross_loads = [load(low_in, inputs), weight(4, 0), load(grad_in, grad), load(hat_in, hat), weight(3, 1)]
    encoder_loads = [load(encoder_in, enc), weight(5, 2), weight(6, 3)]
    output_load = load(d1.at[0], own.at[3 + HALF * ((7 + odd) % 2)])
    enter(ups, first, second, partner)
    for i in range(HALF - 1, 3, -1):
        send(i)

    sums[...] = jnp.zeros_like(sums)
    for at, row in enumerate((5, 6, 8, 9, 11, 12)):
        sums[row : row + 1, :] = feed_sums[at : at + 1, :]
    for copy in attention_loads:
        copy.wait()

    def cross_step(p, carry):
        pair_backward(
            False, p, q, g, o, ctotal, k, v, keys_t, dk, dv, dq, kept, sent, sums, 3, None, None, None
        )

        @pl.when(p == 0)
        def _():
            stage_1(7)

        @pl.when(p == 2)
        def _():
            stage_1(6)
            stage_2(7)

        @pl.when(p == 4)
        def _():
            stage_1(5)
            stage_2(6)
            stage_3(7)

        return carry

    lax.fori_loop(0, pairs, cross_step, 0)
    cross_share = remote(sent, arrived.at[0], ks.at[0], kr.at[0], partner)
    cross_share.start()
    self_loads = [load(*pair) for pair in ((o_in, o), (q_in, q), (k_in, k), (v_in, v))]
    for copy in cross_loads:
        copy.wait()
    put_unit(4, dot_tn(inputs[...], dq[...]))
    states_load = load(states_in, inputs)
    gain_sum = jnp.zeros((1, width), F32)
    shift_sum = jnp.zeros((1, width), F32)
    grad_sum = jnp.zeros((1, width), F32)
    for c in chunks:
        incoming = grad[c, :] + dot_nt(dq[c, :], w[0])
        normed = hat[c, :]
        gain_sum += column_sum(incoming * normed)
        shift_sum += column_sum(incoming)
        value = norm_back(incoming * flat[7:8, :], normed, scale_ref[c, :])
        grad_sum += column_sum(value)
        grad[c, :] = value
        low = value.astype(BF16)
        dq[c, :] = low
        g[c, :] = dot_nt(low, w[1]).astype(BF16)
    sums[2:3, :] = grad_sum
    sums[7:8, :] = gain_sum
    sums[10:11, :] = shift_sum
    stage_1(4)
    stage_2(5)
    stage_3(6)
    stage_4(7)
    last_loads = [weight(2, 0)]
    self_loads[0].wait()
    put_unit(3, dot_tn(o[...].astype(BF16), dq[...]))
    last_loads.append(weight(0, 1))

    def total_kept(number, c):
        low = []
        for at in range(2):
            value = kept[at, c, :].astype(F32) + arrived[number, at, c, :].astype(F32)
            kept[at, c, :] = value.astype(BF16)
            low.append(value)
        return column_sum(low[1])

    for copy in encoder_loads:
        copy.wait()
    cross_share.wait_recv()
    sums[4:5, :] = sum(total_kept(0, c) for c in chunks)
    put_unit(5, dot_tn(enc[...], kept[0]))
    send(2)
    put_unit(6, dot_tn(enc[...], kept[1]))
    output_load.wait()
    send(3)
    for c in chunks:
        hat[c, :] = dot_nt(kept[0, c, :], w[2]) + dot_nt(kept[1, c, :], w[3])
    encoder_store = pltpu.make_async_copy(hat, ge_out, store_sem.at[0])
    encoder_store.start()
    last_loads.append(weight(1, 2))
    stage_2(4)
    stage_3(5)
    stage_4(6)
    cross_share.wait_send()
    for copy in self_loads[1:]:
        copy.wait()
    half = (pairs // 2) * PAIR

    def self_share(n):
        span = pl.ds(n * half, half if n == 0 else width - half)
        return remote(
            sent.at[:, :, span], arrived.at[1, :, :, span], ks.at[1 + n], kr.at[1 + n], partner
        )

    def self_step(p, carry):
        pair_backward(
            True, p, q, g, o, total, k, v, keys_t, dk, dv, dq, kept, sent, sums, 0, own_places, places,
            length,
        )

        @pl.when(p == 0)
        def _():
            stage_1(3)
            stage_3(4)
            stage_4(5)

        @pl.when(p == pairs // 2 - 1)
        def _():
            self_share(0).start()
            stage_1(2)
            stage_2(3)
            stage_4(4)

        @pl.when(p == 3)
        def _():
            stage_3(3)

        @pl.when(p == 4)
        def _():
            stage_2(2)

        @pl.when(p == 5)
        def _():
            stage_3(2)

        return carry

    lax.fori_loop(0, pairs, self_step, 0)
    self_share(1).start()
    states_load.wait()
    put_unit(0, dot_tn(inputs[...], dq[...]))
    stage_4(3)
    self_share(0).wait_recv()
    self_share(1).wait_recv()
    sums[1:2, :] = sum(total_kept(1, c) for c in chunks)
    put_unit(1, dot_tn(inputs[...], kept[0]))
    send(0)
    put_unit(2, dot_tn(inputs[...], kept[1]))
    send(1)
    pack_sums(depth, rows, sums, inner_sum, gv)
    send(VECTORS)
    for copy in last_loads:
        copy.wait()
    stage_1(0)
    stage_4(2)
    grad[chunks[0], :] += dot_nt(dq[chunks[0], :], w[0])
    stage_1(1)
    stage_1(VECTORS)
    stage_2(0)
    for c in chunks:
        value = grad[c, :] + dot_nt(kept[0, c, :], w[1]) + dot_nt(kept[1, c, :], w[2])
        grad[c, :] = value if c is chunks[0] else value + dot_nt(dq[c, :], w[0])
    states_store = pltpu.make_async_copy(grad, gs_out, store_sem.at[1])
    states_store.start()
    stage_2(1)
    stage_2(VECTORS)
    stage_3(0)
    stage_3(1)
    stage_3(VECTORS)
    stage_4(0)
    stage_4(1)
    stage_4(VECTORS)
    encoder_store.wait()
    states_store.wait()
    for n in range(2):
        self_share(n).wait_send()
    for i in range(HALF + 1):
        final_copy(i, 1 - odd).wait_recv()
        final_copy(i, odd).wait_send()
        for a, b in order:
            partner_copy(i, a, b).wait_send()
        for a in range(2):
            second_copy(i, a).wait_send()
        first_copy(i).wait_send()
        for n in range(depth - 1):
            up_copy(i, n).wait_send()


def pack_sums(depth, rows, sums, inner_sum, gv):
    lanes = gv.shape[-1]
    width = sums.shape[1]
    low = sums[...].astype(BF16)
    row = lax.broadcasted_iota(jnp.int32, (VROWS, lanes), 0)
    window_row = lax.broadcasted_iota(jnp.int32, (VROWS, WINDOW), 0)
    inner_low = jnp.zeros((VROWS, WINDOW), F32)
    for at in range(inner_sum.shape[1] // WINDOW):
        piece = inner_sum[:, at * WINDOW : (at + 1) * WINDOW]
        inner_low = jnp.where(window_row == at, piece, inner_low)
    inner_low = inner_low.astype(BF16)
    windows = jnp.concatenate([low[:, i : i + WINDOW] for i in range(0, width, WINDOW)], axis=0)
    count, inner_rows = WINDOW // rows, inner_sum.shape[1] // (4 * depth)
    inner_count = WINDOW // inner_rows
    inner = [
        [
            dot_nn(inner_low, select_lanes(n * inner_rows, part * lanes, inner_rows, lanes))
            for part in range(2)
        ]
        for n in range(inner_count)
    ]
    for n in range(count):
        picked = dot_nn(windows, select_lanes(n * rows, 0, rows, lanes))
        for at in range(width // WINDOW):
            f = at * count + n
            for part in range(2):
                own = picked[at * VROWS : (at + 1) * VROWS] if part == 0 else jnp.zeros_like(row, F32)
                at_inner = f // inner_count
                other = inner[f % inner_count][part][at_inner : at_inner + 1, :]
                gv[part, f // 4, (f // 2) % 2, f % 2] = jnp.where(row == 13, other, own).astype(BF16)


def decode(
    n_fsdp, own_places, places, length, flat, scale, ctotal, total, feed_sums, inner_sum, units, cq, ck,
    cv, co, gmix, low, encoder, hat, grad, q, k, v, o, states, d1, d2,
):
    rows, width = units.shape[-2:]
    depth = n_fsdp // 4
    row_count = states.shape[0]
    steps = HALF + 1
    dma = pltpu.SemaphoreType.DMA
    vmem = pltpu.VMEM
    any_spec = pl.BlockSpec(memory_space=pl.ANY)
    vmem_spec = pl.BlockSpec(memory_space=pltpu.VMEM)
    smem_spec = pl.BlockSpec(memory_space=pltpu.SMEM)
    block, small = (rows, width), (VROWS, LANES)
    narrow = vmem((row_count, width), BF16)
    wide = vmem((row_count, width), F32)
    both = vmem((2, row_count, width), BF16)
    return pl.pallas_call(
        functools.partial(decode_body, depth),
        in_specs=[smem_spec] * 3 + [vmem_spec] * 6 + [any_spec] * 17,
        out_specs=[any_spec] * 2 + [vmem_spec] * 2,
        out_shape=[
            jax.ShapeDtypeStruct((row_count, width), F32),
            jax.ShapeDtypeStruct((row_count, width), F32),
            jax.ShapeDtypeStruct((UNITS, *block), F32),
            jax.ShapeDtypeStruct((2, *small), F32),
        ],
        scratch_shapes=[
            vmem((HALF + 4, depth, 2, 2, *block), BF16),
            vmem((HALF, 4, depth, *block), BF16),
            vmem((HALF, 2, depth, *block), BF16),
            vmem((HALF, depth, *block), BF16),
            vmem((HALF, depth - 1, *block), BF16),
            vmem((4, width, width), BF16),
            narrow, narrow, wide, both, both, narrow, both, both,
            vmem((2, 2, row_count, width), BF16),
            narrow, narrow, wide, wide,
            vmem((2 * row_count, PAIR), F32),
            vmem((2 * row_count, PAIR), F32),
            vmem((PAIR, 2 * row_count), BF16),
            vmem((VROWS, width), F32),
            vmem((2, depth, 2, 2, *small), BF16),
            vmem((4, depth, *small), BF16),
            vmem((2, depth, *small), BF16),
            vmem((depth, *small), BF16),
            vmem((depth - 1, *small), BF16),
            dma((24,)),
            dma((HALF,)),
            dma((2,)),
            dma((steps, depth - 1)),
            dma((steps, depth - 1)),
            dma((steps,)),
            dma((steps,)),
            dma((steps, 2)),
            dma((steps, 2)),
            dma((steps, 4)),
            dma((steps, 4)),
            dma((steps,)),
            dma((steps,)),
            dma((3,)),
            dma((3,)),
        ],
        compiler_params=pltpu.CompilerParams(
            collective_id=3, has_side_effects=True, vmem_limit_bytes=DECODE_LIMIT
        ),
        name="decode",
    )(
        own_places, places, length, flat, scale, ctotal, total, feed_sums, inner_sum, units, cq, ck, cv,
        co, gmix, low, encoder, hat, grad, q, k, v, o, states,
        d1.reshape(-1, depth, 2, 2, *block),
        d2.reshape(depth, 2, 2, UNITS - FIRST, *block),
    )


GROUPS = ((0, 1, 2), (3,), (4,), (5, 6), (7,), (8, 9, 10, 11))


def lay_out_body(shards, *outs):
    rows, width = shards.shape[1:]
    for group, target in zip(GROUPS, outs):
        for at, u in enumerate(group):
            target[:, at * width : (at + 1) * width] = shards[u]
    for at in range(UNITS - FIRST):
        outs[-1][at * rows : (at + 1) * rows, :] = shards[FIRST + at]


def lay_out(shards):
    rows, width = shards.shape[1:]
    shapes = [(rows, width * len(group)) for group in GROUPS] + [((UNITS - FIRST) * rows, width)]
    return pl.pallas_call(
        lay_out_body,
        in_specs=[pl.BlockSpec(memory_space=pltpu.VMEM)],
        out_specs=[pl.BlockSpec(memory_space=pltpu.VMEM)] * len(shapes),
        out_shape=[jax.ShapeDtypeStruct(shape, F32) for shape in shapes],
        name="lay_out",
    )(shards)


def per_device_wide(
    n_ctx,
    n_fsdp,
    states,
    encoded,
    lengths,
    block_order,
    cotangent,
    self_project,
    self_bias,
    self_output,
    self_shift,
    cross_query,
    cross_keyval,
    cross_bias,
    cross_output,
    cross_shift,
    feed_inner,
    inner_bias,
    feed_outer,
    outer_bias,
    norm_gain,
    norm_shift,
):
    local_rows = states.shape[1]
    width = states.shape[2]
    rows = self_output.shape[0]
    local_blocks = local_rows // QBLK
    core = lax.axis_index("ctx")
    own_order = lax.dynamic_slice_in_dim(block_order, core * local_blocks, local_blocks)
    places = block_order
    spread = lambda array: (lax.all_gather(array, "ctx", axis=0, tiled=True),)
    collect = lambda parts: lax.psum_scatter(
        parts[0], "ctx", scatter_dimension=0, tiled=True
    ).astype(F32)

    vectors = jnp.concatenate(
        [
            self_bias,
            self_shift[None],
            cross_bias,
            cross_shift[None],
            outer_bias[None],
            norm_gain,
            norm_shift,
            inner_bias.reshape(-1, rows),
        ],
        axis=0,
    )
    inner_rows = inner_bias.shape[0] // rows
    count = vectors.shape[0]
    pad = ((0, 2 * VROWS - count), (0, LANES - rows))
    units, w_fo, all_vectors = gather_weights(
        n_fsdp, jnp.pad(vectors, pad).reshape(2, VROWS, LANES), self_project, self_output, cross_query,
        cross_keyval, cross_output, feed_inner, feed_outer,
    )
    all_vectors = jnp.transpose(all_vectors, (1, 0, 2, 3)).reshape(n_fsdp, 2 * VROWS, LANES)
    all_vectors = all_vectors[:, :count, :rows].astype(F32)
    inner_full = all_vectors[:, 13:].reshape(1, -1)
    flat = jnp.transpose(all_vectors, (1, 0, 2)).reshape(count, -1)
    b_q, b_v, b_so, b_cq, b_cv = (flat[i] for i in range(5))

    w_q, w_k, w_v, w_so, w_cq, w_ck, w_cv, w_co = (units[i] for i in range(8))

    inputs = states[0]
    encoder_rows = encoded[0]
    queries = ((dot_nn(inputs, w_q) + b_q) * ATTN_SCALE).astype(BF16)
    own_keys = dot_nn(inputs, w_k).astype(BF16)
    own_values = (dot_nn(inputs, w_v) + b_v).astype(BF16)
    own_cross_keys = dot_nn(encoder_rows, w_ck).astype(BF16)
    own_cross_values = (dot_nn(encoder_rows, w_cv) + b_cv).astype(BF16)
    keys, values = spread(own_keys), spread(own_values)
    cross_keys, cross_values = spread(own_cross_keys), spread(own_cross_values)

    attend = functools.partial(attention_forward, places=places, own_places=own_order, length=lengths)
    self_attended, self_total = attend(True, queries, keys, values)
    self_mixed = self_attended.astype(BF16)
    after_self, norm_back_one = jax.vjp(
        layer_norm, inputs.astype(F32) + dot_nn(self_mixed, w_so) + b_so, flat[7], flat[10]
    )
    after_self_low = after_self.astype(BF16)
    cross_queries = ((dot_nn(after_self_low, w_cq) + b_cq) * ATTN_SCALE).astype(BF16)
    cross_attended, cross_total = attend(False, cross_queries, cross_keys, cross_values)
    output, grad_cross_mixed, grad_two, feed_sums, inner_sum, d_low, d_outer = feed_forward(
        own_order, lengths, cross_attended, after_self, cotangent[0], flat[:16], inner_full, units, w_fo
    )
    attend_back = functools.partial(
        attention_backward, places=places, own_places=own_order, length=lengths
    )
    cross_query_grad, ck_parts, cv_parts = attend_back(
        False, cross_queries, grad_cross_mixed, cross_attended, cross_total, cross_keys, cross_values
    )
    cross_query_low = cross_query_grad.astype(BF16)
    d_cq = dot_tn(after_self_low, cross_query_low).astype(BF16)
    ck_grad, cv_grad = collect(ck_parts), collect(cv_parts)
    ck_low, cv_low = ck_grad.astype(BF16), cv_grad.astype(BF16)
    d_ck = dot_tn(encoder_rows, ck_low).astype(BF16)
    d_cv = dot_tn(encoder_rows, cv_low).astype(BF16)
    grad_encoded = dot_nt(ck_low, w_ck) + dot_nt(cv_low, w_cv)
    grad_one, gain_one, shift_one = norm_back_one(grad_two + dot_nt(cross_query_low, w_cq))
    grad_one_low = grad_one.astype(BF16)
    d_so = dot_tn(self_mixed, grad_one_low).astype(BF16)
    grad_self_mixed = dot_nt(grad_one_low, w_so).astype(BF16)
    query_grad, k_parts, v_parts = attend_back(
        True, queries, grad_self_mixed, self_attended, self_total, keys, values
    )
    query_low = query_grad.astype(BF16)
    key_grad, value_grad = collect(k_parts), collect(v_parts)
    key_low, value_low = key_grad.astype(BF16), value_grad.astype(BF16)
    d_q = dot_tn(inputs, query_low).astype(BF16)
    d_k = dot_tn(inputs, key_low).astype(BF16)
    d_v = dot_tn(inputs, value_low).astype(BF16)
    grad_states = grad_one + dot_nt(query_low, w_q) + dot_nt(key_low, w_k) + dot_nt(value_low, w_v)

    column_sum = lambda array: jnp.sum(array, axis=0)
    grad_vectors = jnp.stack(
        [
            column_sum(query_grad),
            column_sum(value_grad),
            column_sum(grad_one),
            column_sum(cross_query_grad),
            column_sum(cv_grad),
            feed_sums[0],
            feed_sums[1],
            gain_one,
            feed_sums[2],
            feed_sums[3],
            shift_one,
            feed_sums[4],
            feed_sums[5],
        ]
    ).reshape(13, n_fsdp, rows)
    inner_vector = inner_sum.reshape(n_fsdp, inner_rows, rows)
    packed = jnp.concatenate([jnp.transpose(grad_vectors, (1, 0, 2)), inner_vector], axis=1)
    packed = jnp.pad(packed, ((0, 0), *pad)).astype(BF16)
    packed = jnp.transpose(packed.reshape(n_fsdp, 2, VROWS, LANES), (1, 0, 2, 3))

    shards, mine = scatter_gradients(
        n_fsdp, [d_q, d_k, d_v, d_so, d_cq, d_ck, d_cv], d_low, d_outer, packed
    )
    if n_ctx > 2:
        groups = [[c for c in range(n_ctx) if c % 2 == odd] for odd in range(2)]
        total = lambda part: lax.psum(part.astype(BF16), "ctx", axis_index_groups=groups).astype(F32)
        shards, mine = total(shards), total(mine)
    mine = mine.reshape(2 * VROWS, LANES)[:, :rows]
    return (
        output[None],
        grad_states[None],
        grad_encoded[None],
        jnp.concatenate([shards[0], shards[1], shards[2]], axis=1),
        mine[0:2],
        shards[3],
        mine[2],
        shards[4],
        jnp.concatenate([shards[5], shards[6]], axis=1),
        mine[3:5],
        shards[7],
        mine[5],
        jnp.concatenate([shards[8 + i] for i in range(4)], axis=1),
        mine[13 : 13 + inner_rows].reshape(-1),
        shards[12:].reshape(-1, width),
        mine[6],
        mine[7:10],
        mine[10:13],
    )


def per_device(
    n_ctx,
    n_fsdp,
    states,
    encoded,
    lengths,
    block_order,
    cotangent,
    self_project,
    self_bias,
    self_output,
    self_shift,
    cross_query,
    cross_keyval,
    cross_bias,
    cross_output,
    cross_shift,
    feed_inner,
    inner_bias,
    feed_outer,
    outer_bias,
    norm_gain,
    norm_shift,
):
    local_rows = states.shape[1]
    width = states.shape[2]
    rows = self_output.shape[0]
    local_blocks = local_rows // QBLK
    core = lax.axis_index("ctx")
    own_order = lax.dynamic_slice_in_dim(block_order, core * local_blocks, local_blocks)
    other_order = lax.dynamic_slice_in_dim(block_order, (1 - core) * local_blocks, local_blocks)
    places = jnp.concatenate([own_order, other_order])
    narrow = jnp.concatenate(
        [
            self_bias,
            self_shift[None],
            cross_bias,
            cross_shift[None],
            outer_bias[None],
            norm_gain,
            norm_shift,
        ],
        axis=0,
    )
    vectors = jnp.concatenate(
        [
            jnp.pad(narrow, ((0, 0), (0, VLANES - rows))),
            jnp.pad(inner_bias[None], ((0, VROWS - 14), (0, VLANES - inner_bias.shape[0]))),
        ],
        axis=0,
    )
    (
        units, w_fo, queries, keys, values, cross_queries, cross_keys, cross_values, self_attended,
        self_total, after_self, after_self_low, hat, scale, cross_attended, cross_total, flat, inner_full,
    ) = encode(
        n_fsdp, own_order, places, lengths, states[0], encoded[0], vectors, self_project, self_output,
        cross_query, cross_keyval, cross_output, feed_inner, feed_outer,
    )
    output, grad_cross_mixed, grad_two, feed_sums, inner_sum, d_low, d_outer = feed_forward(
        own_order, lengths, cross_attended, after_self, cotangent[0], flat, inner_full,
        units.reshape(FIRST, width, width), w_fo.reshape(-1, width),
    )
    grad_states, grad_encoded, shards, mine = decode(
        n_fsdp, own_order, places, lengths, flat, scale, cross_total, self_total, feed_sums, inner_sum,
        units, cross_queries, cross_keys, cross_values, cross_attended, grad_cross_mixed, after_self_low,
        encoded[0], hat, grad_two, queries, keys, values, self_attended, states[0], d_low, d_outer,
    )
    d_sp, d_so, d_cq, d_ckv, d_co, d_fi, d_fo = lay_out(shards)
    narrow = mine[0, :, :rows]
    inner = mine[:, 13].reshape(-1)[: inner_bias.shape[0]]
    return (
        output[None],
        grad_states[None],
        grad_encoded[None],
        d_sp,
        narrow[0:2],
        d_so,
        narrow[2],
        d_cq,
        d_ckv,
        narrow[3:5],
        d_co,
        narrow[5],
        d_fi,
        inner,
        d_fo,
        narrow[6],
        narrow[7:10],
        narrow[10:13],
    )


def solution(mesh):
    return jax.shard_map(
        functools.partial(
            per_device if mesh.shape["ctx"] == 2 else per_device_wide,
            mesh.shape["ctx"],
            mesh.shape["fsdp"],
        ),
        mesh=mesh,
        in_specs=(
            P("fsdp", "ctx", None),
            P("fsdp", "ctx", None),
            P("fsdp"),
            P(),
            P("fsdp", "ctx", None),
            P("fsdp", None),
            P(None, "fsdp"),
            P("fsdp", None),
            P("fsdp"),
            P("fsdp", None),
            P("fsdp", None),
            P(None, "fsdp"),
            P("fsdp", None),
            P("fsdp"),
            P("fsdp", None),
            P("fsdp"),
            P("fsdp", None),
            P("fsdp"),
            P(None, "fsdp"),
            P(None, "fsdp"),
        ),
        out_specs=(
            P("fsdp", "ctx", None),
            P("fsdp", "ctx", None),
            P("fsdp", "ctx", None),
            P("fsdp", None),
            P(None, "fsdp"),
            P("fsdp", None),
            P("fsdp"),
            P("fsdp", None),
            P("fsdp", None),
            P(None, "fsdp"),
            P("fsdp", None),
            P("fsdp"),
            P("fsdp", None),
            P("fsdp"),
            P("fsdp", None),
            P("fsdp"),
            P(None, "fsdp"),
            P(None, "fsdp"),
        ),
        check_vma=False,
    )
```

```python
import functools

import jax
import jax.numpy as jnp
from jax import lax
from jax.experimental import pallas as pl
from jax.experimental.pallas import tpu as pltpu
from jax.sharding import PartitionSpec as P

H = 12
HD = 64
QBLK = 128
PAIR = 2 * HD
ATTN_SCALE = 0.125
MASKED_SCORE = -1e30
EPSILON = 1e-05
MESH = pl.DeviceIdType.MESH
VMEM_LIMIT = 60 * 1024 * 1024
DECODE_LIMIT = 67043328
BF16 = jnp.bfloat16
F32 = jnp.float32


def dot_nn(left, right):
    return lax.dot_general(left, right, (((1,), (0,)), ((), ())), preferred_element_type=F32)


def dot_nt(left, right):
    return lax.dot_general(left, right, (((1,), (1,)), ((), ())), preferred_element_type=F32)


def dot_tn(left, right):
    return lax.dot_general(left, right, (((0,), (0,)), ((), ())), preferred_element_type=F32)


def layer_norm(inputs, scale_vec, shift_vec):
    average = jnp.mean(inputs, axis=-1, keepdims=True)
    centred = inputs - average
    variance = jnp.mean(centred * centred, axis=-1, keepdims=True)
    return centred * lax.rsqrt(variance + EPSILON) * scale_vec + shift_vec


class Places:
    def __init__(self, block_order, own_count):
        self.block_order = block_order
        self.start = lax.axis_index("ctx") * own_count

    def __getitem__(self, i):
        return self.block_order[lax.rem(self.start + i, self.block_order.shape[0])]


def gelu_exact(inputs):
    return jax.nn.gelu(inputs, approximate=False)


def stack_heads(rows):
    first = lax.broadcasted_iota(jnp.int32, rows.shape, 1) < HD
    zero = jnp.zeros_like(rows)
    return jnp.concatenate([jnp.where(first, rows, zero), jnp.where(first, zero, rows)], axis=0)


def unstack_heads(both, count):
    return jnp.concatenate([both[:HD, :count], both[HD:, count:]], axis=0).T


def variants_of(key_count, causal):
    if not causal:
        return [key_count]
    step = max(2 * QBLK, key_count // 4)
    return [step * (i + 1) for i in range(key_count // step)]


def load_keys(causal, places, sources, target):
    block = 0
    for source in sources:
        for local in range(source.shape[0] // QBLK):
            rows = source[local * QBLK : (local + 1) * QBLK, :]
            if causal:
                at = pl.multiple_of(places[block] * QBLK, QBLK)
                target[pl.ds(at, QBLK), :] = rows
            else:
                target[block * QBLK : (block + 1) * QBLK, :] = rows
            block += 1


def masked_scores(causal, keys, both, place, length, count):
    scores = dot_nt(keys, both)
    if causal:
        column = lax.broadcasted_iota(jnp.int32, (1, 2 * count), 1)
        row_place = place * QBLK + jnp.where(column >= count, column - count, column)
        limit = jnp.minimum(row_place, length - 1)
        key_place = lax.broadcasted_iota(jnp.int32, scores.shape, 0)
        scores = jnp.where(key_place <= limit, scores, MASKED_SCORE)
    return scores


def for_each_block(causal, sizes, block_count, own_places, length, body):
    def step(i, carry):
        if not causal:
            body(i, 0, sizes[0])
            return carry
        place = own_places[i]
        needed = jnp.minimum((place + 1) * QBLK, length)
        for at, size in enumerate(sizes):
            low = sizes[at - 1] if at else 0

            @pl.when((needed > low) & (needed <= size))
            def _(size=size):
                body(i, place, size)

        return carry

    lax.fori_loop(0, block_count, step, 0)


def forward_body(causal, n_src, places, own_places, length_ref, q_ref, *refs):
    key_refs, value_refs = refs[:n_src], refs[n_src : 2 * n_src]
    out_ref, total_ref, keys, values_t = refs[2 * n_src :]
    load_keys(causal, places, key_refs, keys)
    length = length_ref[0]
    block = 0
    for source in value_refs:
        for local in range(source.shape[0] // QBLK):
            rows = source[local * QBLK : (local + 1) * QBLK, :].astype(F32).T.astype(BF16)
            at = pl.multiple_of(places[block] * QBLK, QBLK) if causal else block * QBLK
            values_t[:, pl.ds(at, QBLK)] = rows
            block += 1

    def body(i, place, size):
        rows = pl.ds(pl.multiple_of(i * QBLK, QBLK), QBLK)
        both = stack_heads(q_ref[rows, :])
        scores = masked_scores(causal, keys[:size, :], both, place, length, QBLK)
        highest = jnp.max(scores, axis=0, keepdims=True)
        exponent = jnp.exp(scores - highest)
        total = jnp.sum(exponent, axis=0, keepdims=True)
        mixed = dot_nn(values_t[:, :size], exponent.astype(BF16)) * (1.0 / total)
        out_ref[rows, :] = unstack_heads(mixed, QBLK)
        total_ref[0, pl.ds(i, 1), :] = highest + jnp.log(total)

    for_each_block(
        causal,
        variants_of(keys.shape[0], causal),
        q_ref.shape[0] // QBLK,
        own_places,
        length,
        body,
    )


def attention_forward(causal, queries, keys, values, places, own_places, length):
    rows, width = queries.shape
    n_src = len(keys)
    key_count = sum(k.shape[0] for k in keys)
    pairs = width // PAIR
    column = lambda i, *_: (0, i)
    spec = lambda n: pl.BlockSpec((n, PAIR), column)
    return pl.pallas_call(
        functools.partial(forward_body, causal, n_src),
        grid_spec=pltpu.PrefetchScalarGridSpec(
            num_scalar_prefetch=3,
            grid=(pairs,),
            in_specs=[spec(rows)] + [spec(k.shape[0]) for k in (*keys, *values)],
            out_specs=[
                spec(rows),
                pl.BlockSpec((1, rows // QBLK, 2 * QBLK), lambda i, *_: (i, 0, 0)),
            ],
            scratch_shapes=[
                pltpu.VMEM((key_count, PAIR), BF16),
                pltpu.VMEM((PAIR, key_count), BF16),
            ],
        ),
        out_shape=[
            jax.ShapeDtypeStruct((rows, width), F32),
            jax.ShapeDtypeStruct((pairs, rows // QBLK, 2 * QBLK), F32),
        ],
        compiler_params=pltpu.CompilerParams(vmem_limit_bytes=VMEM_LIMIT),
        name="self_forward" if causal else "cross_forward",
    )(places, own_places, length, queries, *keys, *values)


def backward_body(causal, n_src, places, own_places, length_ref, q_ref, g_ref, o_ref, t_ref, *refs):
    key_refs, value_refs = refs[:n_src], refs[n_src : 2 * n_src]
    dq_ref = refs[2 * n_src]
    dk_refs = refs[2 * n_src + 1 : 3 * n_src + 1]
    dv_refs = refs[3 * n_src + 1 : 4 * n_src + 1]
    keys, values, keys_t, dk, dv = refs[4 * n_src + 1 :]
    load_keys(causal, places, key_refs, keys)
    load_keys(causal, places, value_refs, values)
    length = length_ref[0]
    key_count = keys.shape[0]
    for block in range(key_count // QBLK):
        rows = slice(block * QBLK, (block + 1) * QBLK)
        keys_t[:, rows] = keys[rows, :].astype(F32).T.astype(BF16)
    dk[...] = jnp.zeros_like(dk)
    dv[...] = jnp.zeros_like(dv)

    def body(i, place, size):
        rows = pl.ds(pl.multiple_of(i * QBLK, QBLK), QBLK)
        both = stack_heads(q_ref[rows, :])
        grads = g_ref[rows, :]
        both_grads = stack_heads(grads)
        products = (grads.astype(F32) * o_ref[rows, :]).T
        delta = jnp.concatenate(
            [
                jnp.sum(products[:HD], axis=0, keepdims=True),
                jnp.sum(products[HD:], axis=0, keepdims=True),
            ],
            axis=1,
        )
        scores = masked_scores(causal, keys[:size, :], both, place, length, QBLK)
        prob = jnp.exp(scores - t_ref[0, pl.ds(i, 1), :])
        prob_grad = dot_nt(values[:size, :], both_grads)
        score_grad = (prob * (prob_grad - delta)).astype(BF16)
        dv[:size, :] += dot_nn(prob.astype(BF16), both_grads)
        dk[:size, :] += dot_nn(score_grad, both)
        dq = dot_nn(keys_t[:, :size], score_grad)
        dq_ref[rows, :] = unstack_heads(dq, QBLK) * ATTN_SCALE

    for_each_block(
        causal, variants_of(key_count, causal), q_ref.shape[0] // QBLK, own_places, length, body
    )
    block = 0
    for dk_out, dv_out in zip(dk_refs, dv_refs):
        for local in range(dk_out.shape[0] // QBLK):
            at = pl.multiple_of(places[block] * QBLK, QBLK) if causal else block * QBLK
            rows = slice(local * QBLK, (local + 1) * QBLK)
            dk_out[rows, :] = dk[pl.ds(at, QBLK), :].astype(BF16)
            dv_out[rows, :] = dv[pl.ds(at, QBLK), :].astype(BF16)
            block += 1


def attention_backward(
    causal, queries, grads, mixed, totals, keys, values, places, own_places, length
):
    rows, width = queries.shape
    n_src = len(keys)
    key_count = sum(k.shape[0] for k in keys)
    pairs = width // PAIR
    column = lambda i, *_: (0, i)
    spec = lambda n: pl.BlockSpec((n, PAIR), column)
    key_specs = [spec(k.shape[0]) for k in (*keys, *values)]
    outs = pl.pallas_call(
        functools.partial(backward_body, causal, n_src),
        grid_spec=pltpu.PrefetchScalarGridSpec(
            num_scalar_prefetch=3,
            grid=(pairs,),
            in_specs=[
                spec(rows),
                spec(rows),
                spec(rows),
                pl.BlockSpec((1, rows // QBLK, 2 * QBLK), lambda i, *_: (i, 0, 0)),
            ]
            + key_specs,
            out_specs=[spec(rows)] + key_specs,
            scratch_shapes=[
                pltpu.VMEM((key_count, PAIR), BF16),
                pltpu.VMEM((key_count, PAIR), BF16),
                pltpu.VMEM((PAIR, key_count), BF16),
                pltpu.VMEM((key_count, PAIR), F32),
                pltpu.VMEM((key_count, PAIR), F32),
            ],
        ),
        out_shape=[jax.ShapeDtypeStruct((rows, width), F32)]
        + [jax.ShapeDtypeStruct(k.shape, BF16) for k in (*keys, *values)],
        compiler_params=pltpu.CompilerParams(vmem_limit_bytes=VMEM_LIMIT),
        name="self_backward" if causal else "cross_backward",
    )(places, own_places, length, queries, grads, mixed, totals, *keys, *values)
    return outs[0], outs[1 : n_src + 1], outs[n_src + 1 :]


UNITS = 16
FIRST = 12
HALF = UNITS // 2
VECTORS = HALF
VROWS = 16
LANES = 128


def coordinates():
    core, f = lax.axis_index("ctx"), lax.axis_index("fsdp")
    return core, core % 2, f // 4, (f // 2) % 2, f % 2


def flip(odd, y, x, a, b):
    dx = a * (1 - odd) + b * odd
    dy = b * (1 - odd) + a * odd
    return y + dy * (1 - 2 * y), x + dx * (1 - 2 * x)


def peers_of(core, odd, z, y, x, depth):
    fsdp = lambda zz, yy, xx: (zz * 2 + yy) * 2 + xx
    ups = [(core, fsdp((z + k) % depth, y, x)) for k in range(1, depth)]
    first = (core, fsdp(z, *flip(odd, y, x, 1, 0)))
    second = (core, fsdp(z, *flip(odd, y, x, 0, 1)))
    partner = (core + 1 - 2 * odd, fsdp(z, y, x))
    return ups, first, second, partner


def enter(ups, first, second, partner):
    barrier = pltpu.get_barrier_semaphore()
    for peer in (*ups, first, second, partner):
        pl.semaphore_signal(barrier, inc=1, device_id=peer, device_id_type=MESH)
    pl.semaphore_wait(barrier, len(ups) + 3)


def remote(source, target, send, recv, peer):
    return pltpu.make_async_remote_copy(
        source, target, send, recv, device_id=peer, device_id_type=MESH
    )


def unit_set(g1, g2, gv, i, odd, y, x):
    if i == VECTORS:
        return gv.at[odd, :, y, x]
    if 2 * i < FIRST:
        return g1.at[2 * i + odd, :, y, x]
    return g2.at[:, y, x, 2 * i - FIRST + odd]


def unit_block(g1, g2, gv, i, odd, z, y, x):
    if i == VECTORS:
        return gv.at[odd, z, y, x]
    if 2 * i < FIRST:
        return g1.at[2 * i + odd, z, y, x]
    return g2.at[z, y, x, 2 * i - FIRST + odd]


def gather_body(
    depth, vectors, sp, so, cq, ckv, co, fi, fo, g1, g2, gv, own, load_sem, own_sem,
    zs, zr, fs, fr, ss, sr, ps, pr,
):
    core, odd, z, y, x = coordinates()
    ups, first, second, partner = peers_of(core, odd, z, y, x, depth)
    width = so.shape[1]
    rows = so.shape[0]
    sources = (
        [sp.at[:, pl.ds(j * width, width)] for j in range(3)]
        + [so, cq]
        + [ckv.at[:, pl.ds(j * width, width)] for j in range(2)]
        + [co]
        + [fi.at[:, pl.ds(j * width, width)] for j in range(4)]
        + [fo.at[pl.ds(j * rows, rows), :] for j in range(4)]
    )
    loads = [pltpu.make_async_copy(s, own.at[u], load_sem.at[u]) for u, s in enumerate(sources)]
    for load in loads:
        load.start()
    enter(ups, first, second, partner)

    def mine(i):
        return vectors.at[odd] if i == VECTORS else own.at[2 * i + odd]

    def set_of(i, a, b):
        return unit_set(g1, g2, gv, i, odd, *flip(odd, y, x, a, b))

    def up_copy(i, k):
        block = unit_block(g1, g2, gv, i, odd, z, y, x)
        return remote(mine(i), block, zs.at[i, k], zr.at[i, k], ups[k])

    def up_arrival(i, k):
        block = unit_block(g1, g2, gv, i, odd, (z + depth - 1 - k) % depth, y, x)
        return remote(block, block, zs.at[i, k], zr.at[i, k], ups[k])

    def first_copy(i):
        return remote(set_of(i, 0, 0), set_of(i, 0, 0), fs.at[i], fr.at[i], first)

    def second_copy(i, a):
        return remote(set_of(i, a, 0), set_of(i, a, 0), ss.at[i, a], sr.at[i, a], second)

    def partner_copy(i, a, b):
        at = a + 2 * b
        return remote(set_of(i, a, b), set_of(i, a, b), ps.at[i, at], pr.at[i, at], partner)

    def arrival(target, send, recv, peer):
        return remote(target, target, send, recv, peer)

    steps = [VECTORS, *range(HALF)]
    keeps = []
    for i in steps:
        if i != VECTORS:
            loads[2 * i].wait()
            loads[2 * i + 1].wait()
        keep = pltpu.make_async_copy(
            mine(i), unit_block(g1, g2, gv, i, odd, z, y, x), own_sem.at[i]
        )
        keep.start()
        keeps.append(keep)
        for k in range(depth - 1):
            up_copy(i, k).start()
    for step in range(len(steps) + 2):
        if step < len(steps):
            i = steps[step]
            keeps[step].wait()
            for k in range(depth - 1):
                up_arrival(i, k).wait_recv()
            first_copy(i).start()
            second_copy(i, 0).start()
            partner_copy(i, 0, 0).start()
        if 0 <= step - 1 < len(steps):
            i = steps[step - 1]
            arrival(set_of(i, 1, 0), fs.at[i], fr.at[i], first).wait_recv()
            second_copy(i, 1).start()
            partner_copy(i, 1, 0).start()
        if 0 <= step - 2 < len(steps):
            i = steps[step - 2]
            for a in range(2):
                arrival(set_of(i, a, 1), ss.at[i, a], sr.at[i, a], second).wait_recv()
                partner_copy(i, a, 1).start()
    for i in steps:
        for a in range(2):
            for b in range(2):
                at = a + 2 * b
                there = unit_set(g1, g2, gv, i, 1 - odd, *flip(1 - odd, y, x, a, b))
                arrival(there, ps.at[i, at], pr.at[i, at], partner).wait_recv()
                partner_copy(i, a, b).wait_send()
            second_copy(i, a).wait_send()
        first_copy(i).wait_send()
        for k in range(depth - 1):
            up_copy(i, k).wait_send()


def gather_weights(n_fsdp, vectors, sp, so, cq, ckv, co, fi, fo):
    rows, width = so.shape
    depth = n_fsdp // 4
    dma = pltpu.SemaphoreType.DMA
    steps = HALF + 1
    g1, g2, gv = pl.pallas_call(
        functools.partial(gather_body, depth),
        in_specs=[pl.BlockSpec(memory_space=pl.ANY)] * 8,
        out_specs=[pl.BlockSpec(memory_space=pl.ANY)] * 3,
        out_shape=[
            jax.ShapeDtypeStruct((FIRST, depth, 2, 2, rows, width), BF16),
            jax.ShapeDtypeStruct((depth, 2, 2, UNITS - FIRST, rows, width), BF16),
            jax.ShapeDtypeStruct((2, depth, 2, 2, VROWS, LANES), BF16),
        ],
        scratch_shapes=[
            pltpu.VMEM((UNITS, rows, width), BF16),
            dma((UNITS,)),
            dma((steps,)),
            dma((steps, depth - 1)),
            dma((steps, depth - 1)),
            dma((steps,)),
            dma((steps,)),
            dma((steps, 2)),
            dma((steps, 2)),
            dma((steps, 4)),
            dma((steps, 4)),
        ],
        compiler_params=pltpu.CompilerParams(
            collective_id=0, has_side_effects=True, vmem_limit_bytes=VMEM_LIMIT
        ),
        name="gather_weights",
    )(vectors, sp, so, cq, ckv, co, fi, fo)
    return (
        g1.reshape(FIRST, n_fsdp * rows, width),
        g2.reshape(-1, width),
        gv.reshape(2, n_fsdp, VROWS, LANES),
    )


def scatter_body(depth, *refs):
    units = refs[:7]
    (
        g1, g2, gv, out, out_v, own, from_partner, from_second, from_first, from_up, final, final_in,
        own_v, from_partner_v, from_second_v, from_first_v, from_up_v, final_v, final_in_v,
        own_sem, zs, zr, fs, fr, ss, sr, ps, pr, xs, xr,
    ) = refs[7:]
    core, odd, z, y, x = coordinates()
    ups, first, second, partner = peers_of(core, odd, z, y, x, depth)
    order = ((0, 1), (1, 1), (1, 0), (0, 0))

    def pick(i, main, small):
        return small if i == VECTORS else main.at[i]

    def source(i, parity, yy, xx):
        u = 2 * i + parity
        if i == VECTORS:
            return gv.at[parity, :, yy, xx]
        if 2 * i >= FIRST:
            return g2.at[:, yy, xx, u - FIRST]
        if 2 * i >= 8:
            return g1.at[u - 7, :, yy, xx]
        return units[u].at[:, yy, xx] if u < 7 else g1.at[0, :, yy, xx]

    def own_copy(i, a, b, parity):
        at = a + 2 * b
        return pltpu.make_async_copy(
            source(i, parity, *flip(odd, y, x, a, b)),
            pick(i, own, own_v).at[at],
            own_sem.at[i, at],
        )

    def partner_copy(i, a, b, parity):
        at = a + 2 * b
        return remote(
            source(i, parity, *flip(1 - odd, y, x, a, b)),
            pick(i, from_partner, from_partner_v).at[at],
            ps.at[i, at],
            pr.at[i, at],
            partner,
        )

    def second_copy(i, a):
        return remote(
            pick(i, own, own_v).at[a + 2],
            pick(i, from_second, from_second_v).at[a],
            ss.at[i, a],
            sr.at[i, a],
            second,
        )

    def first_copy(i):
        return remote(
            pick(i, own, own_v).at[1],
            pick(i, from_first, from_first_v),
            fs.at[i],
            fr.at[i],
            first,
        )

    def up_copy(i, k):
        return remote(
            pick(i, own, own_v).at[0, (z + 1 + k) % depth],
            pick(i, from_up, from_up_v).at[k],
            zs.at[i, k],
            zr.at[i, k],
            ups[k],
        )

    def final_copy(i):
        return remote(
            pick(i, final, final_v), pick(i, final_in, final_in_v), xs.at[i], xr.at[i], partner
        )

    def add(target, addend):
        def step(j, carry):
            target[j] = target[j] + addend[j]
            return carry

        lax.fori_loop(0, depth, step, 0)

    def start_all(copy, parity_of):
        for i in steps:
            if i != VECTORS and 2 * i < 8:
                for q in range(2):

                    @pl.when(odd == q)
                    def _(i=i, q=q):
                        for a, b in order:
                            copy(i, a, b, parity_of(q)).start()

            else:
                for a, b in order:
                    copy(i, a, b, parity_of(odd)).start()

    steps = [*range(HALF - 1, -1, -1), VECTORS]
    start_all(own_copy, lambda q: q)
    enter(ups, first, second, partner)
    start_all(partner_copy, lambda q: 1 - q)

    for step in range(len(steps) + 3):
        if step < len(steps):
            i = steps[step]
            for a, b in order:
                at = a + 2 * b
                own_copy(i, a, b, 0).wait()
                partner_copy(i, a, b, 0).wait_recv()
                add(pick(i, own, own_v).at[at], pick(i, from_partner, from_partner_v).at[at])
                if b:
                    second_copy(i, a).start()
        if 0 <= step - 1 < len(steps):
            i = steps[step - 1]
            for a in (1, 0):
                second_copy(i, a).wait_recv()
                add(pick(i, own, own_v).at[a], pick(i, from_second, from_second_v).at[a])
                if a:
                    first_copy(i).start()
        if 0 <= step - 2 < len(steps):
            i = steps[step - 2]
            first_copy(i).wait_recv()
            add(pick(i, own, own_v).at[0], pick(i, from_first, from_first_v))
            for k in range(depth - 1):
                up_copy(i, k).start()
        if 0 <= step - 3 < len(steps):
            i = steps[step - 3]
            total = pick(i, own, own_v)[0, z].astype(F32)
            for k in range(depth - 1):
                up_copy(i, k).wait_recv()
                total = total + pick(i, from_up, from_up_v)[k].astype(F32)
            pick(i, final, final_v)[...] = total
            final_copy(i).start()
            if i == VECTORS:
                out_v[odd] = total
            else:
                out[2 * i + odd] = total
    for i in steps:
        final_copy(i).wait()
        if i == VECTORS:
            out_v[1 - odd] = final_in_v[...]
        else:
            out[2 * i + 1 - odd] = final_in[i]
        for a, b in order:
            partner_copy(i, a, b, 0).wait_send()
        for a in range(2):
            second_copy(i, a).wait_send()
        first_copy(i).wait_send()
        for k in range(depth - 1):
            up_copy(i, k).wait_send()


def scatter_gradients(n_fsdp, units, g1, g2, gv):
    width = g1.shape[-1]
    depth = n_fsdp // 4
    rows = width // n_fsdp
    dma = pltpu.SemaphoreType.DMA
    vmem = pltpu.VMEM
    steps = HALF + 1
    block, small = (rows, width), (VROWS, LANES)
    return pl.pallas_call(
        functools.partial(scatter_body, depth),
        in_specs=[pl.BlockSpec(memory_space=pl.ANY)] * 10,
        out_specs=[pl.BlockSpec(memory_space=pltpu.VMEM)] * 2,
        out_shape=[
            jax.ShapeDtypeStruct((UNITS, *block), F32),
            jax.ShapeDtypeStruct((2, *small), F32),
        ],
        scratch_shapes=[
            vmem((HALF, 4, depth, *block), BF16),
            vmem((HALF, 4, depth, *block), BF16),
            vmem((HALF, 2, depth, *block), BF16),
            vmem((HALF, depth, *block), BF16),
            vmem((HALF, depth - 1, *block), BF16),
            vmem((HALF, *block), F32),
            vmem((HALF, *block), F32),
            vmem((4, depth, *small), BF16),
            vmem((4, depth, *small), BF16),
            vmem((2, depth, *small), BF16),
            vmem((depth, *small), BF16),
            vmem((depth - 1, *small), BF16),
            vmem(small, F32),
            vmem(small, F32),
            dma((steps, 4)),
            dma((steps, depth - 1)),
            dma((steps, depth - 1)),
            dma((steps,)),
            dma((steps,)),
            dma((steps, 2)),
            dma((steps, 2)),
            dma((steps, 4)),
            dma((steps, 4)),
            dma((steps,)),
            dma((steps,)),
        ],
        compiler_params=pltpu.CompilerParams(
            collective_id=1, has_side_effects=True, vmem_limit_bytes=VMEM_LIMIT
        ),
        name="scatter_gradients",
    )(
        *[u.reshape(depth, 2, 2, *block) for u in units],
        g1.reshape(-1, depth, 2, 2, *block),
        g2.reshape(depth, 2, 2, UNITS - FIRST, *block),
        gv.reshape(2, depth, 2, 2, *small),
    )


CHUNK = 256
VECTOR_ROWS = (5, 6, 8, 11, 9, 12)


def valid_of(own_places, length, chunk):
    row = lax.broadcasted_iota(jnp.int32, (CHUNK, 1), 0)
    place = row
    for block in range(CHUNK // QBLK):
        base = (own_places[chunk * (CHUNK // QBLK) + block] - block) * QBLK
        place = jnp.where((row >= block * QBLK) & (row < (block + 1) * QBLK), row + base, place)
    return place < length


def norm_stats(value):
    average = jnp.mean(value, axis=-1, keepdims=True)
    centred = value - average
    scale = lax.rsqrt(jnp.mean(centred * centred, axis=-1, keepdims=True) + EPSILON)
    return centred * scale, scale


def norm_back(grad, normed, scale):
    inner = jnp.mean(grad * normed, axis=-1, keepdims=True)
    return (grad - jnp.mean(grad, axis=-1, keepdims=True) - normed * inner) * scale


def feed_body(
    block_order, length_ref, mixed_ref, after_ref, cot_ref, vec_ref, b_fi_ref, g1, g2,
    out_ref, gmix_ref, grad_ref, sums_ref, isum_ref, d1, d2,
    w_co, w_fi, w_fo, mixed_low, normed, scale_ref, cross, cross_low, hidden, slope, grad_inner,
    total, grad_low, buffer, load_sem, store_sem,
):
    rows, width = after_ref.shape
    own_places = Places(block_order, rows // QBLK)
    chunks = [pl.ds(c * CHUNK, CHUNK) for c in range(rows // CHUNK)]
    output_load = pltpu.make_async_copy(g1.at[7], w_co, load_sem.at[0])

    def inner_load(j):
        return pltpu.make_async_copy(g1.at[8 + j], w_fi.at[j], load_sem.at[1 + j])

    def outer_load(j):
        source = g2.at[pl.ds(pl.multiple_of(j * width, width), width), :]
        return pltpu.make_async_copy(source, w_fo.at[j], load_sem.at[5 + j])

    output_load.start()
    for j in range(4):
        inner_load(j).start()
    for j in range(4):
        outer_load(j).start()
    vec = lambda i: vec_ref[VECTOR_ROWS[i] : VECTOR_ROWS[i] + 1, :]
    column_sum = lambda array: jnp.sum(array, axis=0, keepdims=True)

    output_load.wait()
    for c in chunks:
        mixed_low[c, :] = mixed_ref[c, :].astype(BF16)
        value = after_ref[c, :] + dot_nn(mixed_low[c, :], w_co[...]) + vec(0)
        hat, scale = norm_stats(value)
        normed[c, :] = hat
        scale_ref[c, :] = scale
        value = hat * vec(2) + vec(3)
        cross[c, :] = value
        cross_low[c, :] = value.astype(BF16)
        total[c, :] = value + vec(1)

    def forward(j, carry):
        inner_load(j).wait()
        outer_load(j).wait()
        bias = b_fi_ref[:, pl.ds(pl.multiple_of(j * width, width), width)]

        def inner_step(at, carry):
            c = pl.ds(pl.multiple_of(at * CHUNK, CHUNK), CHUNK)
            pre = dot_nn(cross_low[c, :], w_fi[j]) + bias
            share = 0.5 + 0.5 * lax.erf(pre * (0.5**0.5))
            act = (pre * share).astype(BF16)
            hidden[j, c, :] = act
            density = jnp.exp(-0.5 * pre * pre) * ((0.5 / jnp.pi) ** 0.5)
            slope[j, c, :] = (share + pre * density).astype(BF16)
            total[c, :] += dot_nn(act, w_fo[j])
            return carry

        return lax.fori_loop(0, rows // CHUNK, inner_step, carry)

    lax.fori_loop(0, 4, forward, 0)
    gain_sum = jnp.zeros((1, width), F32)
    shift_sum = jnp.zeros((1, width), F32)
    grad_sum = jnp.zeros((1, width), F32)
    for at, c in enumerate(chunks):
        hat, scale = norm_stats(total[c, :])
        valid = valid_of(own_places, length_ref[0], at)
        out_ref[c, :] = jnp.where(valid, hat * vec(4) + vec(5), 0.0)
        incoming = jnp.where(valid, cot_ref[c, :].astype(F32), 0.0)
        gain_sum += column_sum(incoming * hat)
        shift_sum += column_sum(incoming)
        grad = norm_back(incoming * vec(4), hat, scale)
        grad_sum += column_sum(grad)
        total[c, :] = grad
        grad_low[c, :] = grad.astype(BF16)
    sums_ref[1:2, :] = grad_sum
    sums_ref[3:4, :] = gain_sum
    sums_ref[5:6, :] = shift_sum

    def store(at, target):
        return pltpu.make_async_copy(buffer.at[at], target, store_sem.at[at])

    def outer_store(j):
        return store(0, d2.at[pl.ds(pl.multiple_of(j * width, width), width), :])

    def inner_store(j):
        return store(1, d1.at[1 + j])

    def back(j, carry):
        def back_step(at, carry):
            c = pl.ds(pl.multiple_of(at * CHUNK, CHUNK), CHUNK)
            grad = dot_nt(grad_low[c, :], w_fo[j]) * slope[j, c, :].astype(F32)
            low = grad.astype(BF16)
            grad_inner[c, :] = low
            total[c, :] += dot_nt(low, w_fi[j])
            return carry + column_sum(grad)

        isum_ref[:, pl.ds(pl.multiple_of(j * width, width), width)] = lax.fori_loop(
            0, rows // CHUNK, back_step, jnp.zeros((1, width), F32)
        )

        @pl.when(j > 0)
        def _():
            outer_store(j - 1).wait()
            inner_store(j - 1).wait()

        buffer[0] = dot_tn(hidden[j], grad_low[...]).astype(BF16)
        outer_store(j).start()
        buffer[1] = dot_tn(cross_low[...], grad_inner[...]).astype(BF16)
        inner_store(j).start()
        return carry

    lax.fori_loop(0, 4, back, 0)
    gain_sum = jnp.zeros((1, width), F32)
    shift_sum = jnp.zeros((1, width), F32)
    grad_sum = jnp.zeros((1, width), F32)
    for c in chunks:
        incoming = total[c, :]
        hat = normed[c, :]
        gain_sum += column_sum(incoming * hat)
        shift_sum += column_sum(incoming)
        grad = norm_back(incoming * vec(2), hat, scale_ref[c, :])
        grad_sum += column_sum(grad)
        grad_ref[c, :] = grad
        low = grad.astype(BF16)
        grad_low[c, :] = low
        gmix_ref[c, :] = dot_nt(low, w_co[...]).astype(BF16)
    sums_ref[0:1, :] = grad_sum
    sums_ref[2:3, :] = gain_sum
    sums_ref[4:5, :] = shift_sum
    outer_store(3).wait()
    buffer[0] = dot_tn(mixed_low[...], grad_low[...]).astype(BF16)
    store(0, d1.at[0]).start()
    store(0, d1.at[0]).wait()
    inner_store(3).wait()


def feed_forward(block_order, length, mixed, after, cotangent, vectors, inner_bias, units, outer):
    rows, width = after.shape
    hidden = outer.shape[0]
    any_spec = pl.BlockSpec(memory_space=pl.ANY)
    vmem_spec = pl.BlockSpec(memory_space=pltpu.VMEM)
    vmem = pltpu.VMEM
    return pl.pallas_call(
        feed_body,
        in_specs=[pl.BlockSpec(memory_space=pltpu.SMEM)] * 2 + [vmem_spec] * 5 + [any_spec] * 2,
        out_specs=[vmem_spec] * 5 + [any_spec] * 2,
        out_shape=[
            jax.ShapeDtypeStruct((rows, width), F32),
            jax.ShapeDtypeStruct((rows, width), BF16),
            jax.ShapeDtypeStruct((rows, width), F32),
            jax.ShapeDtypeStruct((8, width), F32),
            jax.ShapeDtypeStruct((1, hidden), F32),
            jax.ShapeDtypeStruct((5, width, width), BF16),
            jax.ShapeDtypeStruct((hidden, width), BF16),
        ],
        scratch_shapes=[
            vmem((width, width), BF16),
            vmem((4, width, width), BF16),
            vmem((4, width, width), BF16),
            vmem((rows, width), BF16),
            vmem((rows, width), F32),
            vmem((rows, 1), F32),
            vmem((rows, width), F32),
            vmem((rows, width), BF16),
            vmem((4, rows, width), BF16),
            vmem((4, rows, width), BF16),
            vmem((rows, width), BF16),
            vmem((rows, width), F32),
            vmem((rows, width), BF16),
            vmem((2, width, width), BF16),
            pltpu.SemaphoreType.DMA((9,)),
            pltpu.SemaphoreType.DMA((2,)),
        ],
        compiler_params=pltpu.CompilerParams(vmem_limit_bytes=VMEM_LIMIT),
        name="feed_forward",
    )(block_order, length, mixed, after, cotangent, vectors, inner_bias, units, outer)


VLANES = 256
WINDOW = 384


def spread_lanes(pieces, width):
    count = WINDOW // width
    lanes = pieces[0].shape[1]
    row = lax.broadcasted_iota(jnp.int32, (lanes, WINDOW), 0)
    column = lax.broadcasted_iota(jnp.int32, (lanes, WINDOW), 1)
    windows = [None] * (len(pieces) // count)
    for k in range(count):
        select = ((column == row + k * width) & (row < width)).astype(F32).astype(BF16)
        for w in range(len(windows)):
            part = dot_nn(pieces[w * count + k], select)
            windows[w] = part if k == 0 else windows[w] + part
    return jnp.concatenate(windows, axis=1)


def pair_forward(causal, p, q, k_all, v_all, values_t, out, totals, own_places, places, length):
    lanes = pl.ds(pl.multiple_of(p * PAIR, PAIR), PAIR)
    parts, part_rows = k_all.shape[0], k_all.shape[1]
    for h in range(parts):
        for block in range(part_rows // QBLK):
            rows = slice(block * QBLK, (block + 1) * QBLK)
            at = h * part_rows + block * QBLK
            values_t[:, at : at + QBLK] = v_all[h, rows, lanes].astype(F32).T.astype(BF16)

    def step(i, carry):
        rows = pl.ds(pl.multiple_of(i * QBLK, QBLK), QBLK)
        both = stack_heads(q[rows, lanes])
        scores = [dot_nt(k_all[h, :, lanes], both) for h in range(parts)]
        if causal:
            limit = row_limit(own_places[i], length)
            scores = [
                mask_part(s, limit, places, h * (part_rows // QBLK)) for h, s in enumerate(scores)
            ]
        highest = jnp.max(scores[0], axis=0, keepdims=True)
        for s in scores[1:]:
            highest = jnp.maximum(highest, jnp.max(s, axis=0, keepdims=True))
        total, mixed = 0.0, 0.0
        for h, s in enumerate(scores):
            exponent = jnp.exp(s - highest)
            total += jnp.sum(exponent, axis=0, keepdims=True)
            mixed += dot_nn(
                values_t[:, h * part_rows : (h + 1) * part_rows], exponent.astype(BF16)
            )
        out[rows, lanes] = unstack_heads(mixed * (1.0 / total), QBLK)
        totals[p, pl.ds(i, 1), :] = highest + jnp.log(total)
        return carry

    lax.fori_loop(0, q.shape[0] // QBLK, step, 0)


def row_limit(place, length):
    column = lax.broadcasted_iota(jnp.int32, (1, 2 * QBLK), 1)
    own = place * QBLK + jnp.where(column >= QBLK, column - QBLK, column)
    return jnp.minimum(own, length - 1)


def mask_part(scores, limit, places, first_block):
    row = lax.broadcasted_iota(jnp.int32, (QBLK, 2 * QBLK), 0)
    blocks = []
    for block in range(scores.shape[0] // QBLK):
        part = scores[block * QBLK : (block + 1) * QBLK]
        kept = row <= limit - places[first_block + block] * QBLK
        blocks.append(jnp.where(kept, part, MASKED_SCORE))
    return jnp.concatenate(blocks, axis=0)


def encode_body(
    depth, block_order, length_ref, states, encoder, b_self, b_cross, gains, shifts, singles, sp, so, cq, ckv, co, fi,
    fo, g1, g2, q_out, k_out, v_out, cq_out, ck_out, cv_out, o_out, total_out, after_out, low_out, hat_out,
    scale_out, co_out, ctotal_out, flat_out, inner_out,
    gv, own, spread_in, vectors, w, q, k_all, v_all, c_q, ck_all, cv_all, mixed, after, low, hat, values_t, cvalues_t,
    load_sem, own_sem, weight_sem, store_sem, zs, zr, fs, fr, ss, sr, ps, pr, ks, kr,
):
    core, odd, z, y, x = coordinates()
    ups, first, second, partner = peers_of(core, odd, z, y, x, depth)
    rows, width = so.shape
    length = length_ref[0]
    own_places = places = Places(block_order, states.shape[0] // QBLK)
    sources = (
        [sp.at[:, pl.ds(j * width, width)] for j in (1, 2, 0)]
        + [so, cq]
        + [ckv.at[:, pl.ds(j * width, width)] for j in range(2)]
        + [co]
        + [fi.at[:, pl.ds(j * width, width)] for j in range(4)]
        + [fo.at[pl.ds(j * rows, rows), :] for j in range(4)]
    )
    loads = [pltpu.make_async_copy(s, own.at[u], load_sem.at[u]) for u, s in enumerate(sources)]
    for load in loads:
        load.start()
    spread_in[...] = jnp.zeros_like(spread_in)
    for at, array in ((0, b_self), (3, b_cross), (7, gains), (10, shifts)):
        spread_in[at : at + array.shape[0], :rows] = array[...].astype(F32)
    for at, row in enumerate((2, 5, 6, 13)):
        spread_in[row : row + 1, : singles.shape[1]] = singles[at : at + 1, :].astype(F32)
    vectors[...] = spread_in[...].astype(BF16)
    enter(ups, first, second, partner)

    def mine(i):
        return vectors if i == VECTORS else own.at[2 * i + odd]

    def set_at(i, parity, yy, xx):
        return gv.at[:, yy, xx] if i == VECTORS else unit_set(g1, g2, None, i, parity, yy, xx)

    def block_at(i, zz):
        return gv.at[zz, y, x] if i == VECTORS else unit_block(g1, g2, None, i, odd, zz, y, x)

    def set_of(i, a, b):
        return set_at(i, odd, *flip(odd, y, x, a, b))

    def up_copy(i, k):
        return remote(mine(i), block_at(i, z), zs.at[i, k], zr.at[i, k], ups[k])

    def up_arrival(i, k):
        block = block_at(i, (z + depth - 1 - k) % depth)
        return remote(block, block, zs.at[i, k], zr.at[i, k], ups[k])

    def first_copy(i):
        return remote(set_of(i, 0, 0), set_of(i, 0, 0), fs.at[i], fr.at[i], first)

    def first_arrival(i):
        return remote(set_of(i, 1, 0), set_of(i, 1, 0), fs.at[i], fr.at[i], first)

    def second_copy(i, a):
        return remote(set_of(i, a, 0), set_of(i, a, 0), ss.at[i, a], sr.at[i, a], second)

    def second_arrival(i, a):
        return remote(set_of(i, a, 1), set_of(i, a, 1), ss.at[i, a], sr.at[i, a], second)

    def partner_copy(i, a, b):
        at = a + 2 * b
        return remote(set_of(i, a, b), set_of(i, a, b), ps.at[i, at], pr.at[i, at], partner)

    def partner_arrival(i, a, b):
        at = a + 2 * b
        there = set_at(i, 1 - odd, *flip(1 - odd, y, x, a, b))
        return remote(there, there, ps.at[i, at], pr.at[i, at], partner)

    keeps = {}

    def begin(i):
        keeps[i] = pltpu.make_async_copy(mine(i), block_at(i, z), own_sem.at[i])
        keeps[i].start()
        for k in range(depth - 1):
            up_copy(i, k).start()

    def stage_2(i):
        keeps[i].wait()
        for k in range(depth - 1):
            up_arrival(i, k).wait_recv()
        first_copy(i).start()
        second_copy(i, 0).start()
        if i != VECTORS:
            partner_copy(i, 0, 0).start()

    def stage_3(i):
        first_arrival(i).wait_recv()
        second_copy(i, 1).start()
        if i != VECTORS:
            partner_copy(i, 1, 0).start()

    def stage_4(i):
        for a in range(2):
            second_arrival(i, a).wait_recv()
            if i != VECTORS:
                partner_copy(i, a, 1).start()

    def finish(i):
        for a in range(2):
            for b in range(2):
                partner_arrival(i, a, b).wait_recv()

    def weight(u):
        return pltpu.make_async_copy(
            g1.at[u].reshape(width, width), w.at[u], weight_sem.at[u]
        )

    stores = []

    def store(source, target):
        copy = pltpu.make_async_copy(source, target, store_sem.at[len(stores)])
        copy.start()
        stores.append(copy)

    begin(VECTORS)
    for i in range(HALF):
        loads[2 * i].wait()
        loads[2 * i + 1].wait()
        begin(i)
    stage_2(VECTORS)
    stage_3(VECTORS)
    stage_2(0)
    stage_4(VECTORS)
    flat = spread_lanes([gv[f // 4, (f // 2) % 2, f % 2] for f in range(4 * depth)], rows)
    flat_out[...] = flat
    inner_rows = fo.shape[0]
    inner_out[...] = spread_lanes(
        [gv[f // 4, (f // 2) % 2, f % 2] for f in range(4 * depth)], inner_rows
    )[13:14, :]
    vec = lambda i: flat[i : i + 1, :]
    stage_3(0)
    stage_2(1)
    stage_4(0)
    finish(0)
    for u in range(2):
        weight(u).start()

    row_count = states.shape[0]
    chunks = [pl.ds(c * CHUNK, CHUNK) for c in range(row_count // CHUNK)]
    encoder_count = encoder.shape[0]
    step = min(CHUNK, encoder_count)
    encoder_chunks = [pl.ds(c * step, step) for c in range(encoder_count // step)]

    def share(number, array):
        copy = remote(array.at[0], array.at[1], ks.at[number], kr.at[number], partner)
        copy.start()
        return copy

    weight(0).wait()
    for c in chunks:
        k_all[0, c, :] = dot_nn(states[c, :], w[0]).astype(BF16)
    shares = [share(0, k_all)]
    stage_3(1)
    stage_2(2)
    weight(1).wait()
    for c in chunks:
        v_all[0, c, :] = (dot_nn(states[c, :], w[1]) + vec(1)).astype(BF16)
    shares.append(share(1, v_all))
    stage_2(3)
    stage_4(1)
    finish(1)
    for u in range(2, 4):
        weight(u).start()
    weight(2).wait()
    for c in chunks:
        q[c, :] = ((dot_nn(states[c, :], w[2]) + vec(0)) * ATTN_SCALE).astype(BF16)
    store(q, q_out)
    shares[0].wait_recv()
    shares[1].wait_recv()
    store(k_all, k_out)
    store(v_all, v_out)
    pairs = width // PAIR

    def self_step(p, carry):
        pair_forward(
            True, p, q, k_all, v_all, values_t, mixed, total_out, own_places, places, length
        )

        @pl.when(p == 0)
        def _():
            stage_3(2)
            stage_2(4)

        @pl.when(p == 2)
        def _():
            stage_3(3)
            stage_4(2)
            stage_2(5)

        @pl.when(p == 4)
        def _():
            stage_3(4)
            stage_2(6)

        return carry

    lax.fori_loop(0, pairs, self_step, 0)
    store(mixed, o_out)
    stage_4(3)
    stage_2(7)
    finish(2)
    finish(3)
    for u in (5, 6, 4, 7):
        weight(u).start()
    weight(5).wait()
    for c in encoder_chunks:
        ck_all[0, c, :] = dot_nn(encoder[c, :], w[5]).astype(BF16)
    shares.append(share(2, ck_all))
    weight(6).wait()
    for c in encoder_chunks:
        cv_all[0, c, :] = (dot_nn(encoder[c, :], w[6]) + vec(4)).astype(BF16)
    shares.append(share(3, cv_all))
    weight(3).wait()
    weight(4).wait()
    for c in chunks:
        value = states[c, :].astype(F32) + dot_nn(mixed[c, :].astype(BF16), w[3]) + vec(2)
        normed, scale = norm_stats(value)
        hat[c, :] = normed
        scale_out[c, :] = scale
        value = normed * vec(7) + vec(10)
        after[c, :] = value
        low[c, :] = value.astype(BF16)
        c_q[c, :] = ((dot_nn(low[c, :], w[4]) + vec(3)) * ATTN_SCALE).astype(BF16)
    store(hat, hat_out)
    store(after, after_out)
    store(low, low_out)
    store(c_q, cq_out)
    stage_3(5)
    stage_4(4)
    shares[2].wait_recv()
    shares[3].wait_recv()
    store(ck_all, ck_out)
    store(cv_all, cv_out)
    stores[3].wait()

    def cross_step(p, carry):
        pair_forward(
            False, p, c_q, ck_all, cv_all, cvalues_t, mixed, ctotal_out, None, None, None
        )

        @pl.when(p == 0)
        def _():
            stage_3(6)

        @pl.when(p == 2)
        def _():
            stage_3(7)
            stage_4(5)

        @pl.when(p == 4)
        def _():
            stage_4(6)

        @pl.when(p == 5)
        def _():
            stage_4(7)

        return carry

    lax.fori_loop(0, pairs, cross_step, 0)
    store(mixed, co_out)
    weight(7).wait()
    for at, copy in enumerate(stores):
        if at != 3:
            copy.wait()
    for copy in shares:
        copy.wait_send()
    for i in [VECTORS, *range(HALF)]:
        if i >= 4 and i != VECTORS:
            finish(i)
        for a in range(2):
            for b in range(2):
                if i != VECTORS:
                    partner_copy(i, a, b).wait_send()
            second_copy(i, a).wait_send()
        first_copy(i).wait_send()
        for k in range(depth - 1):
            up_copy(i, k).wait_send()


def encode(
    n_fsdp, block_order, length, states, encoder, b_self, b_cross, gains, shifts, singles, sp, so, cq,
    ckv, co, fi, fo,
):
    rows, width = so.shape
    depth = n_fsdp // 4
    row_count, encoder_count = states.shape[0], encoder.shape[0]
    pairs = width // PAIR
    steps = HALF + 1
    dma = pltpu.SemaphoreType.DMA
    vmem = pltpu.VMEM
    any_spec = pl.BlockSpec(memory_space=pl.ANY)
    vmem_spec = pl.BlockSpec(memory_space=pltpu.VMEM)
    smem_spec = pl.BlockSpec(memory_space=pltpu.SMEM)
    shape = jax.ShapeDtypeStruct
    totals = (pairs, row_count // QBLK, 2 * QBLK)
    outs = [
        (any_spec, (FIRST, depth, 2, 2, rows, width), BF16),
        (any_spec, (depth, 2, 2, UNITS - FIRST, rows, width), BF16),
        (any_spec, (row_count, width), BF16),
        (any_spec, (2, row_count, width), BF16),
        (any_spec, (2, row_count, width), BF16),
        (any_spec, (row_count, width), BF16),
        (any_spec, (2, encoder_count, width), BF16),
        (any_spec, (2, encoder_count, width), BF16),
        (any_spec, (row_count, width), F32),
        (vmem_spec, totals, F32),
        (any_spec, (row_count, width), F32),
        (any_spec, (row_count, width), BF16),
        (any_spec, (row_count, width), F32),
        (vmem_spec, (row_count, 1), F32),
        (any_spec, (row_count, width), F32),
        (vmem_spec, totals, F32),
        (vmem_spec, (VROWS, width), F32),
        (vmem_spec, (1, fo.shape[0] * n_fsdp), F32),
    ]
    return pl.pallas_call(
        functools.partial(encode_body, depth),
        in_specs=[smem_spec] * 2 + [vmem_spec] * 7 + [any_spec] * 7,
        out_specs=[spec for spec, _, _ in outs],
        out_shape=[shape(extent, kind) for _, extent, kind in outs],
        scratch_shapes=[
            vmem((depth, 2, 2, VROWS, VLANES), BF16),
            vmem((UNITS, rows, width), BF16),
            vmem((VROWS, VLANES), F32),
            vmem((VROWS, VLANES), BF16),
            vmem((8, width, width), BF16),
            vmem((row_count, width), BF16),
            vmem((2, row_count, width), BF16),
            vmem((2, row_count, width), BF16),
            vmem((row_count, width), BF16),
            vmem((2, encoder_count, width), BF16),
            vmem((2, encoder_count, width), BF16),
            vmem((row_count, width), F32),
            vmem((row_count, width), F32),
            vmem((row_count, width), BF16),
            vmem((row_count, width), F32),
            vmem((PAIR, 2 * row_count), BF16),
            vmem((PAIR, 2 * encoder_count), BF16),
            dma((UNITS,)),
            dma((steps,)),
            dma((8,)),
            dma((12,)),
            dma((steps, depth - 1)),
            dma((steps, depth - 1)),
            dma((steps,)),
            dma((steps,)),
            dma((steps, 2)),
            dma((steps, 2)),
            dma((steps, 4)),
            dma((steps, 4)),
            dma((4,)),
            dma((4,)),
        ],
        compiler_params=pltpu.CompilerParams(
            collective_id=2, has_side_effects=True, vmem_limit_bytes=VMEM_LIMIT
        ),
        name="encode",
    )(
        block_order, length, states, encoder, b_self, b_cross, gains, shifts, singles, sp, so, cq, ckv, co,
        fi, fo,
    )


def pair_backward(
    causal, p, q, g, o, totals, k_all, v_all, keys_t, dk, dv, dq, kept, sent, sums, sum_row,
    own_places, places, length,
):
    lanes = pl.ds(pl.multiple_of(p * PAIR, PAIR), PAIR)
    parts, part_rows = k_all.shape[0], k_all.shape[1]
    for h in range(parts):
        for block in range(part_rows // QBLK):
            rows = slice(block * QBLK, (block + 1) * QBLK)
            at = h * part_rows + block * QBLK
            keys_t[:, at : at + QBLK] = k_all[h, rows, lanes].astype(F32).T.astype(BF16)
    dk[...] = jnp.zeros_like(dk)
    dv[...] = jnp.zeros_like(dv)

    def step(i, carry):
        rows = pl.ds(pl.multiple_of(i * QBLK, QBLK), QBLK)
        both = stack_heads(q[rows, lanes])
        grads = g[rows, lanes]
        both_grads = stack_heads(grads)
        products = (grads.astype(F32) * o[rows, lanes]).T
        delta = jnp.concatenate(
            [
                jnp.sum(products[:HD], axis=0, keepdims=True),
                jnp.sum(products[HD:], axis=0, keepdims=True),
            ],
            axis=1,
        )
        if causal:
            limit = row_limit(own_places[i], length)
        level = totals[p, pl.ds(i, 1), :]
        query_grad = 0.0
        for h in range(parts):
            span = slice(h * part_rows, (h + 1) * part_rows)
            scores = dot_nt(k_all[h, :, lanes], both)
            if causal:
                scores = mask_part(scores, limit, places, h * (part_rows // QBLK))
            prob = jnp.exp(scores - level)
            prob_grad = dot_nt(v_all[h, :, lanes], both_grads)
            score_grad = (prob * (prob_grad - delta)).astype(BF16)
            dv[span, :] += dot_nn(prob.astype(BF16), both_grads)
            dk[span, :] += dot_nn(score_grad, both)
            query_grad += dot_nn(keys_t[:, span], score_grad)
        query_grad = unstack_heads(query_grad, QBLK) * ATTN_SCALE
        dq[rows, lanes] = query_grad.astype(BF16)
        return carry + jnp.sum(query_grad, axis=0, keepdims=True)

    sums[sum_row : sum_row + 1, lanes] = lax.fori_loop(
        0, q.shape[0] // QBLK, step, jnp.zeros((1, PAIR), F32)
    )
    for at, grad in enumerate((dk, dv)):
        kept[at, :, lanes] = grad[:part_rows, :].astype(BF16)
        sent[at, :, lanes] = grad[part_rows:, :].astype(BF16)


def select_lanes(offset, first, limit, lanes):
    lane = lax.broadcasted_iota(jnp.int32, (WINDOW, lanes), 1) + first
    column = lax.broadcasted_iota(jnp.int32, (WINDOW, lanes), 0)
    return ((column == lane + offset) & (lane < limit)).astype(F32).astype(BF16)


def decode_body(
    depth, block_order, length_ref, flat, scale_ref, ctotal, total, feed_sums, inner_sum,
    units, cq_in, ck_in, cv_in, co_in, gmix_in, low_in, encoder_in, hat_in, grad_in, q_in, k_in, v_in,
    o_in, states_in, d1, d2,
    gs_out, ge_out, out, out_v,
    own, from_partner, from_second, from_first, from_up, w, q, g, o, k, v, dq, kept, sent, arrived,
    inputs, enc, hat, grad, dk, dv, keys_t, sums,
    gv, from_partner_v, from_second_v, from_first_v, from_up_v,
    load_sem, own_sem, store_sem, zs, zr, fs, fr, ss, sr, ps, pr, xs, xr, ks, kr,
):
    core, odd, z, y, x = coordinates()
    ups, first, second, partner = peers_of(core, odd, z, y, x, depth)
    rows, width = units.shape[-2:]
    row_count = q.shape[0]
    length = length_ref[0]
    own_places = places = Places(block_order, row_count // QBLK)
    order = ((0, 1), (1, 1), (1, 0), (0, 0))
    pairs = width // PAIR
    chunks = [pl.ds(c * CHUNK, CHUNK) for c in range(row_count // CHUNK)]
    column_sum = lambda array: jnp.sum(array, axis=0, keepdims=True)


    half = (pairs // 2) * PAIR
    spans = (pl.ds(0, half), pl.ds(half, width - half))

    def base(i):
        return i - VECTORS - 1 if i > VECTORS else i

    def part(i, ref):
        return ref.at[:, :, spans[i > VECTORS]] if base(i) < 2 else ref

    def pick(i, main, small, at=None):
        ref = small if i == VECTORS else main.at[base(i)]
        return part(i, ref if at is None else ref.at[at])

    def kept_set(i, a, b):
        yy, xx = flip(odd, y, x, a, b)
        return gv.at[odd, :, yy, xx] if i == VECTORS else part(i, own.at[base(i), :, yy, xx])

    def sent_set(i, a, b):
        yy, xx = flip(1 - odd, y, x, a, b)
        u = 2 * i + 1 - odd
        if i == VECTORS:
            return gv.at[1 - odd, :, yy, xx]
        if i > VECTORS or i < 4:
            return part(i, own.at[HALF + base(i), :, yy, xx])
        if 2 * i >= FIRST:
            return d2.at[:, yy, xx, u - FIRST]
        return d1.at[u - 7, :, yy, xx]

    def own_copy(i):
        u = 2 * i + odd
        source = d2.at[:, :, :, u - FIRST] if 2 * i >= FIRST else d1.at[u - 7]
        return pltpu.make_async_copy(source, own.at[i], own_sem.at[i])

    def partner_copy(i, a, b):
        at = a + 2 * b
        return remote(
            sent_set(i, a, b),
            pick(i, from_partner, from_partner_v, at),
            ps.at[i, at],
            pr.at[i, at],
            partner,
        )

    def second_copy(i, a):
        target = pick(i, from_second, from_second_v, a)
        return remote(kept_set(i, a, 1), target, ss.at[i, a], sr.at[i, a], second)

    def first_copy(i):
        target = pick(i, from_first, from_first_v)
        return remote(kept_set(i, 1, 0), target, fs.at[i], fr.at[i], first)

    def up_copy(i, n):
        source = kept_set(i, 0, 0).at[(z + 1 + n) % depth]
        target = pick(i, from_up, from_up_v).at[n]
        return remote(source, target, zs.at[i, n], zr.at[i, n], ups[n])

    def result(i, parity):
        if i == VECTORS:
            return out_v.at[parity]
        target = out.at[2 * base(i) + parity]
        return target.at[:, spans[i > VECTORS]] if base(i) < 2 else target

    def final_copy(i, parity):
        target = result(i, parity)
        return remote(target, target, xs.at[i], xr.at[i], partner)

    def add(target, addend):
        def step(j, carry):
            target[j] = target[j] + addend[j]
            return carry

        lax.fori_loop(0, depth, step, 0)

    def send(i):
        for a, b in order:
            partner_copy(i, a, b).start()

    def stage_1(i):
        if HALF > i >= 4:
            own_copy(i).wait()
        for a, b in order:
            partner_copy(i, a, b).wait_recv()
            add(kept_set(i, a, b), pick(i, from_partner, from_partner_v, a + 2 * b))
            if b:
                second_copy(i, a).start()

    def stage_2(i):
        for a in (1, 0):
            second_copy(i, a).wait_recv()
            add(kept_set(i, a, 0), pick(i, from_second, from_second_v, a))
            if a:
                first_copy(i).start()

    def stage_3(i):
        first_copy(i).wait_recv()
        add(kept_set(i, 0, 0), pick(i, from_first, from_first_v))
        for n in range(depth - 1):
            up_copy(i, n).start()

    def stage_4(i):
        value = kept_set(i, 0, 0)[z].astype(F32)
        for n in range(depth - 1):
            up_copy(i, n).wait_recv()
            value = value + pick(i, from_up, from_up_v)[n].astype(F32)
        result(i, odd)[...] = value
        final_copy(i, odd).start()

    def put_unit(u, value, span=slice(None)):
        at = u // 2 + HALF * ((u + odd) % 2)
        own[at, :, :, :, :, span] = value.astype(BF16).reshape(depth, 2, 2, rows, -1)


    loads = []

    def load(source, target):
        copy = pltpu.make_async_copy(source, target, load_sem.at[len(loads)])
        copy.start()
        loads.append(copy)
        return copy

    def weight(u, at):
        return load(units.at[u].reshape(width, width), w.at[at])

    attention_loads = [load(*pair) for pair in ((cq_in, q), (ck_in, k), (cv_in, v), (gmix_in, g), (co_in, o))]
    for i in range(HALF - 1, 3, -1):
        own_copy(i).start()
    cross_loads = [load(low_in, inputs), weight(4, 0), load(grad_in, grad), load(hat_in, hat), weight(3, 1)]
    encoder_loads = [load(encoder_in, enc), weight(5, 2), weight(6, 3)]
    output_load = load(d1.at[0], own.at[3 + HALF * ((7 + odd) % 2)])
    enter(ups, first, second, partner)
    for i in range(HALF - 1, 3, -1):
        send(i)

    sums[...] = jnp.zeros_like(sums)
    for at, row in enumerate((5, 6, 8, 9, 11, 12)):
        sums[row : row + 1, :] = feed_sums[at : at + 1, :]
    for copy in attention_loads:
        copy.wait()

    def cross_step(p, carry):
        pair_backward(
            False, p, q, g, o, ctotal, k, v, keys_t, dk, dv, dq, kept, sent, sums, 3, None, None, None
        )

        @pl.when(p == 0)
        def _():
            stage_1(7)

        @pl.when(p == 1)
        def _():
            stage_1(6)

        @pl.when(p == 2)
        def _():
            stage_2(7)
            stage_1(5)

        @pl.when(p == 4)
        def _():
            stage_2(6)
            stage_1(4)

        @pl.when(p == 5)
        def _():
            stage_3(7)

        return carry

    lax.fori_loop(0, pairs, cross_step, 0)
    cross_share = remote(sent, arrived.at[0], ks.at[0], kr.at[0], partner)
    cross_share.start()
    self_loads = [load(*pair) for pair in ((o_in, o), (q_in, q), (k_in, k), (v_in, v))]
    for copy in cross_loads:
        copy.wait()
    put_unit(4, dot_tn(inputs[...], dq[...]))
    states_load = load(states_in, inputs)
    gain_sum = jnp.zeros((1, width), F32)
    shift_sum = jnp.zeros((1, width), F32)
    grad_sum = jnp.zeros((1, width), F32)
    for c in chunks:
        incoming = grad[c, :] + dot_nt(dq[c, :], w[0])
        normed = hat[c, :]
        gain_sum += column_sum(incoming * normed)
        shift_sum += column_sum(incoming)
        value = norm_back(incoming * flat[7:8, :], normed, scale_ref[c, :])
        grad_sum += column_sum(value)
        grad[c, :] = value
        low = value.astype(BF16)
        dq[c, :] = low
        g[c, :] = dot_nt(low, w[1]).astype(BF16)
    sums[2:3, :] = grad_sum
    sums[7:8, :] = gain_sum
    sums[10:11, :] = shift_sum
    stage_2(5)
    stage_3(6)
    last_loads = [weight(2, 0)]
    self_loads[0].wait()
    put_unit(3, dot_tn(o[...].astype(BF16), dq[...]))
    last_loads.append(weight(0, 1))

    def total_kept(number, c, span=slice(None)):
        low = []
        for at in range(2):
            value = kept[at, c, span].astype(F32) + arrived[number, at, c, span].astype(F32)
            kept[at, c, span] = value.astype(BF16)
            low.append(value)
        return column_sum(low[1])

    for copy in encoder_loads:
        copy.wait()
    cross_share.wait_recv()
    sums[4:5, :] = sum(total_kept(0, c) for c in chunks)
    put_unit(5, dot_tn(enc[...], kept[0]))
    send(2)
    put_unit(6, dot_tn(enc[...], kept[1]))
    output_load.wait()
    send(3)
    for c in chunks:
        hat[c, :] = dot_nt(kept[0, c, :], w[2]) + dot_nt(kept[1, c, :], w[3])
    encoder_store = pltpu.make_async_copy(hat, ge_out, store_sem.at[0])
    encoder_store.start()
    stage_1(3)
    stage_4(7)
    last_loads.append(weight(1, 2))
    stage_1(2)
    stage_2(4)
    cross_share.wait_send()
    for copy in self_loads[1:]:
        copy.wait()

    def self_share(n):
        source, target = sent.at[:, :, spans[n]], arrived.at[1, :, :, spans[n]]
        return remote(source, target, ks.at[1 + n], kr.at[1 + n], partner)

    def self_units(n):
        span = spans[n]
        self_share(n).wait_recv()
        sums[1:2, span] = sum(total_kept(1, c, span) for c in chunks)
        put_unit(1, dot_tn(inputs[...], kept[0, :, span]), span)
        send(0 if n == 0 else VECTORS + 1)
        put_unit(2, dot_tn(inputs[...], kept[1, :, span]), span)
        send(1 if n == 0 else VECTORS + 2)

    def self_step(p, carry):
        pair_backward(
            True, p, q, g, o, total, k, v, keys_t, dk, dv, dq, kept, sent, sums, 0, own_places, places,
            length,
        )

        @pl.when(p == 0)
        def _():
            stage_3(5)
            stage_4(6)

        @pl.when(p == 1)
        def _():
            stage_4(5)

        @pl.when(p == pairs // 2 - 1)
        def _():
            self_share(0).start()
            put_unit(0, dot_tn(inputs[...], dq[:, spans[0]]), spans[0])
            stage_2(3)

        @pl.when(p == 3)
        def _():
            self_units(0)
            stage_2(2)
            stage_3(4)

        @pl.when(p == 4)
        def _():
            stage_1(0)
            stage_1(1)

        @pl.when(p == 5)
        def _():
            stage_3(3)
            stage_4(4)

        return carry

    states_load.wait()
    lax.fori_loop(0, pairs, self_step, 0)
    self_share(1).start()
    put_unit(0, dot_tn(inputs[...], dq[:, spans[1]]), spans[1])
    stage_3(2)
    self_units(1)
    pack_sums(depth, rows, sums, inner_sum, gv)
    send(VECTORS)
    stage_2(0)
    stage_2(1)
    stage_4(3)
    for copy in last_loads:
        copy.wait()
    stage_1(VECTORS + 1)
    stage_1(VECTORS + 2)
    stage_1(VECTORS)
    for c in chunks:
        value = grad[c, :] + dot_nt(kept[0, c, :], w[1]) + dot_nt(kept[1, c, :], w[2])
        grad[c, :] = value + dot_nt(dq[c, :], w[0])
    states_store = pltpu.make_async_copy(grad, gs_out, store_sem.at[1])
    states_store.start()
    stage_3(0)
    stage_4(2)
    stage_3(1)
    stage_2(VECTORS + 1)
    stage_2(VECTORS + 2)
    stage_2(VECTORS)
    stage_4(0)
    stage_4(1)
    stage_3(VECTORS + 1)
    stage_3(VECTORS + 2)
    stage_3(VECTORS)
    stage_4(VECTORS + 1)
    stage_4(VECTORS + 2)
    stage_4(VECTORS)
    encoder_store.wait()
    states_store.wait()
    for n in range(2):
        self_share(n).wait_send()
    for i in range(HALF + 3):
        final_copy(i, 1 - odd).wait_recv()
        final_copy(i, odd).wait_send()
        for a, b in order:
            partner_copy(i, a, b).wait_send()
        for a in range(2):
            second_copy(i, a).wait_send()
        first_copy(i).wait_send()
        for n in range(depth - 1):
            up_copy(i, n).wait_send()


def pack_sums(depth, rows, sums, inner_sum, gv):
    lanes = gv.shape[-1]
    width = sums.shape[1]
    low = sums[...].astype(BF16)
    row = lax.broadcasted_iota(jnp.int32, (VROWS, lanes), 0)
    window_row = lax.broadcasted_iota(jnp.int32, (VROWS, WINDOW), 0)
    inner_low = jnp.zeros((VROWS, WINDOW), F32)
    for at in range(inner_sum.shape[1] // WINDOW):
        piece = inner_sum[:, at * WINDOW : (at + 1) * WINDOW]
        inner_low = jnp.where(window_row == at, piece, inner_low)
    inner_low = inner_low.astype(BF16)
    windows = jnp.concatenate([low[:, i : i + WINDOW] for i in range(0, width, WINDOW)], axis=0)
    count, inner_rows = WINDOW // rows, inner_sum.shape[1] // (4 * depth)
    inner_count = WINDOW // inner_rows
    inner = [
        [
            dot_nn(inner_low, select_lanes(n * inner_rows, part * lanes, inner_rows, lanes))
            for part in range(2)
        ]
        for n in range(inner_count)
    ]
    for n in range(count):
        picked = dot_nn(windows, select_lanes(n * rows, 0, rows, lanes))
        for at in range(width // WINDOW):
            f = at * count + n
            for part in range(2):
                own = picked[at * VROWS : (at + 1) * VROWS] if part == 0 else jnp.zeros_like(row, F32)
                at_inner = f // inner_count
                other = inner[f % inner_count][part][at_inner : at_inner + 1, :]
                gv[part, f // 4, (f // 2) % 2, f % 2] = jnp.where(row == 13, other, own).astype(BF16)


def decode(
    n_fsdp, block_order, length, flat, scale, ctotal, total, feed_sums, inner_sum, units, cq, ck,
    cv, co, gmix, low, encoder, hat, grad, q, k, v, o, states, d1, d2,
):
    rows, width = units.shape[-2:]
    depth = n_fsdp // 4
    row_count = states.shape[0]
    steps = HALF + 3
    dma = pltpu.SemaphoreType.DMA
    vmem = pltpu.VMEM
    any_spec = pl.BlockSpec(memory_space=pl.ANY)
    vmem_spec = pl.BlockSpec(memory_space=pltpu.VMEM)
    smem_spec = pl.BlockSpec(memory_space=pltpu.SMEM)
    block, small = (rows, width), (VROWS, LANES)
    narrow = vmem((row_count, width), BF16)
    wide = vmem((row_count, width), F32)
    both = vmem((2, row_count, width), BF16)
    return pl.pallas_call(
        functools.partial(decode_body, depth),
        in_specs=[smem_spec] * 2 + [vmem_spec] * 6 + [any_spec] * 17,
        out_specs=[any_spec] * 2 + [vmem_spec] * 2,
        out_shape=[
            jax.ShapeDtypeStruct((row_count, width), F32),
            jax.ShapeDtypeStruct((row_count, width), F32),
            jax.ShapeDtypeStruct((UNITS, *block), F32),
            jax.ShapeDtypeStruct((2, *small), F32),
        ],
        scratch_shapes=[
            vmem((HALF + 4, depth, 2, 2, *block), BF16),
            vmem((HALF, 4, depth, *block), BF16),
            vmem((HALF, 2, depth, *block), BF16),
            vmem((HALF, depth, *block), BF16),
            vmem((HALF, depth - 1, *block), BF16),
            vmem((4, width, width), BF16),
            narrow, narrow, wide, both, both, narrow, both, both,
            vmem((2, 2, row_count, width), BF16),
            narrow, narrow, wide, wide,
            vmem((2 * row_count, PAIR), F32),
            vmem((2 * row_count, PAIR), F32),
            vmem((PAIR, 2 * row_count), BF16),
            vmem((VROWS, width), F32),
            vmem((2, depth, 2, 2, *small), BF16),
            vmem((4, depth, *small), BF16),
            vmem((2, depth, *small), BF16),
            vmem((depth, *small), BF16),
            vmem((depth - 1, *small), BF16),
            dma((24,)),
            dma((HALF,)),
            dma((2,)),
            dma((steps, depth - 1)),
            dma((steps, depth - 1)),
            dma((steps,)),
            dma((steps,)),
            dma((steps, 2)),
            dma((steps, 2)),
            dma((steps, 4)),
            dma((steps, 4)),
            dma((steps,)),
            dma((steps,)),
            dma((3,)),
            dma((3,)),
        ],
        compiler_params=pltpu.CompilerParams(
            collective_id=3, has_side_effects=True, vmem_limit_bytes=DECODE_LIMIT
        ),
        name="decode",
    )(
        block_order, length, flat, scale, ctotal, total, feed_sums, inner_sum, units, cq, ck, cv,
        co, gmix, low, encoder, hat, grad, q, k, v, o, states,
        d1.reshape(-1, depth, 2, 2, *block),
        d2.reshape(depth, 2, 2, UNITS - FIRST, *block),
    )


GROUPS = ((0, 1, 2), (3,), (4,), (5, 6), (7,), (8, 9, 10, 11))


VECTOR_GROUPS = ((0, 2), (2, 3), (3, 5), (5, 6), (6, 7), (7, 10), (10, 13))


def lay_out_body(shards, vectors, *outs):
    rows, width = shards.shape[1:]
    for group, target in zip(GROUPS, outs):
        for at, u in enumerate(group):
            target[:, at * width : (at + 1) * width] = shards[u]
    outer = outs[len(GROUPS)]
    for at in range(UNITS - FIRST):
        outer[at * rows : (at + 1) * rows, :] = shards[FIRST + at]
    inner = outs[-1]
    inner[:, :LANES] = vectors[0, 13:14, :]
    inner[:, LANES:] = vectors[1, 13:14, : inner.shape[1] - LANES]
    for (low, high), target in zip(VECTOR_GROUPS, outs[len(GROUPS) + 1 :]):
        target[...] = vectors[0, low:high, :rows]


def lay_out(shards, vectors, inner):
    rows, width = shards.shape[1:]
    shapes = [(rows, width * len(group)) for group in GROUPS] + [((UNITS - FIRST) * rows, width)]
    shapes += [(high - low, rows) for low, high in VECTOR_GROUPS] + [(1, inner)]
    return pl.pallas_call(
        lay_out_body,
        in_specs=[pl.BlockSpec(memory_space=pltpu.VMEM)] * 2,
        out_specs=[pl.BlockSpec(memory_space=pltpu.VMEM)] * len(shapes),
        out_shape=[jax.ShapeDtypeStruct(shape, F32) for shape in shapes],
        name="lay_out",
    )(shards, vectors)


def per_device_wide(
    n_ctx,
    n_fsdp,
    states,
    encoded,
    lengths,
    block_order,
    cotangent,
    self_project,
    self_bias,
    self_output,
    self_shift,
    cross_query,
    cross_keyval,
    cross_bias,
    cross_output,
    cross_shift,
    feed_inner,
    inner_bias,
    feed_outer,
    outer_bias,
    norm_gain,
    norm_shift,
):
    local_rows = states.shape[1]
    width = states.shape[2]
    rows = self_output.shape[0]
    local_blocks = local_rows // QBLK
    core = lax.axis_index("ctx")
    own_order = lax.dynamic_slice_in_dim(block_order, core * local_blocks, local_blocks)
    places = block_order
    spread = lambda array: (lax.all_gather(array, "ctx", axis=0, tiled=True),)
    collect = lambda parts: lax.psum_scatter(
        parts[0], "ctx", scatter_dimension=0, tiled=True
    ).astype(F32)

    vectors = jnp.concatenate(
        [
            self_bias,
            self_shift[None],
            cross_bias,
            cross_shift[None],
            outer_bias[None],
            norm_gain,
            norm_shift,
            inner_bias.reshape(-1, rows),
        ],
        axis=0,
    )
    inner_rows = inner_bias.shape[0] // rows
    count = vectors.shape[0]
    pad = ((0, 2 * VROWS - count), (0, LANES - rows))
    units, w_fo, all_vectors = gather_weights(
        n_fsdp, jnp.pad(vectors, pad).reshape(2, VROWS, LANES), self_project, self_output, cross_query,
        cross_keyval, cross_output, feed_inner, feed_outer,
    )
    all_vectors = jnp.transpose(all_vectors, (1, 0, 2, 3)).reshape(n_fsdp, 2 * VROWS, LANES)
    all_vectors = all_vectors[:, :count, :rows].astype(F32)
    inner_full = all_vectors[:, 13:].reshape(1, -1)
    flat = jnp.transpose(all_vectors, (1, 0, 2)).reshape(count, -1)
    b_q, b_v, b_so, b_cq, b_cv = (flat[i] for i in range(5))

    w_q, w_k, w_v, w_so, w_cq, w_ck, w_cv, w_co = (units[i] for i in range(8))

    inputs = states[0]
    encoder_rows = encoded[0]
    queries = ((dot_nn(inputs, w_q) + b_q) * ATTN_SCALE).astype(BF16)
    own_keys = dot_nn(inputs, w_k).astype(BF16)
    own_values = (dot_nn(inputs, w_v) + b_v).astype(BF16)
    own_cross_keys = dot_nn(encoder_rows, w_ck).astype(BF16)
    own_cross_values = (dot_nn(encoder_rows, w_cv) + b_cv).astype(BF16)
    keys, values = spread(own_keys), spread(own_values)
    cross_keys, cross_values = spread(own_cross_keys), spread(own_cross_values)

    attend = functools.partial(attention_forward, places=places, own_places=own_order, length=lengths)
    self_attended, self_total = attend(True, queries, keys, values)
    self_mixed = self_attended.astype(BF16)
    after_self, norm_back_one = jax.vjp(
        layer_norm, inputs.astype(F32) + dot_nn(self_mixed, w_so) + b_so, flat[7], flat[10]
    )
    after_self_low = after_self.astype(BF16)
    cross_queries = ((dot_nn(after_self_low, w_cq) + b_cq) * ATTN_SCALE).astype(BF16)
    cross_attended, cross_total = attend(False, cross_queries, cross_keys, cross_values)
    output, grad_cross_mixed, grad_two, feed_sums, inner_sum, d_low, d_outer = feed_forward(
        block_order, lengths, cross_attended, after_self, cotangent[0], flat[:16], inner_full, units, w_fo
    )
    attend_back = functools.partial(
        attention_backward, places=places, own_places=own_order, length=lengths
    )
    cross_query_grad, ck_parts, cv_parts = attend_back(
        False, cross_queries, grad_cross_mixed, cross_attended, cross_total, cross_keys, cross_values
    )
    cross_query_low = cross_query_grad.astype(BF16)
    d_cq = dot_tn(after_self_low, cross_query_low).astype(BF16)
    ck_grad, cv_grad = collect(ck_parts), collect(cv_parts)
    ck_low, cv_low = ck_grad.astype(BF16), cv_grad.astype(BF16)
    d_ck = dot_tn(encoder_rows, ck_low).astype(BF16)
    d_cv = dot_tn(encoder_rows, cv_low).astype(BF16)
    grad_encoded = dot_nt(ck_low, w_ck) + dot_nt(cv_low, w_cv)
    grad_one, gain_one, shift_one = norm_back_one(grad_two + dot_nt(cross_query_low, w_cq))
    grad_one_low = grad_one.astype(BF16)
    d_so = dot_tn(self_mixed, grad_one_low).astype(BF16)
    grad_self_mixed = dot_nt(grad_one_low, w_so).astype(BF16)
    query_grad, k_parts, v_parts = attend_back(
        True, queries, grad_self_mixed, self_attended, self_total, keys, values
    )
    query_low = query_grad.astype(BF16)
    key_grad, value_grad = collect(k_parts), collect(v_parts)
    key_low, value_low = key_grad.astype(BF16), value_grad.astype(BF16)
    d_q = dot_tn(inputs, query_low).astype(BF16)
    d_k = dot_tn(inputs, key_low).astype(BF16)
    d_v = dot_tn(inputs, value_low).astype(BF16)
    grad_states = grad_one + dot_nt(query_low, w_q) + dot_nt(key_low, w_k) + dot_nt(value_low, w_v)

    column_sum = lambda array: jnp.sum(array, axis=0)
    grad_vectors = jnp.stack(
        [
            column_sum(query_grad),
            column_sum(value_grad),
            column_sum(grad_one),
            column_sum(cross_query_grad),
            column_sum(cv_grad),
            feed_sums[0],
            feed_sums[1],
            gain_one,
            feed_sums[2],
            feed_sums[3],
            shift_one,
            feed_sums[4],
            feed_sums[5],
        ]
    ).reshape(13, n_fsdp, rows)
    inner_vector = inner_sum.reshape(n_fsdp, inner_rows, rows)
    packed = jnp.concatenate([jnp.transpose(grad_vectors, (1, 0, 2)), inner_vector], axis=1)
    packed = jnp.pad(packed, ((0, 0), *pad)).astype(BF16)
    packed = jnp.transpose(packed.reshape(n_fsdp, 2, VROWS, LANES), (1, 0, 2, 3))

    shards, mine = scatter_gradients(
        n_fsdp, [d_q, d_k, d_v, d_so, d_cq, d_ck, d_cv], d_low, d_outer, packed
    )
    if n_ctx > 2:
        groups = [[c for c in range(n_ctx) if c % 2 == odd] for odd in range(2)]
        total = lambda part: lax.psum(part.astype(BF16), "ctx", axis_index_groups=groups).astype(F32)
        shards, mine = total(shards), total(mine)
    mine = mine.reshape(2 * VROWS, LANES)[:, :rows]
    return (
        output[None],
        grad_states[None],
        grad_encoded[None],
        jnp.concatenate([shards[0], shards[1], shards[2]], axis=1),
        mine[0:2],
        shards[3],
        mine[2],
        shards[4],
        jnp.concatenate([shards[5], shards[6]], axis=1),
        mine[3:5],
        shards[7],
        mine[5],
        jnp.concatenate([shards[8 + i] for i in range(4)], axis=1),
        mine[13 : 13 + inner_rows].reshape(-1),
        shards[12:].reshape(-1, width),
        mine[6],
        mine[7:10],
        mine[10:13],
    )


def per_device(
    n_ctx,
    n_fsdp,
    states,
    encoded,
    lengths,
    block_order,
    cotangent,
    self_project,
    self_bias,
    self_output,
    self_shift,
    cross_query,
    cross_keyval,
    cross_bias,
    cross_output,
    cross_shift,
    feed_inner,
    inner_bias,
    feed_outer,
    outer_bias,
    norm_gain,
    norm_shift,
):
    width = states.shape[2]
    inner = inner_bias.shape[0]
    singles = jnp.stack(
        [jnp.pad(v, (0, inner - v.shape[0])) for v in (self_shift, cross_shift, outer_bias, inner_bias)]
    )
    (
        units, w_fo, queries, keys, values, cross_queries, cross_keys, cross_values, self_attended,
        self_total, after_self, after_self_low, hat, scale, cross_attended, cross_total, flat, inner_full,
    ) = encode(
        n_fsdp, block_order, lengths, states[0], encoded[0], self_bias, cross_bias, norm_gain, norm_shift,
        singles, self_project, self_output, cross_query, cross_keyval, cross_output, feed_inner, feed_outer,
    )
    output, grad_cross_mixed, grad_two, feed_sums, inner_sum, d_low, d_outer = feed_forward(
        block_order, lengths, cross_attended, after_self, cotangent[0], flat, inner_full,
        units.reshape(FIRST, width, width), w_fo.reshape(-1, width),
    )
    grad_states, grad_encoded, shards, mine = decode(
        n_fsdp, block_order, lengths, flat, scale, cross_total, self_total, feed_sums, inner_sum,
        units, cross_queries, cross_keys, cross_values, cross_attended, grad_cross_mixed, after_self_low,
        encoded[0], hat, grad_two, queries, keys, values, self_attended, states[0], d_low, d_outer,
    )
    (
        d_sp, d_so, d_cq, d_ckv, d_co, d_fi, d_fo, d_self_bias, d_self_shift, d_cross_bias, d_cross_shift,
        d_outer_bias, d_gain, d_shift, d_inner_bias,
    ) = lay_out(shards, mine, inner)
    return (
        output[None],
        grad_states[None],
        grad_encoded[None],
        d_sp,
        d_self_bias,
        d_so,
        d_self_shift.reshape(-1),
        d_cq,
        d_ckv,
        d_cross_bias,
        d_co,
        d_cross_shift.reshape(-1),
        d_fi,
        d_inner_bias.reshape(-1),
        d_fo,
        d_outer_bias.reshape(-1),
        d_gain,
        d_shift,
    )


def solution(mesh):
    return jax.shard_map(
        functools.partial(
            per_device if mesh.shape["ctx"] == 2 else per_device_wide,
            mesh.shape["ctx"],
            mesh.shape["fsdp"],
        ),
        mesh=mesh,
        in_specs=(
            P("fsdp", "ctx", None),
            P("fsdp", "ctx", None),
            P("fsdp"),
            P(),
            P("fsdp", "ctx", None),
            P("fsdp", None),
            P(None, "fsdp"),
            P("fsdp", None),
            P("fsdp"),
            P("fsdp", None),
            P("fsdp", None),
            P(None, "fsdp"),
            P("fsdp", None),
            P("fsdp"),
            P("fsdp", None),
            P("fsdp"),
            P("fsdp", None),
            P("fsdp"),
            P(None, "fsdp"),
            P(None, "fsdp"),
        ),
        out_specs=(
            P("fsdp", "ctx", None),
            P("fsdp", "ctx", None),
            P("fsdp", "ctx", None),
            P("fsdp", None),
            P(None, "fsdp"),
            P("fsdp", None),
            P("fsdp"),
            P("fsdp", None),
            P("fsdp", None),
            P(None, "fsdp"),
            P("fsdp", None),
            P("fsdp"),
            P("fsdp", None),
            P("fsdp"),
            P("fsdp", None),
            P("fsdp"),
            P(None, "fsdp"),
            P(None, "fsdp"),
        ),
        check_vma=False,
    )
```

```python
import functools

import jax
import jax.numpy as jnp
from jax import lax
from jax.experimental import pallas as pl
from jax.experimental.pallas import tpu as pltpu
from jax.sharding import PartitionSpec as P

H = 12
HD = 64
QBLK = 128
PAIR = 2 * HD
ATTN_SCALE = 0.125
MASKED_SCORE = -1e30
EPSILON = 1e-05
MESH = pl.DeviceIdType.MESH
VMEM_LIMIT = 60 * 1024 * 1024
DECODE_LIMIT = 67043328
BF16 = jnp.bfloat16
F32 = jnp.float32


def dot_nn(left, right):
    return lax.dot_general(left, right, (((1,), (0,)), ((), ())), preferred_element_type=F32)


def dot_nt(left, right):
    return lax.dot_general(left, right, (((1,), (1,)), ((), ())), preferred_element_type=F32)


def dot_tn(left, right):
    return lax.dot_general(left, right, (((0,), (0,)), ((), ())), preferred_element_type=F32)


def layer_norm(inputs, scale_vec, shift_vec):
    average = jnp.mean(inputs, axis=-1, keepdims=True)
    centred = inputs - average
    variance = jnp.mean(centred * centred, axis=-1, keepdims=True)
    return centred * lax.rsqrt(variance + EPSILON) * scale_vec + shift_vec


class Places:
    def __init__(self, block_order, own_count):
        self.block_order = block_order
        self.start = lax.axis_index("ctx") * own_count

    def __getitem__(self, i):
        return self.block_order[lax.rem(self.start + i, self.block_order.shape[0])]


def gelu_exact(inputs):
    return jax.nn.gelu(inputs, approximate=False)


def stack_heads(rows):
    first = lax.broadcasted_iota(jnp.int32, rows.shape, 1) < HD
    zero = jnp.zeros_like(rows)
    return jnp.concatenate([jnp.where(first, rows, zero), jnp.where(first, zero, rows)], axis=0)


def unstack_heads(both, count):
    return jnp.concatenate([both[:HD, :count], both[HD:, count:]], axis=0).T


def variants_of(key_count, causal):
    if not causal:
        return [key_count]
    step = max(2 * QBLK, key_count // 4)
    return [step * (i + 1) for i in range(key_count // step)]


def load_keys(causal, places, sources, target):
    block = 0
    for source in sources:
        for local in range(source.shape[0] // QBLK):
            rows = source[local * QBLK : (local + 1) * QBLK, :]
            if causal:
                at = pl.multiple_of(places[block] * QBLK, QBLK)
                target[pl.ds(at, QBLK), :] = rows
            else:
                target[block * QBLK : (block + 1) * QBLK, :] = rows
            block += 1


def masked_scores(causal, keys, both, place, length, count):
    scores = dot_nt(keys, both)
    if causal:
        column = lax.broadcasted_iota(jnp.int32, (1, 2 * count), 1)
        row_place = place * QBLK + jnp.where(column >= count, column - count, column)
        limit = jnp.minimum(row_place, length - 1)
        key_place = lax.broadcasted_iota(jnp.int32, scores.shape, 0)
        scores = jnp.where(key_place <= limit, scores, MASKED_SCORE)
    return scores


def for_each_block(causal, sizes, block_count, own_places, length, body):
    def step(i, carry):
        if not causal:
            body(i, 0, sizes[0])
            return carry
        place = own_places[i]
        needed = jnp.minimum((place + 1) * QBLK, length)
        for at, size in enumerate(sizes):
            low = sizes[at - 1] if at else 0

            @pl.when((needed > low) & (needed <= size))
            def _(size=size):
                body(i, place, size)

        return carry

    lax.fori_loop(0, block_count, step, 0)


def forward_body(causal, n_src, places, own_places, length_ref, q_ref, *refs):
    key_refs, value_refs = refs[:n_src], refs[n_src : 2 * n_src]
    out_ref, total_ref, keys, values_t = refs[2 * n_src :]
    load_keys(causal, places, key_refs, keys)
    length = length_ref[0]
    block = 0
    for source in value_refs:
        for local in range(source.shape[0] // QBLK):
            rows = source[local * QBLK : (local + 1) * QBLK, :].astype(F32).T.astype(BF16)
            at = pl.multiple_of(places[block] * QBLK, QBLK) if causal else block * QBLK
            values_t[:, pl.ds(at, QBLK)] = rows
            block += 1

    def body(i, place, size):
        rows = pl.ds(pl.multiple_of(i * QBLK, QBLK), QBLK)
        both = stack_heads(q_ref[rows, :])
        scores = masked_scores(causal, keys[:size, :], both, place, length, QBLK)
        highest = jnp.max(scores, axis=0, keepdims=True)
        exponent = jnp.exp(scores - highest)
        total = jnp.sum(exponent, axis=0, keepdims=True)
        mixed = dot_nn(values_t[:, :size], exponent.astype(BF16)) * (1.0 / total)
        out_ref[rows, :] = unstack_heads(mixed, QBLK)
        total_ref[0, pl.ds(i, 1), :] = highest + jnp.log(total)

    for_each_block(
        causal,
        variants_of(keys.shape[0], causal),
        q_ref.shape[0] // QBLK,
        own_places,
        length,
        body,
    )


def attention_forward(causal, queries, keys, values, places, own_places, length):
    rows, width = queries.shape
    n_src = len(keys)
    key_count = sum(k.shape[0] for k in keys)
    pairs = width // PAIR
    column = lambda i, *_: (0, i)
    spec = lambda n: pl.BlockSpec((n, PAIR), column)
    return pl.pallas_call(
        functools.partial(forward_body, causal, n_src),
        grid_spec=pltpu.PrefetchScalarGridSpec(
            num_scalar_prefetch=3,
            grid=(pairs,),
            in_specs=[spec(rows)] + [spec(k.shape[0]) for k in (*keys, *values)],
            out_specs=[
                spec(rows),
                pl.BlockSpec((1, rows // QBLK, 2 * QBLK), lambda i, *_: (i, 0, 0)),
            ],
            scratch_shapes=[
                pltpu.VMEM((key_count, PAIR), BF16),
                pltpu.VMEM((PAIR, key_count), BF16),
            ],
        ),
        out_shape=[
            jax.ShapeDtypeStruct((rows, width), F32),
            jax.ShapeDtypeStruct((pairs, rows // QBLK, 2 * QBLK), F32),
        ],
        compiler_params=pltpu.CompilerParams(vmem_limit_bytes=VMEM_LIMIT),
        name="self_forward" if causal else "cross_forward",
    )(places, own_places, length, queries, *keys, *values)


def backward_body(causal, n_src, places, own_places, length_ref, q_ref, g_ref, o_ref, t_ref, *refs):
    key_refs, value_refs = refs[:n_src], refs[n_src : 2 * n_src]
    dq_ref = refs[2 * n_src]
    dk_refs = refs[2 * n_src + 1 : 3 * n_src + 1]
    dv_refs = refs[3 * n_src + 1 : 4 * n_src + 1]
    keys, values, keys_t, dk, dv = refs[4 * n_src + 1 :]
    load_keys(causal, places, key_refs, keys)
    load_keys(causal, places, value_refs, values)
    length = length_ref[0]
    key_count = keys.shape[0]
    for block in range(key_count // QBLK):
        rows = slice(block * QBLK, (block + 1) * QBLK)
        keys_t[:, rows] = keys[rows, :].astype(F32).T.astype(BF16)
    dk[...] = jnp.zeros_like(dk)
    dv[...] = jnp.zeros_like(dv)

    def body(i, place, size):
        rows = pl.ds(pl.multiple_of(i * QBLK, QBLK), QBLK)
        both = stack_heads(q_ref[rows, :])
        grads = g_ref[rows, :]
        both_grads = stack_heads(grads)
        products = (grads.astype(F32) * o_ref[rows, :]).T
        delta = jnp.concatenate(
            [
                jnp.sum(products[:HD], axis=0, keepdims=True),
                jnp.sum(products[HD:], axis=0, keepdims=True),
            ],
            axis=1,
        )
        scores = masked_scores(causal, keys[:size, :], both, place, length, QBLK)
        prob = jnp.exp(scores - t_ref[0, pl.ds(i, 1), :])
        prob_grad = dot_nt(values[:size, :], both_grads)
        score_grad = (prob * (prob_grad - delta)).astype(BF16)
        dv[:size, :] += dot_nn(prob.astype(BF16), both_grads)
        dk[:size, :] += dot_nn(score_grad, both)
        dq = dot_nn(keys_t[:, :size], score_grad)
        dq_ref[rows, :] = unstack_heads(dq, QBLK) * ATTN_SCALE

    for_each_block(
        causal, variants_of(key_count, causal), q_ref.shape[0] // QBLK, own_places, length, body
    )
    block = 0
    for dk_out, dv_out in zip(dk_refs, dv_refs):
        for local in range(dk_out.shape[0] // QBLK):
            at = pl.multiple_of(places[block] * QBLK, QBLK) if causal else block * QBLK
            rows = slice(local * QBLK, (local + 1) * QBLK)
            dk_out[rows, :] = dk[pl.ds(at, QBLK), :].astype(BF16)
            dv_out[rows, :] = dv[pl.ds(at, QBLK), :].astype(BF16)
            block += 1


def attention_backward(
    causal, queries, grads, mixed, totals, keys, values, places, own_places, length
):
    rows, width = queries.shape
    n_src = len(keys)
    key_count = sum(k.shape[0] for k in keys)
    pairs = width // PAIR
    column = lambda i, *_: (0, i)
    spec = lambda n: pl.BlockSpec((n, PAIR), column)
    key_specs = [spec(k.shape[0]) for k in (*keys, *values)]
    outs = pl.pallas_call(
        functools.partial(backward_body, causal, n_src),
        grid_spec=pltpu.PrefetchScalarGridSpec(
            num_scalar_prefetch=3,
            grid=(pairs,),
            in_specs=[
                spec(rows),
                spec(rows),
                spec(rows),
                pl.BlockSpec((1, rows // QBLK, 2 * QBLK), lambda i, *_: (i, 0, 0)),
            ]
            + key_specs,
            out_specs=[spec(rows)] + key_specs,
            scratch_shapes=[
                pltpu.VMEM((key_count, PAIR), BF16),
                pltpu.VMEM((key_count, PAIR), BF16),
                pltpu.VMEM((PAIR, key_count), BF16),
                pltpu.VMEM((key_count, PAIR), F32),
                pltpu.VMEM((key_count, PAIR), F32),
            ],
        ),
        out_shape=[jax.ShapeDtypeStruct((rows, width), F32)]
        + [jax.ShapeDtypeStruct(k.shape, BF16) for k in (*keys, *values)],
        compiler_params=pltpu.CompilerParams(vmem_limit_bytes=VMEM_LIMIT),
        name="self_backward" if causal else "cross_backward",
    )(places, own_places, length, queries, grads, mixed, totals, *keys, *values)
    return outs[0], outs[1 : n_src + 1], outs[n_src + 1 :]


UNITS = 16
FIRST = 12
HALF = UNITS // 2
VECTORS = HALF
VROWS = 16
LANES = 128


def coordinates():
    core, f = lax.axis_index("ctx"), lax.axis_index("fsdp")
    return core, core % 2, f // 4, (f // 2) % 2, f % 2


def flip(odd, y, x, a, b):
    dx = a * (1 - odd) + b * odd
    dy = b * (1 - odd) + a * odd
    return y + dy * (1 - 2 * y), x + dx * (1 - 2 * x)


def peers_of(core, odd, z, y, x, depth):
    fsdp = lambda zz, yy, xx: (zz * 2 + yy) * 2 + xx
    ups = [(core, fsdp((z + k) % depth, y, x)) for k in range(1, depth)]
    first = (core, fsdp(z, *flip(odd, y, x, 1, 0)))
    second = (core, fsdp(z, *flip(odd, y, x, 0, 1)))
    partner = (core + 1 - 2 * odd, fsdp(z, y, x))
    return ups, first, second, partner


def enter(ups, first, second, partner):
    barrier = pltpu.get_barrier_semaphore()
    for peer in (*ups, first, second, partner):
        pl.semaphore_signal(barrier, inc=1, device_id=peer, device_id_type=MESH)
    pl.semaphore_wait(barrier, len(ups) + 3)


def remote(source, target, send, recv, peer):
    return pltpu.make_async_remote_copy(
        source, target, send, recv, device_id=peer, device_id_type=MESH
    )


def unit_set(g1, g2, gv, i, odd, y, x):
    if i == VECTORS:
        return gv.at[odd, :, y, x]
    if 2 * i < FIRST:
        return g1.at[2 * i + odd, :, y, x]
    return g2.at[:, y, x, 2 * i - FIRST + odd]


def unit_block(g1, g2, gv, i, odd, z, y, x):
    if i == VECTORS:
        return gv.at[odd, z, y, x]
    if 2 * i < FIRST:
        return g1.at[2 * i + odd, z, y, x]
    return g2.at[z, y, x, 2 * i - FIRST + odd]


def gather_body(
    depth, vectors, sp, so, cq, ckv, co, fi, fo, g1, g2, gv, own, load_sem, own_sem,
    zs, zr, fs, fr, ss, sr, ps, pr,
):
    core, odd, z, y, x = coordinates()
    ups, first, second, partner = peers_of(core, odd, z, y, x, depth)
    width = so.shape[1]
    rows = so.shape[0]
    sources = (
        [sp.at[:, pl.ds(j * width, width)] for j in range(3)]
        + [so, cq]
        + [ckv.at[:, pl.ds(j * width, width)] for j in range(2)]
        + [co]
        + [fi.at[:, pl.ds(j * width, width)] for j in range(4)]
        + [fo.at[pl.ds(j * rows, rows), :] for j in range(4)]
    )
    loads = [pltpu.make_async_copy(s, own.at[u], load_sem.at[u]) for u, s in enumerate(sources)]
    for load in loads:
        load.start()
    enter(ups, first, second, partner)

    def mine(i):
        return vectors.at[odd] if i == VECTORS else own.at[2 * i + odd]

    def set_of(i, a, b):
        return unit_set(g1, g2, gv, i, odd, *flip(odd, y, x, a, b))

    def up_copy(i, k):
        block = unit_block(g1, g2, gv, i, odd, z, y, x)
        return remote(mine(i), block, zs.at[i, k], zr.at[i, k], ups[k])

    def up_arrival(i, k):
        block = unit_block(g1, g2, gv, i, odd, (z + depth - 1 - k) % depth, y, x)
        return remote(block, block, zs.at[i, k], zr.at[i, k], ups[k])

    def first_copy(i):
        return remote(set_of(i, 0, 0), set_of(i, 0, 0), fs.at[i], fr.at[i], first)

    def second_copy(i, a):
        return remote(set_of(i, a, 0), set_of(i, a, 0), ss.at[i, a], sr.at[i, a], second)

    def partner_copy(i, a, b):
        at = a + 2 * b
        return remote(set_of(i, a, b), set_of(i, a, b), ps.at[i, at], pr.at[i, at], partner)

    def arrival(target, send, recv, peer):
        return remote(target, target, send, recv, peer)

    steps = [VECTORS, *range(HALF)]
    keeps = []
    for i in steps:
        if i != VECTORS:
            loads[2 * i].wait()
            loads[2 * i + 1].wait()
        keep = pltpu.make_async_copy(
            mine(i), unit_block(g1, g2, gv, i, odd, z, y, x), own_sem.at[i]
        )
        keep.start()
        keeps.append(keep)
        for k in range(depth - 1):
            up_copy(i, k).start()
    for step in range(len(steps) + 2):
        if step < len(steps):
            i = steps[step]
            keeps[step].wait()
            for k in range(depth - 1):
                up_arrival(i, k).wait_recv()
            first_copy(i).start()
            second_copy(i, 0).start()
            partner_copy(i, 0, 0).start()
        if 0 <= step - 1 < len(steps):
            i = steps[step - 1]
            arrival(set_of(i, 1, 0), fs.at[i], fr.at[i], first).wait_recv()
            second_copy(i, 1).start()
            partner_copy(i, 1, 0).start()
        if 0 <= step - 2 < len(steps):
            i = steps[step - 2]
            for a in range(2):
                arrival(set_of(i, a, 1), ss.at[i, a], sr.at[i, a], second).wait_recv()
                partner_copy(i, a, 1).start()
    for i in steps:
        for a in range(2):
            for b in range(2):
                at = a + 2 * b
                there = unit_set(g1, g2, gv, i, 1 - odd, *flip(1 - odd, y, x, a, b))
                arrival(there, ps.at[i, at], pr.at[i, at], partner).wait_recv()
                partner_copy(i, a, b).wait_send()
            second_copy(i, a).wait_send()
        first_copy(i).wait_send()
        for k in range(depth - 1):
            up_copy(i, k).wait_send()


def gather_weights(n_fsdp, vectors, sp, so, cq, ckv, co, fi, fo):
    rows, width = so.shape
    depth = n_fsdp // 4
    dma = pltpu.SemaphoreType.DMA
    steps = HALF + 1
    g1, g2, gv = pl.pallas_call(
        functools.partial(gather_body, depth),
        in_specs=[pl.BlockSpec(memory_space=pl.ANY)] * 8,
        out_specs=[pl.BlockSpec(memory_space=pl.ANY)] * 3,
        out_shape=[
            jax.ShapeDtypeStruct((FIRST, depth, 2, 2, rows, width), BF16),
            jax.ShapeDtypeStruct((depth, 2, 2, UNITS - FIRST, rows, width), BF16),
            jax.ShapeDtypeStruct((2, depth, 2, 2, VROWS, LANES), BF16),
        ],
        scratch_shapes=[
            pltpu.VMEM((UNITS, rows, width), BF16),
            dma((UNITS,)),
            dma((steps,)),
            dma((steps, depth - 1)),
            dma((steps, depth - 1)),
            dma((steps,)),
            dma((steps,)),
            dma((steps, 2)),
            dma((steps, 2)),
            dma((steps, 4)),
            dma((steps, 4)),
        ],
        compiler_params=pltpu.CompilerParams(
            collective_id=0, has_side_effects=True, vmem_limit_bytes=VMEM_LIMIT
        ),
        name="gather_weights",
    )(vectors, sp, so, cq, ckv, co, fi, fo)
    return (
        g1.reshape(FIRST, n_fsdp * rows, width),
        g2.reshape(-1, width),
        gv.reshape(2, n_fsdp, VROWS, LANES),
    )


def scatter_body(depth, *refs):
    units = refs[:7]
    (
        g1, g2, gv, out, out_v, own, from_partner, from_second, from_first, from_up, final, final_in,
        own_v, from_partner_v, from_second_v, from_first_v, from_up_v, final_v, final_in_v,
        own_sem, zs, zr, fs, fr, ss, sr, ps, pr, xs, xr,
    ) = refs[7:]
    core, odd, z, y, x = coordinates()
    ups, first, second, partner = peers_of(core, odd, z, y, x, depth)
    order = ((0, 1), (1, 1), (1, 0), (0, 0))

    def pick(i, main, small):
        return small if i == VECTORS else main.at[i]

    def source(i, parity, yy, xx):
        u = 2 * i + parity
        if i == VECTORS:
            return gv.at[parity, :, yy, xx]
        if 2 * i >= FIRST:
            return g2.at[:, yy, xx, u - FIRST]
        if 2 * i >= 8:
            return g1.at[u - 7, :, yy, xx]
        return units[u].at[:, yy, xx] if u < 7 else g1.at[0, :, yy, xx]

    def own_copy(i, a, b, parity):
        at = a + 2 * b
        return pltpu.make_async_copy(
            source(i, parity, *flip(odd, y, x, a, b)),
            pick(i, own, own_v).at[at],
            own_sem.at[i, at],
        )

    def partner_copy(i, a, b, parity):
        at = a + 2 * b
        return remote(
            source(i, parity, *flip(1 - odd, y, x, a, b)),
            pick(i, from_partner, from_partner_v).at[at],
            ps.at[i, at],
            pr.at[i, at],
            partner,
        )

    def second_copy(i, a):
        return remote(
            pick(i, own, own_v).at[a + 2],
            pick(i, from_second, from_second_v).at[a],
            ss.at[i, a],
            sr.at[i, a],
            second,
        )

    def first_copy(i):
        return remote(
            pick(i, own, own_v).at[1],
            pick(i, from_first, from_first_v),
            fs.at[i],
            fr.at[i],
            first,
        )

    def up_copy(i, k):
        return remote(
            pick(i, own, own_v).at[0, (z + 1 + k) % depth],
            pick(i, from_up, from_up_v).at[k],
            zs.at[i, k],
            zr.at[i, k],
            ups[k],
        )

    def final_copy(i):
        return remote(
            pick(i, final, final_v), pick(i, final_in, final_in_v), xs.at[i], xr.at[i], partner
        )

    def add(target, addend):
        def step(j, carry):
            target[j] = target[j] + addend[j]
            return carry

        lax.fori_loop(0, depth, step, 0)

    def start_all(copy, parity_of):
        for i in steps:
            if i != VECTORS and 2 * i < 8:
                for q in range(2):

                    @pl.when(odd == q)
                    def _(i=i, q=q):
                        for a, b in order:
                            copy(i, a, b, parity_of(q)).start()

            else:
                for a, b in order:
                    copy(i, a, b, parity_of(odd)).start()

    steps = [*range(HALF - 1, -1, -1), VECTORS]
    start_all(own_copy, lambda q: q)
    enter(ups, first, second, partner)
    start_all(partner_copy, lambda q: 1 - q)

    for step in range(len(steps) + 3):
        if step < len(steps):
            i = steps[step]
            for a, b in order:
                at = a + 2 * b
                own_copy(i, a, b, 0).wait()
                partner_copy(i, a, b, 0).wait_recv()
                add(pick(i, own, own_v).at[at], pick(i, from_partner, from_partner_v).at[at])
                if b:
                    second_copy(i, a).start()
        if 0 <= step - 1 < len(steps):
            i = steps[step - 1]
            for a in (1, 0):
                second_copy(i, a).wait_recv()
                add(pick(i, own, own_v).at[a], pick(i, from_second, from_second_v).at[a])
                if a:
                    first_copy(i).start()
        if 0 <= step - 2 < len(steps):
            i = steps[step - 2]
            first_copy(i).wait_recv()
            add(pick(i, own, own_v).at[0], pick(i, from_first, from_first_v))
            for k in range(depth - 1):
                up_copy(i, k).start()
        if 0 <= step - 3 < len(steps):
            i = steps[step - 3]
            total = pick(i, own, own_v)[0, z].astype(F32)
            for k in range(depth - 1):
                up_copy(i, k).wait_recv()
                total = total + pick(i, from_up, from_up_v)[k].astype(F32)
            pick(i, final, final_v)[...] = total
            final_copy(i).start()
            if i == VECTORS:
                out_v[odd] = total
            else:
                out[2 * i + odd] = total
    for i in steps:
        final_copy(i).wait()
        if i == VECTORS:
            out_v[1 - odd] = final_in_v[...]
        else:
            out[2 * i + 1 - odd] = final_in[i]
        for a, b in order:
            partner_copy(i, a, b, 0).wait_send()
        for a in range(2):
            second_copy(i, a).wait_send()
        first_copy(i).wait_send()
        for k in range(depth - 1):
            up_copy(i, k).wait_send()


def scatter_gradients(n_fsdp, units, g1, g2, gv):
    width = g1.shape[-1]
    depth = n_fsdp // 4
    rows = width // n_fsdp
    dma = pltpu.SemaphoreType.DMA
    vmem = pltpu.VMEM
    steps = HALF + 1
    block, small = (rows, width), (VROWS, LANES)
    return pl.pallas_call(
        functools.partial(scatter_body, depth),
        in_specs=[pl.BlockSpec(memory_space=pl.ANY)] * 10,
        out_specs=[pl.BlockSpec(memory_space=pltpu.VMEM)] * 2,
        out_shape=[
            jax.ShapeDtypeStruct((UNITS, *block), F32),
            jax.ShapeDtypeStruct((2, *small), F32),
        ],
        scratch_shapes=[
            vmem((HALF, 4, depth, *block), BF16),
            vmem((HALF, 4, depth, *block), BF16),
            vmem((HALF, 2, depth, *block), BF16),
            vmem((HALF, depth, *block), BF16),
            vmem((HALF, depth - 1, *block), BF16),
            vmem((HALF, *block), F32),
            vmem((HALF, *block), F32),
            vmem((4, depth, *small), BF16),
            vmem((4, depth, *small), BF16),
            vmem((2, depth, *small), BF16),
            vmem((depth, *small), BF16),
            vmem((depth - 1, *small), BF16),
            vmem(small, F32),
            vmem(small, F32),
            dma((steps, 4)),
            dma((steps, depth - 1)),
            dma((steps, depth - 1)),
            dma((steps,)),
            dma((steps,)),
            dma((steps, 2)),
            dma((steps, 2)),
            dma((steps, 4)),
            dma((steps, 4)),
            dma((steps,)),
            dma((steps,)),
        ],
        compiler_params=pltpu.CompilerParams(
            collective_id=1, has_side_effects=True, vmem_limit_bytes=VMEM_LIMIT
        ),
        name="scatter_gradients",
    )(
        *[u.reshape(depth, 2, 2, *block) for u in units],
        g1.reshape(-1, depth, 2, 2, *block),
        g2.reshape(depth, 2, 2, UNITS - FIRST, *block),
        gv.reshape(2, depth, 2, 2, *small),
    )


CHUNK = 256
VECTOR_ROWS = (5, 6, 8, 11, 9, 12)


def valid_of(own_places, length, chunk):
    row = lax.broadcasted_iota(jnp.int32, (CHUNK, 1), 0)
    place = row
    for block in range(CHUNK // QBLK):
        base = (own_places[chunk * (CHUNK // QBLK) + block] - block) * QBLK
        place = jnp.where((row >= block * QBLK) & (row < (block + 1) * QBLK), row + base, place)
    return place < length


def norm_stats(value):
    average = jnp.mean(value, axis=-1, keepdims=True)
    centred = value - average
    scale = lax.rsqrt(jnp.mean(centred * centred, axis=-1, keepdims=True) + EPSILON)
    return centred * scale, scale


def norm_back(grad, normed, scale):
    inner = jnp.mean(grad * normed, axis=-1, keepdims=True)
    return (grad - jnp.mean(grad, axis=-1, keepdims=True) - normed * inner) * scale


def feed_body(
    block_order, length_ref, mixed_ref, after_ref, cot_ref, vec_ref, b_fi_ref, g1, g2,
    out_ref, gmix_ref, grad_ref, sums_ref, isum_ref, d1, d2,
    w_co, w_fi, w_fo, mixed_low, normed, scale_ref, cross, cross_low, hidden, slope, grad_inner,
    total, grad_low, buffer, load_sem, store_sem,
):
    rows, width = after_ref.shape
    own_places = Places(block_order, rows // QBLK)
    chunks = [pl.ds(c * CHUNK, CHUNK) for c in range(rows // CHUNK)]
    output_load = pltpu.make_async_copy(g1.at[7], w_co, load_sem.at[0])

    def inner_load(j):
        return pltpu.make_async_copy(g1.at[8 + j], w_fi.at[j], load_sem.at[1 + j])

    def outer_load(j):
        source = g2.at[pl.ds(pl.multiple_of(j * width, width), width), :]
        return pltpu.make_async_copy(source, w_fo.at[j], load_sem.at[5 + j])

    output_load.start()
    for j in range(4):
        inner_load(j).start()
    for j in range(4):
        outer_load(j).start()
    vec = lambda i: vec_ref[VECTOR_ROWS[i] : VECTOR_ROWS[i] + 1, :]
    column_sum = lambda array: jnp.sum(array, axis=0, keepdims=True)

    output_load.wait()
    for c in chunks:
        mixed_low[c, :] = mixed_ref[c, :].astype(BF16)
        value = after_ref[c, :] + dot_nn(mixed_low[c, :], w_co[...]) + vec(0)
        hat, scale = norm_stats(value)
        normed[c, :] = hat
        scale_ref[c, :] = scale
        value = hat * vec(2) + vec(3)
        cross[c, :] = value
        cross_low[c, :] = value.astype(BF16)
        total[c, :] = value + vec(1)

    def forward(j, carry):
        inner_load(j).wait()
        outer_load(j).wait()
        bias = b_fi_ref[:, pl.ds(pl.multiple_of(j * width, width), width)]

        def inner_step(at, carry):
            c = pl.ds(pl.multiple_of(at * CHUNK, CHUNK), CHUNK)
            pre = dot_nn(cross_low[c, :], w_fi[j]) + bias
            share = 0.5 + 0.5 * lax.erf(pre * (0.5**0.5))
            act = (pre * share).astype(BF16)
            hidden[j, c, :] = act
            density = jnp.exp(-0.5 * pre * pre) * ((0.5 / jnp.pi) ** 0.5)
            slope[j, c, :] = (share + pre * density).astype(BF16)
            total[c, :] += dot_nn(act, w_fo[j])
            return carry

        return lax.fori_loop(0, rows // CHUNK, inner_step, carry)

    lax.fori_loop(0, 4, forward, 0)
    gain_sum = jnp.zeros((1, width), F32)
    shift_sum = jnp.zeros((1, width), F32)
    grad_sum = jnp.zeros((1, width), F32)
    for at, c in enumerate(chunks):
        hat, scale = norm_stats(total[c, :])
        valid = valid_of(own_places, length_ref[0], at)
        out_ref[c, :] = jnp.where(valid, hat * vec(4) + vec(5), 0.0)
        incoming = jnp.where(valid, cot_ref[c, :].astype(F32), 0.0)
        gain_sum += column_sum(incoming * hat)
        shift_sum += column_sum(incoming)
        grad = norm_back(incoming * vec(4), hat, scale)
        grad_sum += column_sum(grad)
        total[c, :] = grad
        grad_low[c, :] = grad.astype(BF16)
    sums_ref[1:2, :] = grad_sum
    sums_ref[3:4, :] = gain_sum
    sums_ref[5:6, :] = shift_sum

    def store(at, target):
        return pltpu.make_async_copy(buffer.at[at], target, store_sem.at[at])

    def outer_store(j):
        return store(0, d2.at[pl.ds(pl.multiple_of(j * width, width), width), :])

    def inner_store(j):
        return store(1, d1.at[1 + j])

    def back(j, carry):
        def back_step(at, carry):
            c = pl.ds(pl.multiple_of(at * CHUNK, CHUNK), CHUNK)
            grad = dot_nt(grad_low[c, :], w_fo[j]) * slope[j, c, :].astype(F32)
            low = grad.astype(BF16)
            grad_inner[c, :] = low
            total[c, :] += dot_nt(low, w_fi[j])
            return carry + column_sum(grad)

        isum_ref[:, pl.ds(pl.multiple_of(j * width, width), width)] = lax.fori_loop(
            0, rows // CHUNK, back_step, jnp.zeros((1, width), F32)
        )

        @pl.when(j > 0)
        def _():
            outer_store(j - 1).wait()
            inner_store(j - 1).wait()

        buffer[0] = dot_tn(hidden[j], grad_low[...]).astype(BF16)
        outer_store(j).start()
        buffer[1] = dot_tn(cross_low[...], grad_inner[...]).astype(BF16)
        inner_store(j).start()
        return carry

    lax.fori_loop(0, 4, back, 0)
    gain_sum = jnp.zeros((1, width), F32)
    shift_sum = jnp.zeros((1, width), F32)
    grad_sum = jnp.zeros((1, width), F32)
    for c in chunks:
        incoming = total[c, :]
        hat = normed[c, :]
        gain_sum += column_sum(incoming * hat)
        shift_sum += column_sum(incoming)
        grad = norm_back(incoming * vec(2), hat, scale_ref[c, :])
        grad_sum += column_sum(grad)
        grad_ref[c, :] = grad
        low = grad.astype(BF16)
        grad_low[c, :] = low
        gmix_ref[c, :] = dot_nt(low, w_co[...]).astype(BF16)
    sums_ref[0:1, :] = grad_sum
    sums_ref[2:3, :] = gain_sum
    sums_ref[4:5, :] = shift_sum
    outer_store(3).wait()
    buffer[0] = dot_tn(mixed_low[...], grad_low[...]).astype(BF16)
    store(0, d1.at[0]).start()
    store(0, d1.at[0]).wait()
    inner_store(3).wait()


def feed_forward(block_order, length, mixed, after, cotangent, vectors, inner_bias, units, outer):
    rows, width = after.shape
    hidden = outer.shape[0]
    any_spec = pl.BlockSpec(memory_space=pl.ANY)
    vmem_spec = pl.BlockSpec(memory_space=pltpu.VMEM)
    vmem = pltpu.VMEM
    return pl.pallas_call(
        feed_body,
        in_specs=[pl.BlockSpec(memory_space=pltpu.SMEM)] * 2 + [vmem_spec] * 5 + [any_spec] * 2,
        out_specs=[vmem_spec] * 5 + [any_spec] * 2,
        out_shape=[
            jax.ShapeDtypeStruct((rows, width), F32),
            jax.ShapeDtypeStruct((rows, width), BF16),
            jax.ShapeDtypeStruct((rows, width), F32),
            jax.ShapeDtypeStruct((8, width), F32),
            jax.ShapeDtypeStruct((1, hidden), F32),
            jax.ShapeDtypeStruct((5, width, width), BF16),
            jax.ShapeDtypeStruct((hidden, width), BF16),
        ],
        scratch_shapes=[
            vmem((width, width), BF16),
            vmem((4, width, width), BF16),
            vmem((4, width, width), BF16),
            vmem((rows, width), BF16),
            vmem((rows, width), F32),
            vmem((rows, 1), F32),
            vmem((rows, width), F32),
            vmem((rows, width), BF16),
            vmem((4, rows, width), BF16),
            vmem((4, rows, width), BF16),
            vmem((rows, width), BF16),
            vmem((rows, width), F32),
            vmem((rows, width), BF16),
            vmem((2, width, width), BF16),
            pltpu.SemaphoreType.DMA((9,)),
            pltpu.SemaphoreType.DMA((2,)),
        ],
        compiler_params=pltpu.CompilerParams(vmem_limit_bytes=VMEM_LIMIT),
        name="feed_forward",
    )(block_order, length, mixed, after, cotangent, vectors, inner_bias, units, outer)


VLANES = 256
WINDOW = 384


def spread_lanes(pieces, width):
    count = WINDOW // width
    lanes = pieces[0].shape[1]
    row = lax.broadcasted_iota(jnp.int32, (lanes, WINDOW), 0)
    column = lax.broadcasted_iota(jnp.int32, (lanes, WINDOW), 1)
    windows = [None] * (len(pieces) // count)
    for k in range(count):
        select = ((column == row + k * width) & (row < width)).astype(F32).astype(BF16)
        for w in range(len(windows)):
            part = dot_nn(pieces[w * count + k], select)
            windows[w] = part if k == 0 else windows[w] + part
    return jnp.concatenate(windows, axis=1)


def pair_forward(causal, p, q, k_all, v_all, values_t, out, totals, own_places, places, length):
    lanes = pl.ds(pl.multiple_of(p * PAIR, PAIR), PAIR)
    parts, part_rows = k_all.shape[0], k_all.shape[1]
    for h in range(parts):
        for block in range(part_rows // QBLK):
            rows = slice(block * QBLK, (block + 1) * QBLK)
            at = h * part_rows + block * QBLK
            values_t[:, at : at + QBLK] = v_all[h, rows, lanes].astype(F32).T.astype(BF16)

    def step(i, carry):
        rows = pl.ds(pl.multiple_of(i * QBLK, QBLK), QBLK)
        both = stack_heads(q[rows, lanes])
        scores = [dot_nt(k_all[h, :, lanes], both) for h in range(parts)]
        if causal:
            limit = row_limit(own_places[i], length)
            scores = [
                mask_part(s, limit, places, h * (part_rows // QBLK)) for h, s in enumerate(scores)
            ]
        highest = jnp.max(scores[0], axis=0, keepdims=True)
        for s in scores[1:]:
            highest = jnp.maximum(highest, jnp.max(s, axis=0, keepdims=True))
        total, mixed = 0.0, 0.0
        for h, s in enumerate(scores):
            exponent = jnp.exp(s - highest)
            total += jnp.sum(exponent, axis=0, keepdims=True)
            mixed += dot_nn(
                values_t[:, h * part_rows : (h + 1) * part_rows], exponent.astype(BF16)
            )
        out[rows, lanes] = unstack_heads(mixed * (1.0 / total), QBLK)
        totals[p, pl.ds(i, 1), :] = highest + jnp.log(total)
        return carry

    lax.fori_loop(0, q.shape[0] // QBLK, step, 0)


def row_limit(place, length):
    column = lax.broadcasted_iota(jnp.int32, (1, 2 * QBLK), 1)
    own = place * QBLK + jnp.where(column >= QBLK, column - QBLK, column)
    return jnp.minimum(own, length - 1)


def mask_part(scores, limit, places, first_block):
    row = lax.broadcasted_iota(jnp.int32, (QBLK, 2 * QBLK), 0)
    blocks = []
    for block in range(scores.shape[0] // QBLK):
        part = scores[block * QBLK : (block + 1) * QBLK]
        kept = row <= limit - places[first_block + block] * QBLK
        blocks.append(jnp.where(kept, part, MASKED_SCORE))
    return jnp.concatenate(blocks, axis=0)


def encode_body(
    depth, block_order, length_ref, states, encoder, b_self, b_cross, gains, shifts, singles, sp, so, cq, ckv, co, fi,
    fo, g1, g2, q_out, k_out, v_out, cq_out, ck_out, cv_out, o_out, total_out, after_out, low_out, hat_out,
    scale_out, co_out, ctotal_out, flat_out, inner_out,
    gv, own, spread_in, vectors, w, q, k_all, v_all, c_q, ck_all, cv_all, mixed, after, low, hat, values_t, cvalues_t,
    load_sem, own_sem, weight_sem, store_sem, zs, zr, fs, fr, ss, sr, ps, pr, ks, kr,
):
    core, odd, z, y, x = coordinates()
    ups, first, second, partner = peers_of(core, odd, z, y, x, depth)
    rows, width = so.shape
    length = length_ref[0]
    own_places = places = Places(block_order, states.shape[0] // QBLK)
    sources = (
        [sp.at[:, pl.ds(j * width, width)] for j in (1, 2, 0)]
        + [so, cq]
        + [ckv.at[:, pl.ds(j * width, width)] for j in range(2)]
        + [co]
        + [fi.at[:, pl.ds(j * width, width)] for j in range(4)]
        + [fo.at[pl.ds(j * rows, rows), :] for j in range(4)]
    )
    loads = [pltpu.make_async_copy(s, own.at[u], load_sem.at[u]) for u, s in enumerate(sources)]
    for load in loads:
        load.start()
    spread_in[...] = jnp.zeros_like(spread_in)
    for at, array in ((0, b_self), (3, b_cross), (7, gains), (10, shifts)):
        spread_in[at : at + array.shape[0], :rows] = array[...].astype(F32)
    single = singles[...].astype(F32)
    for at, row in enumerate((2, 5, 6)):
        spread_in[row : row + 1, :rows] = single[:, at * rows : (at + 1) * rows]
    inner = single[:, 3 * rows :]
    spread_in[13:14, : inner.shape[1]] = inner
    vectors[...] = spread_in[...].astype(BF16)
    enter(ups, first, second, partner)

    def mine(i):
        return vectors if i == VECTORS else own.at[2 * i + odd]

    def set_at(i, parity, yy, xx):
        return gv.at[:, yy, xx] if i == VECTORS else unit_set(g1, g2, None, i, parity, yy, xx)

    def block_at(i, zz):
        return gv.at[zz, y, x] if i == VECTORS else unit_block(g1, g2, None, i, odd, zz, y, x)

    def set_of(i, a, b):
        return set_at(i, odd, *flip(odd, y, x, a, b))

    def up_copy(i, k):
        return remote(mine(i), block_at(i, z), zs.at[i, k], zr.at[i, k], ups[k])

    def up_arrival(i, k):
        block = block_at(i, (z + depth - 1 - k) % depth)
        return remote(block, block, zs.at[i, k], zr.at[i, k], ups[k])

    def first_copy(i):
        return remote(set_of(i, 0, 0), set_of(i, 0, 0), fs.at[i], fr.at[i], first)

    def first_arrival(i):
        return remote(set_of(i, 1, 0), set_of(i, 1, 0), fs.at[i], fr.at[i], first)

    def second_copy(i, a):
        return remote(set_of(i, a, 0), set_of(i, a, 0), ss.at[i, a], sr.at[i, a], second)

    def second_arrival(i, a):
        return remote(set_of(i, a, 1), set_of(i, a, 1), ss.at[i, a], sr.at[i, a], second)

    def partner_copy(i, a, b):
        at = a + 2 * b
        return remote(set_of(i, a, b), set_of(i, a, b), ps.at[i, at], pr.at[i, at], partner)

    def partner_arrival(i, a, b):
        at = a + 2 * b
        there = set_at(i, 1 - odd, *flip(1 - odd, y, x, a, b))
        return remote(there, there, ps.at[i, at], pr.at[i, at], partner)

    keeps = {}

    def begin(i):
        keeps[i] = pltpu.make_async_copy(mine(i), block_at(i, z), own_sem.at[i])
        keeps[i].start()
        for k in range(depth - 1):
            up_copy(i, k).start()

    def stage_2(i):
        keeps[i].wait()
        for k in range(depth - 1):
            up_arrival(i, k).wait_recv()
        first_copy(i).start()
        second_copy(i, 0).start()
        if i != VECTORS:
            partner_copy(i, 0, 0).start()

    def stage_3(i):
        first_arrival(i).wait_recv()
        second_copy(i, 1).start()
        if i != VECTORS:
            partner_copy(i, 1, 0).start()

    def stage_4(i):
        for a in range(2):
            second_arrival(i, a).wait_recv()
            if i != VECTORS:
                partner_copy(i, a, 1).start()

    def finish(i):
        for a in range(2):
            for b in range(2):
                partner_arrival(i, a, b).wait_recv()

    def weight(u):
        return pltpu.make_async_copy(
            g1.at[u].reshape(width, width), w.at[u], weight_sem.at[u]
        )

    stores = []

    def store(source, target):
        copy = pltpu.make_async_copy(source, target, store_sem.at[len(stores)])
        copy.start()
        stores.append(copy)

    begin(VECTORS)
    for i in range(HALF):
        loads[2 * i].wait()
        loads[2 * i + 1].wait()
        begin(i)
    stage_2(VECTORS)
    stage_3(VECTORS)
    stage_2(0)
    stage_4(VECTORS)
    flat = spread_lanes([gv[f // 4, (f // 2) % 2, f % 2] for f in range(4 * depth)], rows)
    flat_out[...] = flat
    inner_rows = fo.shape[0]
    inner_out[...] = spread_lanes(
        [gv[f // 4, (f // 2) % 2, f % 2] for f in range(4 * depth)], inner_rows
    )[13:14, :]
    vec = lambda i: flat[i : i + 1, :]
    stage_3(0)
    stage_2(1)
    stage_4(0)
    finish(0)
    for u in range(2):
        weight(u).start()

    row_count = states.shape[0]
    chunks = [pl.ds(c * CHUNK, CHUNK) for c in range(row_count // CHUNK)]
    encoder_count = encoder.shape[0]
    step = min(CHUNK, encoder_count)
    encoder_chunks = [pl.ds(c * step, step) for c in range(encoder_count // step)]

    def share(number, array):
        copy = remote(array.at[0], array.at[1], ks.at[number], kr.at[number], partner)
        copy.start()
        return copy

    weight(0).wait()
    for c in chunks:
        k_all[0, c, :] = dot_nn(states[c, :], w[0]).astype(BF16)
    shares = [share(0, k_all)]
    stage_3(1)
    stage_2(2)
    weight(1).wait()
    for c in chunks:
        v_all[0, c, :] = (dot_nn(states[c, :], w[1]) + vec(1)).astype(BF16)
    shares.append(share(1, v_all))
    stage_2(3)
    stage_4(1)
    finish(1)
    for u in range(2, 4):
        weight(u).start()
    weight(2).wait()
    for c in chunks:
        q[c, :] = ((dot_nn(states[c, :], w[2]) + vec(0)) * ATTN_SCALE).astype(BF16)
    store(q, q_out)
    shares[0].wait_recv()
    shares[1].wait_recv()
    store(k_all, k_out)
    store(v_all, v_out)
    pairs = width // PAIR

    def self_step(p, carry):
        pair_forward(
            True, p, q, k_all, v_all, values_t, mixed, total_out, own_places, places, length
        )

        @pl.when(p == 0)
        def _():
            stage_3(2)
            stage_2(4)

        @pl.when(p == 2)
        def _():
            stage_3(3)
            stage_4(2)
            stage_2(5)

        @pl.when(p == 4)
        def _():
            stage_3(4)
            stage_2(6)

        return carry

    lax.fori_loop(0, pairs, self_step, 0)
    store(mixed, o_out)
    stage_4(3)
    stage_2(7)
    finish(2)
    finish(3)
    for u in (5, 6, 4, 7):
        weight(u).start()
    weight(5).wait()
    for c in encoder_chunks:
        ck_all[0, c, :] = dot_nn(encoder[c, :], w[5]).astype(BF16)
    shares.append(share(2, ck_all))
    weight(6).wait()
    for c in encoder_chunks:
        cv_all[0, c, :] = (dot_nn(encoder[c, :], w[6]) + vec(4)).astype(BF16)
    shares.append(share(3, cv_all))
    weight(3).wait()
    weight(4).wait()
    for c in chunks:
        value = states[c, :].astype(F32) + dot_nn(mixed[c, :].astype(BF16), w[3]) + vec(2)
        normed, scale = norm_stats(value)
        hat[c, :] = normed
        scale_out[c, :] = scale
        value = normed * vec(7) + vec(10)
        after[c, :] = value
        low[c, :] = value.astype(BF16)
        c_q[c, :] = ((dot_nn(low[c, :], w[4]) + vec(3)) * ATTN_SCALE).astype(BF16)
    store(hat, hat_out)
    store(after, after_out)
    store(low, low_out)
    store(c_q, cq_out)
    stage_3(5)
    stage_4(4)
    shares[2].wait_recv()
    shares[3].wait_recv()
    store(ck_all, ck_out)
    store(cv_all, cv_out)
    stores[3].wait()

    def cross_step(p, carry):
        pair_forward(
            False, p, c_q, ck_all, cv_all, cvalues_t, mixed, ctotal_out, None, None, None
        )

        @pl.when(p == 0)
        def _():
            stage_3(6)

        @pl.when(p == 2)
        def _():
            stage_3(7)
            stage_4(5)

        @pl.when(p == 4)
        def _():
            stage_4(6)

        @pl.when(p == 5)
        def _():
            stage_4(7)

        return carry

    lax.fori_loop(0, pairs, cross_step, 0)
    store(mixed, co_out)
    weight(7).wait()
    for at, copy in enumerate(stores):
        if at != 3:
            copy.wait()
    for copy in shares:
        copy.wait_send()
    for i in [VECTORS, *range(HALF)]:
        if i >= 4 and i != VECTORS:
            finish(i)
        for a in range(2):
            for b in range(2):
                if i != VECTORS:
                    partner_copy(i, a, b).wait_send()
            second_copy(i, a).wait_send()
        first_copy(i).wait_send()
        for k in range(depth - 1):
            up_copy(i, k).wait_send()


def encode(
    n_fsdp, block_order, length, states, encoder, b_self, b_cross, gains, shifts, singles, sp, so, cq,
    ckv, co, fi, fo,
):
    rows, width = so.shape
    depth = n_fsdp // 4
    row_count, encoder_count = states.shape[0], encoder.shape[0]
    pairs = width // PAIR
    steps = HALF + 1
    dma = pltpu.SemaphoreType.DMA
    vmem = pltpu.VMEM
    any_spec = pl.BlockSpec(memory_space=pl.ANY)
    vmem_spec = pl.BlockSpec(memory_space=pltpu.VMEM)
    smem_spec = pl.BlockSpec(memory_space=pltpu.SMEM)
    shape = jax.ShapeDtypeStruct
    totals = (pairs, row_count // QBLK, 2 * QBLK)
    outs = [
        (any_spec, (FIRST, depth, 2, 2, rows, width), BF16),
        (any_spec, (depth, 2, 2, UNITS - FIRST, rows, width), BF16),
        (any_spec, (row_count, width), BF16),
        (any_spec, (2, row_count, width), BF16),
        (any_spec, (2, row_count, width), BF16),
        (any_spec, (row_count, width), BF16),
        (any_spec, (2, encoder_count, width), BF16),
        (any_spec, (2, encoder_count, width), BF16),
        (any_spec, (row_count, width), F32),
        (vmem_spec, totals, F32),
        (any_spec, (row_count, width), F32),
        (any_spec, (row_count, width), BF16),
        (any_spec, (row_count, width), F32),
        (vmem_spec, (row_count, 1), F32),
        (any_spec, (row_count, width), F32),
        (vmem_spec, totals, F32),
        (vmem_spec, (VROWS, width), F32),
        (vmem_spec, (1, fo.shape[0] * n_fsdp), F32),
    ]
    return pl.pallas_call(
        functools.partial(encode_body, depth),
        in_specs=[smem_spec] * 2 + [vmem_spec] * 7 + [any_spec] * 7,
        out_specs=[spec for spec, _, _ in outs],
        out_shape=[shape(extent, kind) for _, extent, kind in outs],
        scratch_shapes=[
            vmem((depth, 2, 2, VROWS, VLANES), BF16),
            vmem((UNITS, rows, width), BF16),
            vmem((VROWS, VLANES), F32),
            vmem((VROWS, VLANES), BF16),
            vmem((8, width, width), BF16),
            vmem((row_count, width), BF16),
            vmem((2, row_count, width), BF16),
            vmem((2, row_count, width), BF16),
            vmem((row_count, width), BF16),
            vmem((2, encoder_count, width), BF16),
            vmem((2, encoder_count, width), BF16),
            vmem((row_count, width), F32),
            vmem((row_count, width), F32),
            vmem((row_count, width), BF16),
            vmem((row_count, width), F32),
            vmem((PAIR, 2 * row_count), BF16),
            vmem((PAIR, 2 * encoder_count), BF16),
            dma((UNITS,)),
            dma((steps,)),
            dma((8,)),
            dma((12,)),
            dma((steps, depth - 1)),
            dma((steps, depth - 1)),
            dma((steps,)),
            dma((steps,)),
            dma((steps, 2)),
            dma((steps, 2)),
            dma((steps, 4)),
            dma((steps, 4)),
            dma((4,)),
            dma((4,)),
        ],
        compiler_params=pltpu.CompilerParams(
            collective_id=2, has_side_effects=True, vmem_limit_bytes=VMEM_LIMIT
        ),
        name="encode",
    )(
        block_order, length, states, encoder, b_self, b_cross, gains, shifts, singles, sp, so, cq, ckv, co,
        fi, fo,
    )


def pair_backward(
    causal, p, q, g, o, totals, k_all, v_all, keys_t, dk, dv, dq, kept, sent, sums, sum_row,
    own_places, places, length,
):
    lanes = pl.ds(pl.multiple_of(p * PAIR, PAIR), PAIR)
    parts, part_rows = k_all.shape[0], k_all.shape[1]
    for h in range(parts):
        for block in range(part_rows // QBLK):
            rows = slice(block * QBLK, (block + 1) * QBLK)
            at = h * part_rows + block * QBLK
            keys_t[:, at : at + QBLK] = k_all[h, rows, lanes].astype(F32).T.astype(BF16)
    dk[...] = jnp.zeros_like(dk)
    dv[...] = jnp.zeros_like(dv)

    def step(i, carry):
        rows = pl.ds(pl.multiple_of(i * QBLK, QBLK), QBLK)
        both = stack_heads(q[rows, lanes])
        grads = g[rows, lanes]
        both_grads = stack_heads(grads)
        products = (grads.astype(F32) * o[rows, lanes]).T
        delta = jnp.concatenate(
            [
                jnp.sum(products[:HD], axis=0, keepdims=True),
                jnp.sum(products[HD:], axis=0, keepdims=True),
            ],
            axis=1,
        )
        if causal:
            limit = row_limit(own_places[i], length)
        level = totals[p, pl.ds(i, 1), :]
        query_grad = 0.0
        for h in range(parts):
            span = slice(h * part_rows, (h + 1) * part_rows)
            scores = dot_nt(k_all[h, :, lanes], both)
            if causal:
                scores = mask_part(scores, limit, places, h * (part_rows // QBLK))
            prob = jnp.exp(scores - level)
            prob_grad = dot_nt(v_all[h, :, lanes], both_grads)
            score_grad = (prob * (prob_grad - delta)).astype(BF16)
            dv[span, :] += dot_nn(prob.astype(BF16), both_grads)
            dk[span, :] += dot_nn(score_grad, both)
            query_grad += dot_nn(keys_t[:, span], score_grad)
        query_grad = unstack_heads(query_grad, QBLK) * ATTN_SCALE
        dq[rows, lanes] = query_grad.astype(BF16)
        return carry + jnp.sum(query_grad, axis=0, keepdims=True)

    sums[sum_row : sum_row + 1, lanes] = lax.fori_loop(
        0, q.shape[0] // QBLK, step, jnp.zeros((1, PAIR), F32)
    )
    for at, grad in enumerate((dk, dv)):
        kept[at, :, lanes] = grad[:part_rows, :].astype(BF16)
        sent[at, :, lanes] = grad[part_rows:, :].astype(BF16)


def select_lanes(offset, first, limit, lanes):
    lane = lax.broadcasted_iota(jnp.int32, (WINDOW, lanes), 1) + first
    column = lax.broadcasted_iota(jnp.int32, (WINDOW, lanes), 0)
    return ((column == lane + offset) & (lane < limit)).astype(F32).astype(BF16)


def decode_body(
    depth, block_order, length_ref, flat, scale_ref, ctotal, total, feed_sums, inner_sum,
    units, cq_in, ck_in, cv_in, co_in, gmix_in, low_in, encoder_in, hat_in, grad_in, q_in, k_in, v_in,
    o_in, states_in, d1, d2,
    gs_out, ge_out, out, out_v,
    own, from_partner, from_second, from_first, from_up, w, q, g, o, k, v, dq, kept, sent, arrived,
    inputs, enc, hat, grad, dk, dv, keys_t, sums,
    gv, from_partner_v, from_second_v, from_first_v, from_up_v,
    load_sem, own_sem, store_sem, zs, zr, fs, fr, ss, sr, ps, pr, xs, xr, ks, kr,
):
    core, odd, z, y, x = coordinates()
    ups, first, second, partner = peers_of(core, odd, z, y, x, depth)
    rows, width = units.shape[-2:]
    row_count = q.shape[0]
    length = length_ref[0]
    own_places = places = Places(block_order, row_count // QBLK)
    order = ((0, 1), (1, 1), (1, 0), (0, 0))
    pairs = width // PAIR
    chunks = [pl.ds(c * CHUNK, CHUNK) for c in range(row_count // CHUNK)]
    column_sum = lambda array: jnp.sum(array, axis=0, keepdims=True)


    half = (pairs // 2) * PAIR
    spans = (pl.ds(0, half), pl.ds(half, width - half))

    def base(i):
        return i - VECTORS - 1 if i > VECTORS else i

    def part(i, ref):
        return ref.at[:, :, spans[i > VECTORS]] if base(i) < 2 else ref

    def pick(i, main, small, at=None):
        ref = small if i == VECTORS else main.at[base(i)]
        return part(i, ref if at is None else ref.at[at])

    def kept_set(i, a, b):
        yy, xx = flip(odd, y, x, a, b)
        return gv.at[odd, :, yy, xx] if i == VECTORS else part(i, own.at[base(i), :, yy, xx])

    def sent_set(i, a, b):
        yy, xx = flip(1 - odd, y, x, a, b)
        u = 2 * i + 1 - odd
        if i == VECTORS:
            return gv.at[1 - odd, :, yy, xx]
        if i > VECTORS or i < 4:
            return part(i, own.at[HALF + base(i), :, yy, xx])
        if 2 * i >= FIRST:
            return d2.at[:, yy, xx, u - FIRST]
        return d1.at[u - 7, :, yy, xx]

    def own_copy(i):
        u = 2 * i + odd
        source = d2.at[:, :, :, u - FIRST] if 2 * i >= FIRST else d1.at[u - 7]
        return pltpu.make_async_copy(source, own.at[i], own_sem.at[i])

    def partner_copy(i, a, b):
        at = a + 2 * b
        return remote(
            sent_set(i, a, b),
            pick(i, from_partner, from_partner_v, at),
            ps.at[i, at],
            pr.at[i, at],
            partner,
        )

    def second_copy(i, a):
        target = pick(i, from_second, from_second_v, a)
        return remote(kept_set(i, a, 1), target, ss.at[i, a], sr.at[i, a], second)

    def first_copy(i):
        target = pick(i, from_first, from_first_v)
        return remote(kept_set(i, 1, 0), target, fs.at[i], fr.at[i], first)

    def up_copy(i, n):
        source = kept_set(i, 0, 0).at[(z + 1 + n) % depth]
        target = pick(i, from_up, from_up_v).at[n]
        return remote(source, target, zs.at[i, n], zr.at[i, n], ups[n])

    def result(i, parity):
        if i == VECTORS:
            return out_v.at[parity]
        target = out.at[2 * base(i) + parity]
        return target.at[:, spans[i > VECTORS]] if base(i) < 2 else target

    def final_copy(i, parity):
        target = result(i, parity)
        return remote(target, target, xs.at[i], xr.at[i], partner)

    def add(target, addend):
        def step(j, carry):
            target[j] = target[j] + addend[j]
            return carry

        lax.fori_loop(0, depth, step, 0)

    def send(i):
        for a, b in order:
            partner_copy(i, a, b).start()

    def stage_1(i):
        if HALF > i >= 4:
            own_copy(i).wait()
        for a, b in order:
            partner_copy(i, a, b).wait_recv()
            add(kept_set(i, a, b), pick(i, from_partner, from_partner_v, a + 2 * b))
            if b:
                second_copy(i, a).start()

    def stage_2(i):
        for a in (1, 0):
            second_copy(i, a).wait_recv()
            add(kept_set(i, a, 0), pick(i, from_second, from_second_v, a))
            if a:
                first_copy(i).start()

    def stage_3(i):
        first_copy(i).wait_recv()
        add(kept_set(i, 0, 0), pick(i, from_first, from_first_v))
        for n in range(depth - 1):
            up_copy(i, n).start()

    def stage_4(i):
        value = kept_set(i, 0, 0)[z].astype(F32)
        for n in range(depth - 1):
            up_copy(i, n).wait_recv()
            value = value + pick(i, from_up, from_up_v)[n].astype(F32)
        result(i, odd)[...] = value
        final_copy(i, odd).start()

    def put_unit(u, value, span=slice(None)):
        at = u // 2 + HALF * ((u + odd) % 2)
        own[at, :, :, :, :, span] = value.astype(BF16).reshape(depth, 2, 2, rows, -1)


    loads = []

    def load(source, target):
        copy = pltpu.make_async_copy(source, target, load_sem.at[len(loads)])
        copy.start()
        loads.append(copy)
        return copy

    def weight(u, at):
        return load(units.at[u].reshape(width, width), w.at[at])

    attention_loads = [load(*pair) for pair in ((cq_in, q), (ck_in, k), (cv_in, v), (gmix_in, g), (co_in, o))]
    for i in range(HALF - 1, 3, -1):
        own_copy(i).start()
    cross_loads = [load(low_in, inputs), weight(4, 0), load(grad_in, grad), load(hat_in, hat), weight(3, 1)]
    encoder_loads = [load(encoder_in, enc), weight(5, 2), weight(6, 3)]
    output_load = load(d1.at[0], own.at[3 + HALF * ((7 + odd) % 2)])
    enter(ups, first, second, partner)
    for i in range(HALF - 1, 3, -1):
        send(i)

    sums[...] = jnp.zeros_like(sums)
    for at, row in enumerate((5, 6, 8, 9, 11, 12)):
        sums[row : row + 1, :] = feed_sums[at : at + 1, :]
    for copy in attention_loads:
        copy.wait()

    def cross_step(p, carry):
        pair_backward(
            False, p, q, g, o, ctotal, k, v, keys_t, dk, dv, dq, kept, sent, sums, 3, None, None, None
        )

        @pl.when(p == 0)
        def _():
            stage_1(7)

        @pl.when(p == 1)
        def _():
            stage_1(6)

        @pl.when(p == 2)
        def _():
            stage_2(7)
            stage_1(5)

        @pl.when(p == 4)
        def _():
            stage_2(6)
            stage_1(4)

        @pl.when(p == 5)
        def _():
            stage_3(7)

        return carry

    lax.fori_loop(0, pairs, cross_step, 0)
    cross_share = remote(sent, arrived.at[0], ks.at[0], kr.at[0], partner)
    cross_share.start()
    self_loads = [load(*pair) for pair in ((o_in, o), (q_in, q), (k_in, k), (v_in, v))]
    for copy in cross_loads:
        copy.wait()
    put_unit(4, dot_tn(inputs[...], dq[...]))
    states_load = load(states_in, inputs)
    gain_sum = jnp.zeros((1, width), F32)
    shift_sum = jnp.zeros((1, width), F32)
    grad_sum = jnp.zeros((1, width), F32)
    for c in chunks:
        incoming = grad[c, :] + dot_nt(dq[c, :], w[0])
        normed = hat[c, :]
        gain_sum += column_sum(incoming * normed)
        shift_sum += column_sum(incoming)
        value = norm_back(incoming * flat[7:8, :], normed, scale_ref[c, :])
        grad_sum += column_sum(value)
        grad[c, :] = value
        low = value.astype(BF16)
        dq[c, :] = low
        g[c, :] = dot_nt(low, w[1]).astype(BF16)
    sums[2:3, :] = grad_sum
    sums[7:8, :] = gain_sum
    sums[10:11, :] = shift_sum
    stage_2(5)
    stage_3(6)
    last_loads = [weight(2, 0)]
    self_loads[0].wait()
    put_unit(3, dot_tn(o[...].astype(BF16), dq[...]))
    last_loads.append(weight(0, 1))

    def total_kept(number, c, span=slice(None)):
        low = []
        for at in range(2):
            value = kept[at, c, span].astype(F32) + arrived[number, at, c, span].astype(F32)
            kept[at, c, span] = value.astype(BF16)
            low.append(value)
        return column_sum(low[1])

    for copy in encoder_loads:
        copy.wait()
    cross_share.wait_recv()
    sums[4:5, :] = sum(total_kept(0, c) for c in chunks)
    put_unit(5, dot_tn(enc[...], kept[0]))
    send(2)
    put_unit(6, dot_tn(enc[...], kept[1]))
    output_load.wait()
    send(3)
    for c in chunks:
        hat[c, :] = dot_nt(kept[0, c, :], w[2]) + dot_nt(kept[1, c, :], w[3])
    encoder_store = pltpu.make_async_copy(hat, ge_out, store_sem.at[0])
    encoder_store.start()
    stage_1(3)
    stage_4(7)
    last_loads.append(weight(1, 2))
    stage_1(2)
    stage_2(4)
    cross_share.wait_send()
    for copy in self_loads[1:]:
        copy.wait()

    def self_share(n):
        source, target = sent.at[:, :, spans[n]], arrived.at[1, :, :, spans[n]]
        return remote(source, target, ks.at[1 + n], kr.at[1 + n], partner)

    def self_units(n):
        span = spans[n]
        self_share(n).wait_recv()
        sums[1:2, span] = sum(total_kept(1, c, span) for c in chunks)
        put_unit(1, dot_tn(inputs[...], kept[0, :, span]), span)
        send(0 if n == 0 else VECTORS + 1)
        put_unit(2, dot_tn(inputs[...], kept[1, :, span]), span)
        send(1 if n == 0 else VECTORS + 2)

    def self_step(p, carry):
        pair_backward(
            True, p, q, g, o, total, k, v, keys_t, dk, dv, dq, kept, sent, sums, 0, own_places, places,
            length,
        )

        @pl.when(p == 0)
        def _():
            stage_3(5)
            stage_4(6)

        @pl.when(p == 1)
        def _():
            stage_4(5)

        @pl.when(p == pairs // 2 - 1)
        def _():
            self_share(0).start()
            put_unit(0, dot_tn(inputs[...], dq[:, spans[0]]), spans[0])
            stage_2(3)

        @pl.when(p == 3)
        def _():
            self_units(0)
            stage_2(2)
            stage_3(4)

        @pl.when(p == 4)
        def _():
            stage_1(0)
            stage_1(1)

        @pl.when(p == 5)
        def _():
            stage_3(3)
            stage_4(4)

        return carry

    states_load.wait()
    lax.fori_loop(0, pairs, self_step, 0)
    self_share(1).start()
    put_unit(0, dot_tn(inputs[...], dq[:, spans[1]]), spans[1])
    stage_3(2)
    self_units(1)
    pack_sums(depth, rows, sums, inner_sum, gv)
    send(VECTORS)
    stage_2(0)
    stage_2(1)
    stage_4(3)
    for copy in last_loads:
        copy.wait()
    stage_1(VECTORS + 1)
    stage_1(VECTORS + 2)
    stage_1(VECTORS)
    for c in chunks:
        value = grad[c, :] + dot_nt(kept[0, c, :], w[1]) + dot_nt(kept[1, c, :], w[2])
        grad[c, :] = value + dot_nt(dq[c, :], w[0])
    states_store = pltpu.make_async_copy(grad, gs_out, store_sem.at[1])
    states_store.start()
    stage_3(0)
    stage_4(2)
    stage_3(1)
    stage_2(VECTORS + 1)
    stage_2(VECTORS + 2)
    stage_2(VECTORS)
    stage_4(0)
    stage_4(1)
    stage_3(VECTORS + 1)
    stage_3(VECTORS + 2)
    stage_3(VECTORS)
    stage_4(VECTORS + 1)
    stage_4(VECTORS + 2)
    stage_4(VECTORS)
    encoder_store.wait()
    states_store.wait()
    for n in range(2):
        self_share(n).wait_send()
    for i in range(HALF + 3):
        final_copy(i, 1 - odd).wait_recv()
        final_copy(i, odd).wait_send()
        for a, b in order:
            partner_copy(i, a, b).wait_send()
        for a in range(2):
            second_copy(i, a).wait_send()
        first_copy(i).wait_send()
        for n in range(depth - 1):
            up_copy(i, n).wait_send()


def pack_sums(depth, rows, sums, inner_sum, gv):
    lanes = gv.shape[-1]
    width = sums.shape[1]
    low = sums[...].astype(BF16)
    row = lax.broadcasted_iota(jnp.int32, (VROWS, lanes), 0)
    window_row = lax.broadcasted_iota(jnp.int32, (VROWS, WINDOW), 0)
    inner_low = jnp.zeros((VROWS, WINDOW), F32)
    for at in range(inner_sum.shape[1] // WINDOW):
        piece = inner_sum[:, at * WINDOW : (at + 1) * WINDOW]
        inner_low = jnp.where(window_row == at, piece, inner_low)
    inner_low = inner_low.astype(BF16)
    windows = jnp.concatenate([low[:, i : i + WINDOW] for i in range(0, width, WINDOW)], axis=0)
    count, inner_rows = WINDOW // rows, inner_sum.shape[1] // (4 * depth)
    inner_count = WINDOW // inner_rows
    inner = [
        [
            dot_nn(inner_low, select_lanes(n * inner_rows, part * lanes, inner_rows, lanes))
            for part in range(2)
        ]
        for n in range(inner_count)
    ]
    for n in range(count):
        picked = dot_nn(windows, select_lanes(n * rows, 0, rows, lanes))
        for at in range(width // WINDOW):
            f = at * count + n
            for part in range(2):
                own = picked[at * VROWS : (at + 1) * VROWS] if part == 0 else jnp.zeros_like(row, F32)
                at_inner = f // inner_count
                other = inner[f % inner_count][part][at_inner : at_inner + 1, :]
                gv[part, f // 4, (f // 2) % 2, f % 2] = jnp.where(row == 13, other, own).astype(BF16)


def decode(
    n_fsdp, block_order, length, flat, scale, ctotal, total, feed_sums, inner_sum, units, cq, ck,
    cv, co, gmix, low, encoder, hat, grad, q, k, v, o, states, d1, d2,
):
    rows, width = units.shape[-2:]
    depth = n_fsdp // 4
    row_count = states.shape[0]
    steps = HALF + 3
    dma = pltpu.SemaphoreType.DMA
    vmem = pltpu.VMEM
    any_spec = pl.BlockSpec(memory_space=pl.ANY)
    vmem_spec = pl.BlockSpec(memory_space=pltpu.VMEM)
    smem_spec = pl.BlockSpec(memory_space=pltpu.SMEM)
    block, small = (rows, width), (VROWS, LANES)
    narrow = vmem((row_count, width), BF16)
    wide = vmem((row_count, width), F32)
    both = vmem((2, row_count, width), BF16)
    return pl.pallas_call(
        functools.partial(decode_body, depth),
        in_specs=[smem_spec] * 2 + [vmem_spec] * 6 + [any_spec] * 17,
        out_specs=[any_spec] * 2 + [vmem_spec] * 2,
        out_shape=[
            jax.ShapeDtypeStruct((row_count, width), F32),
            jax.ShapeDtypeStruct((row_count, width), F32),
            jax.ShapeDtypeStruct((UNITS, *block), F32),
            jax.ShapeDtypeStruct((2, *small), F32),
        ],
        scratch_shapes=[
            vmem((HALF + 4, depth, 2, 2, *block), BF16),
            vmem((HALF, 4, depth, *block), BF16),
            vmem((HALF, 2, depth, *block), BF16),
            vmem((HALF, depth, *block), BF16),
            vmem((HALF, depth - 1, *block), BF16),
            vmem((4, width, width), BF16),
            narrow, narrow, wide, both, both, narrow, both, both,
            vmem((2, 2, row_count, width), BF16),
            narrow, narrow, wide, wide,
            vmem((2 * row_count, PAIR), F32),
            vmem((2 * row_count, PAIR), F32),
            vmem((PAIR, 2 * row_count), BF16),
            vmem((VROWS, width), F32),
            vmem((2, depth, 2, 2, *small), BF16),
            vmem((4, depth, *small), BF16),
            vmem((2, depth, *small), BF16),
            vmem((depth, *small), BF16),
            vmem((depth - 1, *small), BF16),
            dma((24,)),
            dma((HALF,)),
            dma((2,)),
            dma((steps, depth - 1)),
            dma((steps, depth - 1)),
            dma((steps,)),
            dma((steps,)),
            dma((steps, 2)),
            dma((steps, 2)),
            dma((steps, 4)),
            dma((steps, 4)),
            dma((steps,)),
            dma((steps,)),
            dma((3,)),
            dma((3,)),
        ],
        compiler_params=pltpu.CompilerParams(
            collective_id=3, has_side_effects=True, vmem_limit_bytes=DECODE_LIMIT
        ),
        name="decode",
    )(
        block_order, length, flat, scale, ctotal, total, feed_sums, inner_sum, units, cq, ck, cv,
        co, gmix, low, encoder, hat, grad, q, k, v, o, states,
        d1.reshape(-1, depth, 2, 2, *block),
        d2.reshape(depth, 2, 2, UNITS - FIRST, *block),
    )


GROUPS = ((0, 1, 2), (3,), (4,), (5, 6), (7,), (8, 9, 10, 11))


VECTOR_GROUPS = ((0, 2), (2, 3), (3, 5), (5, 6), (6, 7), (7, 10), (10, 13))


def lay_out_body(shards, vectors, *outs):
    rows, width = shards.shape[1:]
    for group, target in zip(GROUPS, outs):
        for at, u in enumerate(group):
            target[:, at * width : (at + 1) * width] = shards[u]
    outer = outs[len(GROUPS)]
    for at in range(UNITS - FIRST):
        outer[at * rows : (at + 1) * rows, :] = shards[FIRST + at]
    inner = outs[-1]
    inner[:, :LANES] = vectors[0, 13:14, :]
    inner[:, LANES:] = vectors[1, 13:14, : inner.shape[1] - LANES]
    for (low, high), target in zip(VECTOR_GROUPS, outs[len(GROUPS) + 1 :]):
        target[...] = vectors[0, low:high, :rows]


def lay_out(shards, vectors, inner):
    rows, width = shards.shape[1:]
    shapes = [(rows, width * len(group)) for group in GROUPS] + [((UNITS - FIRST) * rows, width)]
    shapes += [(high - low, rows) for low, high in VECTOR_GROUPS] + [(1, inner)]
    return pl.pallas_call(
        lay_out_body,
        in_specs=[pl.BlockSpec(memory_space=pltpu.VMEM)] * 2,
        out_specs=[pl.BlockSpec(memory_space=pltpu.VMEM)] * len(shapes),
        out_shape=[jax.ShapeDtypeStruct(shape, F32) for shape in shapes],
        name="lay_out",
    )(shards, vectors)


def per_device_wide(
    n_ctx,
    n_fsdp,
    states,
    encoded,
    lengths,
    block_order,
    cotangent,
    self_project,
    self_bias,
    self_output,
    self_shift,
    cross_query,
    cross_keyval,
    cross_bias,
    cross_output,
    cross_shift,
    feed_inner,
    inner_bias,
    feed_outer,
    outer_bias,
    norm_gain,
    norm_shift,
):
    local_rows = states.shape[1]
    width = states.shape[2]
    rows = self_output.shape[0]
    local_blocks = local_rows // QBLK
    core = lax.axis_index("ctx")
    own_order = lax.dynamic_slice_in_dim(block_order, core * local_blocks, local_blocks)
    places = block_order
    spread = lambda array: (lax.all_gather(array, "ctx", axis=0, tiled=True),)
    collect = lambda parts: lax.psum_scatter(
        parts[0], "ctx", scatter_dimension=0, tiled=True
    ).astype(F32)

    vectors = jnp.concatenate(
        [
            self_bias,
            self_shift[None],
            cross_bias,
            cross_shift[None],
            outer_bias[None],
            norm_gain,
            norm_shift,
            inner_bias.reshape(-1, rows),
        ],
        axis=0,
    )
    inner_rows = inner_bias.shape[0] // rows
    count = vectors.shape[0]
    pad = ((0, 2 * VROWS - count), (0, LANES - rows))
    units, w_fo, all_vectors = gather_weights(
        n_fsdp, jnp.pad(vectors, pad).reshape(2, VROWS, LANES), self_project, self_output, cross_query,
        cross_keyval, cross_output, feed_inner, feed_outer,
    )
    all_vectors = jnp.transpose(all_vectors, (1, 0, 2, 3)).reshape(n_fsdp, 2 * VROWS, LANES)
    all_vectors = all_vectors[:, :count, :rows].astype(F32)
    inner_full = all_vectors[:, 13:].reshape(1, -1)
    flat = jnp.transpose(all_vectors, (1, 0, 2)).reshape(count, -1)
    b_q, b_v, b_so, b_cq, b_cv = (flat[i] for i in range(5))

    w_q, w_k, w_v, w_so, w_cq, w_ck, w_cv, w_co = (units[i] for i in range(8))

    inputs = states[0]
    encoder_rows = encoded[0]
    queries = ((dot_nn(inputs, w_q) + b_q) * ATTN_SCALE).astype(BF16)
    own_keys = dot_nn(inputs, w_k).astype(BF16)
    own_values = (dot_nn(inputs, w_v) + b_v).astype(BF16)
    own_cross_keys = dot_nn(encoder_rows, w_ck).astype(BF16)
    own_cross_values = (dot_nn(encoder_rows, w_cv) + b_cv).astype(BF16)
    keys, values = spread(own_keys), spread(own_values)
    cross_keys, cross_values = spread(own_cross_keys), spread(own_cross_values)

    attend = functools.partial(attention_forward, places=places, own_places=own_order, length=lengths)
    self_attended, self_total = attend(True, queries, keys, values)
    self_mixed = self_attended.astype(BF16)
    after_self, norm_back_one = jax.vjp(
        layer_norm, inputs.astype(F32) + dot_nn(self_mixed, w_so) + b_so, flat[7], flat[10]
    )
    after_self_low = after_self.astype(BF16)
    cross_queries = ((dot_nn(after_self_low, w_cq) + b_cq) * ATTN_SCALE).astype(BF16)
    cross_attended, cross_total = attend(False, cross_queries, cross_keys, cross_values)
    output, grad_cross_mixed, grad_two, feed_sums, inner_sum, d_low, d_outer = feed_forward(
        block_order, lengths, cross_attended, after_self, cotangent[0], flat[:16], inner_full, units, w_fo
    )
    attend_back = functools.partial(
        attention_backward, places=places, own_places=own_order, length=lengths
    )
    cross_query_grad, ck_parts, cv_parts = attend_back(
        False, cross_queries, grad_cross_mixed, cross_attended, cross_total, cross_keys, cross_values
    )
    cross_query_low = cross_query_grad.astype(BF16)
    d_cq = dot_tn(after_self_low, cross_query_low).astype(BF16)
    ck_grad, cv_grad = collect(ck_parts), collect(cv_parts)
    ck_low, cv_low = ck_grad.astype(BF16), cv_grad.astype(BF16)
    d_ck = dot_tn(encoder_rows, ck_low).astype(BF16)
    d_cv = dot_tn(encoder_rows, cv_low).astype(BF16)
    grad_encoded = dot_nt(ck_low, w_ck) + dot_nt(cv_low, w_cv)
    grad_one, gain_one, shift_one = norm_back_one(grad_two + dot_nt(cross_query_low, w_cq))
    grad_one_low = grad_one.astype(BF16)
    d_so = dot_tn(self_mixed, grad_one_low).astype(BF16)
    grad_self_mixed = dot_nt(grad_one_low, w_so).astype(BF16)
    query_grad, k_parts, v_parts = attend_back(
        True, queries, grad_self_mixed, self_attended, self_total, keys, values
    )
    query_low = query_grad.astype(BF16)
    key_grad, value_grad = collect(k_parts), collect(v_parts)
    key_low, value_low = key_grad.astype(BF16), value_grad.astype(BF16)
    d_q = dot_tn(inputs, query_low).astype(BF16)
    d_k = dot_tn(inputs, key_low).astype(BF16)
    d_v = dot_tn(inputs, value_low).astype(BF16)
    grad_states = grad_one + dot_nt(query_low, w_q) + dot_nt(key_low, w_k) + dot_nt(value_low, w_v)

    column_sum = lambda array: jnp.sum(array, axis=0)
    grad_vectors = jnp.stack(
        [
            column_sum(query_grad),
            column_sum(value_grad),
            column_sum(grad_one),
            column_sum(cross_query_grad),
            column_sum(cv_grad),
            feed_sums[0],
            feed_sums[1],
            gain_one,
            feed_sums[2],
            feed_sums[3],
            shift_one,
            feed_sums[4],
            feed_sums[5],
        ]
    ).reshape(13, n_fsdp, rows)
    inner_vector = inner_sum.reshape(n_fsdp, inner_rows, rows)
    packed = jnp.concatenate([jnp.transpose(grad_vectors, (1, 0, 2)), inner_vector], axis=1)
    packed = jnp.pad(packed, ((0, 0), *pad)).astype(BF16)
    packed = jnp.transpose(packed.reshape(n_fsdp, 2, VROWS, LANES), (1, 0, 2, 3))

    shards, mine = scatter_gradients(
        n_fsdp, [d_q, d_k, d_v, d_so, d_cq, d_ck, d_cv], d_low, d_outer, packed
    )
    if n_ctx > 2:
        groups = [[c for c in range(n_ctx) if c % 2 == odd] for odd in range(2)]
        total = lambda part: lax.psum(part.astype(BF16), "ctx", axis_index_groups=groups).astype(F32)
        shards, mine = total(shards), total(mine)
    mine = mine.reshape(2 * VROWS, LANES)[:, :rows]
    return (
        output[None],
        grad_states[None],
        grad_encoded[None],
        jnp.concatenate([shards[0], shards[1], shards[2]], axis=1),
        mine[0:2],
        shards[3],
        mine[2],
        shards[4],
        jnp.concatenate([shards[5], shards[6]], axis=1),
        mine[3:5],
        shards[7],
        mine[5],
        jnp.concatenate([shards[8 + i] for i in range(4)], axis=1),
        mine[13 : 13 + inner_rows].reshape(-1),
        shards[12:].reshape(-1, width),
        mine[6],
        mine[7:10],
        mine[10:13],
    )


def per_device(
    n_ctx,
    n_fsdp,
    states,
    encoded,
    lengths,
    block_order,
    cotangent,
    self_project,
    self_bias,
    self_output,
    self_shift,
    cross_query,
    cross_keyval,
    cross_bias,
    cross_output,
    cross_shift,
    feed_inner,
    inner_bias,
    feed_outer,
    outer_bias,
    norm_gain,
    norm_shift,
):
    width = states.shape[2]
    inner = inner_bias.shape[0]
    singles = jnp.concatenate([self_shift, cross_shift, outer_bias, inner_bias])[None]
    (
        units, w_fo, queries, keys, values, cross_queries, cross_keys, cross_values, self_attended,
        self_total, after_self, after_self_low, hat, scale, cross_attended, cross_total, flat, inner_full,
    ) = encode(
        n_fsdp, block_order, lengths, states[0], encoded[0], self_bias, cross_bias, norm_gain, norm_shift,
        singles, self_project, self_output, cross_query, cross_keyval, cross_output, feed_inner, feed_outer,
    )
    output, grad_cross_mixed, grad_two, feed_sums, inner_sum, d_low, d_outer = feed_forward(
        block_order, lengths, cross_attended, after_self, cotangent[0], flat, inner_full,
        units.reshape(FIRST, width, width), w_fo.reshape(-1, width),
    )
    grad_states, grad_encoded, shards, mine = decode(
        n_fsdp, block_order, lengths, flat, scale, cross_total, self_total, feed_sums, inner_sum,
        units, cross_queries, cross_keys, cross_values, cross_attended, grad_cross_mixed, after_self_low,
        encoded[0], hat, grad_two, queries, keys, values, self_attended, states[0], d_low, d_outer,
    )
    (
        d_sp, d_so, d_cq, d_ckv, d_co, d_fi, d_fo, d_self_bias, d_self_shift, d_cross_bias, d_cross_shift,
        d_outer_bias, d_gain, d_shift, d_inner_bias,
    ) = lay_out(shards, mine, inner)
    return (
        output[None],
        grad_states[None],
        grad_encoded[None],
        d_sp,
        d_self_bias,
        d_so,
        d_self_shift.reshape(-1),
        d_cq,
        d_ckv,
        d_cross_bias,
        d_co,
        d_cross_shift.reshape(-1),
        d_fi,
        d_inner_bias.reshape(-1),
        d_fo,
        d_outer_bias.reshape(-1),
        d_gain,
        d_shift,
    )


def solution(mesh):
    return jax.shard_map(
        functools.partial(
            per_device if mesh.shape["ctx"] == 2 else per_device_wide,
            mesh.shape["ctx"],
            mesh.shape["fsdp"],
        ),
        mesh=mesh,
        in_specs=(
            P("fsdp", "ctx", None),
            P("fsdp", "ctx", None),
            P("fsdp"),
            P(),
            P("fsdp", "ctx", None),
            P("fsdp", None),
            P(None, "fsdp"),
            P("fsdp", None),
            P("fsdp"),
            P("fsdp", None),
            P("fsdp", None),
            P(None, "fsdp"),
            P("fsdp", None),
            P("fsdp"),
            P("fsdp", None),
            P("fsdp"),
            P("fsdp", None),
            P("fsdp"),
            P(None, "fsdp"),
            P(None, "fsdp"),
        ),
        out_specs=(
            P("fsdp", "ctx", None),
            P("fsdp", "ctx", None),
            P("fsdp", "ctx", None),
            P("fsdp", None),
            P(None, "fsdp"),
            P("fsdp", None),
            P("fsdp"),
            P("fsdp", None),
            P("fsdp", None),
            P(None, "fsdp"),
            P("fsdp", None),
            P("fsdp"),
            P("fsdp", None),
            P("fsdp"),
            P("fsdp", None),
            P("fsdp"),
            P(None, "fsdp"),
            P(None, "fsdp"),
        ),
        check_vma=False,
    )
```
